32 devices in a mesh: fsdp: 8 (over z, x), tp: 4 (over y, core).
Axes of the slice: x: 2, y: 2, z: 4, core: 2. Of those that a mesh axis runs over, the one named last changes fastest.
Arguments:
- inputs: bfloat16 [32768, 512], P(('fsdp', 'tp')), may hold values from -6 to 6
- segments: int32 [8, 4096], P('fsdp', 'tp'), may hold values from 0 to 20, as said below
- out_grad: bfloat16 [32768, 512], P(('fsdp', 'tp')), may hold values from -6 to 6
- first_gain: bfloat16 [512], replicated, may hold values from 0.5 to 1.5
- first_shift: bfloat16 [512], replicated, may hold values from -3 to 3
- qkv_weight: bfloat16 [512, 3, 512], P('fsdp', None, 'tp'), may hold values from -0.375 to 0.375
- qv_bias: bfloat16 [2, 512], replicated, may hold values from -3 to 3
- out_weight: bfloat16 [512, 512], P('tp', 'fsdp'), may hold values from -1 to 1
- out_bias: bfloat16 [512], replicated, may hold values from -3 to 3
- second_gain: bfloat16 [512], replicated, may hold values from 0.5 to 1.5
- second_shift: bfloat16 [512], replicated, may hold values from -3 to 3
- fc_weight: bfloat16 [512, 2048], P('fsdp', 'tp'), may hold values from -0.25 to 0.25
- fc_bias: bfloat16 [2048], replicated, may hold values from -3 to 3
- proj_weight: bfloat16 [2048, 512], P('tp', 'fsdp'), may hold values from -0.125 to 0.125
- proj_bias: bfloat16 [512], replicated, may hold values from -3 to 3
Outputs:
- layer_out: bfloat16 [32768, 512], P(('fsdp', 'tp'))
- input_grad: bfloat16 [32768, 512], P(('fsdp', 'tp'))
- first_gain_grad: float32 [512], replicated
- first_shift_grad: float32 [512], replicated
- qkv_weight_grad: float32 [512, 3, 512], P('fsdp', None, 'tp')
- qv_bias_grad: float32 [2, 512], replicated
- out_weight_grad: float32 [512, 512], P('tp', 'fsdp')
- out_bias_grad: float32 [512], replicated
- second_gain_grad: float32 [512], replicated
- second_shift_grad: float32 [512], replicated
- fc_weight_grad: float32 [512, 2048], P('fsdp', 'tp')
- fc_bias_grad: float32 [2048], replicated
- proj_weight_grad: float32 [2048, 512], P('tp', 'fsdp')
- proj_bias_grad: float32 [512], replicated
The draws below stay inside these ranges and needn't reach their ends.
Inputs may be any that keep to these rules, and one draw needn't show every extreme that they name: `segments`: along each sequence the numbers start at 1 and rise by one from document to document; each document has 200 to 2000 tokens, and in one sequence every document has exactly 200; 0 marks padding, which only follows the last whole document of a sequence.
All inputs are finite; a program needn't handle non-finite values.
Results may differ from the reference program's by a relative error of at most 0.018.
The reference program's roundings to bfloat16 on the way count: a program that leaves them out, or rounds other values in their place, can miss the bound.
Values may be sent and summed in bfloat16 or wider, within the bound.
A program may use at most 128 MiB of HBM per device.

```python
import jax
import jax.numpy as jnp
from jax import lax

D = 512
H = 8
HD = 64
FF = 2048
SEQ_LEN = 4096
DOC_MIN = 200
DOC_MAX = 2000
TOKENS = 32768
N_FSDP = 8


def draw_segments(key, part):
    doc_slots = SEQ_LEN // DOC_MIN + 1
    length_key = jax.random.fold_in(key, 11)
    row_key = jax.random.fold_in(key, 23)
    lengths = jax.random.randint(length_key, (N_FSDP, doc_slots), DOC_MIN, DOC_MAX + 1, dtype=jnp.int32)
    short_row = jax.random.randint(row_key, (), 0, N_FSDP, dtype=jnp.int32)
    row_ids = jnp.arange(N_FSDP, dtype=jnp.int32)
    lengths = jnp.where((row_ids == short_row)[:, None], jnp.int32(DOC_MIN), lengths).astype(jnp.int32)
    doc_ends = jnp.cumsum(lengths, axis=1).astype(jnp.int32)
    positions = jnp.arange(SEQ_LEN, dtype=jnp.int32)
    before = jnp.sum((doc_ends[:, None, :] <= positions[None, :, None]).astype(jnp.int32), axis=2)
    own_end = jnp.take_along_axis(doc_ends, before, axis=1)
    return jnp.where(own_end <= SEQ_LEN, before + 1, 0).astype(jnp.int32)


def spiked(entries, stream_key, source, target, blocks, factor):
    def block_of(axis_at):
        return (jnp.arange(entries.shape[axis_at]) // (entries.shape[axis_at] // blocks)).reshape((-1,) + (1,) * (entries.ndim - 1 - axis_at))

    near = jax.random.permutation(stream_key, blocks)[block_of(target)]
    second = (block_of(target) + blocks // 2) % blocks
    return jnp.where((block_of(source) == near) | (block_of(source) == second), factor * entries, entries)


def block_levels(own_key, shape, split, low, high):
    loudness, own = 1.0, jax.random.fold_in(own_key, 6)
    for position, parts in split:
        heights = jnp.exp(jax.random.uniform(jax.random.fold_in(own, position), (parts,), jnp.float32, low / len(split), high / len(split)))
        loudness = loudness * jnp.repeat(heights, shape[position] // parts).reshape([-1 if axis == position else 1 for axis in range(len(shape))])
    return loudness


def noise(key, extent, deviation, most, cuts=(), held_as=jnp.bfloat16):
    level = block_levels(key, extent, cuts, -0.22, 0.18) if cuts else 1.0
    array = jax.random.normal(key, extent, jnp.float32) * deviation * level
    return jnp.minimum(jnp.maximum(array, -most), most).astype(held_as)


def gaussian_with(own_key, dims, scale, reach, cuts, heavy, kind=jnp.bfloat16):
    entries = scale * jax.random.normal(own_key, dims, jnp.float32)
    if cuts:
        entries = entries * block_levels(own_key, dims, cuts, -0.22, 0.18)
    return jnp.clip(spiked(entries, jax.random.fold_in(own_key, 3), *heavy), -reach, reach).astype(kind)


def setup_inputs(seed: int = 0) -> dict:
    splits = jax.random.split(jax.random.key(seed), 16)
    return {
        "inputs": gaussian_with(splits[0], (TOKENS, D), 1.0, 6.0, ((0, 32),), (0, 1, 32, 2.75)),
        "segments": draw_segments(jax.random.fold_in(splits[15], 71), 0),
        "out_grad": gaussian_with(splits[2], (TOKENS, D), 1.0, 6.0, ((0, 32),), (0, 1, 32, 2.75)),
        "first_gain": jnp.clip(1.0 + 0.1 * jax.random.normal(splits[3], (D,), jnp.float32), 0.5, 1.5).astype(jnp.bfloat16),
        "first_shift": noise(splits[4], (D,), 0.3, 3.0),
        "qkv_weight": noise(splits[5], (D, 3, D), (D // 2) ** -0.5, 0.375, ((0, 8), (2, 4))),
        "qv_bias": noise(splits[6], (2, D), 0.3, 3.0),
        "out_weight": noise(splits[7], (D, D), (D // 16) ** -0.5, 1.0, ((0, 4), (1, 8))),
        "out_bias": noise(splits[8], (D,), 0.3, 3.0),
        "second_gain": jnp.clip(1.0 + 0.1 * jax.random.normal(splits[9], (D,), jnp.float32), 0.5, 1.5).astype(jnp.bfloat16),
        "second_shift": noise(splits[10], (D,), 0.3, 3.0),
        "fc_weight": noise(splits[11], (D, FF), D ** -0.5, 0.25, ((0, 8), (1, 4))),
        "fc_bias": noise(splits[12], (FF,), 0.3, 3.0),
        "proj_weight": noise(splits[13], (FF, D), FF ** -0.5, 0.125, ((0, 4), (1, 8))),
        "proj_bias": noise(splits[14], (D,), 0.3, 3.0),
    }


@jax.custom_vjp
def low(v):
    return lax.optimization_barrier(v.astype(jnp.bfloat16)).astype(jnp.float32)

@jax.custom_vjp
def low_back(v):
    return v

def low_keep(v):
    return (low(v), None)

def low_pass(kept, grad):
    return (grad,)

def back_keep(v):
    return (v, None)

def back_low(kept, grad):
    return (low(grad),)
low.defvjp(low_keep, low_pass)
low_back.defvjp(back_keep, back_low)
epsilon = 1e-05
gelu_slope = 1.702
masked_score = -1e+30
highest = lax.Precision.HIGHEST

def norm_rows(values_in, gain_vec, shift_vec):
    mean_row = lax.optimization_barrier(jnp.mean(values_in, axis=-1, keepdims=True))
    centred = values_in - mean_row
    inverse = lax.rsqrt(lax.optimization_barrier(jnp.mean(centred * centred, axis=-1, keepdims=True)) + epsilon)
    return centred * inverse * gain_vec + shift_vec

def allowed(seg_query, pos_query, seg_key, pos_key):
    same_doc = seg_query[:, None] == seg_key[None, :]
    causal = pos_key[None, :] <= pos_query[:, None]
    living = (seg_query[:, None] != 0) | (pos_key[None, :] == pos_query[:, None])
    return same_doc & causal & living

def both_ways(value):
    return low_back(low(value))

def sequence_forward(resid_in, seg_seq, params):
    first_gain, first_shift, qkv_weight, qv_bias, out_weight, out_bias, second_gain, second_shift, fc_weight, fc_bias, proj_weight, proj_bias = params
    seq_rows = resid_in.shape[0]
    block_rows = min(512, seq_rows)
    blocks = seq_rows // block_rows
    normed_one = low(norm_rows(resid_in, first_gain, first_shift))
    projected = jnp.einsum('sd,dje->sje', normed_one, qkv_weight, precision=highest)
    queries = both_ways(projected[:, 0] + qv_bias[0]).reshape(seq_rows, H, HD)
    keys_all = both_ways(projected[:, 1]).reshape(seq_rows, H, HD)
    values_all = both_ways(projected[:, 2] + qv_bias[1]).reshape(seq_rows, H, HD)
    positions = jnp.arange(seq_rows, dtype=jnp.int32)

    def one_block(q_blk, seg_blk, pos_blk, key_arr, value_arr):
        raw_scores = jnp.einsum('qhe,khe->hqk', q_blk, key_arr, precision=highest)
        scores = low_back(raw_scores) * HD ** (-0.5)
        allowed_mask = allowed(seg_blk, pos_blk, seg_seq, positions)
        scores = jnp.where(allowed_mask[None], scores, masked_score)
        log_norm = jax.nn.logsumexp(scores, axis=-1, keepdims=True)
        softmax_w = low(jnp.exp(scores - log_norm))
        return jnp.einsum('hqk,khe->qhe', softmax_w, value_arr, precision=highest)
    checked = jax.checkpoint(one_block)
    attn_raw = lax.map(lambda pieces: checked(pieces[0], pieces[1], pieces[2], keys_all, values_all), (queries.reshape(blocks, block_rows, H, HD), seg_seq.reshape(blocks, block_rows), positions.reshape(blocks, block_rows)))
    live_rows = (seg_seq != 0).astype(jnp.float32)
    attn_out = both_ways(attn_raw.reshape(seq_rows, H * HD) * live_rows[:, None])
    branch = low_back(jnp.dot(attn_out, out_weight, precision=highest) + out_bias)
    hidden = resid_in + branch
    normed_two = low(norm_rows(hidden, second_gain, second_shift))
    pre_act = low_back(jnp.dot(normed_two, fc_weight, precision=highest) + fc_bias)
    act_low = low(pre_act * jax.nn.sigmoid(gelu_slope * pre_act))
    return hidden + jnp.dot(act_low, proj_weight, precision=highest) + proj_bias

def reference(inputs, segments, out_grad, first_gain, first_shift, qkv_weight, qv_bias, out_weight, out_bias, second_gain, second_shift, fc_weight, fc_bias, proj_weight, proj_bias):
    params = tuple((item.astype(jnp.float32) for item in (first_gain, first_shift, qkv_weight, qv_bias, out_weight, out_bias, second_gain, second_shift, fc_weight, fc_bias, proj_weight, proj_bias)))
    rows_in = inputs.astype(jnp.float32).reshape(N_FSDP, SEQ_LEN, D)
    grads_in = out_grad.astype(jnp.float32).reshape(N_FSDP, SEQ_LEN, D)
    zero_grads = jax.tree.map(jnp.zeros_like, params)

    def one_sequence(running, pieces):
        resid_in, seg_seq, grad_seq = pieces

        def forward_here(resid_arg, param_arg):
            return sequence_forward(resid_arg, seg_seq, param_arg)
        result, pullback = jax.vjp(forward_here, resid_in, params)
        grad_resid, grad_params = pullback(grad_seq)
        running = jax.tree.map(lambda left, right: left + right, running, grad_params)
        return (running, (result, grad_resid))
    totals, (results, resid_grads) = lax.scan(one_sequence, zero_grads, (rows_in, segments, grads_in))
    layer_out = results.reshape(TOKENS, D).astype(jnp.bfloat16)
    input_grad = resid_grads.reshape(TOKENS, D).astype(jnp.bfloat16)
    return (layer_out, input_grad, totals[0], totals[1], totals[2], totals[3], totals[4], totals[5], totals[6], totals[7], totals[8], totals[9], totals[10], totals[11])
```

```python
import functools

import jax
import jax.numpy as jnp
from jax import lax
from jax.experimental import pallas as pl
from jax.experimental.pallas import tpu as pltpu
from jax.sharding import PartitionSpec as P

HD = 64
FF = 2048


epsilon = 1e-05
gelu_slope = 1.702
VMEM_LIMIT = 60 << 20


def split_up(value, dim, peers):
    dims = value.shape
    pieces = value.reshape(*dims[:dim], peers, dims[dim] // peers, *dims[dim + 1 :])
    return jnp.moveaxis(pieces, dim, 0)


def sent_and_summed(value, axis, dim):
    pieces = split_up(value, dim, lax.axis_size(axis))
    arrived = lax.all_to_all(pieces, axis, split_axis=0, concat_axis=0, tiled=True)
    return arrived.astype(jnp.float32).sum(axis=0)


def layer_norm(values_in, gain_vec, shift_vec):
    mean_row = jnp.mean(values_in, axis=-1, keepdims=True)
    centred = values_in - mean_row
    inverse = lax.rsqrt(jnp.mean(centred * centred, axis=-1, keepdims=True) + epsilon)
    normed = centred * inverse
    return (normed * gain_vec + shift_vec, normed, inverse)


def norm_back(grad_out, normed, inverse, gain_vec):
    scaled = grad_out * gain_vec
    grad_in = inverse * (
        scaled
        - jnp.mean(scaled, axis=-1, keepdims=True)
        - normed * jnp.mean(scaled * normed, axis=-1, keepdims=True)
    )
    return (grad_in, jnp.sum(grad_out * normed, axis=0), jnp.sum(grad_out, axis=0))


f32 = jnp.float32
bf16 = jnp.bfloat16
LOG2E = 1.4426950408889634
BLOCK = 512
TRANSPOSED = (((1,), (1,)), ((), ()))


def dot_t(left, right):
    return lax.dot_general(left, right, TRANSPOSED, preferred_element_type=f32)


def dot_n(left, right):
    return jnp.dot(left, right, preferred_element_type=f32)


def three_parts(value):
    top = value.astype(bf16)
    rest = value - top.astype(f32)
    mid = rest.astype(bf16)
    return top, mid, (rest - mid.astype(f32)).astype(bf16)


def diagonal_mask(start_ref, row_at, size):
    key_pos = lax.broadcasted_iota(jnp.int32, (size, 1), 0)
    query_pos = lax.broadcasted_iota(jnp.int32, (1, size), 1)
    first = start_ref[0:1, pl.ds(row_at, size)] - row_at
    return (key_pos >= first) & (key_pos <= query_pos)


def attend_kernel(
    low_ref, qa_ref, ka_ref, vt_ref, start_ref, out_ref, qb_ref, s0, s1, a0, a1, *, size, blocks
):
    score_bufs, acc_bufs = (s0, s1), (a0, a1)
    heads = range(qa_ref.shape[0])
    lane = lax.broadcasted_iota(jnp.int32, (size, 128), 1)

    def query_block(i, carry):
        row_at = pl.multiple_of(i * size, size)

        def score(h, j, top, diag):
            keys = ka_ref[h, pl.ds(pl.multiple_of(j * size, size), size), :]
            s = dot_t(keys, qa_ref[h, pl.ds(row_at, size), :])
            if diag:
                s = jnp.where(diagonal_mask(start_ref, row_at, size), s, -3e38)
            score_bufs[h][...] = s
            col_max = jnp.max(s, axis=0, keepdims=True)
            return col_max if top is None else jnp.maximum(top, col_max)

        def gather_values(h, j, old, new, first):
            p = jnp.exp2(score_bufs[h][...] * LOG2E - new * LOG2E).astype(bf16)
            part = dot_n(vt_ref[h, :, pl.ds(pl.multiple_of(j * size, size), size)], p)
            if first:
                acc_bufs[h][...] = part
            else:
                acc_bufs[h][...] = acc_bufs[h][...] * jnp.exp2((old - new) * LOG2E) + part

        low = low_ref[i]
        m0 = score(0, i, None, True)
        m1 = score(1, i, None, True)
        gather_values(0, i, None, m0, True)
        m0n = score(0, jnp.minimum(low, i), m0, False)
        gather_values(1, i, None, m1, True)

        def body(j, c):
            m0, m0n, m1 = c
            m1n = score(1, j, m1, False)
            gather_values(0, j, m0, m0n, False)
            m0nn = score(0, jnp.minimum(j + 1, blocks - 1), m0n, False)
            gather_values(1, j, m1, m1n, False)
            return m0n, m0nn, m1n

        m0, _, m1 = lax.fori_loop(low, i, body, (m0, m0n, m1))
        for h, top in ((0, m0), (1, m1)):
            total = acc_bufs[h][64:65, :]
            out = acc_bufs[h][0:64, :] / total
            out_ref[pl.ds(row_at, size), 64 * h : 64 * h + 64] = out.T.astype(out_ref.dtype)
            norm = jnp.broadcast_to(-(top + jnp.log(total)), (8, size)).T[:, 0:1]
            n0, n1, n2 = three_parts(norm)
            rows = qa_ref[h, pl.ds(row_at, size), :]
            rows = jnp.where(lane == 96, n0, jnp.where(lane == 97, n1, jnp.where(lane == 98, n2, rows)))
            qb_ref[h, pl.ds(row_at, size), :] = rows
        return carry

    lax.fori_loop(0, blocks, query_block, 0)


def attend(low, qa, ka, vt, start, size):
    heads, rows, _ = qa.shape
    vmem = pl.BlockSpec(memory_space=pltpu.VMEM)
    return pl.pallas_call(
        functools.partial(attend_kernel, size=size, blocks=rows // size),
        grid_spec=pltpu.PrefetchScalarGridSpec(
            num_scalar_prefetch=1,
            grid=(),
            in_specs=[vmem] * 4,
            out_specs=[vmem] * 2,
            scratch_shapes=[pltpu.VMEM((size, size), f32)] * heads
            + [pltpu.VMEM((vt.shape[1], size), f32)] * heads,
        ),
        out_shape=[
            jax.ShapeDtypeStruct((rows, HD * heads), bf16),
            jax.ShapeDtypeStruct(qa.shape, bf16),
        ],
        compiler_params=pltpu.CompilerParams(vmem_limit_bytes=VMEM_LIMIT),
        cost_estimate=pl.CostEstimate(
            flops=rows * rows * HD * heads, bytes_accessed=8 << 20, transcendentals=rows * rows
        ),
        name="attend",
    )(low, qa, ka, vt, start)


def attend_back_kernel(
    low_ref, qb_ref, ka_ref, va_ref, kt_ref, g_ref, o_ref, start_ref, grad_ref,
    ga_ref, dk_ref, dv_ref, q0, q1, *, size, blocks
):
    query_accs = (q0, q1)
    lane = lax.broadcasted_iota(jnp.int32, (size, 64), 1)

    def query_block(i, carry):
        row_at = pl.multiple_of(i * size, size)
        g_rows = g_ref[pl.ds(row_at, size), :]
        product = g_rows.astype(f32) * o_ref[pl.ds(row_at, size), :].astype(f32)
        for h in range(2):
            cols = slice(64 * h, 64 * h + 64)
            n0, n1, n2 = three_parts(-jnp.sum(product[:, cols], axis=1, keepdims=True))
            zero = jnp.zeros((size, 64), bf16)
            extra = jnp.where(lane == 0, n0, jnp.where(lane == 1, n1, jnp.where(lane == 2, n2, zero)))
            ga_ref[h] = jnp.concatenate([g_rows[:, cols], extra], axis=1)

        def block(h, j, diag):
            key_at = pl.multiple_of(j * size, size)
            keys = ka_ref[h, pl.ds(key_at, size), :]
            q_rows = qb_ref[h, pl.ds(row_at, size), :]
            g_head = ga_ref[h]
            s = dot_t(keys, q_rows)
            if diag:
                s = jnp.where(diagonal_mask(start_ref, row_at, size), s, -3e38)
            p = jnp.exp2(s * LOG2E)
            dp = dot_t(va_ref[h, pl.ds(key_at, size), :], g_head)
            ds = (p * dp).astype(bf16)
            dv = dot_n(p.astype(bf16), g_head[:, 0:64])
            dk = dot_n(ds, q_rows[:, 0:64])
            dq = dot_n(kt_ref[h, :, pl.ds(key_at, size)], ds)
            if diag:
                dv_ref[h, pl.ds(key_at, size), :] = dv
                dk_ref[h, pl.ds(key_at, size), :] = dk
                query_accs[h][...] = dq
            else:
                dv_ref[h, pl.ds(key_at, size), :] += dv
                dk_ref[h, pl.ds(key_at, size), :] += dk
                query_accs[h][...] += dq

        block(0, i, True)
        block(1, i, True)

        def body(j, c):
            block(0, j, False)
            block(1, j, False)
            return c

        lax.fori_loop(low_ref[i], i, body, 0)
        both = jnp.concatenate([query_accs[0][...], query_accs[1][...]], axis=0) * HD ** (-0.5)
        grad_ref[pl.ds(row_at, size), 0:128] = both.T.astype(bf16)
        return carry

    lax.fori_loop(0, blocks, query_block, 0)

    def finish(i, carry):
        row_at = pl.multiple_of(i * size, size)
        for ref, at in ((dk_ref, 128), (dv_ref, 256)):
            both = jnp.concatenate([ref[0, pl.ds(row_at, size), :], ref[1, pl.ds(row_at, size), :]], axis=1)
            grad_ref[pl.ds(row_at, size), at : at + 128] = both.astype(bf16)
        return carry

    lax.fori_loop(0, blocks, finish, 0)


def attend_back(low, qb, ka, va, kt, g, o, start, size):
    heads, rows, _ = qb.shape
    vmem = pl.BlockSpec(memory_space=pltpu.VMEM)
    return pl.pallas_call(
        functools.partial(attend_back_kernel, size=size, blocks=rows // size),
        grid_spec=pltpu.PrefetchScalarGridSpec(
            num_scalar_prefetch=1,
            grid=(),
            in_specs=[vmem] * 7,
            out_specs=vmem,
            scratch_shapes=[
                pltpu.VMEM((heads, size, 128), bf16),
                pltpu.VMEM((heads, rows, HD), f32),
                pltpu.VMEM((heads, rows, HD), f32),
            ]
            + [pltpu.VMEM((HD, size), f32)] * heads,
        ),
        out_shape=jax.ShapeDtypeStruct((rows, 3 * HD * heads), bf16),
        compiler_params=pltpu.CompilerParams(vmem_limit_bytes=VMEM_LIMIT),
        cost_estimate=pl.CostEstimate(
            flops=2 * rows * rows * HD * heads, bytes_accessed=16 << 20, transcendentals=rows * rows
        ),
        name="attend_back",
    )(low, qb, ka, va, kt, g, o, start)


def with_extras(head_rows, seg_all):
    rows = seg_all.shape[0]
    number = jnp.arange(32, dtype=jnp.int32)[None, :]
    same = seg_all[:, None] == number
    tail = jnp.zeros((rows, 32), bf16)
    ones = jnp.zeros((rows, 32), bf16).at[:, 0:3].set(1)
    other = jnp.where(same, 0.0, -1e30).astype(bf16)
    own = same.astype(bf16)
    queries, keys, values = head_rows
    heads = queries.shape[1] // HD
    scaled = (queries.astype(f32) * HD ** (-0.5)).astype(bf16)

    def put(rows_in, *more):
        return jnp.stack(
            [
                jnp.concatenate([rows_in[:, HD * h : HD * h + HD], *more], axis=1)
                for h in range(heads)
            ]
        )

    qa = put(scaled, other, tail)
    ka = put(keys, own, ones)
    va = put(values, ones, tail)
    vt = jnp.swapaxes(va[:, :, 0:80], 1, 2)
    kt = jnp.swapaxes(ka[:, :, 0:HD], 1, 2)
    return qa, ka, va, vt, kt


def document_starts(seg_all):
    positions = jnp.arange(seg_all.shape[0], dtype=jnp.int32)
    number = jnp.arange(32, dtype=jnp.int32)[:, None]
    before = jnp.sum(((seg_all > 0) & (seg_all < number)).astype(jnp.int32), axis=1)
    own = jnp.sum(jnp.where(seg_all == number, before[:, None], 0), axis=0)
    return jnp.where(seg_all == 0, positions, own)


def local(
    inputs,
    segments,
    out_grad,
    first_gain,
    first_shift,
    qkv_weight,
    qv_bias,
    out_weight,
    out_bias,
    second_gain,
    second_shift,
    fc_weight,
    fc_bias,
    proj_weight,
    proj_bias,
):
    tp_index = lax.axis_index("tp")
    qkv_full, out_full, fc_full, proj_full = (
        lax.all_gather(qkv_weight, "fsdp", axis=0, tiled=True),
        lax.all_gather(out_weight, "fsdp", axis=1, tiled=True),
        lax.all_gather(fc_weight, "fsdp", axis=0, tiled=True),
        lax.all_gather(proj_weight, "fsdp", axis=1, tiled=True),
    )
    model_width = inputs.shape[1]
    head_cols = qkv_full.shape[2]
    hidden_cols = fc_full.shape[1]
    resid_in = inputs.astype(jnp.float32)
    normed_one, hat_one, inv_one = layer_norm(
        resid_in, first_gain.astype(jnp.float32), first_shift.astype(jnp.float32)
    )
    lowered_one = normed_one.astype(jnp.bfloat16)
    seq_normed, seg_rows = (
        lax.all_gather(lowered_one, "tp", axis=0, tiled=True),
        lax.all_gather(segments, "tp", axis=1, tiled=True),
    )
    seg_all = seg_rows[0]
    seq_rows = seq_normed.shape[0]
    projected = jnp.einsum("sd,dje->sje", seq_normed, qkv_full, preferred_element_type=jnp.float32)
    bias_here = lax.dynamic_slice_in_dim(qv_bias, tp_index * head_cols, head_cols, 1).astype(
        jnp.float32
    )
    queries = (projected[:, 0] + bias_here[0]).astype(bf16)
    keys_all = projected[:, 1].astype(bf16)
    values_all = (projected[:, 2] + bias_here[1]).astype(bf16)
    live_rows = (seg_all != 0).astype(bf16)
    start = document_starts(seg_all)
    size = min(BLOCK, seq_rows)
    low = start[::size] // size
    start_rows = jnp.broadcast_to(start[None], (8, seq_rows))
    qa, ka, va, vt, kt = with_extras((queries, keys_all, values_all), seg_all)
    raw_out, qb = attend(low, qa, ka, vt, start_rows, size)
    attn_low = raw_out * live_rows[:, None]
    attn_sum = lax.psum_scatter(
        jnp.dot(attn_low, out_full, preferred_element_type=jnp.float32).astype(jnp.bfloat16),
        "tp",
        scatter_dimension=0,
        tiled=True,
    ).astype(jnp.float32)
    hidden = resid_in + attn_sum + out_bias.astype(jnp.float32)
    normed_two, hat_two, inv_two = layer_norm(
        hidden, second_gain.astype(jnp.float32), second_shift.astype(jnp.float32)
    )
    lowered_two = normed_two.astype(jnp.bfloat16)
    mlp_in = lax.all_gather(lowered_two, "tp", axis=0, tiled=True)
    fc_bias_here = lax.dynamic_slice_in_dim(fc_bias, tp_index * hidden_cols, hidden_cols, 0)
    pre_act = jnp.dot(mlp_in, fc_full, preferred_element_type=jnp.float32) + fc_bias_here.astype(
        jnp.float32
    )
    sigmoid_pre = jax.nn.sigmoid(gelu_slope * pre_act)
    act_low = (pre_act * sigmoid_pre).astype(jnp.bfloat16)
    mlp_sum = lax.psum_scatter(
        jnp.dot(act_low, proj_full, preferred_element_type=jnp.float32).astype(jnp.bfloat16),
        "tp",
        scatter_dimension=0,
        tiled=True,
    ).astype(jnp.float32)
    grad_rows = lax.all_gather(out_grad, "tp", axis=0, tiled=True)
    layer_out = (hidden + mlp_sum + proj_bias.astype(jnp.float32)).astype(jnp.bfloat16)
    proj_grad = jnp.einsum("sf,sd->fd", act_low, grad_rows, preferred_element_type=jnp.float32)
    grad_act = jnp.einsum("sd,fd->sf", grad_rows, proj_full, preferred_element_type=jnp.float32)
    grad_pre = grad_act * (sigmoid_pre + gelu_slope * pre_act * sigmoid_pre * (1.0 - sigmoid_pre))
    grad_pre_low = grad_pre.astype(jnp.bfloat16)
    fc_grad = jnp.einsum("sd,sf->df", mlp_in, grad_pre_low, preferred_element_type=jnp.float32)
    fc_bias_part = jnp.sum(grad_pre_low.astype(jnp.float32), axis=0)
    grad_normed_two = lax.psum_scatter(
        jnp.einsum("sf,df->sd", grad_pre_low, fc_full, preferred_element_type=jnp.float32).astype(
            jnp.bfloat16
        ),
        "tp",
        scatter_dimension=0,
        tiled=True,
    ).astype(jnp.float32)
    fc_bias_full = lax.dynamic_update_slice_in_dim(
        jnp.zeros((FF,), jnp.float32), fc_bias_part, tp_index * hidden_cols, 0
    )
    resid_grad = out_grad.astype(jnp.float32)
    grad_hidden_ln, second_gain_part, second_shift_part = norm_back(
        grad_normed_two, hat_two, inv_two, second_gain.astype(jnp.float32)
    )
    grad_hidden = resid_grad + grad_hidden_ln
    grad_hidden_low = grad_hidden.astype(jnp.bfloat16)
    out_bias_part = jnp.sum(grad_hidden_low.astype(jnp.float32), axis=0)
    proj_bias_part = jnp.sum(resid_grad, axis=0)
    seq_grad = lax.all_gather(grad_hidden_low, "tp", axis=0, tiled=True)
    out_w_grad = jnp.einsum("sc,sd->cd", attn_low, seq_grad, preferred_element_type=jnp.float32)
    grad_attn = jnp.einsum("sd,cd->sc", seq_grad, out_full, preferred_element_type=jnp.float32)
    grad_attn_low = grad_attn.astype(bf16) * live_rows[:, None]
    grad_qkv = attend_back(low, qb, ka, va, kt, grad_attn_low, raw_out, start_rows, size).reshape(
        seq_rows, 3, head_cols
    )
    qkv_w_grad = jnp.einsum("sd,sje->dje", seq_normed, grad_qkv, preferred_element_type=jnp.float32)
    qv_part = jnp.sum(grad_qkv[:, 0::2].astype(jnp.float32), axis=0)
    grad_normed_one = lax.psum_scatter(
        jnp.einsum("sje,dje->sd", grad_qkv, qkv_full, preferred_element_type=jnp.float32).astype(
            jnp.bfloat16
        ),
        "tp",
        scatter_dimension=0,
        tiled=True,
    ).astype(jnp.float32)
    qv_full = lax.dynamic_update_slice_in_dim(
        jnp.zeros((2, model_width), jnp.float32), qv_part, tp_index * head_cols, 1
    )
    grad_in_ln, first_gain_part, first_shift_part = norm_back(
        grad_normed_one, hat_one, inv_one, first_gain.astype(jnp.float32)
    )
    input_grad = (grad_hidden + grad_in_ln).astype(jnp.bfloat16)
    qkv_w_grad, out_w_grad, fc_grad, proj_grad = (
        sent_and_summed(qkv_w_grad.astype(jnp.bfloat16), "fsdp", 0),
        sent_and_summed(out_w_grad.astype(jnp.bfloat16), "fsdp", 1),
        sent_and_summed(fc_grad.astype(jnp.bfloat16), "fsdp", 0),
        sent_and_summed(proj_grad.astype(jnp.bfloat16), "fsdp", 1),
    )
    (
        first_gain_grad,
        first_shift_grad,
        qv_bias_grad,
        out_bias_grad,
        second_gain_grad,
        second_shift_grad,
        fc_bias_grad,
        proj_bias_grad,
    ) = lax.psum(
        (
            first_gain_part,
            first_shift_part,
            qv_full,
            out_bias_part,
            second_gain_part,
            second_shift_part,
            fc_bias_full,
            proj_bias_part,
        ),
        ("fsdp", "tp"),
    )
    return (
        layer_out,
        input_grad,
        first_gain_grad,
        first_shift_grad,
        qkv_w_grad,
        qv_bias_grad,
        out_w_grad,
        out_bias_grad,
        second_gain_grad,
        second_shift_grad,
        fc_grad,
        fc_bias_grad,
        proj_grad,
        proj_bias_grad,
    )


def solution(mesh):
    return jax.shard_map(
        local,
        mesh=mesh,
        in_specs=(
            P(("fsdp", "tp"), None),
            P("fsdp", "tp"),
            P(("fsdp", "tp"), None),
            P(),
            P(),
            P("fsdp", None, "tp"),
            P(),
            P("tp", "fsdp"),
            P(),
            P(),
            P(),
            P("fsdp", "tp"),
            P(),
            P("tp", "fsdp"),
            P(),
        ),
        out_specs=(
            P(("fsdp", "tp"), None),
            P(("fsdp", "tp"), None),
            P(),
            P(),
            P("fsdp", None, "tp"),
            P(),
            P("tp", "fsdp"),
            P(),
            P(),
            P(),
            P("fsdp", "tp"),
            P(),
            P("tp", "fsdp"),
            P(),
        ),
        check_vma=False,
    )
```

```python
import functools

import jax
import jax.numpy as jnp
from jax import lax
from jax.experimental import pallas as pl
from jax.experimental.pallas import tpu as pltpu
from jax.sharding import PartitionSpec as P

HD = 64
VMEM_LIMIT = 60 << 20
epsilon = 1e-05
gelu_slope = 1.702


def layer_norm(values_in, gain_vec, shift_vec):
    mean_row = jnp.mean(values_in, axis=-1, keepdims=True)
    centred = values_in - mean_row
    inverse = lax.rsqrt(jnp.mean(centred * centred, axis=-1, keepdims=True) + epsilon)
    normed = centred * inverse
    return (normed * gain_vec + shift_vec, normed, inverse)


def norm_back(grad_out, normed, inverse, gain_vec):
    scaled = grad_out * gain_vec
    grad_in = inverse * (
        scaled
        - jnp.mean(scaled, axis=-1, keepdims=True)
        - normed * jnp.mean(scaled * normed, axis=-1, keepdims=True)
    )
    return (grad_in, jnp.sum(grad_out * normed, axis=0), jnp.sum(grad_out, axis=0))


f32 = jnp.float32
bf16 = jnp.bfloat16
LOG2E = 1.4426950408889634
BLOCK = 512
TRANSPOSED = (((1,), (1,)), ((), ()))


def dot_t(left, right):
    return lax.dot_general(left, right, TRANSPOSED, preferred_element_type=f32)


def dot_n(left, right):
    return jnp.dot(left, right, preferred_element_type=f32)


def three_parts(value):
    top = value.astype(bf16)
    rest = value - top.astype(f32)
    mid = rest.astype(bf16)
    return top, mid, (rest - mid.astype(f32)).astype(bf16)


def diagonal_mask(start_ref, row_at, size):
    key_pos = lax.broadcasted_iota(jnp.int32, (size, 1), 0)
    query_pos = lax.broadcasted_iota(jnp.int32, (1, size), 1)
    first = start_ref[0:1, pl.ds(row_at, size)] - row_at
    return (key_pos >= first) & (key_pos <= query_pos)


def attend_kernel(
    low_ref, qa_ref, ka_ref, vt_ref, start_ref, out_ref, qb_ref, s0, s1, a0, a1, *, size, blocks
):
    score_bufs, acc_bufs = (s0, s1), (a0, a1)
    heads = range(qa_ref.shape[0])
    lane = lax.broadcasted_iota(jnp.int32, (size, 128), 1)

    def query_block(i, carry):
        row_at = pl.multiple_of(i * size, size)

        def score(h, j, top, diag):
            keys = ka_ref[h, pl.ds(pl.multiple_of(j * size, size), size), :]
            s = dot_t(keys, qa_ref[h, pl.ds(row_at, size), :])
            if diag:
                s = jnp.where(diagonal_mask(start_ref, row_at, size), s, -3e38)
            score_bufs[h][...] = s
            col_max = jnp.max(s, axis=0, keepdims=True)
            return col_max if top is None else jnp.maximum(top, col_max)

        def gather_values(h, j, old, new, first):
            p = jnp.exp2(score_bufs[h][...] * LOG2E - new * LOG2E).astype(bf16)
            part = dot_n(vt_ref[h, :, pl.ds(pl.multiple_of(j * size, size), size)], p)
            if first:
                acc_bufs[h][...] = part
            else:
                acc_bufs[h][...] = acc_bufs[h][...] * jnp.exp2((old - new) * LOG2E) + part

        low = low_ref[i]
        m0 = score(0, i, None, True)
        m1 = score(1, i, None, True)
        gather_values(0, i, None, m0, True)
        m0n = score(0, jnp.minimum(low, i), m0, False)
        gather_values(1, i, None, m1, True)

        def body(j, c):
            m0, m0n, m1 = c
            m1n = score(1, j, m1, False)
            gather_values(0, j, m0, m0n, False)
            m0nn = score(0, jnp.minimum(j + 1, blocks - 1), m0n, False)
            gather_values(1, j, m1, m1n, False)
            return m0n, m0nn, m1n

        m0, _, m1 = lax.fori_loop(low, i, body, (m0, m0n, m1))
        for h, top in ((0, m0), (1, m1)):
            total = acc_bufs[h][64:65, :]
            out = acc_bufs[h][0:64, :] / total
            rows = qa_ref[h, pl.ds(row_at, size), :]
            live = jnp.where(rows[:, 64:65].astype(f32) != 0.0, 1.0, 0.0)
            out_ref[pl.ds(row_at, size), 64 * h : 64 * h + 64] = (out.T * live).astype(out_ref.dtype)
            norm = jnp.broadcast_to(-(top + jnp.log(total)), (8, size)).T[:, 0:1]
            n0, n1, n2 = three_parts(norm)
            rows = jnp.where(lane == 96, n0, jnp.where(lane == 97, n1, jnp.where(lane == 98, n2, rows)))
            qb_ref[h, pl.ds(row_at, size), :] = rows
        return carry

    lax.fori_loop(0, blocks, query_block, 0)


def attend(low, qa, ka, vt, start, size):
    heads, rows, _ = qa.shape
    vmem = pl.BlockSpec(memory_space=pltpu.VMEM)
    return pl.pallas_call(
        functools.partial(attend_kernel, size=size, blocks=rows // size),
        grid_spec=pltpu.PrefetchScalarGridSpec(
            num_scalar_prefetch=1,
            grid=(),
            in_specs=[vmem] * 4,
            out_specs=[vmem] * 2,
            scratch_shapes=[pltpu.VMEM((size, size), f32)] * heads
            + [pltpu.VMEM((vt.shape[1], size), f32)] * heads,
        ),
        out_shape=[
            jax.ShapeDtypeStruct((rows, HD * heads), bf16),
            jax.ShapeDtypeStruct(qa.shape, bf16),
        ],
        compiler_params=pltpu.CompilerParams(vmem_limit_bytes=VMEM_LIMIT),
        cost_estimate=pl.CostEstimate(
            flops=rows * rows * HD * heads, bytes_accessed=8 << 20, transcendentals=rows * rows
        ),
        name="attend",
    )(low, qa, ka, vt, start)


def attend_back_kernel(
    low_ref, qb_ref, ka_ref, va_ref, kt_ref, g_ref, o_ref, start_ref, grad_ref,
    ga_ref, dk_ref, dv_ref, q0, q1, *, size, blocks
):
    query_accs = (q0, q1)
    lane = lax.broadcasted_iota(jnp.int32, (size, 64), 1)

    def query_block(i, carry):
        row_at = pl.multiple_of(i * size, size)
        g_rows = g_ref[pl.ds(row_at, size), :]
        product = g_rows.astype(f32) * o_ref[pl.ds(row_at, size), :].astype(f32)
        for h in range(2):
            cols = slice(64 * h, 64 * h + 64)
            n0, n1, n2 = three_parts(-jnp.sum(product[:, cols], axis=1, keepdims=True))
            zero = jnp.zeros((size, 64), bf16)
            extra = jnp.where(lane == 0, n0, jnp.where(lane == 1, n1, jnp.where(lane == 2, n2, zero)))
            ga_ref[h] = jnp.concatenate([g_rows[:, cols], extra], axis=1)

        def block(h, j, diag):
            key_at = pl.multiple_of(j * size, size)
            keys = ka_ref[h, pl.ds(key_at, size), :]
            q_rows = qb_ref[h, pl.ds(row_at, size), :]
            g_head = ga_ref[h]
            s = dot_t(keys, q_rows)
            if diag:
                s = jnp.where(diagonal_mask(start_ref, row_at, size), s, -3e38)
            p = jnp.exp2(s * LOG2E)
            dp = dot_t(va_ref[h, pl.ds(key_at, size), :], g_head)
            ds = (p * dp).astype(bf16)
            dv = dot_n(p.astype(bf16), g_head[:, 0:64])
            dk = dot_n(ds, q_rows[:, 0:64])
            dq = dot_n(kt_ref[h, :, pl.ds(key_at, size)], ds)
            if diag:
                dv_ref[h, pl.ds(key_at, size), :] = dv
                dk_ref[h, pl.ds(key_at, size), :] = dk
                query_accs[h][...] = dq
            else:
                dv_ref[h, pl.ds(key_at, size), :] += dv
                dk_ref[h, pl.ds(key_at, size), :] += dk
                query_accs[h][...] += dq

        block(0, i, True)
        block(1, i, True)

        def body(j, c):
            block(0, j, False)
            block(1, j, False)
            return c

        lax.fori_loop(low_ref[i], i, body, 0)
        both = jnp.concatenate([query_accs[0][...], query_accs[1][...]], axis=0) * HD ** (-0.5)
        grad_ref[pl.ds(row_at, size), 0:128] = both.T.astype(bf16)
        return carry

    lax.fori_loop(0, blocks, query_block, 0)

    def finish(i, carry):
        row_at = pl.multiple_of(i * size, size)
        for ref, at in ((dk_ref, 128), (dv_ref, 256)):
            both = jnp.concatenate([ref[0, pl.ds(row_at, size), :], ref[1, pl.ds(row_at, size), :]], axis=1)
            grad_ref[pl.ds(row_at, size), at : at + 128] = both.astype(bf16)
        return carry

    lax.fori_loop(0, blocks, finish, 0)


def attend_back(low, qb, ka, va, kt, g, o, start, size):
    heads, rows, _ = qb.shape
    vmem = pl.BlockSpec(memory_space=pltpu.VMEM)
    return pl.pallas_call(
        functools.partial(attend_back_kernel, size=size, blocks=rows // size),
        grid_spec=pltpu.PrefetchScalarGridSpec(
            num_scalar_prefetch=1,
            grid=(),
            in_specs=[vmem] * 7,
            out_specs=vmem,
            scratch_shapes=[
                pltpu.VMEM((heads, size, 128), bf16),
                pltpu.VMEM((heads, rows, HD), f32),
                pltpu.VMEM((heads, rows, HD), f32),
            ]
            + [pltpu.VMEM((HD, size), f32)] * heads,
        ),
        out_shape=jax.ShapeDtypeStruct((rows, 3 * HD * heads), bf16),
        compiler_params=pltpu.CompilerParams(vmem_limit_bytes=VMEM_LIMIT),
        cost_estimate=pl.CostEstimate(
            flops=2 * rows * rows * HD * heads, bytes_accessed=16 << 20, transcendentals=rows * rows
        ),
        name="attend_back",
    )(low, qb, ka, va, kt, g, o, start)


def prepare_kernel(x_ref, w_ref, bias_ref, seg_ref, qa_ref, ka_ref, va_ref, vt_ref, kt_ref):
    size = x_ref.shape[0]
    heads = qa_ref.shape[0]
    width = HD * heads
    projected = dot_n(x_ref[...], w_ref[...]) + bias_ref[0:1, :]
    queries = (projected[:, 0:width].astype(bf16).astype(f32) * HD ** (-0.5)).astype(bf16)
    keys = projected[:, width : 2 * width].astype(bf16)
    values = projected[:, 2 * width : 3 * width].astype(bf16)
    number = lax.broadcasted_iota(jnp.int32, (size, 64), 1).astype(f32)
    seg = jnp.broadcast_to(seg_ref[0:1, :].astype(f32), (8, size)).T[:, 0:1]
    same = seg == number
    other = jnp.where(same | (number > 31), 0.0, -1e30).astype(bf16)
    lanes = lax.broadcasted_iota(jnp.int32, (size, 64), 1)
    key_tail = jnp.where((same & (lanes < 32)) | ((lanes >= 32) & (lanes < 35)), 1.0, 0.0).astype(bf16)
    value_tail = jnp.where(lanes < 3, 1.0, 0.0).astype(bf16)
    for h in range(heads):
        cols = slice(HD * h, HD * h + HD)
        qa_ref[h] = jnp.concatenate([queries[:, cols], other], axis=1)
        ka_ref[h] = jnp.concatenate([keys[:, cols], key_tail], axis=1)
        va_ref[h] = jnp.concatenate([values[:, cols], value_tail], axis=1)
        turned = jnp.concatenate([values[:, cols], keys[:, cols]], axis=1).astype(f32).T.astype(bf16)
        vt_ref[h, 0:64, :] = turned[0:64, :]
        vt_ref[h, 64:80, :] = jnp.where(
            lax.broadcasted_iota(jnp.int32, (16, size), 0) == 0, 1.0, 0.0
        ).astype(bf16)
        kt_ref[h] = turned[64:128, :]


def prepare(x, w, bias, seg_rows, size):
    rows, width = x.shape
    heads = w.shape[1] // (3 * HD)
    wide = pl.BlockSpec((heads, size, 128), lambda i: (0, i, 0))
    shape = jax.ShapeDtypeStruct((heads, rows, 128), bf16)
    return pl.pallas_call(
        prepare_kernel,
        grid=(rows // size,),
        in_specs=[
            pl.BlockSpec((size, width), lambda i: (i, 0)),
            pl.BlockSpec(w.shape, lambda i: (0, 0)),
            pl.BlockSpec(bias.shape, lambda i: (0, 0)),
            pl.BlockSpec((8, size), lambda i: (0, i)),
        ],
        out_specs=[
            wide,
            wide,
            wide,
            pl.BlockSpec((heads, 80, size), lambda i: (0, 0, i)),
            pl.BlockSpec((heads, 64, size), lambda i: (0, 0, i)),
        ],
        out_shape=[
            shape,
            shape,
            shape,
            jax.ShapeDtypeStruct((heads, 80, rows), bf16),
            jax.ShapeDtypeStruct((heads, 64, rows), bf16),
        ],
        compiler_params=pltpu.CompilerParams(vmem_limit_bytes=VMEM_LIMIT),
        cost_estimate=pl.CostEstimate(
            flops=2 * rows * width * w.shape[1], bytes_accessed=14 << 20, transcendentals=0
        ),
        name="prepare",
    )(x, w, bias, seg_rows)


def document_starts(seg_all):
    positions = jnp.arange(seg_all.shape[0], dtype=jnp.int32)
    number = jnp.arange(32, dtype=jnp.int32)[:, None]
    before = jnp.sum(((seg_all > 0) & (seg_all < number)).astype(jnp.int32), axis=1)
    own = jnp.sum(jnp.where(seg_all == number, before[:, None], 0), axis=0)
    return jnp.where(seg_all == 0, positions, own)


MESH = pl.DeviceIdType.MESH


def greet(peers):
    barrier = pltpu.get_barrier_semaphore()
    for peer in peers:
        pl.semaphore_signal(barrier, inc=1, device_id=peer, device_id_type=MESH)
    pl.semaphore_wait(barrier, len(peers))


def push(source, target, send_sem, recv_sem, peer):
    copy = pltpu.make_async_remote_copy(
        src_ref=source,
        dst_ref=target,
        send_sem=send_sem,
        recv_sem=recv_sem,
        device_id=peer,
        device_id_type=MESH,
    )
    copy.start()
    return copy


def quad():
    me = lax.axis_index("tp")
    side = me + 1 - 2 * lax.rem(me, 2)
    across = lax.rem(me + 2, 4)
    far = lax.rem(side + 2, 4)
    return me, side, across, far


def comm_call(kernel, name, number, out_shape, in_specs, out_specs, scratch, moved, *operands):
    return pl.pallas_call(
        kernel,
        out_shape=out_shape,
        in_specs=in_specs,
        out_specs=out_specs,
        scratch_shapes=scratch,
        compiler_params=pltpu.CompilerParams(
            collective_id=number, has_side_effects=True, vmem_limit_bytes=VMEM_LIMIT
        ),
        cost_estimate=pl.CostEstimate(flops=0, bytes_accessed=moved, transcendentals=0),
        name=name,
    )(*operands)


def in_vmem():
    return pl.BlockSpec(memory_space=pltpu.VMEM)


def anywhere():
    return pl.BlockSpec(memory_space=pl.ANY)


def gather_kernel(x_ref, seg_ref, all_ref, segs_ref, sy, ry, ss, rs, sf, rf, sg, rg, own, own_seg, *, parts):
    me, side, across, far = quad()
    rows = x_ref.shape[0]
    step = rows // parts
    greet([{"tp": side}, {"tp": across}, {"tp": far}])

    def rows_of(owner, part):
        return all_ref.at[pl.ds(owner * rows + part * step, step)]

    sent = []
    for k, peer in enumerate((across, far, side)):
        sent.append(push(seg_ref, segs_ref.at[me], sg.at[k], rg.at[k], {"tp": peer}))
    for part in range(parts):
        mine = x_ref.at[pl.ds(part * step, step)]
        sent.append(push(mine, rows_of(me, part), sy.at[part], ry.at[part], {"tp": across}))
    for part in range(parts):
        mine = x_ref.at[pl.ds(part * step, step)]
        sent.append(push(mine, rows_of(me, part), ss.at[part], rs.at[part], {"tp": side}))
    keep = pltpu.make_async_copy(x_ref, all_ref.at[pl.ds(me * rows, rows)], own)
    keep.start()
    keep_seg = pltpu.make_async_copy(seg_ref, segs_ref.at[me], own_seg)
    keep_seg.start()
    for part in range(parts):
        here = rows_of(across, part)
        pltpu.make_async_remote_copy(
            here, here, sy.at[part], ry.at[part], {"tp": across}, MESH
        ).wait_recv()
        sent.append(push(here, here, sf.at[part], rf.at[part], {"tp": side}))
    for part in range(parts):
        there = rows_of(side, part)
        pltpu.make_async_remote_copy(there, there, ss.at[part], rs.at[part], {"tp": side}, MESH).wait_recv()
    for part in range(parts):
        there = rows_of(far, part)
        pltpu.make_async_remote_copy(there, there, sf.at[part], rf.at[part], {"tp": side}, MESH).wait_recv()
    for k, peer in enumerate((across, far, side)):
        there = segs_ref.at[peer]
        pltpu.make_async_remote_copy(there, there, sg.at[k], rg.at[k], {"tp": peer}, MESH).wait_recv()
    keep.wait()
    keep_seg.wait()
    for copy in sent:
        copy.wait_send()


def gather_rows(x, segments, number, parts=4):
    rows, width = x.shape
    dma = pltpu.SemaphoreType.DMA
    return comm_call(
        functools.partial(gather_kernel, parts=parts),
        "gather_rows",
        number,
        [
            jax.ShapeDtypeStruct((4 * rows, width), x.dtype),
            jax.ShapeDtypeStruct((4, *segments.shape), segments.dtype),
        ],
        [in_vmem(), in_vmem()],
        [anywhere(), anywhere()],
        [dma((parts,))] * 6 + [dma((3,))] * 2 + [dma, dma],
        60 << 20,
        x,
        segments,
    )


def exchange_kernel(x_ref, out_ref, sems, rems, own):
    me, side, across, far = quad()
    rows = x_ref.shape[0] // 4
    greet([{"tp": side}, {"tp": across}, {"tp": far}])
    sent = []
    for k, peer in enumerate((far, across, side)):
        mine = x_ref.at[pl.ds(peer * rows, rows)]
        sent.append(push(mine, out_ref.at[me], sems.at[k], rems.at[k], {"tp": peer}))
    keep = pltpu.make_async_copy(x_ref.at[pl.ds(me * rows, rows)], out_ref.at[me], own)
    keep.start()
    for k, peer in enumerate((far, across, side)):
        there = out_ref.at[peer]
        pltpu.make_async_remote_copy(there, there, sems.at[k], rems.at[k], {"tp": peer}, MESH).wait_recv()
    keep.wait()
    for copy in sent:
        copy.wait_send()


def exchange(x, number, name):
    rows, width = x.shape
    dma = pltpu.SemaphoreType.DMA
    return comm_call(
        exchange_kernel,
        name,
        number,
        jax.ShapeDtypeStruct((4, rows // 4, width), x.dtype),
        [in_vmem()],
        in_vmem(),
        [dma((3,)), dma((3,)), dma],
        30 << 20,
        x,
    )


def fold_kernel(x_ref, out_ref, sum_buf, sa, ra, sb, rb, sy, ry, side_far, side_own, over, *, parts):
    me, side, across, far = quad()
    rows = out_ref.shape[0]
    step = rows // parts
    greet([{"tp": side}, {"tp": across}])

    def piece(owner, part):
        return pl.ds(owner * rows + part * step, step)

    sent = []
    for part in range(parts):
        here = pl.ds(part * step, step)
        sent.append(
            push(x_ref.at[piece(far, part)], side_far.at[here], sa.at[part], ra.at[part], {"tp": side})
        )
    for part in range(parts):
        here = pl.ds(part * step, step)
        sent.append(
            push(x_ref.at[piece(side, part)], side_own.at[here], sb.at[part], rb.at[part], {"tp": side})
        )
    for part in range(parts):
        here = pl.ds(part * step, step)
        block = side_far.at[here]
        pltpu.make_async_remote_copy(block, block, sa.at[part], ra.at[part], {"tp": side}, MESH).wait_recv()
        total = x_ref[piece(across, part), :].astype(f32) + side_far[here, :].astype(f32)
        sum_buf[here, :] = total.astype(sum_buf.dtype)
        sent.append(push(sum_buf.at[here], over.at[here], sy.at[part], ry.at[part], {"tp": across}))
    for part in range(parts):
        here = pl.ds(part * step, step)
        block = side_own.at[here]
        pltpu.make_async_remote_copy(block, block, sb.at[part], rb.at[part], {"tp": side}, MESH).wait_recv()
        out_ref[here, :] = x_ref[piece(me, part), :].astype(f32) + side_own[here, :].astype(f32)
    for part in range(parts):
        here = pl.ds(part * step, step)
        block = over.at[here]
        pltpu.make_async_remote_copy(block, block, sy.at[part], ry.at[part], {"tp": across}, MESH).wait_recv()
        out_ref[here, :] += over[here, :].astype(f32)
    for copy in sent:
        copy.wait_send()


def fold_rows(x, number, parts=4):
    rows, width = x.shape[0] // 4, x.shape[1]
    dma = pltpu.SemaphoreType.DMA
    return comm_call(
        functools.partial(fold_kernel, parts=parts),
        "fold_rows",
        number,
        jax.ShapeDtypeStruct((rows, width), f32),
        [in_vmem()],
        in_vmem(),
        [pltpu.VMEM((rows, width), x.dtype)]
        + [dma((parts,))] * 6
        + [pltpu.VMEM((rows, width), x.dtype)] * 3,
        60 << 20,
        x,
    )


def all_sum_kernel(x_ref, out_ref, sems, rems, inbox, *, hops):
    greet([{axis: flip(axis, bit)} for axis, bit in hops])
    out_ref[...] = x_ref[...]
    for k, (axis, bit) in enumerate(hops):
        peer = {axis: flip(axis, bit)}
        copy = push(out_ref, inbox.at[k], sems.at[k], rems.at[k], peer)
        copy.wait()
        out_ref[...] = out_ref[...] + inbox[k]


def flip(axis, bit):
    me = lax.axis_index(axis)
    return me + bit - 2 * bit * lax.rem(me // bit, 2)


def bits_of(axis):
    size, bits, bit = lax.axis_size(axis), [], 1
    while bit < size:
        bits.append((axis, bit))
        bit *= 2
    return bits


def all_sum(x, number):
    hops = bits_of("tp") + bits_of("fsdp")
    dma = pltpu.SemaphoreType.DMA
    count = len(hops)
    return comm_call(
        functools.partial(all_sum_kernel, hops=hops),
        "all_sum",
        number,
        jax.ShapeDtypeStruct(x.shape, f32),
        [in_vmem()],
        in_vmem(),
        [dma((count,)), dma((count,)), pltpu.VMEM((count, *x.shape), f32)],
        10 << 20,
        x,
    )


def fold_shards_kernel(x_ref, out_ref, sems, rems, *bufs, hops):
    greet([{axis: flip(axis, bit)} for axis, bit in hops])
    blocks = x_ref.shape[0]
    count = len(hops)
    current = x_ref
    for k, (axis, bit) in enumerate(hops):
        peer = flip(axis, bit)
        mine = lax.rem(lax.axis_index(axis) // bit, 2)
        half = current.shape[0] // 2
        stage, inbox = bufs[2 * k], bufs[2 * k + 1]
        for n in range(half):
            stage[n] = current[2 * n + 1 - mine]
        copy = push(stage, inbox, sems.at[k], rems.at[k], {axis: peer})
        copy.wait()
        if k == count - 1:
            out_ref[...] = current[mine].astype(f32) + inbox[0].astype(f32)
        else:
            keep = bufs[2 * count + k]
            for n in range(half):
                keep[n] = (current[2 * n + mine].astype(f32) + inbox[n].astype(f32)).astype(keep.dtype)
            current = keep


def fold_shards(x, number):
    hops = bits_of("fsdp")
    count = len(hops)
    blocks, rows, width = x.shape
    dma = pltpu.SemaphoreType.DMA
    halves = [blocks >> (k + 1) for k in range(count)]
    bufs = []
    for half in halves:
        bufs += [pltpu.VMEM((half, rows, width), x.dtype)] * 2
    bufs += [pltpu.VMEM((half, rows, width), x.dtype) for half in halves[:-1]]
    return comm_call(
        functools.partial(fold_shards_kernel, hops=hops),
        "fold_shards",
        number,
        jax.ShapeDtypeStruct((rows, width), f32),
        [in_vmem()],
        in_vmem(),
        [dma((count,)), dma((count,))] + bufs,
        60 << 20,
        x,
    )


def spread(value, axis):
    bits = bits_of(axis)[::-1]
    size = lax.axis_size(axis)
    me = lax.axis_index(axis)
    for k, (_, bit) in enumerate(bits):
        other = lax.ppermute(value, axis, [(n, n ^ bit) for n in range(size)])
        high = lax.rem(me // bit, 2) == 1
        value = jnp.stack([jnp.where(high, other, value), jnp.where(high, value, other)], axis=k)
    return value.reshape(size, *value.shape[len(bits) :])


def fold_bits(value, axis):
    size = lax.axis_size(axis)
    for _, bit in bits_of(axis):
        own = lax.rem(lax.axis_index(axis) // bit, 2)
        pairs = value.reshape(value.shape[0] // 2, 2, *value.shape[1:])
        sent = lax.dynamic_index_in_dim(pairs, 1 - own, 1, keepdims=False)
        kept = lax.dynamic_index_in_dim(pairs, own, 1, keepdims=False)
        arrived = lax.ppermute(sent, axis, [(n, n ^ bit) for n in range(size)])
        value = (kept.astype(f32) + arrived.astype(f32)).astype(bf16)
    return value[0]


def local(
    inputs,
    segments,
    out_grad,
    first_gain,
    first_shift,
    qkv_weight,
    qv_bias,
    out_weight,
    out_bias,
    second_gain,
    second_shift,
    fc_weight,
    fc_bias,
    proj_weight,
    proj_bias,
):
    tp_index = lax.axis_index("tp")
    slices = lax.axis_size("tp")
    rows_here, model_width = inputs.shape
    shard_rows = qkv_weight.shape[0]
    head_cols = qkv_weight.shape[2]
    hidden_cols = fc_weight.shape[1]
    qkv_full = spread(qkv_weight.reshape(shard_rows, 3 * head_cols), "fsdp").reshape(
        model_width, 3 * head_cols
    )
    packed = jnp.concatenate([fc_weight, proj_weight.T, out_weight.T], axis=1)
    packed = spread(packed, "fsdp").reshape(model_width, packed.shape[1])
    packed = spread(packed, "tp")
    fc_full = packed[:, :, 0:hidden_cols]
    proj_full = packed[:, :, hidden_cols : 2 * hidden_cols]
    out_full = packed[:, :, 2 * hidden_cols :]

    resid_in = inputs.astype(f32)
    normed_one, hat_one, inv_one = layer_norm(
        resid_in, first_gain.astype(f32), first_shift.astype(f32)
    )
    seq_normed, seg_parts = gather_rows(normed_one.astype(bf16), segments, 0)
    seq_rows = seq_normed.shape[0]
    seg_all = seg_parts.reshape(seq_rows)
    start = document_starts(seg_all)
    size = min(BLOCK, seq_rows)
    low = start[::size] // size
    start_rows = jnp.broadcast_to(start[None], (8, seq_rows))
    seg_rows = jnp.broadcast_to(seg_all[None], (8, seq_rows))
    qv_here = lax.dynamic_slice_in_dim(qv_bias, tp_index * head_cols, head_cols, 1).astype(f32)
    bias_here = jnp.concatenate([qv_here[0], jnp.zeros((head_cols,), f32), qv_here[1]])
    bias_rows = jnp.broadcast_to(bias_here[None], (8, 3 * head_cols))
    qa, ka, va, vt, kt = prepare(seq_normed, qkv_full, bias_rows, seg_rows, size)
    attn_out, qb = attend(low, qa, ka, vt, start_rows, size)
    attn_here = exchange(attn_out, 1, "exchange_out")

    hidden = (
        resid_in
        + jnp.einsum("prc,pdc->rd", attn_here, out_full, preferred_element_type=f32)
        + out_bias.astype(f32)
    )
    normed_two, hat_two, inv_two = layer_norm(
        hidden, second_gain.astype(f32), second_shift.astype(f32)
    )
    mlp_in = normed_two.astype(bf16)
    pre_act = jnp.einsum("sd,tdf->tsf", mlp_in, fc_full, preferred_element_type=f32) + fc_bias.astype(
        f32
    ).reshape(slices, 1, hidden_cols)
    sigmoid_pre = jax.nn.sigmoid(gelu_slope * pre_act)
    act_low = (pre_act * sigmoid_pre).astype(bf16)
    layer_out = (
        hidden
        + jnp.einsum("tsf,tdf->sd", act_low, proj_full, preferred_element_type=f32)
        + proj_bias.astype(f32)
    ).astype(bf16)
    proj_grad = jnp.einsum("sd,tsf->tdf", out_grad, act_low, preferred_element_type=f32)
    grad_act = jnp.einsum("sd,tdf->tsf", out_grad, proj_full, preferred_element_type=f32)
    grad_pre = grad_act * (sigmoid_pre + gelu_slope * pre_act * sigmoid_pre * (1.0 - sigmoid_pre))
    grad_pre_low = grad_pre.astype(bf16)
    fc_grad = jnp.einsum("sd,tsf->tdf", mlp_in, grad_pre_low, preferred_element_type=f32)
    fc_bias_part = jnp.sum(grad_pre_low.astype(f32), axis=1).reshape(-1)
    grad_normed_two = jnp.einsum("tsf,tdf->sd", grad_pre_low, fc_full, preferred_element_type=f32)
    resid_grad = out_grad.astype(f32)
    grad_hidden_ln, second_gain_part, second_shift_part = norm_back(
        grad_normed_two, hat_two, inv_two, second_gain.astype(f32)
    )
    grad_hidden = resid_grad + grad_hidden_ln
    grad_hidden_low = grad_hidden.astype(bf16)
    out_bias_part = jnp.sum(grad_hidden_low.astype(f32), axis=0)
    proj_bias_part = jnp.sum(resid_grad, axis=0)
    out_grad_part = jnp.einsum(
        "sd,psc->pdc", grad_hidden_low, attn_here, preferred_element_type=f32
    )
    live_here = (segments[0] != 0).astype(bf16)
    grad_attn = jnp.einsum("sd,pdc->psc", grad_hidden_low, out_full, preferred_element_type=f32).astype(
        bf16
    ) * live_here[None, :, None]
    grad_attn_seq = exchange(
        grad_attn.reshape(slices * rows_here, head_cols), 2, "exchange_grad"
    ).reshape(seq_rows, head_cols)
    folded = fold_bits(
        jnp.concatenate(
            [fc_grad.astype(bf16), proj_grad.astype(bf16), out_grad_part.astype(bf16)], axis=2
        ),
        "tp",
    )
    grad_qkv = attend_back(low, qb, ka, va, kt, grad_attn_seq, attn_out, start_rows, size)
    qkv_w_grad = jnp.einsum("sd,sj->dj", seq_normed, grad_qkv, preferred_element_type=f32)
    col_sums = jnp.sum(grad_qkv.astype(f32), axis=0)
    partial = jnp.einsum("sj,dj->sd", grad_qkv, qkv_full, preferred_element_type=f32).astype(bf16)
    grad_normed_one = fold_rows(partial, 3)
    grad_in_ln, first_gain_part, first_shift_part = norm_back(
        grad_normed_one, hat_one, inv_one, first_gain.astype(f32)
    )
    input_grad = (grad_hidden + grad_in_ln).astype(bf16)
    shards = model_width // shard_rows
    every = jnp.concatenate([folded, qkv_w_grad.astype(bf16)], axis=1).reshape(
        shards, shard_rows, -1
    )
    summed = fold_shards(every, 4)
    fc_w_grad = summed[:, 0:hidden_cols]
    proj_w_grad = summed[:, hidden_cols : 2 * hidden_cols].T
    out_w_grad = summed[:, 2 * hidden_cols : 2 * hidden_cols + head_cols].T
    qkv_grad = summed[:, 2 * hidden_cols + head_cols :].reshape(shard_rows, 3, head_cols)
    qv_part = jnp.stack([col_sums[0:head_cols], col_sums[2 * head_cols :]])
    qv_full = lax.dynamic_update_slice_in_dim(
        jnp.zeros((2, model_width), f32), qv_part, tp_index * head_cols, 1
    )
    vectors = [
        first_gain_part,
        first_shift_part,
        qv_full.reshape(-1),
        out_bias_part,
        second_gain_part,
        second_shift_part,
        fc_bias_part,
        proj_bias_part,
    ]
    totals = all_sum(jnp.concatenate(vectors).reshape(-1, 128), 5).reshape(-1)
    pieces, at = [], 0
    for vector in vectors:
        pieces.append(totals[at : at + vector.shape[0]])
        at += vector.shape[0]
    (
        first_gain_grad,
        first_shift_grad,
        qv_bias_grad,
        out_bias_grad,
        second_gain_grad,
        second_shift_grad,
        fc_bias_grad,
        proj_bias_grad,
    ) = pieces
    return (
        layer_out,
        input_grad,
        first_gain_grad,
        first_shift_grad,
        qkv_grad,
        qv_bias_grad.reshape(2, model_width),
        out_w_grad,
        out_bias_grad,
        second_gain_grad,
        second_shift_grad,
        fc_w_grad,
        fc_bias_grad,
        proj_w_grad,
        proj_bias_grad,
    )


def solution(mesh):
    return jax.shard_map(
        local,
        mesh=mesh,
        in_specs=(
            P(("fsdp", "tp"), None),
            P("fsdp", "tp"),
            P(("fsdp", "tp"), None),
            P(),
            P(),
            P("fsdp", None, "tp"),
            P(),
            P("tp", "fsdp"),
            P(),
            P(),
            P(),
            P("fsdp", "tp"),
            P(),
            P("tp", "fsdp"),
            P(),
        ),
        out_specs=(
            P(("fsdp", "tp"), None),
            P(("fsdp", "tp"), None),
            P(),
            P(),
            P("fsdp", None, "tp"),
            P(),
            P("tp", "fsdp"),
            P(),
            P(),
            P(),
            P("fsdp", "tp"),
            P(),
            P("tp", "fsdp"),
            P(),
        ),
        check_vma=False,
    )
```

```python
import functools

import jax
import jax.numpy as jnp
from jax import lax
from jax.experimental import pallas as pl
from jax.experimental.pallas import tpu as pltpu
from jax.sharding import PartitionSpec as P

HD = 64
VMEM_LIMIT = 60 << 20
epsilon = 1e-05
gelu_slope = 1.702


def layer_norm(values_in, gain_vec, shift_vec):
    mean_row = jnp.mean(values_in, axis=-1, keepdims=True)
    centred = values_in - mean_row
    inverse = lax.rsqrt(jnp.mean(centred * centred, axis=-1, keepdims=True) + epsilon)
    normed = centred * inverse
    return (normed * gain_vec + shift_vec, normed, inverse)


def norm_back(grad_out, normed, inverse, gain_vec):
    scaled = grad_out * gain_vec
    grad_in = inverse * (
        scaled
        - jnp.mean(scaled, axis=-1, keepdims=True)
        - normed * jnp.mean(scaled * normed, axis=-1, keepdims=True)
    )
    return (grad_in, jnp.sum(grad_out * normed, axis=0), jnp.sum(grad_out, axis=0))


f32 = jnp.float32
bf16 = jnp.bfloat16
LOG2E = 1.4426950408889634
BLOCK = 512
TRANSPOSED = (((1,), (1,)), ((), ()))


def dot_t(left, right):
    return lax.dot_general(left, right, TRANSPOSED, preferred_element_type=f32)


def dot_n(left, right):
    return jnp.dot(left, right, preferred_element_type=f32)


def three_parts(value):
    top = value.astype(bf16)
    rest = value - top.astype(f32)
    mid = rest.astype(bf16)
    return top, mid, (rest - mid.astype(f32)).astype(bf16)


def diagonal_mask(start_ref, row_at, size):
    key_pos = lax.broadcasted_iota(jnp.int32, (size, 1), 0)
    query_pos = lax.broadcasted_iota(jnp.int32, (1, size), 1)
    first = start_ref[0:1, pl.ds(row_at, size)] - row_at
    return (key_pos >= first) & (key_pos <= query_pos)


def attend_kernel(
    low_ref, qa_ref, ka_ref, vt_ref, start_ref, out_ref, qb_ref, s0, s1, a0, a1, *, size, blocks
):
    score_bufs, acc_bufs = (s0, s1), (a0, a1)
    heads = range(qa_ref.shape[0])
    lane = lax.broadcasted_iota(jnp.int32, (size, 128), 1)

    def query_block(i, carry):
        row_at = pl.multiple_of(i * size, size)

        def score(h, j, top, diag):
            keys = ka_ref[h, pl.ds(pl.multiple_of(j * size, size), size), :]
            s = dot_t(keys, qa_ref[h, pl.ds(row_at, size), :])
            if diag:
                s = jnp.where(diagonal_mask(start_ref, row_at, size), s, -3e38)
            score_bufs[h][...] = s
            col_max = jnp.max(s, axis=0, keepdims=True)
            return col_max if top is None else jnp.maximum(top, col_max)

        def gather_values(h, j, old, new, first):
            p = jnp.exp2(score_bufs[h][...] * LOG2E - new * LOG2E).astype(bf16)
            part = dot_n(vt_ref[h, :, pl.ds(pl.multiple_of(j * size, size), size)], p)
            if first:
                acc_bufs[h][...] = part
            else:
                acc_bufs[h][...] = acc_bufs[h][...] * jnp.exp2((old - new) * LOG2E) + part

        low = low_ref[i]
        m0 = score(0, i, None, True)
        m1 = score(1, i, None, True)
        gather_values(0, i, None, m0, True)
        m0n = score(0, jnp.minimum(low, i), m0, False)
        gather_values(1, i, None, m1, True)

        def body(j, c):
            m0, m0n, m1 = c
            m1n = score(1, j, m1, False)
            gather_values(0, j, m0, m0n, False)
            m0nn = score(0, jnp.minimum(j + 1, blocks - 1), m0n, False)
            gather_values(1, j, m1, m1n, False)
            return m0n, m0nn, m1n

        m0, _, m1 = lax.fori_loop(low, i, body, (m0, m0n, m1))
        for h, top in ((0, m0), (1, m1)):
            total = acc_bufs[h][64:65, :]
            out = acc_bufs[h][0:64, :] / total
            rows = qa_ref[h, pl.ds(row_at, size), :]
            live = jnp.where(rows[:, 64:65].astype(f32) != 0.0, 1.0, 0.0)
            out_ref[pl.ds(row_at, size), 64 * h : 64 * h + 64] = (out.T * live).astype(out_ref.dtype)
            norm = jnp.broadcast_to(-(top + jnp.log(total)), (8, size)).T[:, 0:1]
            n0, n1, n2 = three_parts(norm)
            rows = jnp.where(lane == 96, n0, jnp.where(lane == 97, n1, jnp.where(lane == 98, n2, rows)))
            qb_ref[h, pl.ds(row_at, size), :] = rows
        return carry

    lax.fori_loop(0, blocks, query_block, 0)


def attend(low, qa, ka, vt, start, size):
    heads, rows, _ = qa.shape
    vmem = pl.BlockSpec(memory_space=pltpu.VMEM)
    return pl.pallas_call(
        functools.partial(attend_kernel, size=size, blocks=rows // size),
        grid_spec=pltpu.PrefetchScalarGridSpec(
            num_scalar_prefetch=1,
            grid=(),
            in_specs=[vmem] * 4,
            out_specs=[vmem] * 2,
            scratch_shapes=[pltpu.VMEM((size, size), f32)] * heads
            + [pltpu.VMEM((vt.shape[1], size), f32)] * heads,
        ),
        out_shape=[
            jax.ShapeDtypeStruct((rows, HD * heads), bf16),
            jax.ShapeDtypeStruct(qa.shape, bf16),
        ],
        compiler_params=pltpu.CompilerParams(vmem_limit_bytes=VMEM_LIMIT),
        cost_estimate=pl.CostEstimate(
            flops=14 * rows * rows * HD * heads, bytes_accessed=8 << 20, transcendentals=rows * rows
        ),
        name="attend",
    )(low, qa, ka, vt, start)


def attend_back_kernel(
    low_ref, qb_ref, ka_ref, va_ref, kt_ref, g_ref, o_ref, start_ref, grad_ref,
    ga_ref, dk_ref, dv_ref, q0, q1, *, size, blocks
):
    query_accs = (q0, q1)
    lane = lax.broadcasted_iota(jnp.int32, (size, 64), 1)

    def query_block(i, carry):
        row_at = pl.multiple_of(i * size, size)
        g_rows = g_ref[pl.ds(row_at, size), :]
        product = g_rows.astype(f32) * o_ref[pl.ds(row_at, size), :].astype(f32)
        for h in range(2):
            cols = slice(64 * h, 64 * h + 64)
            n0, n1, n2 = three_parts(-jnp.sum(product[:, cols], axis=1, keepdims=True))
            zero = jnp.zeros((size, 64), bf16)
            extra = jnp.where(lane == 0, n0, jnp.where(lane == 1, n1, jnp.where(lane == 2, n2, zero)))
            ga_ref[h] = jnp.concatenate([g_rows[:, cols], extra], axis=1)

        def block(h, j, diag):
            key_at = pl.multiple_of(j * size, size)
            keys = ka_ref[h, pl.ds(key_at, size), :]
            q_rows = qb_ref[h, pl.ds(row_at, size), :]
            g_head = ga_ref[h]
            s = dot_t(keys, q_rows)
            if diag:
                s = jnp.where(diagonal_mask(start_ref, row_at, size), s, -3e38)
            p = jnp.exp2(s * LOG2E)
            dp = dot_t(va_ref[h, pl.ds(key_at, size), :], g_head)
            ds = (p * dp).astype(bf16)
            dv = dot_n(p.astype(bf16), g_head[:, 0:64])
            dk = dot_n(ds, q_rows[:, 0:64])
            dq = dot_n(kt_ref[h, :, pl.ds(key_at, size)], ds)
            if diag:
                dv_ref[h, pl.ds(key_at, size), :] = dv
                dk_ref[h, pl.ds(key_at, size), :] = dk
                query_accs[h][...] = dq
            else:
                dv_ref[h, pl.ds(key_at, size), :] += dv
                dk_ref[h, pl.ds(key_at, size), :] += dk
                query_accs[h][...] += dq

        block(0, i, True)
        block(1, i, True)

        def body(j, c):
            block(0, j, False)
            block(1, j, False)
            return c

        lax.fori_loop(low_ref[i], i, body, 0)
        both = jnp.concatenate([query_accs[0][...], query_accs[1][...]], axis=0) * HD ** (-0.5)
        grad_ref[pl.ds(row_at, size), 0:128] = both.T.astype(bf16)
        return carry

    lax.fori_loop(0, blocks, query_block, 0)

    def finish(i, carry):
        row_at = pl.multiple_of(i * size, size)
        for ref, at in ((dk_ref, 128), (dv_ref, 256)):
            both = jnp.concatenate([ref[0, pl.ds(row_at, size), :], ref[1, pl.ds(row_at, size), :]], axis=1)
            grad_ref[pl.ds(row_at, size), at : at + 128] = both.astype(bf16)
        return carry

    lax.fori_loop(0, blocks, finish, 0)


def attend_back(low, qb, ka, va, kt, g, o, start, size):
    heads, rows, _ = qb.shape
    vmem = pl.BlockSpec(memory_space=pltpu.VMEM)
    return pl.pallas_call(
        functools.partial(attend_back_kernel, size=size, blocks=rows // size),
        grid_spec=pltpu.PrefetchScalarGridSpec(
            num_scalar_prefetch=1,
            grid=(),
            in_specs=[vmem] * 7,
            out_specs=vmem,
            scratch_shapes=[
                pltpu.VMEM((heads, size, 128), bf16),
                pltpu.VMEM((heads, rows, HD), f32),
                pltpu.VMEM((heads, rows, HD), f32),
            ]
            + [pltpu.VMEM((HD, size), f32)] * heads,
        ),
        out_shape=jax.ShapeDtypeStruct((rows, 3 * HD * heads), bf16),
        compiler_params=pltpu.CompilerParams(vmem_limit_bytes=VMEM_LIMIT),
        cost_estimate=pl.CostEstimate(
            flops=24 * rows * rows * HD * heads, bytes_accessed=16 << 20, transcendentals=rows * rows
        ),
        name="attend_back",
    )(low, qb, ka, va, kt, g, o, start)


def document_starts(seg_all):
    positions = jnp.arange(seg_all.shape[0], dtype=jnp.int32)
    number = jnp.arange(32, dtype=jnp.int32)[:, None]
    before = jnp.sum(((seg_all > 0) & (seg_all < number)).astype(jnp.int32), axis=1)
    own = jnp.sum(jnp.where(seg_all == number, before[:, None], 0), axis=0)
    return jnp.where(seg_all == 0, positions, own)


MESH = pl.DeviceIdType.MESH


def greet(peers):
    barrier = pltpu.get_barrier_semaphore()
    for peer in peers:
        pl.semaphore_signal(barrier, inc=1, device_id=peer, device_id_type=MESH)
    pl.semaphore_wait(barrier, len(peers))


def push(source, target, send_sem, recv_sem, peer):
    copy = pltpu.make_async_remote_copy(
        src_ref=source,
        dst_ref=target,
        send_sem=send_sem,
        recv_sem=recv_sem,
        device_id=peer,
        device_id_type=MESH,
    )
    copy.start()
    return copy


def quad():
    me = lax.axis_index("tp")
    side = me + 1 - 2 * lax.rem(me, 2)
    across = lax.rem(me + 2, 4)
    far = lax.rem(side + 2, 4)
    return me, side, across, far


def comm_call(kernel, name, number, out_shape, in_specs, out_specs, scratch, moved, *operands):
    return pl.pallas_call(
        kernel,
        out_shape=out_shape,
        in_specs=in_specs,
        out_specs=out_specs,
        scratch_shapes=scratch,
        compiler_params=pltpu.CompilerParams(
            collective_id=number, has_side_effects=True, vmem_limit_bytes=VMEM_LIMIT
        ),
        cost_estimate=pl.CostEstimate(flops=0, bytes_accessed=moved, transcendentals=0),
        name=name,
    )(*operands)


def in_vmem():
    return pl.BlockSpec(memory_space=pltpu.VMEM)


def anywhere():
    return pl.BlockSpec(memory_space=pl.ANY)


def flipped(axis, mask):
    me, index, bit = lax.axis_index(axis), lax.axis_index(axis), 1
    while bit <= mask:
        if mask & bit:
            index = index + bit - 2 * bit * lax.rem(me // bit, 2)
        bit *= 2
    return index


def awaited(ref, send_sem, recv_sem, peer):
    return pltpu.make_async_remote_copy(ref, ref, send_sem, recv_sem, peer, MESH)


def hop_masks(size):
    hops, bit = [], size // 2
    while bit >= 1:
        hops.append((bit, [high + bit for high in range(0, size, 2 * bit)]))
        bit //= 2
    return hops


def enter_kernel(
    x_ref, norm_ref, bias_ref, seg_ref, w0, w1, w2, w3,
    normed_ref, segs_ref, qa_ref, ka_ref, va_ref, vt_ref, kt_ref, f0, f1, f2, f3,
    x_all, normed_s, qa_s, ka_s, va_s, vt_s, kt_s,
    sy, ry, ss, rs, sf, rf, sg, rg, sw, rw, own, own_w, outs, *, parts
):
    me, side, across, far = quad()
    rows = x_ref.shape[0]
    step = rows // parts
    shards = f0.shape[0]
    heads = qa_ref.shape[0]
    width = HD * heads
    shard = lax.axis_index("fsdp")
    hops = hop_masks(shards)
    greet(
        [{"tp": side}, {"tp": across}, {"tp": far}]
        + [{"fsdp": flipped("fsdp", bit)} for bit, _ in hops]
    )
    sent = []

    def rows_of(owner, part):
        return x_all.at[pl.ds(pl.multiple_of(owner * rows + part * step, step), step)]

    groups = ((w0, f0), (w1, f1), (w2, f2), (w3, f3))
    for part in range(parts):
        mine = x_ref.at[pl.ds(part * step, step)]
        sent.append(push(mine, rows_of(me, part), sy.at[part], ry.at[part], {"tp": across}))

    def send_hop(g, hop):
        bit, masks = hops[hop]
        source, full = groups[g]
        peer = {"fsdp": flipped("fsdp", bit)}
        if hop > 0:
            before, arrived = hops[hop - 1]
            for mask in arrived:
                block = full.at[flipped("fsdp", mask)]
                awaited(block, sw.at[g, mask], rw.at[g, mask], {"fsdp": flipped("fsdp", before)}).wait_recv()
        for mask in masks:
            if mask == bit:
                block = source
            else:
                block = full.at[flipped("fsdp", mask - bit)]
            target = full.at[flipped("fsdp", mask - bit)]
            sent.append(push(block, target, sw.at[g, mask], rw.at[g, mask], peer))

    def end_hops(g):
        bit, arrived = hops[-1]
        for mask in arrived:
            block = groups[g][1].at[flipped("fsdp", mask)]
            awaited(block, sw.at[g, mask], rw.at[g, mask], {"fsdp": flipped("fsdp", bit)}).wait_recv()

    send_hop(0, 0)
    for k, peer in enumerate((across, far, side)):
        sent.append(push(seg_ref, segs_ref.at[me], sg.at[k], rg.at[k], {"tp": peer}))
    for part in range(parts):
        mine = x_ref.at[pl.ds(part * step, step)]
        sent.append(push(mine, rows_of(me, part), ss.at[part], rs.at[part], {"tp": side}))
    for g in (1, 2, 3):
        send_hop(g, 0)
    kept = [
        pltpu.make_async_copy(x_ref, x_all.at[pl.ds(pl.multiple_of(me * rows, rows), rows)], own.at[0]),
        pltpu.make_async_copy(seg_ref, segs_ref.at[me], own.at[1]),
    ] + [pltpu.make_async_copy(source, full.at[shard], own_w.at[g]) for g, (source, full) in enumerate(groups)]
    for copy in kept:
        copy.start()

    def forward(part):
        here = rows_of(across, part)
        awaited(here, sy.at[part], ry.at[part], {"tp": across}).wait_recv()
        return push(here, here, sf.at[part], rf.at[part], {"tp": side})

    waves = sorted(
        ((hop + g, g, hop) for hop in range(1, len(hops)) for g in range(4)), key=lambda w: (w[0], w[1])
    )
    first_last = [n for n, wave in enumerate(waves) if wave[1] == 0][-1]
    for _, g, hop in waves[: first_last + 1]:
        send_hop(g, hop)
    sent.append(forward(0))
    for k, peer in enumerate((across, far, side)):
        awaited(segs_ref.at[peer], sg.at[k], rg.at[k], {"tp": peer}).wait_recv()
    for part in range(parts):
        awaited(rows_of(side, part), ss.at[part], rs.at[part], {"tp": side}).wait_recv()
    for copy in kept:
        copy.wait()
    later = waves[first_last + 1 :]
    for _, g, hop in later[: (len(later) + 1) // 2]:
        send_hop(g, hop)
    sent.append(forward(1))
    end_hops(0)

    gain, shift = norm_ref[0:1, :], norm_ref[1:2, :]
    bias = bias_ref[0:1, :]
    number = lax.broadcasted_iota(jnp.int32, (step, 64), 1)
    number_f = number.astype(f32)
    key_ones = (number >= 32) & (number < 35)
    value_tail = jnp.where(number < 3, 1.0, 0.0).astype(bf16)
    ones_row = jnp.where(lax.broadcasted_iota(jnp.int32, (16, step), 0) == 0, 1.0, 0.0).astype(bf16)

    def copies_out(owner, part):
        row = pl.multiple_of(owner * rows + part * step, step)
        slot = owner * parts + part
        span = pl.ds(row, step)
        pairs = [(normed_s.at[span], normed_ref.at[span])]
        for a, b in ((qa_s, qa_ref), (ka_s, ka_ref), (va_s, va_ref)):
            pairs.append((a.at[:, span, :], b.at[:, span, :]))
        for a, b in ((vt_s, vt_ref), (kt_s, kt_ref)):
            pairs.append((a.at[:, :, span], b.at[:, :, span]))
        return [pltpu.make_async_copy(a, b, outs.at[n, slot]) for n, (a, b) in enumerate(pairs)]

    def compute(owner, part):
        row = pl.multiple_of(owner * rows + part * step, step)
        span = pl.ds(row, step)
        x = x_all[span, :].astype(f32)
        centred = x - jnp.mean(x, axis=-1, keepdims=True)
        inverse = lax.rsqrt(jnp.mean(centred * centred, axis=-1, keepdims=True) + epsilon)
        normed = (centred * inverse * gain + shift).astype(bf16)
        normed_s[span, :] = normed
        weights = f0[...].reshape(shards * f0.shape[1], 3 * width)
        projected = dot_n(normed, weights) + bias
        queries = (projected[:, 0:width].astype(bf16).astype(f32) * HD ** (-0.5)).astype(bf16)
        keys = projected[:, width : 2 * width].astype(bf16)
        values = projected[:, 2 * width : 3 * width].astype(bf16)
        seg = segs_ref[owner, 0:1, pl.ds(pl.multiple_of(part * step, step), step)].astype(f32)
        seg = jnp.broadcast_to(seg, (8, step)).T[:, 0:1]
        same = (seg == number_f) & (number < 32)
        other = jnp.where(same | (number > 31), 0.0, -1e30).astype(bf16)
        key_tail = jnp.where(same | key_ones, 1.0, 0.0).astype(bf16)
        for h in range(heads):
            cols = slice(HD * h, HD * h + HD)
            qa_s[h, span, :] = jnp.concatenate([queries[:, cols], other], axis=1)
            ka_s[h, span, :] = jnp.concatenate([keys[:, cols], key_tail], axis=1)
            va_s[h, span, :] = jnp.concatenate([values[:, cols], value_tail], axis=1)
            turned = jnp.concatenate([values[:, cols], keys[:, cols]], axis=1).astype(f32).T.astype(bf16)
            vt_s[h, 0:64, span] = turned[0:64, :]
            vt_s[h, 64:80, span] = ones_row
            kt_s[h, :, span] = turned[64:128, :]
        for copy in copies_out(owner, part):
            copy.start()

    def near(k, carry):
        part = lax.rem(k, parts)
        compute(me + (k // parts) * (side - me), part)
        return carry

    lax.fori_loop(0, 2 * parts, near, 0)
    for _, g, hop in later[(len(later) + 1) // 2 :]:
        send_hop(g, hop)

    def distant(part, carry):
        compute(across, part)
        awaited(rows_of(far, part), sf.at[part], rf.at[part], {"tp": side}).wait_recv()
        compute(far, part)
        return carry

    for part in range(2, parts):
        sent.append(forward(part))
        lax.fori_loop(part - 2, part - 1, distant, 0)
    lax.fori_loop(parts - 2, parts, distant, 0)
    for g in (1, 2, 3):
        end_hops(g)

    def drain(k, carry):
        for copy in copies_out(k // parts, lax.rem(k, parts)):
            copy.wait()
        return carry

    lax.fori_loop(0, 4 * parts, drain, 0)
    for copy in sent:
        copy.wait_send()


def enter(x, norm_rows, bias_rows, segments, weights, number, parts=4):
    rows, width = x.shape
    seq_rows = 4 * rows
    shards = lax.axis_size("fsdp")
    heads = weights[0].shape[1] // (3 * HD)
    dma = pltpu.SemaphoreType.DMA
    wide = (heads, seq_rows, 128)
    full = [(shards, *w.shape) for w in weights]
    shapes = [(seq_rows, width), wide, wide, wide, (heads, 80, seq_rows), (heads, 64, seq_rows)]
    made = [jax.ShapeDtypeStruct(s, bf16) for s in shapes]
    return comm_call(
        functools.partial(enter_kernel, parts=parts),
        "enter",
        number,
        [made[0], jax.ShapeDtypeStruct((4, *segments.shape), segments.dtype)]
        + made[1:]
        + [jax.ShapeDtypeStruct(s, bf16) for s in full],
        [in_vmem()] * 8,
        [anywhere(), in_vmem()] + [anywhere()] * 5 + [in_vmem()] + [anywhere()] * 3,
        [pltpu.VMEM((seq_rows, width), bf16)]
        + [pltpu.VMEM(s, bf16) for s in shapes]
        + [dma((parts,))] * 6
        + [dma((3,))] * 2
        + [dma((4, shards))] * 2
        + [dma((2,)), dma((4,)), dma((6, 4 * parts))],
        60 << 20,
        x,
        norm_rows,
        bias_rows,
        segments,
        *weights,
    )


def exchange_kernel(x_ref, out_ref, sems, rems, own):
    me, side, across, far = quad()
    rows = x_ref.shape[0] // 4
    greet([{"tp": side}, {"tp": across}, {"tp": far}])
    sent = []
    for k, peer in enumerate((far, across, side)):
        mine = x_ref.at[pl.ds(peer * rows, rows)]
        sent.append(push(mine, out_ref.at[me], sems.at[k], rems.at[k], {"tp": peer}))
    keep = pltpu.make_async_copy(x_ref.at[pl.ds(me * rows, rows)], out_ref.at[me], own)
    keep.start()
    for k, peer in enumerate((far, across, side)):
        there = out_ref.at[peer]
        pltpu.make_async_remote_copy(there, there, sems.at[k], rems.at[k], {"tp": peer}, MESH).wait_recv()
    keep.wait()
    for copy in sent:
        copy.wait_send()


def exchange(x, number, name):
    rows, width = x.shape
    dma = pltpu.SemaphoreType.DMA
    return comm_call(
        exchange_kernel,
        name,
        number,
        jax.ShapeDtypeStruct((4, rows // 4, width), x.dtype),
        [in_vmem()],
        in_vmem(),
        [dma((3,)), dma((3,)), dma],
        30 << 20,
        x,
    )


def fold_kernel(x_ref, out_ref, sum_buf, sa, ra, sb, rb, sy, ry, side_far, side_own, over, *, parts):
    me, side, across, far = quad()
    rows = out_ref.shape[0]
    step = rows // parts
    greet([{"tp": side}, {"tp": across}])

    def piece(owner, part):
        return pl.ds(owner * rows + part * step, step)

    sent = []
    for part in range(parts):
        here = pl.ds(part * step, step)
        sent.append(
            push(x_ref.at[piece(far, part)], side_far.at[here], sa.at[part], ra.at[part], {"tp": side})
        )
    for part in range(parts):
        here = pl.ds(part * step, step)
        sent.append(
            push(x_ref.at[piece(side, part)], side_own.at[here], sb.at[part], rb.at[part], {"tp": side})
        )
    for part in range(parts):
        here = pl.ds(part * step, step)
        block = side_far.at[here]
        pltpu.make_async_remote_copy(block, block, sa.at[part], ra.at[part], {"tp": side}, MESH).wait_recv()
        total = x_ref[piece(across, part), :].astype(f32) + side_far[here, :].astype(f32)
        sum_buf[here, :] = total.astype(sum_buf.dtype)
        sent.append(push(sum_buf.at[here], over.at[here], sy.at[part], ry.at[part], {"tp": across}))
    for part in range(parts):
        here = pl.ds(part * step, step)
        block = side_own.at[here]
        pltpu.make_async_remote_copy(block, block, sb.at[part], rb.at[part], {"tp": side}, MESH).wait_recv()
        out_ref[here, :] = x_ref[piece(me, part), :].astype(f32) + side_own[here, :].astype(f32)
    for part in range(parts):
        here = pl.ds(part * step, step)
        block = over.at[here]
        pltpu.make_async_remote_copy(block, block, sy.at[part], ry.at[part], {"tp": across}, MESH).wait_recv()
        out_ref[here, :] += over[here, :].astype(f32)
    for copy in sent:
        copy.wait_send()


def fold_rows(x, number, parts=4):
    rows, width = x.shape[0] // 4, x.shape[1]
    dma = pltpu.SemaphoreType.DMA
    return comm_call(
        functools.partial(fold_kernel, parts=parts),
        "fold_rows",
        number,
        jax.ShapeDtypeStruct((rows, width), f32),
        [in_vmem()],
        in_vmem(),
        [pltpu.VMEM((rows, width), x.dtype)]
        + [dma((parts,))] * 6
        + [pltpu.VMEM((rows, width), x.dtype)] * 3,
        60 << 20,
        x,
    )


def all_sum_kernel(x_ref, out_ref, sems, rems, inbox, *, hops):
    greet([{axis: flip(axis, bit)} for axis, bit in hops])
    out_ref[...] = x_ref[...]
    for k, (axis, bit) in enumerate(hops):
        peer = {axis: flip(axis, bit)}
        copy = push(out_ref, inbox.at[k], sems.at[k], rems.at[k], peer)
        copy.wait()
        out_ref[...] = out_ref[...] + inbox[k]


def flip(axis, bit):
    me = lax.axis_index(axis)
    return me + bit - 2 * bit * lax.rem(me // bit, 2)


def bits_of(axis):
    size, bits, bit = lax.axis_size(axis), [], 1
    while bit < size:
        bits.append((axis, bit))
        bit *= 2
    return bits


def all_sum(x, number):
    hops = bits_of("tp") + bits_of("fsdp")
    dma = pltpu.SemaphoreType.DMA
    count = len(hops)
    return comm_call(
        functools.partial(all_sum_kernel, hops=hops),
        "all_sum",
        number,
        jax.ShapeDtypeStruct(x.shape, f32),
        [in_vmem()],
        in_vmem(),
        [dma((count,)), dma((count,)), pltpu.VMEM((count, *x.shape), f32)],
        10 << 20,
        x,
    )


def fold_shards_kernel(x_ref, out_ref, sems, rems, *bufs, hops):
    greet([{axis: flip(axis, bit)} for axis, bit in hops])
    blocks = x_ref.shape[0]
    count = len(hops)
    current = x_ref
    for k, (axis, bit) in enumerate(hops):
        peer = flip(axis, bit)
        mine = lax.rem(lax.axis_index(axis) // bit, 2)
        half = current.shape[0] // 2
        stage, inbox = bufs[2 * k], bufs[2 * k + 1]
        for n in range(half):
            stage[n] = current[2 * n + 1 - mine]
        copy = push(stage, inbox, sems.at[k], rems.at[k], {axis: peer})
        copy.wait()
        if k == count - 1:
            out_ref[...] = current[mine].astype(f32) + inbox[0].astype(f32)
        else:
            keep = bufs[2 * count + k]
            for n in range(half):
                keep[n] = (current[2 * n + mine].astype(f32) + inbox[n].astype(f32)).astype(keep.dtype)
            current = keep


def fold_shards(x, number):
    hops = bits_of("fsdp")
    count = len(hops)
    blocks, rows, width = x.shape
    dma = pltpu.SemaphoreType.DMA
    halves = [blocks >> (k + 1) for k in range(count)]
    bufs = []
    for half in halves:
        bufs += [pltpu.VMEM((half, rows, width), x.dtype)] * 2
    bufs += [pltpu.VMEM((half, rows, width), x.dtype) for half in halves[:-1]]
    return comm_call(
        functools.partial(fold_shards_kernel, hops=hops),
        "fold_shards",
        number,
        jax.ShapeDtypeStruct((rows, width), f32),
        [in_vmem()],
        in_vmem(),
        [dma((count,)), dma((count,))] + bufs,
        60 << 20,
        x,
    )


def spread(value, axis):
    bits = bits_of(axis)[::-1]
    size = lax.axis_size(axis)
    me = lax.axis_index(axis)
    for k, (_, bit) in enumerate(bits):
        other = lax.ppermute(value, axis, [(n, n ^ bit) for n in range(size)])
        high = lax.rem(me // bit, 2) == 1
        value = jnp.stack([jnp.where(high, other, value), jnp.where(high, value, other)], axis=k)
    return value.reshape(size, *value.shape[len(bits) :])


def fold_bits(value, axis):
    size = lax.axis_size(axis)
    for _, bit in bits_of(axis):
        own = lax.rem(lax.axis_index(axis) // bit, 2)
        pairs = value.reshape(value.shape[0] // 2, 2, *value.shape[1:])
        sent = lax.dynamic_index_in_dim(pairs, 1 - own, 1, keepdims=False)
        kept = lax.dynamic_index_in_dim(pairs, own, 1, keepdims=False)
        arrived = lax.ppermute(sent, axis, [(n, n ^ bit) for n in range(size)])
        value = (kept.astype(f32) + arrived.astype(f32)).astype(bf16)
    return value[0]


def local(
    inputs,
    segments,
    out_grad,
    first_gain,
    first_shift,
    qkv_weight,
    qv_bias,
    out_weight,
    out_bias,
    second_gain,
    second_shift,
    fc_weight,
    fc_bias,
    proj_weight,
    proj_bias,
):
    tp_index = lax.axis_index("tp")
    slices = lax.axis_size("tp")
    rows_here, model_width = inputs.shape
    shard_rows = qkv_weight.shape[0]
    head_cols = qkv_weight.shape[2]
    hidden_cols = fc_weight.shape[1]
    qv_here = lax.dynamic_slice_in_dim(qv_bias, tp_index * head_cols, head_cols, 1).astype(f32)
    bias_here = jnp.concatenate([qv_here[0], jnp.zeros((head_cols,), f32), qv_here[1]])
    bias_rows = jnp.broadcast_to(bias_here[None], (8, 3 * head_cols))
    norm_rows = jnp.concatenate(
        [first_gain[None], first_shift[None], jnp.zeros((6, model_width), bf16)], axis=0
    ).astype(f32)
    seq_normed, seg_parts, qa, ka, va, vt, kt, qkv_full, fc_slice, proj_slice, out_slice = enter(
        inputs,
        norm_rows,
        bias_rows,
        segments,
        (qkv_weight.reshape(shard_rows, 3 * head_cols), fc_weight, proj_weight.T, out_weight.T),
        0,
    )
    qkv_full = qkv_full.reshape(model_width, 3 * head_cols)
    packed = jnp.concatenate([fc_slice, proj_slice, out_slice], axis=2)
    packed = spread(packed.reshape(model_width, packed.shape[2]), "tp")
    fc_full = packed[:, :, 0:hidden_cols]
    proj_full = packed[:, :, hidden_cols : 2 * hidden_cols]
    out_full = packed[:, :, 2 * hidden_cols :]

    resid_in = inputs.astype(f32)
    _, hat_one, inv_one = layer_norm(
        resid_in, first_gain.astype(f32), first_shift.astype(f32)
    )
    seq_rows = seq_normed.shape[0]
    seg_all = seg_parts.reshape(seq_rows)
    start = document_starts(seg_all)
    size = min(BLOCK, seq_rows)
    low = start[::size] // size
    start_rows = jnp.broadcast_to(start[None], (8, seq_rows))
    attn_out, qb = attend(low, qa, ka, vt, start_rows, size)
    attn_here = exchange(attn_out, 1, "exchange_out")

    hidden = (
        resid_in
        + jnp.einsum("prc,pdc->rd", attn_here, out_full, preferred_element_type=f32)
        + out_bias.astype(f32)
    )
    normed_two, hat_two, inv_two = layer_norm(
        hidden, second_gain.astype(f32), second_shift.astype(f32)
    )
    mlp_in = normed_two.astype(bf16)
    pre_act = jnp.einsum("sd,tdf->tsf", mlp_in, fc_full, preferred_element_type=f32) + fc_bias.astype(
        f32
    ).reshape(slices, 1, hidden_cols)
    sigmoid_pre = jax.nn.sigmoid(gelu_slope * pre_act)
    act_low = (pre_act * sigmoid_pre).astype(bf16)
    layer_out = (
        hidden
        + jnp.einsum("tsf,tdf->sd", act_low, proj_full, preferred_element_type=f32)
        + proj_bias.astype(f32)
    ).astype(bf16)
    proj_grad = jnp.einsum("sd,tsf->tdf", out_grad, act_low, preferred_element_type=f32)
    grad_act = jnp.einsum("sd,tdf->tsf", out_grad, proj_full, preferred_element_type=f32)
    grad_pre = grad_act * (sigmoid_pre + gelu_slope * pre_act * sigmoid_pre * (1.0 - sigmoid_pre))
    grad_pre_low = grad_pre.astype(bf16)
    fc_grad = jnp.einsum("sd,tsf->tdf", mlp_in, grad_pre_low, preferred_element_type=f32)
    fc_bias_part = jnp.sum(grad_pre_low.astype(f32), axis=1).reshape(-1)
    grad_normed_two = jnp.einsum("tsf,tdf->sd", grad_pre_low, fc_full, preferred_element_type=f32)
    resid_grad = out_grad.astype(f32)
    grad_hidden_ln, second_gain_part, second_shift_part = norm_back(
        grad_normed_two, hat_two, inv_two, second_gain.astype(f32)
    )
    grad_hidden = resid_grad + grad_hidden_ln
    grad_hidden_low = grad_hidden.astype(bf16)
    out_bias_part = jnp.sum(grad_hidden_low.astype(f32), axis=0)
    proj_bias_part = jnp.sum(resid_grad, axis=0)
    out_grad_part = jnp.einsum(
        "sd,psc->pdc", grad_hidden_low, attn_here, preferred_element_type=f32
    )
    live_here = (segments[0] != 0).astype(bf16)
    grad_attn = jnp.einsum("sd,pdc->psc", grad_hidden_low, out_full, preferred_element_type=f32).astype(
        bf16
    ) * live_here[None, :, None]
    grad_attn_seq = exchange(
        grad_attn.reshape(slices * rows_here, head_cols), 2, "exchange_grad"
    ).reshape(seq_rows, head_cols)
    folded = fold_bits(
        jnp.concatenate(
            [fc_grad.astype(bf16), proj_grad.astype(bf16), out_grad_part.astype(bf16)], axis=2
        ),
        "tp",
    )
    grad_qkv = attend_back(low, qb, ka, va, kt, grad_attn_seq, attn_out, start_rows, size)
    qkv_w_grad = jnp.einsum("sd,sj->dj", seq_normed, grad_qkv, preferred_element_type=f32)
    col_sums = jnp.sum(grad_qkv.astype(f32), axis=0)
    partial = jnp.einsum("sj,dj->sd", grad_qkv, qkv_full, preferred_element_type=f32).astype(bf16)
    grad_normed_one = fold_rows(partial, 3)
    grad_in_ln, first_gain_part, first_shift_part = norm_back(
        grad_normed_one, hat_one, inv_one, first_gain.astype(f32)
    )
    input_grad = (grad_hidden + grad_in_ln).astype(bf16)
    shards = model_width // shard_rows
    every = jnp.concatenate([folded, qkv_w_grad.astype(bf16)], axis=1).reshape(
        shards, shard_rows, -1
    )
    summed = fold_shards(every, 4)
    fc_w_grad = summed[:, 0:hidden_cols]
    proj_w_grad = summed[:, hidden_cols : 2 * hidden_cols].T
    out_w_grad = summed[:, 2 * hidden_cols : 2 * hidden_cols + head_cols].T
    qkv_grad = summed[:, 2 * hidden_cols + head_cols :].reshape(shard_rows, 3, head_cols)
    qv_part = jnp.stack([col_sums[0:head_cols], col_sums[2 * head_cols :]])
    qv_full = lax.dynamic_update_slice_in_dim(
        jnp.zeros((2, model_width), f32), qv_part, tp_index * head_cols, 1
    )
    vectors = [
        first_gain_part,
        first_shift_part,
        qv_full.reshape(-1),
        out_bias_part,
        second_gain_part,
        second_shift_part,
        fc_bias_part,
        proj_bias_part,
    ]
    totals = all_sum(jnp.concatenate(vectors).reshape(-1, 128), 5).reshape(-1)
    pieces, at = [], 0
    for vector in vectors:
        pieces.append(totals[at : at + vector.shape[0]])
        at += vector.shape[0]
    (
        first_gain_grad,
        first_shift_grad,
        qv_bias_grad,
        out_bias_grad,
        second_gain_grad,
        second_shift_grad,
        fc_bias_grad,
        proj_bias_grad,
    ) = pieces
    return (
        layer_out,
        input_grad,
        first_gain_grad,
        first_shift_grad,
        qkv_grad,
        qv_bias_grad.reshape(2, model_width),
        out_w_grad,
        out_bias_grad,
        second_gain_grad,
        second_shift_grad,
        fc_w_grad,
        fc_bias_grad,
        proj_w_grad,
        proj_bias_grad,
    )


def solution(mesh):
    return jax.shard_map(
        local,
        mesh=mesh,
        in_specs=(
            P(("fsdp", "tp"), None),
            P("fsdp", "tp"),
            P(("fsdp", "tp"), None),
            P(),
            P(),
            P("fsdp", None, "tp"),
            P(),
            P("tp", "fsdp"),
            P(),
            P(),
            P(),
            P("fsdp", "tp"),
            P(),
            P("tp", "fsdp"),
            P(),
        ),
        out_specs=(
            P(("fsdp", "tp"), None),
            P(("fsdp", "tp"), None),
            P(),
            P(),
            P("fsdp", None, "tp"),
            P(),
            P("tp", "fsdp"),
            P(),
            P(),
            P(),
            P("fsdp", "tp"),
            P(),
            P("tp", "fsdp"),
            P(),
        ),
        check_vma=False,
    )
```

```python
import functools

import jax
import jax.numpy as jnp
from jax import lax
from jax.experimental import pallas as pl
from jax.experimental.pallas import tpu as pltpu
from jax.sharding import PartitionSpec as P

HD = 64
VMEM_LIMIT = 60 << 20
epsilon = 1e-05
gelu_slope = 1.702


def layer_norm(values_in, gain_vec, shift_vec):
    mean_row = jnp.mean(values_in, axis=-1, keepdims=True)
    centred = values_in - mean_row
    inverse = lax.rsqrt(jnp.mean(centred * centred, axis=-1, keepdims=True) + epsilon)
    normed = centred * inverse
    return (normed * gain_vec + shift_vec, normed, inverse)


def norm_back(grad_out, normed, inverse, gain_vec):
    scaled = grad_out * gain_vec
    grad_in = inverse * (
        scaled
        - jnp.mean(scaled, axis=-1, keepdims=True)
        - normed * jnp.mean(scaled * normed, axis=-1, keepdims=True)
    )
    return (grad_in, jnp.sum(grad_out * normed, axis=0), jnp.sum(grad_out, axis=0))


f32 = jnp.float32
bf16 = jnp.bfloat16
LOG2E = 1.4426950408889634
BLOCK = 512
TRANSPOSED = (((1,), (1,)), ((), ()))


def dot_t(left, right):
    return lax.dot_general(left, right, TRANSPOSED, preferred_element_type=f32)


def dot_n(left, right):
    return jnp.dot(left, right, preferred_element_type=f32)


def three_parts(value):
    top = value.astype(bf16)
    rest = value - top.astype(f32)
    mid = rest.astype(bf16)
    return top, mid, (rest - mid.astype(f32)).astype(bf16)


def diagonal_mask(start_ref, row_at, size):
    key_pos = lax.broadcasted_iota(jnp.int32, (size, 1), 0)
    query_pos = lax.broadcasted_iota(jnp.int32, (1, size), 1)
    first = start_ref[0:1, pl.ds(row_at, size)] - row_at
    return (key_pos >= first) & (key_pos <= query_pos)


def attend_kernel(
    low_ref, qa_ref, ka_ref, vt_ref, start_ref, out_ref, qb_ref, s0, s1, a0, a1, *, size, blocks
):
    score_bufs, acc_bufs = (s0, s1), (a0, a1)
    heads = range(qa_ref.shape[0])
    lane = lax.broadcasted_iota(jnp.int32, (size, 128), 1)

    def query_block(i, carry):
        row_at = pl.multiple_of(i * size, size)

        def score(h, j, top, diag):
            keys = ka_ref[h, pl.ds(pl.multiple_of(j * size, size), size), :]
            s = dot_t(keys, qa_ref[h, pl.ds(row_at, size), :])
            if diag:
                s = jnp.where(diagonal_mask(start_ref, row_at, size), s, -3e38)
            score_bufs[h][...] = s
            col_max = jnp.max(s, axis=0, keepdims=True)
            return col_max if top is None else jnp.maximum(top, col_max)

        def gather_values(h, j, old, new, first):
            p = jnp.exp2(score_bufs[h][...] * LOG2E - new * LOG2E).astype(bf16)
            part = dot_n(vt_ref[h, :, pl.ds(pl.multiple_of(j * size, size), size)], p)
            if first:
                acc_bufs[h][...] = part
            else:
                acc_bufs[h][...] = acc_bufs[h][...] * jnp.exp2((old - new) * LOG2E) + part

        low = low_ref[i]
        m0 = score(0, i, None, True)
        m1 = score(1, i, None, True)
        gather_values(0, i, None, m0, True)
        m0n = score(0, jnp.minimum(low, i), m0, False)
        gather_values(1, i, None, m1, True)

        def body(j, c):
            m0, m0n, m1 = c
            m1n = score(1, j, m1, False)
            gather_values(0, j, m0, m0n, False)
            m0nn = score(0, jnp.minimum(j + 1, blocks - 1), m0n, False)
            gather_values(1, j, m1, m1n, False)
            return m0n, m0nn, m1n

        m0, _, m1 = lax.fori_loop(low, i, body, (m0, m0n, m1))
        for h, top in ((0, m0), (1, m1)):
            total = acc_bufs[h][64:65, :]
            out = acc_bufs[h][0:64, :] / total
            rows = qa_ref[h, pl.ds(row_at, size), :]
            live = jnp.where(rows[:, 64:65].astype(f32) != 0.0, 1.0, 0.0)
            out_ref[pl.ds(row_at, size), 64 * h : 64 * h + 64] = (out.T * live).astype(out_ref.dtype)
            norm = jnp.broadcast_to(-(top + jnp.log(total)), (8, size)).T[:, 0:1]
            n0, n1, n2 = three_parts(norm)
            rows = jnp.where(lane == 96, n0, jnp.where(lane == 97, n1, jnp.where(lane == 98, n2, rows)))
            qb_ref[h, pl.ds(row_at, size), :] = rows
        return carry

    lax.fori_loop(0, blocks, query_block, 0)


def attend(low, qa, ka, vt, start, size):
    heads, rows, _ = qa.shape
    vmem = pl.BlockSpec(memory_space=pltpu.VMEM)
    return pl.pallas_call(
        functools.partial(attend_kernel, size=size, blocks=rows // size),
        grid_spec=pltpu.PrefetchScalarGridSpec(
            num_scalar_prefetch=1,
            grid=(),
            in_specs=[vmem] * 4,
            out_specs=[vmem] * 2,
            scratch_shapes=[pltpu.VMEM((size, size), f32)] * heads
            + [pltpu.VMEM((vt.shape[1], size), f32)] * heads,
        ),
        out_shape=[
            jax.ShapeDtypeStruct((rows, HD * heads), bf16),
            jax.ShapeDtypeStruct(qa.shape, bf16),
        ],
        compiler_params=pltpu.CompilerParams(vmem_limit_bytes=VMEM_LIMIT),
        cost_estimate=pl.CostEstimate(
            flops=14 * rows * rows * HD * heads, bytes_accessed=8 << 20, transcendentals=rows * rows
        ),
        name="attend",
    )(low, qa, ka, vt, start)


def attend_back_kernel(
    low_ref, qb_ref, ka_ref, va_ref, kt_ref, g_ref, o_ref, start_ref, grad_ref,
    ga_ref, dk_ref, dv_ref, q0, q1, *, size, blocks
):
    query_accs = (q0, q1)
    lane = lax.broadcasted_iota(jnp.int32, (size, 64), 1)

    def query_block(i, carry):
        row_at = pl.multiple_of(i * size, size)
        g_rows = g_ref[pl.ds(row_at, size), :]
        product = g_rows.astype(f32) * o_ref[pl.ds(row_at, size), :].astype(f32)
        for h in range(2):
            cols = slice(64 * h, 64 * h + 64)
            n0, n1, n2 = three_parts(-jnp.sum(product[:, cols], axis=1, keepdims=True))
            zero = jnp.zeros((size, 64), bf16)
            extra = jnp.where(lane == 0, n0, jnp.where(lane == 1, n1, jnp.where(lane == 2, n2, zero)))
            ga_ref[h] = jnp.concatenate([g_rows[:, cols], extra], axis=1)

        def block(h, j, diag):
            key_at = pl.multiple_of(j * size, size)
            keys = ka_ref[h, pl.ds(key_at, size), :]
            q_rows = qb_ref[h, pl.ds(row_at, size), :]
            g_head = ga_ref[h]
            s = dot_t(keys, q_rows)
            if diag:
                s = jnp.where(diagonal_mask(start_ref, row_at, size), s, -3e38)
            p = jnp.exp2(s * LOG2E)
            dp = dot_t(va_ref[h, pl.ds(key_at, size), :], g_head)
            ds = (p * dp).astype(bf16)
            dv = dot_n(p.astype(bf16), g_head[:, 0:64])
            dk = dot_n(ds, q_rows[:, 0:64])
            dq = dot_n(kt_ref[h, :, pl.ds(key_at, size)], ds)
            if diag:
                dv_ref[h, pl.ds(key_at, size), :] = dv
                dk_ref[h, pl.ds(key_at, size), :] = dk
                query_accs[h][...] = dq
            else:
                dv_ref[h, pl.ds(key_at, size), :] += dv
                dk_ref[h, pl.ds(key_at, size), :] += dk
                query_accs[h][...] += dq

        block(0, i, True)
        block(1, i, True)

        def body(j, c):
            block(0, j, False)
            block(1, j, False)
            return c

        lax.fori_loop(low_ref[i], i, body, 0)
        both = jnp.concatenate([query_accs[0][...], query_accs[1][...]], axis=0) * HD ** (-0.5)
        grad_ref[pl.ds(row_at, size), 0:128] = both.T.astype(bf16)
        return carry

    lax.fori_loop(0, blocks, query_block, 0)

    def finish(i, carry):
        row_at = pl.multiple_of(i * size, size)
        for ref, at in ((dk_ref, 128), (dv_ref, 256)):
            both = jnp.concatenate([ref[0, pl.ds(row_at, size), :], ref[1, pl.ds(row_at, size), :]], axis=1)
            grad_ref[pl.ds(row_at, size), at : at + 128] = both.astype(bf16)
        return carry

    lax.fori_loop(0, blocks, finish, 0)


def attend_back(low, qb, ka, va, kt, g, o, start, size):
    heads, rows, _ = qb.shape
    vmem = pl.BlockSpec(memory_space=pltpu.VMEM)
    return pl.pallas_call(
        functools.partial(attend_back_kernel, size=size, blocks=rows // size),
        grid_spec=pltpu.PrefetchScalarGridSpec(
            num_scalar_prefetch=1,
            grid=(),
            in_specs=[vmem] * 7,
            out_specs=vmem,
            scratch_shapes=[
                pltpu.VMEM((heads, size, 128), bf16),
                pltpu.VMEM((heads, rows, HD), f32),
                pltpu.VMEM((heads, rows, HD), f32),
            ]
            + [pltpu.VMEM((HD, size), f32)] * heads,
        ),
        out_shape=jax.ShapeDtypeStruct((rows, 3 * HD * heads), bf16),
        compiler_params=pltpu.CompilerParams(vmem_limit_bytes=VMEM_LIMIT),
        cost_estimate=pl.CostEstimate(
            flops=24 * rows * rows * HD * heads, bytes_accessed=16 << 20, transcendentals=rows * rows
        ),
        name="attend_back",
    )(low, qb, ka, va, kt, g, o, start)


def document_starts(seg_all):
    positions = jnp.arange(seg_all.shape[0], dtype=jnp.int32)
    number = jnp.arange(32, dtype=jnp.int32)[:, None]
    before = jnp.sum(((seg_all > 0) & (seg_all < number)).astype(jnp.int32), axis=1)
    own = jnp.sum(jnp.where(seg_all == number, before[:, None], 0), axis=0)
    return jnp.where(seg_all == 0, positions, own)


MESH = pl.DeviceIdType.MESH


def greet(peers):
    barrier = pltpu.get_barrier_semaphore()
    for peer in peers:
        pl.semaphore_signal(barrier, inc=1, device_id=peer, device_id_type=MESH)
    pl.semaphore_wait(barrier, len(peers))


def push(source, target, send_sem, recv_sem, peer):
    copy = pltpu.make_async_remote_copy(
        src_ref=source,
        dst_ref=target,
        send_sem=send_sem,
        recv_sem=recv_sem,
        device_id=peer,
        device_id_type=MESH,
    )
    copy.start()
    return copy


def quad():
    me = lax.axis_index("tp")
    side = me + 1 - 2 * lax.rem(me, 2)
    across = lax.rem(me + 2, 4)
    far = lax.rem(side + 2, 4)
    return me, side, across, far


def comm_call(kernel, name, number, out_shape, in_specs, out_specs, scratch, moved, *operands):
    return pl.pallas_call(
        kernel,
        out_shape=out_shape,
        in_specs=in_specs,
        out_specs=out_specs,
        scratch_shapes=scratch,
        compiler_params=pltpu.CompilerParams(
            collective_id=number, has_side_effects=True, vmem_limit_bytes=VMEM_LIMIT
        ),
        cost_estimate=pl.CostEstimate(flops=0, bytes_accessed=moved, transcendentals=0),
        name=name,
    )(*operands)


def in_vmem():
    return pl.BlockSpec(memory_space=pltpu.VMEM)


def anywhere():
    return pl.BlockSpec(memory_space=pl.ANY)


def flipped(axis, mask):
    me, index, bit = lax.axis_index(axis), lax.axis_index(axis), 1
    while bit <= mask:
        if mask & bit:
            index = index + bit - 2 * bit * lax.rem(me // bit, 2)
        bit *= 2
    return index


def awaited(ref, send_sem, recv_sem, peer):
    return pltpu.make_async_remote_copy(ref, ref, send_sem, recv_sem, peer, MESH)


def hop_masks(size):
    hops, bit = [], size // 2
    while bit >= 1:
        hops.append((bit, [high + bit for high in range(0, size, 2 * bit)]))
        bit //= 2
    return hops


def enter_kernel(
    x_ref, norm_ref, bias_ref, seg_ref, w0, w1, w2, w3,
    normed_ref, segs_ref, qa_ref, ka_ref, va_ref, vt_ref, kt_ref, f0, f1, f2, f3,
    x_all, normed_s, qa_s, ka_s, va_s, vt_s, kt_s,
    sy, ry, ss, rs, sf, rf, sg, rg, sw, rw, own, own_w, outs, *, parts
):
    me, side, across, far = quad()
    rows = x_ref.shape[0]
    step = rows // parts
    shards = f0.shape[0]
    heads = qa_ref.shape[0]
    width = HD * heads
    shard = lax.axis_index("fsdp")
    hops = hop_masks(shards)
    greet(
        [{"tp": side}, {"tp": across}, {"tp": far}]
        + [{"fsdp": flipped("fsdp", bit)} for bit, _ in hops]
    )
    sent = []

    def rows_of(owner, part):
        return x_all.at[pl.ds(pl.multiple_of(owner * rows + part * step, step), step)]

    groups = ((w0, f0), (w1, f1), (w2, f2), (w3, f3))
    for part in range(parts):
        mine = x_ref.at[pl.ds(part * step, step)]
        sent.append(push(mine, rows_of(me, part), sy.at[part], ry.at[part], {"tp": across}))

    def send_hop(g, hop):
        bit, masks = hops[hop]
        source, full = groups[g]
        peer = {"fsdp": flipped("fsdp", bit)}
        if hop > 0:
            before, arrived = hops[hop - 1]
            for mask in arrived:
                block = full.at[flipped("fsdp", mask)]
                awaited(block, sw.at[g, mask], rw.at[g, mask], {"fsdp": flipped("fsdp", before)}).wait_recv()
        for mask in masks:
            if mask == bit:
                block = source
            else:
                block = full.at[flipped("fsdp", mask - bit)]
            target = full.at[flipped("fsdp", mask - bit)]
            sent.append(push(block, target, sw.at[g, mask], rw.at[g, mask], peer))

    def end_hops(g):
        bit, arrived = hops[-1]
        for mask in arrived:
            block = groups[g][1].at[flipped("fsdp", mask)]
            awaited(block, sw.at[g, mask], rw.at[g, mask], {"fsdp": flipped("fsdp", bit)}).wait_recv()

    send_hop(0, 0)
    for k, peer in enumerate((across, far, side)):
        sent.append(push(seg_ref, segs_ref.at[me], sg.at[k], rg.at[k], {"tp": peer}))
    for part in range(parts):
        mine = x_ref.at[pl.ds(part * step, step)]
        sent.append(push(mine, rows_of(me, part), ss.at[part], rs.at[part], {"tp": side}))
    for g in (1, 2, 3):
        send_hop(g, 0)
    kept = [
        pltpu.make_async_copy(x_ref, x_all.at[pl.ds(pl.multiple_of(me * rows, rows), rows)], own.at[0]),
        pltpu.make_async_copy(seg_ref, segs_ref.at[me], own.at[1]),
    ] + [pltpu.make_async_copy(source, full.at[shard], own_w.at[g]) for g, (source, full) in enumerate(groups)]
    for copy in kept:
        copy.start()

    def forward(part):
        here = rows_of(across, part)
        awaited(here, sy.at[part], ry.at[part], {"tp": across}).wait_recv()
        return push(here, here, sf.at[part], rf.at[part], {"tp": side})

    waves = sorted(
        ((hop + g, g, hop) for hop in range(1, len(hops)) for g in range(4)), key=lambda w: (w[0], w[1])
    )
    first_last = [n for n, wave in enumerate(waves) if wave[1] == 0][-1]
    for _, g, hop in waves[: first_last + 1]:
        send_hop(g, hop)
    sent.append(forward(0))
    for k, peer in enumerate((across, far, side)):
        awaited(segs_ref.at[peer], sg.at[k], rg.at[k], {"tp": peer}).wait_recv()
    for part in range(parts):
        awaited(rows_of(side, part), ss.at[part], rs.at[part], {"tp": side}).wait_recv()
    for copy in kept:
        copy.wait()
    later = waves[first_last + 1 :]
    for _, g, hop in later[: (len(later) + 1) // 2]:
        send_hop(g, hop)
    sent.append(forward(1))
    end_hops(0)

    gain, shift = norm_ref[0:1, :], norm_ref[1:2, :]
    bias = bias_ref[0:1, :]
    number = lax.broadcasted_iota(jnp.int32, (step, 64), 1)
    number_f = number.astype(f32)
    key_ones = (number >= 32) & (number < 35)
    value_tail = jnp.where(number < 3, 1.0, 0.0).astype(bf16)
    ones_row = jnp.where(lax.broadcasted_iota(jnp.int32, (16, step), 0) == 0, 1.0, 0.0).astype(bf16)

    def copies_out(owner, part):
        row = pl.multiple_of(owner * rows + part * step, step)
        slot = owner * parts + part
        span = pl.ds(row, step)
        pairs = [(normed_s.at[span], normed_ref.at[span])]
        for a, b in ((qa_s, qa_ref), (ka_s, ka_ref), (va_s, va_ref)):
            pairs.append((a.at[:, span, :], b.at[:, span, :]))
        for a, b in ((vt_s, vt_ref), (kt_s, kt_ref)):
            pairs.append((a.at[:, :, span], b.at[:, :, span]))
        return [pltpu.make_async_copy(a, b, outs.at[n, slot]) for n, (a, b) in enumerate(pairs)]

    def compute(owner, part):
        row = pl.multiple_of(owner * rows + part * step, step)
        span = pl.ds(row, step)
        x = x_all[span, :].astype(f32)
        centred = x - jnp.mean(x, axis=-1, keepdims=True)
        inverse = lax.rsqrt(jnp.mean(centred * centred, axis=-1, keepdims=True) + epsilon)
        normed = (centred * inverse * gain + shift).astype(bf16)
        normed_s[span, :] = normed
        weights = f0[...].reshape(shards * f0.shape[1], 3 * width)
        projected = dot_n(normed, weights) + bias
        queries = (projected[:, 0:width].astype(bf16).astype(f32) * HD ** (-0.5)).astype(bf16)
        keys = projected[:, width : 2 * width].astype(bf16)
        values = projected[:, 2 * width : 3 * width].astype(bf16)
        seg = segs_ref[owner, 0:1, pl.ds(pl.multiple_of(part * step, step), step)].astype(f32)
        seg = jnp.broadcast_to(seg, (8, step)).T[:, 0:1]
        same = (seg == number_f) & (number < 32)
        other = jnp.where(same | (number > 31), 0.0, -1e30).astype(bf16)
        key_tail = jnp.where(same | key_ones, 1.0, 0.0).astype(bf16)
        for h in range(heads):
            cols = slice(HD * h, HD * h + HD)
            qa_s[h, span, :] = jnp.concatenate([queries[:, cols], other], axis=1)
            ka_s[h, span, :] = jnp.concatenate([keys[:, cols], key_tail], axis=1)
            va_s[h, span, :] = jnp.concatenate([values[:, cols], value_tail], axis=1)
            turned = jnp.concatenate([values[:, cols], keys[:, cols]], axis=1).astype(f32).T.astype(bf16)
            vt_s[h, 0:64, span] = turned[0:64, :]
            vt_s[h, 64:80, span] = ones_row
            kt_s[h, :, span] = turned[64:128, :]
        for copy in copies_out(owner, part):
            copy.start()

    def near(k, carry):
        part = lax.rem(k, parts)
        compute(me + (k // parts) * (side - me), part)
        return carry

    lax.fori_loop(0, 2 * parts, near, 0)
    for _, g, hop in later[(len(later) + 1) // 2 :]:
        send_hop(g, hop)

    def distant(part, carry):
        compute(across, part)
        awaited(rows_of(far, part), sf.at[part], rf.at[part], {"tp": side}).wait_recv()
        compute(far, part)
        return carry

    for part in range(2, parts):
        sent.append(forward(part))
        lax.fori_loop(part - 2, part - 1, distant, 0)
    lax.fori_loop(parts - 2, parts, distant, 0)
    for g in (1, 2, 3):
        end_hops(g)

    def drain(k, carry):
        for copy in copies_out(k // parts, lax.rem(k, parts)):
            copy.wait()
        return carry

    lax.fori_loop(0, 4 * parts, drain, 0)
    for copy in sent:
        copy.wait_send()


def enter(x, norm_rows, bias_rows, segments, weights, number, parts=4):
    rows, width = x.shape
    seq_rows = 4 * rows
    shards = lax.axis_size("fsdp")
    heads = weights[0].shape[1] // (3 * HD)
    dma = pltpu.SemaphoreType.DMA
    wide = (heads, seq_rows, 128)
    full = [(shards, *w.shape) for w in weights]
    shapes = [(seq_rows, width), wide, wide, wide, (heads, 80, seq_rows), (heads, 64, seq_rows)]
    made = [jax.ShapeDtypeStruct(s, bf16) for s in shapes]
    return comm_call(
        functools.partial(enter_kernel, parts=parts),
        "enter",
        number,
        [made[0], jax.ShapeDtypeStruct((4, *segments.shape), segments.dtype)]
        + made[1:]
        + [jax.ShapeDtypeStruct(s, bf16) for s in full],
        [in_vmem()] * 8,
        [anywhere(), in_vmem()] + [anywhere()] * 5 + [in_vmem()] + [anywhere()] * 3,
        [pltpu.VMEM((seq_rows, width), bf16)]
        + [pltpu.VMEM(s, bf16) for s in shapes]
        + [dma((parts,))] * 6
        + [dma((3,))] * 2
        + [dma((4, shards))] * 2
        + [dma((2,)), dma((4,)), dma((6, 4 * parts))],
        60 << 20,
        x,
        norm_rows,
        bias_rows,
        segments,
        *weights,
    )


def exchange_out_kernel(x_ref, o0, o1, o2, c0, c1, c2, out_ref, g0, g1, g2, sems, rems, ws, wr, own):
    me, side, across, far = quad()
    rows = x_ref.shape[0] // 4
    greet([{"tp": side}, {"tp": across}, {"tp": far}])
    peers = {1: side, 2: across, 3: far}

    def mine(owner):
        return x_ref.at[pl.ds(pl.multiple_of(owner * rows, rows), rows)]

    weights = ((o0, c0, g0), (o1, c1, g1), (o2, c2, g2))
    sent = [push(mine(peers[k]), out_ref.at[k], sems.at[k], rems.at[k], {"tp": peers[k]}) for k in (3, 2, 1)]
    for n, (here, over, full) in enumerate(weights):
        sent.append(push(here, full.at[1], ws.at[0, n], wr.at[0, n], {"tp": side}))
        sent.append(push(over, full.at[3], ws.at[1, n], wr.at[1, n], {"tp": side}))
    kept = [pltpu.make_async_copy(mine(me), out_ref.at[0], own.at[0])]
    for n, (here, over, full) in enumerate(weights):
        kept.append(pltpu.make_async_copy(here, full.at[0], own.at[2 * n + 1]))
        kept.append(pltpu.make_async_copy(over, full.at[2], own.at[2 * n + 2]))
    for copy in kept:
        copy.start()
    for copy in kept:
        copy.wait()
    for copy in sent:
        copy.wait()


def exchange_out(x, own, over, number):
    rows, width = x.shape
    dma = pltpu.SemaphoreType.DMA
    return comm_call(
        exchange_out_kernel,
        "exchange_out",
        number,
        [jax.ShapeDtypeStruct((4, rows // 4, width), x.dtype)]
        + [jax.ShapeDtypeStruct((4, *w.shape), w.dtype) for w in own],
        [in_vmem()] * 7,
        [in_vmem()] * 4,
        [dma((4,)), dma((4,)), dma((2, 3)), dma((2, 3)), dma((7,))],
        60 << 20,
        x,
        *own,
        *over,
    )


def exchange_grad_kernel(
    x_ref, g0, g1, g2, out_ref, k0, k1, k2, a0, a1, a2, sems, rems, ws, wr, own, *boxes
):
    me, side, across, far = quad()
    greet([{"tp": side}, {"tp": across}, {"tp": far}])
    peers = {1: side, 2: across, 3: far}
    rows = x_ref.shape[1]

    def slot(owner):
        return out_ref.at[pl.ds(pl.multiple_of(owner * rows, rows), rows)]

    sent = [push(x_ref.at[k], slot(me), sems.at[k], rems.at[k], {"tp": peers[k]}) for k in (3, 2)]
    grads = ((g0, k0, a0), (g1, k1, a1), (g2, k2, a2))
    folded = []
    for n, (grad, _, _) in enumerate(grads):
        folded.append(push(grad.at[3], boxes[2 * n + 1], ws.at[1, n], wr.at[1, n], {"tp": side}))
        folded.append(push(grad.at[1], boxes[2 * n], ws.at[0, n], wr.at[0, n], {"tp": side}))
    sent.append(push(x_ref.at[1], slot(me), sems.at[1], rems.at[1], {"tp": side}))
    keep = pltpu.make_async_copy(x_ref.at[0], slot(me), own)
    keep.start()
    for n, (grad, kept, over) in enumerate(grads):
        folded[2 * n].wait()
        over[...] = (grad[2].astype(f32) + boxes[2 * n + 1][...].astype(f32)).astype(bf16)
        folded[2 * n + 1].wait()
        kept[...] = (grad[0].astype(f32) + boxes[2 * n][...].astype(f32)).astype(bf16)
    keep.wait()
    for k, peer in ((3, far), (2, across), (1, side)):
        awaited(slot(peer), sems.at[k], rems.at[k], {"tp": peer}).wait_recv()
    for copy in sent:
        copy.wait_send()


def exchange_grad(x, grads, number):
    _, rows, width = x.shape
    dma = pltpu.SemaphoreType.DMA
    pieces = [jax.ShapeDtypeStruct(g.shape[1:], g.dtype) for g in grads]
    boxes = []
    for g in grads:
        boxes += [pltpu.VMEM(g.shape[1:], g.dtype)] * 2
    return comm_call(
        exchange_grad_kernel,
        "exchange_grad",
        number,
        [jax.ShapeDtypeStruct((4 * rows, width), x.dtype)] + pieces + pieces,
        [in_vmem()] * 4,
        [in_vmem()] * 7,
        [dma((4,)), dma((4,)), dma((2, 3)), dma((2, 3)), dma] + boxes,
        60 << 20,
        x,
        *grads,
    )


def leave_kernel(
    grad_ref, normed_ref, w_ref, k0, k1, k2, a0, a1, a2, early_ref,
    rows_ref, s0, s1, s2, s3, cols_ref, early_out,
    far_out, own_out, sum_buf, side_far, side_own, over, dw_acc, early_box,
    sa, ra, sb, rb, sy, ry, sw, rw, se, re, *bufs, parts, hops, all_hops
):
    me, side, across, far = quad()
    rows = rows_ref.shape[0]
    step = rows // parts
    greet([{"tp": side}, {"tp": across}] + [{axis: flip(axis, bit)} for axis, bit in hops])
    count = len(hops)
    outs = (s0, s1, s2, s3)
    mlp = ((k0, a0), (k1, a1), (k2, a2))
    current = bufs[0:4]
    boxes = [bufs[4 + g * count : 4 + (g + 1) * count] for g in range(4)]
    keeps = [bufs[4 + 4 * count + g * (count - 1) : 4 + 4 * count + (g + 1) * (count - 1)] for g in range(4)]
    sent = []

    def begin(g):
        kept, arrived = mlp[g]
        current[g][...] = (kept[...].astype(f32) + arrived[...].astype(f32)).astype(bf16)

    def hop_parts(g, k):
        axis, bit = hops[k]
        source = current[g] if k == 0 else keeps[g][k - 1]
        half = lax.rem(lax.axis_index(axis) // bit, 2)
        return {axis: flip(axis, bit)}, source, half, boxes[g][k]

    def hop_send(g, k):
        peer, source, half, box = hop_parts(g, k)
        sent.append(push(source.at[:, 1 - half], box, sw.at[g, k], rw.at[g, k], peer))

    def hop_add(g, k):
        peer, source, half, box = hop_parts(g, k)
        awaited(box, sw.at[g, k], rw.at[g, k], peer).wait_recv()
        if k == count - 1:
            outs[g][...] = source[0, half].astype(f32) + box[0].astype(f32)
        else:
            target = keeps[g][k]
            for n in range(box.shape[0]):
                total = source[n, half].astype(f32) + box[n].astype(f32)
                target[n // 2, n % 2] = total.astype(bf16)
            hop_send(g, k + 1)

    def early_send(k):
        axis, bit = all_hops[k]
        sent.append(push(early_out.at[k], early_box.at[k], se.at[k], re.at[k], {axis: flip(axis, bit)}))

    def early_add(k):
        axis, bit = all_hops[k]
        awaited(early_box.at[k], se.at[k], re.at[k], {axis: flip(axis, bit)}).wait_recv()
        early_out[k + 1] = early_out[k] + early_box[k]
        if k + 1 < len(all_hops):
            early_send(k + 1)

    def span(owner, part):
        return pl.ds(pl.multiple_of(owner * rows + part * step, step), step)

    def piece(part):
        return pl.ds(pl.multiple_of(part * step, step), step)

    def partial(owner, part):
        return dot_t(grad_ref[span(owner, part), :], w_ref[...])

    def give_far(part, carry):
        here = piece(part)
        far_out[here, :] = partial(far, part).astype(bf16)
        push(far_out.at[here], side_far.at[here], sa.at[part], ra.at[part], {"tp": side})
        return carry

    def give_over(part, carry):
        here = piece(part)
        mine = partial(across, part)
        awaited(side_far.at[here], sa.at[part], ra.at[part], {"tp": side}).wait_recv()
        sum_buf[here, :] = (mine + side_far[here, :].astype(f32)).astype(bf16)
        push(sum_buf.at[here], over.at[here], sy.at[part], ry.at[part], {"tp": across})
        return carry

    def give_own(part, carry):
        here = piece(part)
        own_out[here, :] = partial(side, part).astype(bf16)
        push(own_out.at[here], side_own.at[here], sb.at[part], rb.at[part], {"tp": side})
        return carry

    def take_own(part, carry):
        here = piece(part)
        mine = partial(me, part)
        awaited(side_own.at[here], sb.at[part], rb.at[part], {"tp": side}).wait_recv()
        rows_ref[here, :] = mine + side_own[here, :].astype(f32)
        return carry

    def take_over(part, carry):
        here = piece(part)
        awaited(over.at[here], sy.at[part], ry.at[part], {"tp": across}).wait_recv()
        rows_ref[here, :] += over[here, :].astype(f32)
        return carry

    def drain(part, carry):
        here = piece(part)
        awaited(far_out.at[here], sa.at[part], ra.at[part], {"tp": side}).wait_send()
        awaited(own_out.at[here], sb.at[part], rb.at[part], {"tp": side}).wait_send()
        awaited(sum_buf.at[here], sy.at[part], ry.at[part], {"tp": across}).wait_send()
        return carry

    lax.fori_loop(0, parts, give_far, 0)
    begin(0)
    hop_send(0, 0)
    early_out[0] = early_ref[...]
    early_send(0)
    lax.fori_loop(0, parts, give_over, 0)
    for g in (1, 2):
        begin(g)
        hop_send(g, 0)
    chunk = 512
    dw_acc[...] = jnp.zeros_like(dw_acc)
    cols_ref[...] = jnp.zeros_like(cols_ref)
    ones = jnp.ones((8, chunk), bf16)

    def weight_grad(n, carry):
        at = pl.ds(pl.multiple_of(n * chunk, chunk), chunk)
        g = grad_ref[at, :]
        dw_acc[...] += lax.dot_general(
            normed_ref[at, :], g, (((0,), (0,)), ((), ())), preferred_element_type=f32
        )
        cols_ref[...] += dot_n(ones, g)
        return carry

    lax.fori_loop(0, grad_ref.shape[0] // chunk, weight_grad, 0)
    current[3][...] = dw_acc[...].astype(bf16).reshape(current[3].shape)
    hop_send(3, 0)
    lax.fori_loop(0, parts, give_own, 0)
    early_add(0)
    order = sorted(((k + g, g, k) for g in range(4) for k in range(count)), key=lambda w: (w[0], w[1]))
    later = list(range(1, len(all_hops)))
    for n, (_, g, k) in enumerate(order):
        hop_add(g, k)
        if n % 2 == 1 and later:
            early_add(later.pop(0))
        if n == len(order) // 2:
            lax.fori_loop(0, parts, take_own, 0)
    for k in later:
        early_add(k)
    lax.fori_loop(0, parts, take_over, 0)
    lax.fori_loop(0, parts, drain, 0)
    for copy in sent:
        copy.wait_send()


def leave(grad, normed, w, kept, came, early, number, parts=4):
    rows, width = grad.shape[0] // 4, w.shape[0]
    dma = pltpu.SemaphoreType.DMA
    hops = bits_of("fsdp")
    all_hops = bits_of("tp") + hops
    count = len(hops)
    shards = lax.axis_size("fsdp")
    shard = width // shards
    widths = [k.shape[1] for k in kept] + [grad.shape[1]]
    split = (shards // 2, 2, shard)
    current = [pltpu.VMEM((*split, n), bf16) for n in widths]
    boxes = [pltpu.VMEM((shards >> (k + 1), shard, n), bf16) for n in widths for k in range(count)]
    keeps = [pltpu.VMEM((shards >> (k + 2), 2, shard, n), bf16) for n in widths for k in range(count - 1)]
    pieces = [x.reshape(*split, x.shape[1]) for x in (*kept, *came)]
    return comm_call(
        functools.partial(leave_kernel, parts=parts, hops=hops, all_hops=all_hops),
        "leave",
        number,
        [jax.ShapeDtypeStruct((rows, width), f32)]
        + [jax.ShapeDtypeStruct((shard, n), f32) for n in widths]
        + [
            jax.ShapeDtypeStruct((8, grad.shape[1]), f32),
            jax.ShapeDtypeStruct((len(all_hops) + 1, *early.shape), f32),
        ],
        [in_vmem()] * 10,
        [in_vmem()] * 7,
        [pltpu.VMEM((rows, width), bf16)] * 6
        + [pltpu.VMEM((width, grad.shape[1]), f32), pltpu.VMEM((len(all_hops), *early.shape), f32)]
        + [dma((parts,))] * 6
        + [dma((4, count))] * 2
        + [dma((len(all_hops),))] * 2
        + current
        + boxes
        + keeps,
        60 << 20,
        grad,
        normed,
        w,
        *pieces,
        early,
    )


def all_sum_kernel(x_ref, out_ref, sems, rems, inbox, *, hops):
    greet([{axis: flip(axis, bit)} for axis, bit in hops])
    out_ref[...] = x_ref[...]
    for k, (axis, bit) in enumerate(hops):
        peer = {axis: flip(axis, bit)}
        copy = push(out_ref, inbox.at[k], sems.at[k], rems.at[k], peer)
        copy.wait()
        out_ref[...] = out_ref[...] + inbox[k]


def flip(axis, bit):
    me = lax.axis_index(axis)
    return me + bit - 2 * bit * lax.rem(me // bit, 2)


def bits_of(axis):
    size, bits, bit = lax.axis_size(axis), [], 1
    while bit < size:
        bits.append((axis, bit))
        bit *= 2
    return bits


def all_sum(x, number):
    hops = bits_of("tp") + bits_of("fsdp")
    dma = pltpu.SemaphoreType.DMA
    count = len(hops)
    return comm_call(
        functools.partial(all_sum_kernel, hops=hops),
        "all_sum",
        number,
        jax.ShapeDtypeStruct(x.shape, f32),
        [in_vmem()],
        in_vmem(),
        [dma((count,)), dma((count,)), pltpu.VMEM((count, *x.shape), f32)],
        10 << 20,
        x,
    )


def relative(value):
    me = lax.axis_index("tp")
    pairs = value.reshape(2, 2, *value.shape[1:])
    pairs = jnp.where(lax.rem(me, 2) == 1, pairs[:, ::-1], pairs)
    pairs = jnp.where(me // 2 == 1, pairs[::-1], pairs)
    return pairs.reshape(value.shape)


def across(value):
    return lax.ppermute(value, "tp", [(n, n ^ 2) for n in range(4)])


def local(
    inputs,
    segments,
    out_grad,
    first_gain,
    first_shift,
    qkv_weight,
    qv_bias,
    out_weight,
    out_bias,
    second_gain,
    second_shift,
    fc_weight,
    fc_bias,
    proj_weight,
    proj_bias,
):
    tp_index = lax.axis_index("tp")
    slices = lax.axis_size("tp")
    rows_here, model_width = inputs.shape
    shard_rows = qkv_weight.shape[0]
    head_cols = qkv_weight.shape[2]
    hidden_cols = fc_weight.shape[1]
    qv_here = lax.dynamic_slice_in_dim(qv_bias, tp_index * head_cols, head_cols, 1).astype(f32)
    bias_here = jnp.concatenate([qv_here[0], jnp.zeros((head_cols,), f32), qv_here[1]])
    bias_rows = jnp.broadcast_to(bias_here[None], (8, 3 * head_cols))
    norm_rows = jnp.concatenate(
        [first_gain[None], first_shift[None], jnp.zeros((6, model_width), bf16)], axis=0
    ).astype(f32)
    seq_normed, seg_parts, qa, ka, va, vt, kt, qkv_full, fc_slice, proj_slice, out_slice = enter(
        inputs,
        norm_rows,
        bias_rows,
        segments,
        (qkv_weight.reshape(shard_rows, 3 * head_cols), fc_weight, proj_weight.T, out_weight.T),
        0,
    )
    qkv_full = qkv_full.reshape(model_width, 3 * head_cols)
    own = [w.reshape(model_width, w.shape[2]) for w in (fc_slice, proj_slice, out_slice)]
    over = [across(w) for w in own]

    resid_in = inputs.astype(f32)
    _, hat_one, inv_one = layer_norm(
        resid_in, first_gain.astype(f32), first_shift.astype(f32)
    )
    seq_rows = seq_normed.shape[0]
    seg_all = seg_parts.reshape(seq_rows)
    start = document_starts(seg_all)
    size = min(BLOCK, seq_rows)
    low = start[::size] // size
    start_rows = jnp.broadcast_to(start[None], (8, seq_rows))
    attn_out, qb = attend(low, qa, ka, vt, start_rows, size)
    attn_here, fc_full, proj_full, out_full = exchange_out(attn_out, own, over, 1)

    hidden = (
        resid_in
        + jnp.einsum("prc,pdc->rd", attn_here, out_full, preferred_element_type=f32)
        + out_bias.astype(f32)
    )
    normed_two, hat_two, inv_two = layer_norm(
        hidden, second_gain.astype(f32), second_shift.astype(f32)
    )
    mlp_in = normed_two.astype(bf16)
    pre_act = jnp.einsum("sd,tdf->tsf", mlp_in, fc_full, preferred_element_type=f32) + relative(
        fc_bias.astype(f32).reshape(slices, 1, hidden_cols)
    )
    sigmoid_pre = jax.nn.sigmoid(gelu_slope * pre_act)
    act_low = (pre_act * sigmoid_pre).astype(bf16)
    layer_out = (
        hidden
        + jnp.einsum("tsf,tdf->sd", act_low, proj_full, preferred_element_type=f32)
        + proj_bias.astype(f32)
    ).astype(bf16)
    proj_grad = jnp.einsum("sd,tsf->tdf", out_grad, act_low, preferred_element_type=f32)
    grad_act = jnp.einsum("sd,tdf->tsf", out_grad, proj_full, preferred_element_type=f32)
    grad_pre = grad_act * (sigmoid_pre + gelu_slope * pre_act * sigmoid_pre * (1.0 - sigmoid_pre))
    grad_pre_low = grad_pre.astype(bf16)
    fc_grad = jnp.einsum("sd,tsf->tdf", mlp_in, grad_pre_low, preferred_element_type=f32)
    fc_bias_part = relative(jnp.sum(grad_pre_low.astype(f32), axis=1)).reshape(-1)
    grad_normed_two = jnp.einsum("tsf,tdf->sd", grad_pre_low, fc_full, preferred_element_type=f32)
    resid_grad = out_grad.astype(f32)
    grad_hidden_ln, second_gain_part, second_shift_part = norm_back(
        grad_normed_two, hat_two, inv_two, second_gain.astype(f32)
    )
    grad_hidden = resid_grad + grad_hidden_ln
    grad_hidden_low = grad_hidden.astype(bf16)
    out_bias_part = jnp.sum(grad_hidden_low.astype(f32), axis=0)
    proj_bias_part = jnp.sum(resid_grad, axis=0)
    out_grad_part = jnp.einsum(
        "sd,psc->pdc", grad_hidden_low, attn_here, preferred_element_type=f32
    )
    live_here = (segments[0] != 0).astype(bf16)
    grad_attn = jnp.einsum("sd,pdc->psc", grad_hidden_low, out_full, preferred_element_type=f32).astype(
        bf16
    ) * live_here[None, :, None]
    grad_attn_seq, *halves = exchange_grad(
        grad_attn, (fc_grad.astype(bf16), proj_grad.astype(bf16), out_grad_part.astype(bf16)), 2
    )
    kept, came = halves[0:3], [across(half) for half in halves[3:6]]
    grad_qkv = attend_back(low, qb, ka, va, kt, grad_attn_seq, attn_out, start_rows, size)
    early = [out_bias_part, second_gain_part, second_shift_part, fc_bias_part, proj_bias_part]
    grad_normed_one, fc_w_grad, proj_w_grad, out_w_grad, qkv_grad, col_sums, early_sums = leave(
        grad_qkv, seq_normed, qkv_full, kept, came, jnp.concatenate(early).reshape(-1, 128), 3
    )
    grad_in_ln, first_gain_part, first_shift_part = norm_back(
        grad_normed_one, hat_one, inv_one, first_gain.astype(f32)
    )
    input_grad = (grad_hidden + grad_in_ln).astype(bf16)
    proj_w_grad = proj_w_grad.T
    out_w_grad = out_w_grad.T
    qkv_grad = qkv_grad.reshape(shard_rows, 3, head_cols)
    col_sums = col_sums[0]
    qv_part = jnp.stack([col_sums[0:head_cols], col_sums[2 * head_cols :]])
    qv_full = lax.dynamic_update_slice_in_dim(
        jnp.zeros((2, model_width), f32), qv_part, tp_index * head_cols, 1
    )
    late = [first_gain_part, first_shift_part, qv_full.reshape(-1)]
    late_sums = all_sum(jnp.concatenate(late).reshape(-1, 128), 4)

    def pieces(totals, vectors):
        totals, found, at = totals.reshape(-1), [], 0
        for vector in vectors:
            found.append(totals[at : at + vector.shape[0]])
            at += vector.shape[0]
        return found

    first_gain_grad, first_shift_grad, qv_bias_grad = pieces(late_sums, late)
    out_bias_grad, second_gain_grad, second_shift_grad, fc_bias_grad, proj_bias_grad = pieces(
        early_sums[-1], early
    )
    return (
        layer_out,
        input_grad,
        first_gain_grad,
        first_shift_grad,
        qkv_grad,
        qv_bias_grad.reshape(2, model_width),
        out_w_grad,
        out_bias_grad,
        second_gain_grad,
        second_shift_grad,
        fc_w_grad,
        fc_bias_grad,
        proj_w_grad,
        proj_bias_grad,
    )


def solution(mesh):
    return jax.shard_map(
        local,
        mesh=mesh,
        in_specs=(
            P(("fsdp", "tp"), None),
            P("fsdp", "tp"),
            P(("fsdp", "tp"), None),
            P(),
            P(),
            P("fsdp", None, "tp"),
            P(),
            P("tp", "fsdp"),
            P(),
            P(),
            P(),
            P("fsdp", "tp"),
            P(),
            P("tp", "fsdp"),
            P(),
        ),
        out_specs=(
            P(("fsdp", "tp"), None),
            P(("fsdp", "tp"), None),
            P(),
            P(),
            P("fsdp", None, "tp"),
            P(),
            P("tp", "fsdp"),
            P(),
            P(),
            P(),
            P("fsdp", "tp"),
            P(),
            P("tp", "fsdp"),
            P(),
        ),
        check_vma=False,
    )
```

```python
import functools

import jax
import jax.numpy as jnp
from jax import lax
from jax.experimental import pallas as pl
from jax.experimental.pallas import tpu as pltpu
from jax.sharding import PartitionSpec as P

HD = 64
VMEM_LIMIT = 60 << 20
epsilon = 1e-05
gelu_slope = 1.702


def layer_norm(values_in, gain_vec, shift_vec):
    mean_row = jnp.mean(values_in, axis=-1, keepdims=True)
    centred = values_in - mean_row
    inverse = lax.rsqrt(jnp.mean(centred * centred, axis=-1, keepdims=True) + epsilon)
    normed = centred * inverse
    return (normed * gain_vec + shift_vec, normed, inverse)


def norm_back(grad_out, normed, inverse, gain_vec):
    scaled = grad_out * gain_vec
    grad_in = inverse * (
        scaled
        - jnp.mean(scaled, axis=-1, keepdims=True)
        - normed * jnp.mean(scaled * normed, axis=-1, keepdims=True)
    )
    return (grad_in, jnp.sum(grad_out * normed, axis=0), jnp.sum(grad_out, axis=0))


f32 = jnp.float32
bf16 = jnp.bfloat16
LOG2E = 1.4426950408889634
BLOCK = 512
TRANSPOSED = (((1,), (1,)), ((), ()))


def dot_t(left, right):
    return lax.dot_general(left, right, TRANSPOSED, preferred_element_type=f32)


def dot_n(left, right):
    return jnp.dot(left, right, preferred_element_type=f32)


def three_parts(value):
    top = value.astype(bf16)
    rest = value - top.astype(f32)
    mid = rest.astype(bf16)
    return top, mid, (rest - mid.astype(f32)).astype(bf16)


def diagonal_mask(seg_ref, row_at, size):
    key_pos = lax.broadcasted_iota(jnp.int32, (size, 1), 0)
    query_pos = lax.broadcasted_iota(jnp.int32, (1, size), 1)
    here = seg_ref.shape[2]
    seg = seg_ref[row_at // here, 0:1, pl.ds(pl.multiple_of(lax.rem(row_at, here), size), size)]
    first = jnp.where(seg == 0, query_pos, 0)
    return (key_pos >= first) & (key_pos <= query_pos)


def attend_kernel(
    low_ref, qa_ref, ka_ref, vt_ref, start_ref, out_ref, qb_ref, s0, s1, a0, a1, *, size, blocks
):
    score_bufs, acc_bufs = (s0, s1), (a0, a1)
    heads = range(qa_ref.shape[0])
    lane = lax.broadcasted_iota(jnp.int32, (size, 128), 1)

    def query_block(i, carry):
        row_at = pl.multiple_of(i * size, size)

        def score(h, j, top, diag):
            keys = ka_ref[h, pl.ds(pl.multiple_of(j * size, size), size), :]
            s = dot_t(keys, qa_ref[h, pl.ds(row_at, size), :])
            if diag:
                s = jnp.where(diagonal_mask(start_ref, row_at, size), s, -3e38)
            score_bufs[h][...] = s
            col_max = jnp.max(s, axis=0, keepdims=True)
            return col_max if top is None else jnp.maximum(top, col_max)

        def gather_values(h, j, old, new, first):
            p = jnp.exp2(score_bufs[h][...] * LOG2E - new * LOG2E).astype(bf16)
            part = dot_n(vt_ref[h, :, pl.ds(pl.multiple_of(j * size, size), size)], p)
            if first:
                acc_bufs[h][...] = part
            else:
                acc_bufs[h][...] = acc_bufs[h][...] * jnp.exp2((old - new) * LOG2E) + part

        low = low_ref[i]
        m0 = score(0, i, None, True)
        m1 = score(1, i, None, True)
        gather_values(0, i, None, m0, True)
        m0n = score(0, jnp.minimum(low, i), m0, False)
        gather_values(1, i, None, m1, True)

        def body(j, c):
            m0, m0n, m1 = c
            m1n = score(1, j, m1, False)
            gather_values(0, j, m0, m0n, False)
            m0nn = score(0, jnp.minimum(j + 1, blocks - 1), m0n, False)
            gather_values(1, j, m1, m1n, False)
            return m0n, m0nn, m1n

        m0, _, m1 = lax.fori_loop(low, i, body, (m0, m0n, m1))
        for h, top in ((0, m0), (1, m1)):
            total = acc_bufs[h][64:65, :]
            out = acc_bufs[h][0:64, :] / total
            rows = qa_ref[h, pl.ds(row_at, size), :]
            live = jnp.where(rows[:, 64:65].astype(f32) != 0.0, 1.0, 0.0)
            out_ref[pl.ds(row_at, size), 64 * h : 64 * h + 64] = (out.T * live).astype(out_ref.dtype)
            norm = jnp.broadcast_to(-(top + jnp.log(total)), (8, size)).T[:, 0:1]
            n0, n1, n2 = three_parts(norm)
            rows = jnp.where(lane == 96, n0, jnp.where(lane == 97, n1, jnp.where(lane == 98, n2, rows)))
            qb_ref[h, pl.ds(row_at, size), :] = rows
        return carry

    lax.fori_loop(0, blocks, query_block, 0)


def attend(low, qa, ka, vt, start, size):
    heads, rows, _ = qa.shape
    vmem = pl.BlockSpec(memory_space=pltpu.VMEM)
    return pl.pallas_call(
        functools.partial(attend_kernel, size=size, blocks=rows // size),
        grid_spec=pltpu.PrefetchScalarGridSpec(
            num_scalar_prefetch=1,
            grid=(),
            in_specs=[vmem] * 4,
            out_specs=[vmem] * 2,
            scratch_shapes=[pltpu.VMEM((size, size), f32)] * heads
            + [pltpu.VMEM((vt.shape[1], size), f32)] * heads,
        ),
        out_shape=[
            jax.ShapeDtypeStruct((rows, HD * heads), bf16),
            jax.ShapeDtypeStruct(qa.shape, bf16),
        ],
        compiler_params=pltpu.CompilerParams(vmem_limit_bytes=VMEM_LIMIT),
        cost_estimate=pl.CostEstimate(
            flops=14 * rows * rows * HD * heads, bytes_accessed=8 << 20, transcendentals=rows * rows
        ),
        name="attend",
    )(low, qa, ka, vt, start)


def attend_back_kernel(
    low_ref, qb_ref, ka_ref, va_ref, kt_ref, g_ref, o_ref, start_ref, grad_ref,
    ga_ref, dk_ref, dv_ref, q0, q1, *, size, blocks
):
    query_accs = (q0, q1)
    lane = lax.broadcasted_iota(jnp.int32, (size, 64), 1)

    def query_block(i, carry):
        row_at = pl.multiple_of(i * size, size)
        g_rows = g_ref[pl.ds(row_at, size), :]
        product = g_rows.astype(f32) * o_ref[pl.ds(row_at, size), :].astype(f32)
        for h in range(2):
            cols = slice(64 * h, 64 * h + 64)
            n0, n1, n2 = three_parts(-jnp.sum(product[:, cols], axis=1, keepdims=True))
            zero = jnp.zeros((size, 64), bf16)
            extra = jnp.where(lane == 0, n0, jnp.where(lane == 1, n1, jnp.where(lane == 2, n2, zero)))
            ga_ref[h] = jnp.concatenate([g_rows[:, cols], extra], axis=1)

        def block(h, j, diag):
            key_at = pl.multiple_of(j * size, size)
            keys = ka_ref[h, pl.ds(key_at, size), :]
            q_rows = qb_ref[h, pl.ds(row_at, size), :]
            g_head = ga_ref[h]
            s = dot_t(keys, q_rows)
            if diag:
                s = jnp.where(diagonal_mask(start_ref, row_at, size), s, -3e38)
            p = jnp.exp2(s * LOG2E)
            dp = dot_t(va_ref[h, pl.ds(key_at, size), :], g_head)
            ds = (p * dp).astype(bf16)
            dv = dot_n(p.astype(bf16), g_head[:, 0:64])
            dk = dot_n(ds, q_rows[:, 0:64])
            dq = dot_n(kt_ref[h, :, pl.ds(key_at, size)], ds)
            if diag:
                dv_ref[h, pl.ds(key_at, size), :] = dv
                dk_ref[h, pl.ds(key_at, size), :] = dk
                query_accs[h][...] = dq
            else:
                dv_ref[h, pl.ds(key_at, size), :] += dv
                dk_ref[h, pl.ds(key_at, size), :] += dk
                query_accs[h][...] += dq

        block(0, i, True)
        block(1, i, True)

        def body(j, c):
            block(0, j, False)
            block(1, j, False)
            return c

        lax.fori_loop(low_ref[i], i, body, 0)
        both = jnp.concatenate([query_accs[0][...], query_accs[1][...]], axis=0) * HD ** (-0.5)
        grad_ref[pl.ds(row_at, size), 0:128] = both.T.astype(bf16)
        return carry

    lax.fori_loop(0, blocks, query_block, 0)

    def finish(i, carry):
        row_at = pl.multiple_of(i * size, size)
        for ref, at in ((dk_ref, 128), (dv_ref, 256)):
            both = jnp.concatenate([ref[0, pl.ds(row_at, size), :], ref[1, pl.ds(row_at, size), :]], axis=1)
            grad_ref[pl.ds(row_at, size), at : at + 128] = both.astype(bf16)
        return carry

    lax.fori_loop(0, blocks, finish, 0)


def attend_back(low, qb, ka, va, kt, g, o, start, size):
    heads, rows, _ = qb.shape
    vmem = pl.BlockSpec(memory_space=pltpu.VMEM)
    return pl.pallas_call(
        functools.partial(attend_back_kernel, size=size, blocks=rows // size),
        grid_spec=pltpu.PrefetchScalarGridSpec(
            num_scalar_prefetch=1,
            grid=(),
            in_specs=[vmem] * 7,
            out_specs=vmem,
            scratch_shapes=[
                pltpu.VMEM((heads, size, 128), bf16),
                pltpu.VMEM((heads, rows, HD), f32),
                pltpu.VMEM((heads, rows, HD), f32),
            ]
            + [pltpu.VMEM((HD, size), f32)] * heads,
        ),
        out_shape=jax.ShapeDtypeStruct((rows, 3 * HD * heads), bf16),
        compiler_params=pltpu.CompilerParams(vmem_limit_bytes=VMEM_LIMIT),
        cost_estimate=pl.CostEstimate(
            flops=24 * rows * rows * HD * heads, bytes_accessed=16 << 20, transcendentals=rows * rows
        ),
        name="attend_back",
    )(low, qb, ka, va, kt, g, o, start)


def first_blocks(seg_all, size):
    firsts = seg_all[::size]
    before = jnp.sum(((seg_all > 0) & (seg_all < firsts[:, None])).astype(jnp.int32), axis=1)
    own = jnp.arange(firsts.shape[0], dtype=jnp.int32)
    return jnp.where(firsts == 0, own, before // size)


MESH = pl.DeviceIdType.MESH


def greet(peers):
    barrier = pltpu.get_barrier_semaphore()
    for peer in peers:
        pl.semaphore_signal(barrier, inc=1, device_id=peer, device_id_type=MESH)
    pl.semaphore_wait(barrier, len(peers))


def push(source, target, send_sem, recv_sem, peer):
    copy = pltpu.make_async_remote_copy(
        src_ref=source,
        dst_ref=target,
        send_sem=send_sem,
        recv_sem=recv_sem,
        device_id=peer,
        device_id_type=MESH,
    )
    copy.start()
    return copy


def quad():
    me = lax.axis_index("tp")
    side = me + 1 - 2 * lax.rem(me, 2)
    across = lax.rem(me + 2, 4)
    far = lax.rem(side + 2, 4)
    return me, side, across, far


def comm_call(kernel, name, number, out_shape, in_specs, out_specs, scratch, moved, *operands):
    return pl.pallas_call(
        kernel,
        out_shape=out_shape,
        in_specs=in_specs,
        out_specs=out_specs,
        scratch_shapes=scratch,
        compiler_params=pltpu.CompilerParams(
            collective_id=number, has_side_effects=True, vmem_limit_bytes=VMEM_LIMIT
        ),
        cost_estimate=pl.CostEstimate(flops=0, bytes_accessed=moved, transcendentals=0),
        name=name,
    )(*operands)


def in_vmem():
    return pl.BlockSpec(memory_space=pltpu.VMEM)


def anywhere():
    return pl.BlockSpec(memory_space=pl.ANY)


def flipped(axis, mask):
    me, index, bit = lax.axis_index(axis), lax.axis_index(axis), 1
    while bit <= mask:
        if mask & bit:
            index = index + bit - 2 * bit * lax.rem(me // bit, 2)
        bit *= 2
    return index


def awaited(ref, send_sem, recv_sem, peer):
    return pltpu.make_async_remote_copy(ref, ref, send_sem, recv_sem, peer, MESH)


def hop_masks(size):
    hops, bit = [], size // 2
    while bit >= 1:
        hops.append((bit, [high + bit for high in range(0, size, 2 * bit)]))
        bit //= 2
    return hops


def enter_kernel(
    x_ref, gain_ref, shift_ref, bias_ref, seg_ref, w0, w1, w2, w3,
    normed_ref, segs_ref, qa_ref, ka_ref, va_ref, vt_ref, kt_ref, f0, f1,
    x_all, normed_s, qa_s, ka_s, va_s, vt_s, kt_s,
    sy, ry, ss, rs, sf, rf, sg, rg, sw, rw, own, own_w, outs, *, parts
):
    me, side, across, far = quad()
    rows = x_ref.shape[0]
    step = rows // parts
    shards = f0.shape[0]
    heads = qa_ref.shape[0]
    width = HD * heads
    shard = lax.axis_index("fsdp")
    hops = hop_masks(shards)
    greet(
        [{"tp": side}, {"tp": across}, {"tp": far}]
        + [{"fsdp": flipped("fsdp", bit)} for bit, _ in hops]
    )
    sent = []

    def rows_of(owner, part):
        return x_all.at[pl.ds(pl.multiple_of(owner * rows + part * step, step), step)]

    sources = (w0, w1, w2, w3)

    def block_of(g, index):
        if g == 0:
            return f0.at[index]
        at = sum(w.shape[1] for w in sources[1:g])
        return f1.at[index, :, pl.ds(at, sources[g].shape[1])]

    def send_hop(g, hop):
        bit, masks = hops[hop]
        peer = {"fsdp": flipped("fsdp", bit)}
        if hop > 0:
            before, arrived = hops[hop - 1]
            for mask in arrived:
                block = block_of(g, flipped("fsdp", mask))
                awaited(block, sw.at[g, mask], rw.at[g, mask], {"fsdp": flipped("fsdp", before)}).wait_recv()
        for mask in masks:
            target = block_of(g, flipped("fsdp", mask - bit))
            block = sources[g] if mask == bit else target
            sent.append(push(block, target, sw.at[g, mask], rw.at[g, mask], peer))

    def end_hops(g):
        bit, arrived = hops[-1]
        for mask in arrived:
            block = block_of(g, flipped("fsdp", mask))
            awaited(block, sw.at[g, mask], rw.at[g, mask], {"fsdp": flipped("fsdp", bit)}).wait_recv()

    for k, peer in enumerate((across, far, side)):
        sent.append(push(seg_ref, segs_ref.at[me], sg.at[k], rg.at[k], {"tp": peer}))
    send_hop(0, 0)
    for part in range(parts):
        mine = x_ref.at[pl.ds(part * step, step)]
        sent.append(push(mine, rows_of(me, part), sy.at[part], ry.at[part], {"tp": across}))
    for g in (1, 2, 3):
        send_hop(g, 0)
    for part in range(parts):
        mine = x_ref.at[pl.ds(part * step, step)]
        sent.append(push(mine, rows_of(me, part), ss.at[part], rs.at[part], {"tp": side}))
    kept = [
        pltpu.make_async_copy(x_ref, x_all.at[pl.ds(pl.multiple_of(me * rows, rows), rows)], own.at[0]),
        pltpu.make_async_copy(seg_ref, segs_ref.at[me], own.at[1]),
    ] + [pltpu.make_async_copy(source, block_of(g, shard), own_w.at[g]) for g, source in enumerate(sources)]
    for copy in kept:
        copy.start()
    waves = sorted(
        ((hop + g, g, hop) for hop in range(1, len(hops)) for g in range(4)), key=lambda w: (w[0], w[1])
    )
    for _, g, hop in waves:
        send_hop(g, hop)
    for k, peer in enumerate((across, far, side)):
        awaited(segs_ref.at[peer], sg.at[k], rg.at[k], {"tp": peer}).wait_recv()
    for part in range(parts):
        awaited(rows_of(side, part), ss.at[part], rs.at[part], {"tp": side}).wait_recv()
    for copy in kept:
        copy.wait()
    end_hops(0)

    gain, shift = gain_ref[...].astype(f32), shift_ref[...].astype(f32)
    bias_at = pl.ds(pl.multiple_of(me * width, width), width)
    query_bias = bias_ref[0:1, bias_at].astype(f32)
    value_bias = bias_ref[1:2, bias_at].astype(f32)
    number = lax.broadcasted_iota(jnp.int32, (step, 64), 1)
    number_f = number.astype(f32)
    key_ones = (number >= 32) & (number < 35)
    value_tail = jnp.where(number < 3, 1.0, 0.0).astype(bf16)
    ones_row = jnp.where(lax.broadcasted_iota(jnp.int32, (16, step), 0) == 0, 1.0, 0.0).astype(bf16)

    def copies_out(owner, part):
        row = pl.multiple_of(owner * rows + part * step, step)
        slot = owner * parts + part
        span = pl.ds(row, step)
        pairs = [(normed_s.at[span], normed_ref.at[span])]
        for a, b in ((qa_s, qa_ref), (ka_s, ka_ref), (va_s, va_ref)):
            pairs.append((a.at[:, span, :], b.at[:, span, :]))
        for a, b in ((vt_s, vt_ref), (kt_s, kt_ref)):
            pairs.append((a.at[:, :, span], b.at[:, :, span]))
        return [pltpu.make_async_copy(a, b, outs.at[n, slot]) for n, (a, b) in enumerate(pairs)]

    def compute(owner, part):
        row = pl.multiple_of(owner * rows + part * step, step)
        span = pl.ds(row, step)
        x = x_all[span, :].astype(f32)
        centred = x - jnp.mean(x, axis=-1, keepdims=True)
        inverse = lax.rsqrt(jnp.mean(centred * centred, axis=-1, keepdims=True) + epsilon)
        normed = (centred * inverse * gain + shift).astype(bf16)
        normed_s[span, :] = normed
        weights = f0[...].reshape(shards * f0.shape[1], 3 * width)
        projected = dot_n(normed, weights)
        queries = ((projected[:, 0:width] + query_bias).astype(bf16).astype(f32) * HD ** (-0.5)).astype(bf16)
        keys = projected[:, width : 2 * width].astype(bf16)
        values = (projected[:, 2 * width : 3 * width] + value_bias).astype(bf16)
        seg = segs_ref[owner, 0:1, pl.ds(pl.multiple_of(part * step, step), step)].astype(f32)
        seg = jnp.broadcast_to(seg, (8, step)).T[:, 0:1]
        same = (seg == number_f) & (number < 32)
        other = jnp.where(same | (number > 31), 0.0, -1e30).astype(bf16)
        key_tail = jnp.where(same | key_ones, 1.0, 0.0).astype(bf16)
        for h in range(heads):
            cols = slice(HD * h, HD * h + HD)
            qa_s[h, span, :] = jnp.concatenate([queries[:, cols], other], axis=1)
            ka_s[h, span, :] = jnp.concatenate([keys[:, cols], key_tail], axis=1)
            va_s[h, span, :] = jnp.concatenate([values[:, cols], value_tail], axis=1)
            turned = jnp.concatenate([values[:, cols], keys[:, cols]], axis=1).astype(f32).T.astype(bf16)
            vt_s[h, 0:64, span] = turned[0:64, :]
            vt_s[h, 64:80, span] = ones_row
            kt_s[h, :, span] = turned[64:128, :]
        for copy in copies_out(owner, part):
            copy.start()

    def work(k, carry):
        distant = k // (2 * parts)
        part = lax.rem(k // 2, parts)
        second = lax.rem(k, 2)

        @pl.when((distant == 0) & (second == 0))
        def _():
            here = rows_of(across, part)
            awaited(here, sy.at[part], ry.at[part], {"tp": across}).wait_recv()
            push(here, here, sf.at[part], rf.at[part], {"tp": side})

        @pl.when((distant == 1) & (second == 1))
        def _():
            awaited(rows_of(far, part), sf.at[part], rf.at[part], {"tp": side}).wait_recv()

        first = me + distant * (across - me)
        compute(first + second * (side - me + distant * (far - across - side + me)), part)
        return carry

    lax.fori_loop(0, 4 * parts, work, 0)
    for g in (1, 2, 3):
        end_hops(g)

    def drain(k, carry):
        for copy in copies_out(k // parts, lax.rem(k, parts)):
            copy.wait()
        return carry

    lax.fori_loop(0, 4 * parts, drain, 0)
    for part in range(parts):
        awaited(rows_of(across, part), sf.at[part], rf.at[part], {"tp": side}).wait_send()
    for copy in sent:
        copy.wait_send()


def enter(x, gain, shift, bias, segments, weights, number, parts=4):
    rows, width = x.shape
    seq_rows = 4 * rows
    shards = lax.axis_size("fsdp")
    heads = weights[0].shape[1] // (3 * HD)
    dma = pltpu.SemaphoreType.DMA
    wide = (heads, seq_rows, 128)
    shard_rows = weights[0].shape[0]
    full = [(shards, *weights[0].shape), (shards, shard_rows, sum(w.shape[1] for w in weights[1:]))]
    shapes = [(seq_rows, width), wide, wide, wide, (heads, 80, seq_rows), (heads, 64, seq_rows)]
    made = [jax.ShapeDtypeStruct(s, bf16) for s in shapes]
    return comm_call(
        functools.partial(enter_kernel, parts=parts),
        "enter",
        number,
        [made[0], jax.ShapeDtypeStruct((4, *segments.shape), segments.dtype)]
        + made[1:]
        + [jax.ShapeDtypeStruct(s, bf16) for s in full],
        [in_vmem()] * 9,
        [anywhere(), in_vmem()] + [anywhere()] * 5 + [in_vmem(), anywhere()],
        [pltpu.VMEM((seq_rows, width), bf16)]
        + [pltpu.VMEM(s, bf16) for s in shapes]
        + [dma((parts,))] * 6
        + [dma((3,))] * 2
        + [dma((4, shards))] * 2
        + [dma((2,)), dma((4,)), dma((6, 4 * parts))],
        60 << 20,
        x,
        gain,
        shift,
        bias,
        segments,
        *weights,
    )


def exchange_out_kernel(x_ref, o_ref, c_ref, out_ref, g0, g1, g2, sems, rems, ws, wr, own):
    me, side, across, far = quad()
    rows = x_ref.shape[0] // 4
    greet([{"tp": side}, {"tp": across}, {"tp": far}])
    peers = {1: side, 2: across, 3: far}

    def mine(owner):
        return x_ref.at[pl.ds(pl.multiple_of(owner * rows, rows), rows)]

    weights, at = [], 0
    for full in (g0, g1, g2):
        cols = pl.ds(at, full.shape[2])
        weights.append((o_ref.at[:, cols], c_ref.at[:, cols], full))
        at += full.shape[2]
    sent = [push(mine(peers[k]), out_ref.at[k], sems.at[k], rems.at[k], {"tp": peers[k]}) for k in (3, 2, 1)]
    for n, (here, over, full) in enumerate(weights):
        sent.append(push(here, full.at[1], ws.at[0, n], wr.at[0, n], {"tp": side}))
        sent.append(push(over, full.at[3], ws.at[1, n], wr.at[1, n], {"tp": side}))
    kept = [pltpu.make_async_copy(mine(me), out_ref.at[0], own.at[0])]
    for n, (here, over, full) in enumerate(weights):
        kept.append(pltpu.make_async_copy(here, full.at[0], own.at[2 * n + 1]))
        kept.append(pltpu.make_async_copy(over, full.at[2], own.at[2 * n + 2]))
    for copy in kept:
        copy.start()
    for copy in kept:
        copy.wait()
    for copy in sent:
        copy.wait()


def exchange_out(x, own, over, widths, number):
    rows, width = x.shape
    dma = pltpu.SemaphoreType.DMA
    return comm_call(
        exchange_out_kernel,
        "exchange_out",
        number,
        [jax.ShapeDtypeStruct((4, rows // 4, width), x.dtype)]
        + [jax.ShapeDtypeStruct((4, own.shape[0], w), own.dtype) for w in widths],
        [in_vmem()] * 3,
        [in_vmem()] * 4,
        [dma((4,)), dma((4,)), dma((2, 3)), dma((2, 3)), dma((7,))],
        60 << 20,
        x,
        own,
        over,
    )


def exchange_grad_kernel(
    x_ref, g0, g1, g2, out_ref, kept_ref, over_ref, sems, rems, ws, wr, own, *boxes
):
    me, side, across, far = quad()
    greet([{"tp": side}, {"tp": across}, {"tp": far}])
    peers = {1: side, 2: across, 3: far}
    rows = x_ref.shape[1]

    def slot(owner):
        return out_ref.at[pl.ds(pl.multiple_of(owner * rows, rows), rows)]

    sent = [push(x_ref.at[k], slot(me), sems.at[k], rems.at[k], {"tp": peers[k]}) for k in (3, 2)]
    grads = (g0, g1, g2)
    folded = []
    for n, grad in enumerate(grads):
        folded.append(push(grad.at[3], boxes[2 * n + 1], ws.at[1, n], wr.at[1, n], {"tp": side}))
        folded.append(push(grad.at[1], boxes[2 * n], ws.at[0, n], wr.at[0, n], {"tp": side}))
    sent.append(push(x_ref.at[1], slot(me), sems.at[1], rems.at[1], {"tp": side}))
    keep = pltpu.make_async_copy(x_ref.at[0], slot(me), own)
    keep.start()
    at = 0
    for n, grad in enumerate(grads):
        cols = slice(at, at + grad.shape[2])
        at += grad.shape[2]
        folded[2 * n].wait()
        over_ref[:, cols] = (grad[2].astype(f32) + boxes[2 * n + 1][...].astype(f32)).astype(bf16)
        folded[2 * n + 1].wait()
        kept_ref[:, cols] = (grad[0].astype(f32) + boxes[2 * n][...].astype(f32)).astype(bf16)
    keep.wait()
    for k, peer in ((3, far), (2, across), (1, side)):
        awaited(slot(peer), sems.at[k], rems.at[k], {"tp": peer}).wait_recv()
    for copy in sent:
        copy.wait_send()


def exchange_grad(x, grads, number):
    _, rows, width = x.shape
    dma = pltpu.SemaphoreType.DMA
    piece = jax.ShapeDtypeStruct((grads[0].shape[1], sum(g.shape[2] for g in grads)), x.dtype)
    boxes = []
    for g in grads:
        boxes += [pltpu.VMEM(g.shape[1:], g.dtype)] * 2
    return comm_call(
        exchange_grad_kernel,
        "exchange_grad",
        number,
        [jax.ShapeDtypeStruct((4 * rows, width), x.dtype), piece, piece],
        [in_vmem()] * 4,
        [in_vmem()] * 3,
        [dma((4,)), dma((4,)), dma((2, 3)), dma((2, 3)), dma] + boxes,
        60 << 20,
        x,
        *grads,
    )


def leave_kernel(
    grad_ref, normed_ref, w_ref, kept_ref, came_ref, early_ref, x_ref, gain_ref, resid_ref,
    input_ref, s0, s1, s2, s3, early_out, late_out,
    rows_ref, far_out, own_out, sum_buf, side_far, side_own, over, dw_acc, cols_ref,
    late_ref, early_mid, late_mid, early_one, early_two, late_one, late_two,
    sa, ra, sb, rb, sy, ry, sw, rw, se, re, sl, rl, se2, re2, sl2, rl2, *bufs, parts, hops
):
    me, side, across, far = quad()
    rows = rows_ref.shape[0]
    step = rows // parts
    shard, shards = lax.axis_index("fsdp"), early_two.shape[0]
    barrier = pltpu.get_barrier_semaphore()
    for peer in (side, across, far):
        pl.semaphore_signal(barrier, inc=1, device_id={"tp": peer}, device_id_type=MESH)

    def other(k):
        return {"fsdp": lax.rem(shard + k, shards)}

    def signal(k, carry):
        pl.semaphore_signal(barrier, inc=1, device_id=other(k), device_id_type=MESH)
        return carry

    lax.fori_loop(1, shards, signal, 0)
    pl.semaphore_wait(barrier, 3 + shards - 1)
    count = len(hops)
    outs = (s0, s1, s2, s3)
    current = bufs[0:4]
    boxes = [bufs[4 + g * count : 4 + (g + 1) * count] for g in range(4)]
    keeps = [bufs[4 + 4 * count + g * (count - 1) : 4 + 4 * count + (g + 1) * (count - 1)] for g in range(4)]
    sent = []

    def begin(g):
        at = sum(c.shape[3] for c in current[0:g])
        cols = slice(at, at + current[g].shape[3])
        total = kept_ref[:, :, :, cols].astype(f32) + came_ref[:, :, :, cols].astype(f32)
        current[g][...] = total.astype(bf16)

    def hop_parts(g, k):
        axis, bit = hops[k]
        source = current[g] if k == 0 else keeps[g][k - 1]
        half = lax.rem(lax.axis_index(axis) // bit, 2)
        return {axis: flip(axis, bit)}, source, half, boxes[g][k]

    def hop_send(g, k):
        peer, source, half, box = hop_parts(g, k)
        sent.append(push(source.at[:, 1 - half], box, sw.at[g, k], rw.at[g, k], peer))

    def hop_add(g, k):
        peer, source, half, box = hop_parts(g, k)
        awaited(box, sw.at[g, k], rw.at[g, k], peer).wait_recv()
        if k == count - 1:
            outs[g][...] = source[0, half].astype(f32) + box[0].astype(f32)
        else:
            target = keeps[g][k]
            for n in range(box.shape[0]):
                total = source[n, half].astype(f32) + box[n].astype(f32)
                target[n // 2, n % 2] = total.astype(bf16)
            hop_send(g, k + 1)

    def tp_send(value, box, send, recv):
        box[me] = value[...]
        for k, peer in enumerate((side, across, far)):
            sent.append(push(value, box.at[me], send.at[k], recv.at[me], {"tp": peer}))

    def tp_sum(value, box, send, recv):
        for k, peer in enumerate((side, across, far)):
            awaited(box.at[peer], send.at[k], recv.at[peer], {"tp": peer}).wait_recv()
        value[...] = box[0] + box[1] + box[2] + box[3]

    def fsdp_send(value, box, send, recv):
        box[shard] = value[...]

        def give(k, carry):
            push(value, box.at[shard], send.at[k], recv.at[shard], other(k))
            return carry

        lax.fori_loop(1, shards, give, 0)

    def fsdp_sum(value, target, box, send, recv):
        def take(k, carry):
            peer = lax.rem(shard + k, shards)
            copy = awaited(box.at[peer], send.at[k], recv.at[peer], other(k))
            copy.wait_recv()
            copy.wait_send()
            return carry

        lax.fori_loop(1, shards, take, 0)
        target[...] = lax.fori_loop(1, shards, lambda n, total: total + box[n], box[0])

    def span(owner, part):
        return pl.ds(pl.multiple_of(owner * rows + part * step, step), step)

    def piece(part):
        return pl.ds(pl.multiple_of(part * step, step), step)

    def partial(owner, part):
        return dot_t(grad_ref[span(owner, part), :], w_ref[...])

    def give_far(part, carry):
        here = piece(part)
        far_out[here, :] = partial(far, part).astype(bf16)
        push(far_out.at[here], side_far.at[here], sa.at[part], ra.at[part], {"tp": side})
        return carry

    def give_over(part, carry):
        here = piece(part)
        mine = partial(across, part)
        awaited(side_far.at[here], sa.at[part], ra.at[part], {"tp": side}).wait_recv()
        sum_buf[here, :] = (mine + side_far[here, :].astype(f32)).astype(bf16)
        push(sum_buf.at[here], over.at[here], sy.at[part], ry.at[part], {"tp": across})
        return carry

    def give_own(part, carry):
        here = piece(part)
        own_out[here, :] = partial(side, part).astype(bf16)
        push(own_out.at[here], side_own.at[here], sb.at[part], rb.at[part], {"tp": side})
        return carry

    def take_own(part, carry):
        here = piece(part)
        mine = partial(me, part)
        awaited(side_own.at[here], sb.at[part], rb.at[part], {"tp": side}).wait_recv()
        rows_ref[here, :] = mine + side_own[here, :].astype(f32)
        return carry

    gain = gain_ref[...].astype(f32)

    def take_over(part, carry):
        here = piece(part)
        x = x_ref[here, :].astype(f32)
        centred = x - jnp.mean(x, axis=-1, keepdims=True)
        inverse = lax.rsqrt(jnp.mean(centred * centred, axis=-1, keepdims=True) + epsilon)
        normed = centred * inverse
        awaited(over.at[here], sy.at[part], ry.at[part], {"tp": across}).wait_recv()
        grad = rows_ref[here, :] + over[here, :].astype(f32)
        grad_in, gain_part, shift_part = norm_back(grad, normed, inverse, gain)
        input_ref[here, :] = (resid_ref[here, :] + grad_in).astype(bf16)
        late_ref[0:1, :] += gain_part[None]
        late_ref[1:2, :] += shift_part[None]
        return carry

    def drain(part, carry):
        here = piece(part)
        awaited(far_out.at[here], sa.at[part], ra.at[part], {"tp": side}).wait_send()
        awaited(own_out.at[here], sb.at[part], rb.at[part], {"tp": side}).wait_send()
        awaited(sum_buf.at[here], sy.at[part], ry.at[part], {"tp": across}).wait_send()
        return carry

    tp_send(early_ref, early_one, se, re)
    lax.fori_loop(0, parts, give_far, 0)
    begin(0)
    hop_send(0, 0)
    tp_sum(early_mid, early_one, se, re)
    fsdp_send(early_mid, early_two, se2, re2)
    lax.fori_loop(0, parts, give_over, 0)
    for g in (1, 2):
        begin(g)
        hop_send(g, 0)
    chunk = 512
    dw_acc[...] = jnp.zeros_like(dw_acc)
    cols_ref[...] = jnp.zeros_like(cols_ref)
    ones = jnp.ones((8, chunk), bf16)

    def weight_grad(n, carry):
        at = pl.ds(pl.multiple_of(n * chunk, chunk), chunk)
        g = grad_ref[at, :]
        dw_acc[...] += lax.dot_general(
            normed_ref[at, :], g, (((0,), (0,)), ((), ())), preferred_element_type=f32
        )
        cols_ref[...] += dot_n(ones, g)
        return carry

    lax.fori_loop(0, grad_ref.shape[0] // chunk, weight_grad, 0)
    current[3][...] = dw_acc[...].astype(bf16).reshape(current[3].shape)
    hop_send(3, 0)
    late_ref[...] = jnp.zeros_like(late_ref)
    wide = cols_ref.shape[1] // 3
    qv_at = pl.ds(pl.multiple_of(me * wide, wide), wide)
    late_ref[2:3, qv_at] = cols_ref[0:1, 0:wide]
    late_ref[3:4, qv_at] = cols_ref[0:1, 2 * wide : 3 * wide]
    lax.fori_loop(0, parts, give_own, 0)
    order = sorted(((k + g, g, k) for g in range(4) for k in range(count)), key=lambda w: (w[0], w[1]))
    for n, (_, g, k) in enumerate(order):
        hop_add(g, k)
        if n == len(order) // 2:
            lax.fori_loop(0, parts, take_own, 0)
    lax.fori_loop(0, parts, take_over, 0)
    tp_send(late_ref, late_one, sl, rl)
    fsdp_sum(early_mid, early_out, early_two, se2, re2)
    tp_sum(late_mid, late_one, sl, rl)
    fsdp_send(late_mid, late_two, sl2, rl2)
    lax.fori_loop(0, parts, drain, 0)
    fsdp_sum(late_mid, late_out, late_two, sl2, rl2)
    for copy in sent:
        copy.wait_send()


def leave(grad, normed, w, kept, came, widths, early, x, gain, resid, number, parts=4):
    rows, width = grad.shape[0] // 4, w.shape[0]
    dma = pltpu.SemaphoreType.DMA
    hops = bits_of("fsdp")
    count = len(hops)
    shards = lax.axis_size("fsdp")
    shard = width // shards
    widths = [*widths, grad.shape[1]]
    split = (shards // 2, 2, shard)
    current = [pltpu.VMEM((*split, n), bf16) for n in widths]
    boxes = [pltpu.VMEM((shards >> (k + 1), shard, n), bf16) for n in widths for k in range(count)]
    keeps = [pltpu.VMEM((shards >> (k + 2), 2, shard, n), bf16) for n in widths for k in range(count - 1)]
    late = (4, width)
    return comm_call(
        functools.partial(leave_kernel, parts=parts, hops=hops),
        "leave",
        number,
        [jax.ShapeDtypeStruct((rows, width), bf16)]
        + [jax.ShapeDtypeStruct((shard, n), f32) for n in widths]
        + [jax.ShapeDtypeStruct(early.shape, f32), jax.ShapeDtypeStruct(late, f32)],
        [in_vmem()] * 9,
        [in_vmem()] * 7,
        [pltpu.VMEM((rows, width), f32)]
        + [pltpu.VMEM((rows, width), bf16)] * 6
        + [pltpu.VMEM((width, grad.shape[1]), f32), pltpu.VMEM((8, grad.shape[1]), f32)]
        + [pltpu.VMEM(late, f32), pltpu.VMEM(early.shape, f32), pltpu.VMEM(late, f32)]
        + [pltpu.VMEM((n, *shape), f32) for shape in (early.shape, late) for n in (4, shards)]
        + [dma((parts,))] * 6
        + [dma((4, count))] * 2
        + [dma((3,)), dma((4,))] * 2
        + [dma((shards,))] * 4
        + current
        + boxes
        + keeps,
        60 << 20,
        grad,
        normed,
        w,
        kept.reshape(*split, kept.shape[1]),
        came.reshape(*split, came.shape[1]),
        early,
        x,
        gain,
        resid,
    )


def flip(axis, bit):
    me = lax.axis_index(axis)
    return me + bit - 2 * bit * lax.rem(me // bit, 2)


def bits_of(axis):
    size, bits, bit = lax.axis_size(axis), [], 1
    while bit < size:
        bits.append((axis, bit))
        bit *= 2
    return bits


def relative(value):
    me = lax.axis_index("tp")
    pairs = value.reshape(2, 2, *value.shape[1:])
    pairs = jnp.where(lax.rem(me, 2) == 1, pairs[:, ::-1], pairs)
    pairs = jnp.where(me // 2 == 1, pairs[::-1], pairs)
    return pairs.reshape(value.shape)


def across(value):
    return lax.ppermute(value, "tp", [(n, n ^ 2) for n in range(4)])


def local(
    inputs,
    segments,
    out_grad,
    first_gain,
    first_shift,
    qkv_weight,
    qv_bias,
    out_weight,
    out_bias,
    second_gain,
    second_shift,
    fc_weight,
    fc_bias,
    proj_weight,
    proj_bias,
):
    slices = lax.axis_size("tp")
    rows_here, model_width = inputs.shape
    shard_rows = qkv_weight.shape[0]
    head_cols = qkv_weight.shape[2]
    hidden_cols = fc_weight.shape[1]
    seq_normed, seg_parts, qa, ka, va, vt, kt, qkv_full, own = enter(
        inputs,
        first_gain[None],
        first_shift[None],
        qv_bias,
        segments,
        (qkv_weight.reshape(shard_rows, 3 * head_cols), fc_weight, proj_weight.T, out_weight.T),
        0,
    )
    qkv_full = qkv_full.reshape(model_width, 3 * head_cols)
    own = own.reshape(model_width, own.shape[2])
    over = across(own)
    widths = (hidden_cols, hidden_cols, head_cols)

    resid_in = inputs.astype(f32)
    seq_rows = seq_normed.shape[0]
    seg_all = seg_parts.reshape(seq_rows)
    size = min(BLOCK, rows_here)
    low = first_blocks(seg_all, size)
    attn_out, qb = attend(low, qa, ka, vt, seg_parts, size)
    attn_here, fc_full, proj_full, out_full = exchange_out(attn_out, own, over, widths, 1)

    hidden = (
        resid_in
        + jnp.einsum("prc,pdc->rd", attn_here, out_full, preferred_element_type=f32)
        + out_bias.astype(f32)
    )
    normed_two, hat_two, inv_two = layer_norm(
        hidden, second_gain.astype(f32), second_shift.astype(f32)
    )
    mlp_in = normed_two.astype(bf16)
    pre_act = jnp.einsum("sd,tdf->tsf", mlp_in, fc_full, preferred_element_type=f32) + relative(
        fc_bias.astype(f32).reshape(slices, 1, hidden_cols)
    )
    sigmoid_pre = jax.nn.sigmoid(gelu_slope * pre_act)
    act_low = (pre_act * sigmoid_pre).astype(bf16)
    layer_out = (
        hidden
        + jnp.einsum("tsf,tdf->sd", act_low, proj_full, preferred_element_type=f32)
        + proj_bias.astype(f32)
    ).astype(bf16)
    proj_grad = jnp.einsum("sd,tsf->tdf", out_grad, act_low, preferred_element_type=f32)
    grad_act = jnp.einsum("sd,tdf->tsf", out_grad, proj_full, preferred_element_type=f32)
    grad_pre = grad_act * (sigmoid_pre + gelu_slope * pre_act * sigmoid_pre * (1.0 - sigmoid_pre))
    grad_pre_low = grad_pre.astype(bf16)
    fc_grad = jnp.einsum("sd,tsf->tdf", mlp_in, grad_pre_low, preferred_element_type=f32)
    fc_bias_part = relative(jnp.sum(grad_pre_low.astype(f32), axis=1)).reshape(-1)
    grad_normed_two = jnp.einsum("tsf,tdf->sd", grad_pre_low, fc_full, preferred_element_type=f32)
    resid_grad = out_grad.astype(f32)
    grad_hidden_ln, second_gain_part, second_shift_part = norm_back(
        grad_normed_two, hat_two, inv_two, second_gain.astype(f32)
    )
    grad_hidden = resid_grad + grad_hidden_ln
    grad_hidden_low = grad_hidden.astype(bf16)
    out_bias_part = jnp.sum(grad_hidden_low.astype(f32), axis=0)
    proj_bias_part = jnp.sum(resid_grad, axis=0)
    out_grad_part = jnp.einsum(
        "sd,psc->pdc", grad_hidden_low, attn_here, preferred_element_type=f32
    )
    live_here = (segments[0] != 0).astype(bf16)
    grad_attn = jnp.einsum("sd,pdc->psc", grad_hidden_low, out_full, preferred_element_type=f32).astype(
        bf16
    ) * live_here[None, :, None]
    grad_attn_seq, kept, passed = exchange_grad(
        grad_attn, (fc_grad.astype(bf16), proj_grad.astype(bf16), out_grad_part.astype(bf16)), 2
    )
    came = across(passed)
    grad_qkv = attend_back(low, qb, ka, va, kt, grad_attn_seq, attn_out, seg_parts, size)
    early = [out_bias_part, second_gain_part, second_shift_part, fc_bias_part, proj_bias_part]
    input_grad, fc_w_grad, proj_w_grad, out_w_grad, qkv_grad, early_sums, late_sums = leave(
        grad_qkv,
        seq_normed,
        qkv_full,
        kept,
        came,
        widths,
        jnp.concatenate(early).reshape(-1, 128),
        inputs,
        first_gain[None],
        grad_hidden,
        3,
    )
    proj_w_grad = proj_w_grad.T
    out_w_grad = out_w_grad.T
    qkv_grad = qkv_grad.reshape(shard_rows, 3, head_cols)
    totals, found, at = early_sums.reshape(-1), [], 0
    for vector in early:
        found.append(totals[at : at + vector.shape[0]])
        at += vector.shape[0]
    out_bias_grad, second_gain_grad, second_shift_grad, fc_bias_grad, proj_bias_grad = found
    first_gain_grad, first_shift_grad = late_sums[0], late_sums[1]
    qv_bias_grad = late_sums[2:4]

    return (
        layer_out,
        input_grad,
        first_gain_grad,
        first_shift_grad,
        qkv_grad,
        qv_bias_grad,
        out_w_grad,
        out_bias_grad,
        second_gain_grad,
        second_shift_grad,
        fc_w_grad,
        fc_bias_grad,
        proj_w_grad,
        proj_bias_grad,
    )


def solution(mesh):
    return jax.shard_map(
        local,
        mesh=mesh,
        in_specs=(
            P(("fsdp", "tp"), None),
            P("fsdp", "tp"),
            P(("fsdp", "tp"), None),
            P(),
            P(),
            P("fsdp", None, "tp"),
            P(),
            P("tp", "fsdp"),
            P(),
            P(),
            P(),
            P("fsdp", "tp"),
            P(),
            P("tp", "fsdp"),
            P(),
        ),
        out_specs=(
            P(("fsdp", "tp"), None),
            P(("fsdp", "tp"), None),
            P(),
            P(),
            P("fsdp", None, "tp"),
            P(),
            P("tp", "fsdp"),
            P(),
            P(),
            P(),
            P("fsdp", "tp"),
            P(),
            P("tp", "fsdp"),
            P(),
        ),
        check_vma=False,
    )
```

```python
import functools

import jax
import jax.numpy as jnp
from jax import lax
from jax.experimental import pallas as pl
from jax.experimental.pallas import tpu as pltpu
from jax.sharding import PartitionSpec as P

HD = 64
VMEM_LIMIT = 60 << 20
epsilon = 1e-05
gelu_slope = 1.702


def layer_norm(values_in, gain_vec, shift_vec):
    mean_row = jnp.mean(values_in, axis=-1, keepdims=True)
    centred = values_in - mean_row
    inverse = lax.rsqrt(jnp.mean(centred * centred, axis=-1, keepdims=True) + epsilon)
    normed = centred * inverse
    return (normed * gain_vec + shift_vec, normed, inverse)


def norm_back(grad_out, normed, inverse, gain_vec):
    scaled = grad_out * gain_vec
    grad_in = inverse * (
        scaled
        - jnp.mean(scaled, axis=-1, keepdims=True)
        - normed * jnp.mean(scaled * normed, axis=-1, keepdims=True)
    )
    return (grad_in, jnp.sum(grad_out * normed, axis=0), jnp.sum(grad_out, axis=0))


f32 = jnp.float32
bf16 = jnp.bfloat16
LOG2E = 1.4426950408889634
BLOCK = 512
TRANSPOSED = (((1,), (1,)), ((), ()))


def dot_t(left, right):
    return lax.dot_general(left, right, TRANSPOSED, preferred_element_type=f32)


def dot_n(left, right):
    return jnp.dot(left, right, preferred_element_type=f32)


def three_parts(value):
    top = value.astype(bf16)
    rest = value - top.astype(f32)
    mid = rest.astype(bf16)
    return top, mid, (rest - mid.astype(f32)).astype(bf16)


def diagonal_mask(seg_ref, row_at, size):
    key_pos = lax.broadcasted_iota(jnp.int32, (size, 1), 0)
    query_pos = lax.broadcasted_iota(jnp.int32, (1, size), 1)
    here = seg_ref.shape[2]
    seg = seg_ref[row_at // here, 0:1, pl.ds(pl.multiple_of(lax.rem(row_at, here), size), size)]
    first = jnp.where(seg == 0, query_pos, 0)
    return (key_pos >= first) & (key_pos <= query_pos)


def attend_kernel(
    low_ref, qa_ref, ka_ref, vt_ref, start_ref, out_ref, qb_ref, s0, s1, a0, a1, *, size, blocks
):
    score_bufs, acc_bufs = (s0, s1), (a0, a1)
    heads = range(qa_ref.shape[0])
    lane = lax.broadcasted_iota(jnp.int32, (size, 128), 1)

    def query_block(i, carry):
        row_at = pl.multiple_of(i * size, size)

        def score(h, j, top, diag):
            keys = ka_ref[h, pl.ds(pl.multiple_of(j * size, size), size), :]
            s = dot_t(keys, qa_ref[h, pl.ds(row_at, size), :])
            if diag:
                s = jnp.where(diagonal_mask(start_ref, row_at, size), s, -3e38)
            score_bufs[h][...] = s
            col_max = jnp.max(s, axis=0, keepdims=True)
            return col_max if top is None else jnp.maximum(top, col_max)

        def gather_values(h, j, old, new, first):
            p = jnp.exp2(score_bufs[h][...] * LOG2E - new * LOG2E).astype(bf16)
            part = dot_n(vt_ref[h, :, pl.ds(pl.multiple_of(j * size, size), size)], p)
            if first:
                acc_bufs[h][...] = part
            else:
                acc_bufs[h][...] = acc_bufs[h][...] * jnp.exp2((old - new) * LOG2E) + part

        low = low_ref[i]
        m0 = score(0, i, None, True)
        m1 = score(1, i, None, True)
        gather_values(0, i, None, m0, True)
        m0n = score(0, jnp.minimum(low, i), m0, False)
        gather_values(1, i, None, m1, True)

        def body(j, c):
            m0, m0n, m1 = c
            m1n = score(1, j, m1, False)
            gather_values(0, j, m0, m0n, False)
            m0nn = score(0, jnp.minimum(j + 1, blocks - 1), m0n, False)
            gather_values(1, j, m1, m1n, False)
            return m0n, m0nn, m1n

        m0, _, m1 = lax.fori_loop(low, i, body, (m0, m0n, m1))
        for h, top in ((0, m0), (1, m1)):
            total = acc_bufs[h][64:65, :]
            out = acc_bufs[h][0:64, :] / total
            rows = qa_ref[h, pl.ds(row_at, size), :]
            live = jnp.where(rows[:, 64:65].astype(f32) != 0.0, 1.0, 0.0)
            out_ref[pl.ds(row_at, size), 64 * h : 64 * h + 64] = (out.T * live).astype(out_ref.dtype)
            norm = jnp.broadcast_to(-(top + jnp.log(total)), (8, size)).T[:, 0:1]
            n0, n1, n2 = three_parts(norm)
            rows = jnp.where(lane == 96, n0, jnp.where(lane == 97, n1, jnp.where(lane == 98, n2, rows)))
            qb_ref[h, pl.ds(row_at, size), :] = rows
        return carry

    lax.fori_loop(0, blocks, query_block, 0)


def attend(low, qa, ka, vt, start, size):
    heads, rows, _ = qa.shape
    vmem = pl.BlockSpec(memory_space=pltpu.VMEM)
    return pl.pallas_call(
        functools.partial(attend_kernel, size=size, blocks=rows // size),
        grid_spec=pltpu.PrefetchScalarGridSpec(
            num_scalar_prefetch=1,
            grid=(),
            in_specs=[vmem] * 4,
            out_specs=[vmem] * 2,
            scratch_shapes=[pltpu.VMEM((size, size), f32)] * heads
            + [pltpu.VMEM((vt.shape[1], size), f32)] * heads,
        ),
        out_shape=[
            jax.ShapeDtypeStruct((rows, HD * heads), bf16),
            jax.ShapeDtypeStruct(qa.shape, bf16),
        ],
        compiler_params=pltpu.CompilerParams(vmem_limit_bytes=VMEM_LIMIT),
        cost_estimate=pl.CostEstimate(
            flops=14 * rows * rows * HD * heads, bytes_accessed=8 << 20, transcendentals=rows * rows
        ),
        name="attend",
    )(low, qa, ka, vt, start)


def attend_back_kernel(
    low_ref, qb_ref, ka_ref, va_ref, kt_ref, g_ref, o_ref, start_ref, grad_ref,
    ga_ref, dk_ref, dv_ref, q0, q1, *, size, blocks
):
    query_accs = (q0, q1)
    lane = lax.broadcasted_iota(jnp.int32, (size, 64), 1)

    def query_block(i, carry):
        row_at = pl.multiple_of(i * size, size)
        g_rows = g_ref[pl.ds(row_at, size), :]
        product = g_rows.astype(f32) * o_ref[pl.ds(row_at, size), :].astype(f32)
        for h in range(2):
            cols = slice(64 * h, 64 * h + 64)
            n0, n1, n2 = three_parts(-jnp.sum(product[:, cols], axis=1, keepdims=True))
            zero = jnp.zeros((size, 64), bf16)
            extra = jnp.where(lane == 0, n0, jnp.where(lane == 1, n1, jnp.where(lane == 2, n2, zero)))
            ga_ref[h] = jnp.concatenate([g_rows[:, cols], extra], axis=1)

        def block(h, j, diag):
            key_at = pl.multiple_of(j * size, size)
            keys = ka_ref[h, pl.ds(key_at, size), :]
            q_rows = qb_ref[h, pl.ds(row_at, size), :]
            g_head = ga_ref[h]
            s = dot_t(keys, q_rows)
            if diag:
                s = jnp.where(diagonal_mask(start_ref, row_at, size), s, -3e38)
            p = jnp.exp2(s * LOG2E)
            dp = dot_t(va_ref[h, pl.ds(key_at, size), :], g_head)
            ds = (p * dp).astype(bf16)
            dv = dot_n(p.astype(bf16), g_head[:, 0:64])
            dk = dot_n(ds, q_rows[:, 0:64])
            dq = dot_n(kt_ref[h, :, pl.ds(key_at, size)], ds)
            if diag:
                dv_ref[h, pl.ds(key_at, size), :] = dv
                dk_ref[h, pl.ds(key_at, size), :] = dk
                query_accs[h][...] = dq
            else:
                dv_ref[h, pl.ds(key_at, size), :] += dv
                dk_ref[h, pl.ds(key_at, size), :] += dk
                query_accs[h][...] += dq

        block(0, i, True)
        block(1, i, True)

        def body(j, c):
            block(0, j, False)
            block(1, j, False)
            return c

        lax.fori_loop(low_ref[i], i, body, 0)
        both = jnp.concatenate([query_accs[0][...], query_accs[1][...]], axis=0) * HD ** (-0.5)
        grad_ref[pl.ds(row_at, size), 0:128] = both.T.astype(bf16)
        return carry

    lax.fori_loop(0, blocks, query_block, 0)

    def finish(i, carry):
        row_at = pl.multiple_of(i * size, size)
        for ref, at in ((dk_ref, 128), (dv_ref, 256)):
            both = jnp.concatenate([ref[0, pl.ds(row_at, size), :], ref[1, pl.ds(row_at, size), :]], axis=1)
            grad_ref[pl.ds(row_at, size), at : at + 128] = both.astype(bf16)
        return carry

    lax.fori_loop(0, blocks, finish, 0)


def attend_back(low, qb, ka, va, kt, g, o, start, size):
    heads, rows, _ = qb.shape
    vmem = pl.BlockSpec(memory_space=pltpu.VMEM)
    return pl.pallas_call(
        functools.partial(attend_back_kernel, size=size, blocks=rows // size),
        grid_spec=pltpu.PrefetchScalarGridSpec(
            num_scalar_prefetch=1,
            grid=(),
            in_specs=[vmem] * 7,
            out_specs=vmem,
            scratch_shapes=[
                pltpu.VMEM((heads, size, 128), bf16),
                pltpu.VMEM((heads, rows, HD), f32),
                pltpu.VMEM((heads, rows, HD), f32),
            ]
            + [pltpu.VMEM((HD, size), f32)] * heads,
        ),
        out_shape=jax.ShapeDtypeStruct((rows, 3 * HD * heads), bf16),
        compiler_params=pltpu.CompilerParams(vmem_limit_bytes=VMEM_LIMIT),
        cost_estimate=pl.CostEstimate(
            flops=24 * rows * rows * HD * heads, bytes_accessed=16 << 20, transcendentals=rows * rows
        ),
        name="attend_back",
    )(low, qb, ka, va, kt, g, o, start)


def first_blocks(seg_all, size):
    firsts = seg_all[::size]
    before = jnp.sum(((seg_all > 0) & (seg_all < firsts[:, None])).astype(jnp.int32), axis=1)
    own = jnp.arange(firsts.shape[0], dtype=jnp.int32)
    return jnp.where(firsts == 0, own, before // size)


MESH = pl.DeviceIdType.MESH


def greet(peers):
    barrier = pltpu.get_barrier_semaphore()
    for peer in peers:
        pl.semaphore_signal(barrier, inc=1, device_id=peer, device_id_type=MESH)
    pl.semaphore_wait(barrier, len(peers))


def push(source, target, send_sem, recv_sem, peer):
    copy = pltpu.make_async_remote_copy(
        src_ref=source,
        dst_ref=target,
        send_sem=send_sem,
        recv_sem=recv_sem,
        device_id=peer,
        device_id_type=MESH,
    )
    copy.start()
    return copy


def quad():
    me = lax.axis_index("tp")
    side = me + 1 - 2 * lax.rem(me, 2)
    across = lax.rem(me + 2, 4)
    far = lax.rem(side + 2, 4)
    return me, side, across, far


def comm_call(kernel, name, number, out_shape, in_specs, out_specs, scratch, moved, *operands):
    return pl.pallas_call(
        kernel,
        out_shape=out_shape,
        in_specs=in_specs,
        out_specs=out_specs,
        scratch_shapes=scratch,
        compiler_params=pltpu.CompilerParams(
            collective_id=number, has_side_effects=True, vmem_limit_bytes=VMEM_LIMIT
        ),
        cost_estimate=pl.CostEstimate(flops=0, bytes_accessed=moved, transcendentals=0),
        name=name,
    )(*operands)


def in_vmem():
    return pl.BlockSpec(memory_space=pltpu.VMEM)


def anywhere():
    return pl.BlockSpec(memory_space=pl.ANY)


def flipped(axis, mask):
    me, index, bit = lax.axis_index(axis), lax.axis_index(axis), 1
    while bit <= mask:
        if mask & bit:
            index = index + bit - 2 * bit * lax.rem(me // bit, 2)
        bit *= 2
    return index


def awaited(ref, send_sem, recv_sem, peer):
    return pltpu.make_async_remote_copy(ref, ref, send_sem, recv_sem, peer, MESH)


def hop_masks(size):
    hops, bit = [], size // 2
    while bit >= 1:
        hops.append((bit, [high + bit for high in range(0, size, 2 * bit)]))
        bit //= 2
    return hops


def enter_kernel(
    x_ref, gain_ref, shift_ref, bias_ref, seg_ref, w0, w1, w2, w3,
    normed_ref, segs_ref, qa_ref, ka_ref, va_ref, vt_ref, kt_ref, f0, f1,
    x_all, normed_s, qa_s, ka_s, va_s, vt_s, kt_s,
    sy, ry, ss, rs, sf, rf, sg, rg, sw, rw, own, own_w, outs, *, parts
):
    me, side, across, far = quad()
    rows = x_ref.shape[0]
    step = rows // parts
    shards = f0.shape[0]
    heads = qa_ref.shape[0]
    width = HD * heads
    shard = lax.axis_index("fsdp")
    hops = hop_masks(shards)
    greet(
        [{"tp": side}, {"tp": across}, {"tp": far}]
        + [{"fsdp": flipped("fsdp", bit)} for bit, _ in hops]
    )
    sent = []

    def rows_of(owner, part):
        return x_all.at[pl.ds(pl.multiple_of(owner * rows + part * step, step), step)]

    sources = (w0, w1, w2, w3)

    def block_of(g, index):
        if g == 0:
            return f0.at[index]
        at = sum(w.shape[1] for w in sources[1:g])
        return f1.at[index, :, pl.ds(at, sources[g].shape[1])]

    def send_hop(g, hop):
        bit, masks = hops[hop]
        peer = {"fsdp": flipped("fsdp", bit)}
        if hop > 0:
            before, arrived = hops[hop - 1]
            for mask in arrived:
                block = block_of(g, flipped("fsdp", mask))
                awaited(block, sw.at[g, mask], rw.at[g, mask], {"fsdp": flipped("fsdp", before)}).wait_recv()
        for mask in masks:
            target = block_of(g, flipped("fsdp", mask - bit))
            block = sources[g] if mask == bit else target
            sent.append(push(block, target, sw.at[g, mask], rw.at[g, mask], peer))

    def end_hops(g):
        bit, arrived = hops[-1]
        for mask in arrived:
            block = block_of(g, flipped("fsdp", mask))
            awaited(block, sw.at[g, mask], rw.at[g, mask], {"fsdp": flipped("fsdp", bit)}).wait_recv()

    for k, peer in enumerate((across, far, side)):
        sent.append(push(seg_ref, segs_ref.at[me], sg.at[k], rg.at[k], {"tp": peer}))
    send_hop(0, 0)
    for part in range(parts):
        mine = x_ref.at[pl.ds(part * step, step)]
        sent.append(push(mine, rows_of(me, part), sy.at[part], ry.at[part], {"tp": across}))
    send_hop(0, 1)
    for g in (1, 2, 3):
        send_hop(g, 0)
    for part in range(parts):
        mine = x_ref.at[pl.ds(part * step, step)]
        sent.append(push(mine, rows_of(me, part), ss.at[part], rs.at[part], {"tp": side}))
    kept = [
        pltpu.make_async_copy(x_ref, x_all.at[pl.ds(pl.multiple_of(me * rows, rows), rows)], own.at[0]),
        pltpu.make_async_copy(seg_ref, segs_ref.at[me], own.at[1]),
    ] + [pltpu.make_async_copy(source, block_of(g, shard), own_w.at[g]) for g, source in enumerate(sources)]
    for copy in kept:
        copy.start()
    waves = sorted(
        ((hop + g, g, hop) for hop in range(1, len(hops)) for g in range(4)), key=lambda w: (w[0], w[1])
    )
    for _, g, hop in waves[1:2]:
        send_hop(g, hop)
    for k, peer in enumerate((across, far, side)):
        awaited(segs_ref.at[peer], sg.at[k], rg.at[k], {"tp": peer}).wait_recv()
    for part in range(parts):
        awaited(rows_of(side, part), ss.at[part], rs.at[part], {"tp": side}).wait_recv()
    for copy in kept:
        copy.wait()
    gain, shift = gain_ref[...].astype(f32), shift_ref[...].astype(f32)

    def norm(owner, part):
        span = pl.ds(pl.multiple_of(owner * rows + part * step, step), step)
        x = x_all[span, :].astype(f32)
        centred = x - jnp.mean(x, axis=-1, keepdims=True)
        inverse = lax.rsqrt(jnp.mean(centred * centred, axis=-1, keepdims=True) + epsilon)
        normed_s[span, :] = (centred * inverse * gain + shift).astype(bf16)

    def norm_near(k, carry):
        norm(me + lax.rem(k, 2) * (side - me), k // 2)
        return carry

    lax.fori_loop(0, 2 * parts, norm_near, 0)
    for _, g, hop in waves[2:]:
        send_hop(g, hop)
    end_hops(0)
    bias_at = pl.ds(pl.multiple_of(me * width, width), width)
    query_bias = bias_ref[0:1, bias_at].astype(f32)
    value_bias = bias_ref[1:2, bias_at].astype(f32)
    number = lax.broadcasted_iota(jnp.int32, (step, 64), 1)
    number_f = number.astype(f32)
    key_ones = (number >= 32) & (number < 35)
    value_tail = jnp.where(number < 3, 1.0, 0.0).astype(bf16)
    ones_row = jnp.where(lax.broadcasted_iota(jnp.int32, (16, step), 0) == 0, 1.0, 0.0).astype(bf16)

    def copies_out(owner, part):
        row = pl.multiple_of(owner * rows + part * step, step)
        slot = owner * parts + part
        span = pl.ds(row, step)
        pairs = [(normed_s.at[span], normed_ref.at[span])]
        for a, b in ((qa_s, qa_ref), (ka_s, ka_ref), (va_s, va_ref)):
            pairs.append((a.at[:, span, :], b.at[:, span, :]))
        for a, b in ((vt_s, vt_ref), (kt_s, kt_ref)):
            pairs.append((a.at[:, :, span], b.at[:, :, span]))
        return [pltpu.make_async_copy(a, b, outs.at[n, slot]) for n, (a, b) in enumerate(pairs)]

    def compute(owner, part):
        row = pl.multiple_of(owner * rows + part * step, step)
        span = pl.ds(row, step)
        normed = normed_s[span, :]
        weights = f0[...].reshape(shards * f0.shape[1], 3 * width)
        projected = dot_n(normed, weights)
        queries = ((projected[:, 0:width] + query_bias).astype(bf16).astype(f32) * HD ** (-0.5)).astype(bf16)
        keys = projected[:, width : 2 * width].astype(bf16)
        values = (projected[:, 2 * width : 3 * width] + value_bias).astype(bf16)
        seg = segs_ref[owner, 0:1, pl.ds(pl.multiple_of(part * step, step), step)].astype(f32)
        seg = jnp.broadcast_to(seg, (8, step)).T[:, 0:1]
        same = (seg == number_f) & (number < 32)
        other = jnp.where(same | (number > 31), 0.0, -1e30).astype(bf16)
        key_tail = jnp.where(same | key_ones, 1.0, 0.0).astype(bf16)
        for h in range(heads):
            cols = slice(HD * h, HD * h + HD)
            qa_s[h, span, :] = jnp.concatenate([queries[:, cols], other], axis=1)
            ka_s[h, span, :] = jnp.concatenate([keys[:, cols], key_tail], axis=1)
            va_s[h, span, :] = jnp.concatenate([values[:, cols], value_tail], axis=1)
            turned = jnp.concatenate([values[:, cols], keys[:, cols]], axis=1).astype(f32).T.astype(bf16)
            vt_s[h, 0:64, span] = turned[0:64, :]
            vt_s[h, 64:80, span] = ones_row
            kt_s[h, :, span] = turned[64:128, :]
        for copy in copies_out(owner, part):
            copy.start()

    def work(k, carry):
        distant = k // (2 * parts)
        part = lax.rem(k // 2, parts)
        second = lax.rem(k, 2)

        @pl.when((distant == 0) & (second == 0))
        def _():
            here = rows_of(across, part)
            awaited(here, sy.at[part], ry.at[part], {"tp": across}).wait_recv()
            push(here, here, sf.at[part], rf.at[part], {"tp": side})

        @pl.when((distant == 1) & (second == 1))
        def _():
            awaited(rows_of(far, part), sf.at[part], rf.at[part], {"tp": side}).wait_recv()

        @pl.when(distant == 1)
        def _():
            norm(across + second * (far - across), part)

        first = me + distant * (across - me)
        compute(first + second * (side - me + distant * (far - across - side + me)), part)
        return carry

    lax.fori_loop(0, 4 * parts, work, 0)
    for g in (1, 2, 3):
        end_hops(g)

    def drain(k, carry):
        for copy in copies_out(k // parts, lax.rem(k, parts)):
            copy.wait()
        return carry

    lax.fori_loop(0, 4 * parts, drain, 0)
    for part in range(parts):
        awaited(rows_of(across, part), sf.at[part], rf.at[part], {"tp": side}).wait_send()
    for copy in sent:
        copy.wait_send()


def enter(x, gain, shift, bias, segments, weights, number, parts=4):
    rows, width = x.shape
    seq_rows = 4 * rows
    shards = lax.axis_size("fsdp")
    heads = weights[0].shape[1] // (3 * HD)
    dma = pltpu.SemaphoreType.DMA
    wide = (heads, seq_rows, 128)
    shard_rows = weights[0].shape[0]
    full = [(shards, *weights[0].shape), (shards, shard_rows, sum(w.shape[1] for w in weights[1:]))]
    shapes = [(seq_rows, width), wide, wide, wide, (heads, 80, seq_rows), (heads, 64, seq_rows)]
    made = [jax.ShapeDtypeStruct(s, bf16) for s in shapes]
    return comm_call(
        functools.partial(enter_kernel, parts=parts),
        "enter",
        number,
        [made[0], jax.ShapeDtypeStruct((4, *segments.shape), segments.dtype)]
        + made[1:]
        + [jax.ShapeDtypeStruct(s, bf16) for s in full],
        [in_vmem()] * 9,
        [anywhere(), in_vmem()] + [anywhere()] * 5 + [in_vmem(), anywhere()],
        [pltpu.VMEM((seq_rows, width), bf16)]
        + [pltpu.VMEM(s, bf16) for s in shapes]
        + [dma((parts,))] * 6
        + [dma((3,))] * 2
        + [dma((4, shards))] * 2
        + [dma((2,)), dma((4,)), dma((6, 4 * parts))],
        60 << 20,
        x,
        gain,
        shift,
        bias,
        segments,
        *weights,
    )


def exchange_out_kernel(x_ref, o_ref, c_ref, out_ref, g0, g1, g2, sems, rems, ws, wr, own):
    me, side, across, far = quad()
    rows = x_ref.shape[0] // 4
    greet([{"tp": side}, {"tp": across}, {"tp": far}])
    peers = {1: side, 2: across, 3: far}

    def mine(owner):
        return x_ref.at[pl.ds(pl.multiple_of(owner * rows, rows), rows)]

    weights, at = [], 0
    for full in (g0, g1, g2):
        cols = pl.ds(at, full.shape[2])
        weights.append((o_ref.at[:, cols], c_ref.at[:, cols], full))
        at += full.shape[2]
    sent = [push(mine(peers[k]), out_ref.at[k], sems.at[k], rems.at[k], {"tp": peers[k]}) for k in (3, 2, 1)]
    for n, (here, over, full) in enumerate(weights):
        sent.append(push(here, full.at[1], ws.at[0, n], wr.at[0, n], {"tp": side}))
        sent.append(push(over, full.at[3], ws.at[1, n], wr.at[1, n], {"tp": side}))
    kept = [pltpu.make_async_copy(mine(me), out_ref.at[0], own.at[0])]
    for n, (here, over, full) in enumerate(weights):
        kept.append(pltpu.make_async_copy(here, full.at[0], own.at[2 * n + 1]))
        kept.append(pltpu.make_async_copy(over, full.at[2], own.at[2 * n + 2]))
    for copy in kept:
        copy.start()
    for copy in kept:
        copy.wait()
    for copy in sent:
        copy.wait()


def exchange_out(x, own, over, widths, number):
    rows, width = x.shape
    dma = pltpu.SemaphoreType.DMA
    return comm_call(
        exchange_out_kernel,
        "exchange_out",
        number,
        [jax.ShapeDtypeStruct((4, rows // 4, width), x.dtype)]
        + [jax.ShapeDtypeStruct((4, own.shape[0], w), own.dtype) for w in widths],
        [in_vmem()] * 3,
        [in_vmem()] + [anywhere()] * 3,
        [dma((4,)), dma((4,)), dma((2, 3)), dma((2, 3)), dma((7,))],
        60 << 20,
        x,
        own,
        over,
    )


def exchange_grad_kernel(
    x_ref, g0, g1, g2, out_ref, kept_ref, over_ref, sems, rems, ws, wr, own, loads, *boxes
):
    me, side, across, far = quad()
    greet([{"tp": side}, {"tp": across}, {"tp": far}])
    peers = {1: side, 2: across, 3: far}
    rows = x_ref.shape[1]

    def slot(owner):
        return out_ref.at[pl.ds(pl.multiple_of(owner * rows, rows), rows)]

    grads = (g0, g1, g2)
    count = len(grads)
    own_bufs = boxes[2 * count :]
    loading = []
    for n, grad in enumerate(grads):
        for k in (0, 1):
            loading.append(pltpu.make_async_copy(grad.at[2 * k], own_bufs[2 * n + k], loads.at[n, k]))
    for copy in loading:
        copy.start()
    sent = [push(x_ref.at[k], slot(me), sems.at[k], rems.at[k], {"tp": peers[k]}) for k in (3, 2)]
    folded = []
    for n, grad in enumerate(grads):
        folded.append(push(grad.at[3], boxes[2 * n + 1], ws.at[1, n], wr.at[1, n], {"tp": side}))
        folded.append(push(grad.at[1], boxes[2 * n], ws.at[0, n], wr.at[0, n], {"tp": side}))
    sent.append(push(x_ref.at[1], slot(me), sems.at[1], rems.at[1], {"tp": side}))
    keep = pltpu.make_async_copy(x_ref.at[0], slot(me), own)
    keep.start()
    at = 0
    for n, grad in enumerate(grads):
        cols = slice(at, at + grad.shape[2])
        at += grad.shape[2]
        loading[2 * n].wait()
        loading[2 * n + 1].wait()
        folded[2 * n].wait()
        over_ref[:, cols] = (own_bufs[2 * n + 1][...].astype(f32) + boxes[2 * n + 1][...].astype(f32)).astype(bf16)
        folded[2 * n + 1].wait()
        kept_ref[:, cols] = (own_bufs[2 * n][...].astype(f32) + boxes[2 * n][...].astype(f32)).astype(bf16)
    keep.wait()
    for k, peer in ((3, far), (2, across), (1, side)):
        awaited(slot(peer), sems.at[k], rems.at[k], {"tp": peer}).wait_recv()
    for copy in sent:
        copy.wait_send()


def exchange_grad(x, grads, number):
    _, rows, width = x.shape
    dma = pltpu.SemaphoreType.DMA
    piece = jax.ShapeDtypeStruct((grads[0].shape[1], sum(g.shape[2] for g in grads)), x.dtype)
    boxes = []
    for g in grads:
        boxes += [pltpu.VMEM(g.shape[1:], g.dtype)] * 2
    return comm_call(
        exchange_grad_kernel,
        "exchange_grad",
        number,
        [jax.ShapeDtypeStruct((4 * rows, width), x.dtype), piece, piece],
        [in_vmem()] + [anywhere()] * 3,
        [in_vmem()] * 3,
        [dma((4,)), dma((4,)), dma((2, 3)), dma((2, 3)), dma, dma((3, 2))] + boxes * 2,
        60 << 20,
        x,
        *grads,
    )


def leave_kernel(
    grad_ref, normed_in, w_ref, kept_ref, came_ref, early_ref, x_in, gain_ref, resid_in,
    input_ref, s0, s1, s2, s3, early_out, late_out,
    rows_ref, far_out, own_out, sum_buf, side_far, side_own, over, dw_acc, cols_ref,
    late_ref, early_mid, late_mid, early_one, early_two, late_one, late_two,
    normed_ref, x_ref, resid_ref, loads,
    sa, ra, sb, rb, sy, ry, sw, rw, se, re, sl, rl, se2, re2, sl2, rl2, *bufs, parts, hops
):
    me, side, across, far = quad()
    rows = rows_ref.shape[0]
    step = rows // parts
    shard, shards = lax.axis_index("fsdp"), early_two.shape[0]
    pairs = ((normed_in, normed_ref), (x_in, x_ref), (resid_in, resid_ref))
    loading = [pltpu.make_async_copy(a, b, loads.at[n]) for n, (a, b) in enumerate(pairs)]
    for copy in loading:
        copy.start()
    barrier = pltpu.get_barrier_semaphore()
    for peer in (side, across, far):
        pl.semaphore_signal(barrier, inc=1, device_id={"tp": peer}, device_id_type=MESH)

    def other(k):
        return {"fsdp": lax.rem(shard + k, shards)}

    def signal(k, carry):
        pl.semaphore_signal(barrier, inc=1, device_id=other(k), device_id_type=MESH)
        return carry

    lax.fori_loop(1, shards, signal, 0)
    pl.semaphore_wait(barrier, 3 + shards - 1)
    count = len(hops)
    outs = (s0, s1, s2, s3)
    current = bufs[0:4]
    boxes = [bufs[4 + g * count : 4 + (g + 1) * count] for g in range(4)]
    keeps = [bufs[4 + 4 * count + g * (count - 1) : 4 + 4 * count + (g + 1) * (count - 1)] for g in range(4)]
    sent = []

    def begin(g):
        at = sum(c.shape[3] for c in current[0:g])
        cols = slice(at, at + current[g].shape[3])
        total = kept_ref[:, :, :, cols].astype(f32) + came_ref[:, :, :, cols].astype(f32)
        current[g][...] = total.astype(bf16)

    def hop_parts(g, k):
        axis, bit = hops[k]
        source = current[g] if k == 0 else keeps[g][k - 1]
        half = lax.rem(lax.axis_index(axis) // bit, 2)
        return {axis: flip(axis, bit)}, source, half, boxes[g][k]

    def hop_send(g, k):
        peer, source, half, box = hop_parts(g, k)
        sent.append(push(source.at[:, 1 - half], box, sw.at[g, k], rw.at[g, k], peer))

    def hop_add(g, k):
        peer, source, half, box = hop_parts(g, k)
        awaited(box, sw.at[g, k], rw.at[g, k], peer).wait_recv()
        if k == count - 1:
            outs[g][...] = source[0, half].astype(f32) + box[0].astype(f32)
        else:
            target = keeps[g][k]
            for n in range(box.shape[0]):
                total = source[n, half].astype(f32) + box[n].astype(f32)
                target[n // 2, n % 2] = total.astype(bf16)
            hop_send(g, k + 1)

    def tp_send(value, box, send, recv):
        box[me] = value[...]
        for k, peer in enumerate((side, across, far)):
            sent.append(push(value, box.at[me], send.at[k], recv.at[me], {"tp": peer}))

    def tp_sum(value, box, send, recv):
        for k, peer in enumerate((side, across, far)):
            awaited(box.at[peer], send.at[k], recv.at[peer], {"tp": peer}).wait_recv()
        value[...] = box[0] + box[1] + box[2] + box[3]

    def fsdp_send(value, box, send, recv):
        box[shard] = value[...]

        def give(k, carry):
            push(value, box.at[shard], send.at[k], recv.at[shard], other(k))
            return carry

        lax.fori_loop(1, shards, give, 0)

    def fsdp_sum(value, target, box, send, recv):
        def take(k, carry):
            peer = lax.rem(shard + k, shards)
            copy = awaited(box.at[peer], send.at[k], recv.at[peer], other(k))
            copy.wait_recv()
            copy.wait_send()
            return carry

        lax.fori_loop(1, shards, take, 0)
        target[...] = lax.fori_loop(1, shards, lambda n, total: total + box[n], box[0])

    def span(owner, part):
        return pl.ds(pl.multiple_of(owner * rows + part * step, step), step)

    def piece(part):
        return pl.ds(pl.multiple_of(part * step, step), step)

    def partial(owner, part):
        return dot_t(grad_ref[span(owner, part), :], w_ref[...])

    def give_far(part, carry):
        here = piece(part)
        far_out[here, :] = partial(far, part).astype(bf16)
        push(far_out.at[here], side_far.at[here], sa.at[part], ra.at[part], {"tp": side})
        return carry

    def give_over(part, carry):
        here = piece(part)
        mine = partial(across, part)
        awaited(side_far.at[here], sa.at[part], ra.at[part], {"tp": side}).wait_recv()
        sum_buf[here, :] = (mine + side_far[here, :].astype(f32)).astype(bf16)
        push(sum_buf.at[here], over.at[here], sy.at[part], ry.at[part], {"tp": across})
        return carry

    def give_own(part, carry):
        here = piece(part)
        own_out[here, :] = partial(side, part).astype(bf16)
        push(own_out.at[here], side_own.at[here], sb.at[part], rb.at[part], {"tp": side})
        return carry

    def take_own(part, carry):
        here = piece(part)
        mine = partial(me, part)
        awaited(side_own.at[here], sb.at[part], rb.at[part], {"tp": side}).wait_recv()
        rows_ref[here, :] = mine + side_own[here, :].astype(f32)
        return carry

    gain = gain_ref[...].astype(f32)

    def take_over(part, carry):
        here = piece(part)
        x = x_ref[here, :].astype(f32)
        centred = x - jnp.mean(x, axis=-1, keepdims=True)
        inverse = lax.rsqrt(jnp.mean(centred * centred, axis=-1, keepdims=True) + epsilon)
        normed = centred * inverse
        awaited(over.at[here], sy.at[part], ry.at[part], {"tp": across}).wait_recv()
        grad = rows_ref[here, :] + over[here, :].astype(f32)
        grad_in, gain_part, shift_part = norm_back(grad, normed, inverse, gain)
        input_ref[here, :] = (resid_ref[here, :] + grad_in).astype(bf16)
        late_ref[0:1, :] += gain_part[None]
        late_ref[1:2, :] += shift_part[None]
        return carry

    def drain(part, carry):
        here = piece(part)
        awaited(far_out.at[here], sa.at[part], ra.at[part], {"tp": side}).wait_send()
        awaited(own_out.at[here], sb.at[part], rb.at[part], {"tp": side}).wait_send()
        awaited(sum_buf.at[here], sy.at[part], ry.at[part], {"tp": across}).wait_send()
        return carry

    chunk = 512
    steps = grad_ref.shape[0] // chunk
    dw_acc[...] = jnp.zeros_like(dw_acc)
    cols_ref[...] = jnp.zeros_like(cols_ref)
    ones = jnp.ones((8, chunk), bf16)

    def weight_grad(n, carry):
        at = pl.ds(pl.multiple_of(n * chunk, chunk), chunk)
        g = grad_ref[at, :]
        dw_acc[...] += lax.dot_general(
            normed_ref[at, :], g, (((0,), (0,)), ((), ())), preferred_element_type=f32
        )
        cols_ref[...] += dot_n(ones, g)
        return carry

    tp_send(early_ref, early_one, se, re)
    lax.fori_loop(0, parts, give_far, 0)
    for g in (0, 1):
        begin(g)
        hop_send(g, 0)
    lax.fori_loop(0, parts, give_over, 0)
    begin(2)
    hop_send(2, 0)
    for copy in loading:
        copy.wait()
    lax.fori_loop(0, steps // 2, weight_grad, 0)
    hop_add(0, 0)
    lax.fori_loop(steps // 2, steps, weight_grad, 0)
    current[3][...] = dw_acc[...].astype(bf16).reshape(current[3].shape)
    hop_send(3, 0)
    tp_sum(early_mid, early_one, se, re)
    fsdp_send(early_mid, early_two, se2, re2)
    hop_add(1, 0)
    late_ref[...] = jnp.zeros_like(late_ref)
    wide = cols_ref.shape[1] // 3
    qv_at = pl.ds(pl.multiple_of(me * wide, wide), wide)
    late_ref[2:3, qv_at] = cols_ref[0:1, 0:wide]
    late_ref[3:4, qv_at] = cols_ref[0:1, 2 * wide : 3 * wide]
    lax.fori_loop(0, parts, give_own, 0)
    order = sorted(((k + g, g, k) for g in range(4) for k in range(count)), key=lambda w: (w[0], w[1]))
    order = [(g, k) for _, g, k in order if (g, k) not in ((0, 0), (1, 0))]
    lax.fori_loop(0, parts, take_own, 0)
    taken = {len(order) * share // 10: span for share, span in ((6, (0, 2)), (7, (2, 3)), (9, (3, 4)))}
    for n, (g, k) in enumerate(order):
        if n in taken:
            first, last = taken[n]
            lax.fori_loop(first * parts // 4, last * parts // 4, take_over, 0)
        if n == len(order) - 1:
            tp_send(late_ref, late_one, sl, rl)
        hop_add(g, k)
    fsdp_sum(early_mid, early_out, early_two, se2, re2)
    tp_sum(late_mid, late_one, sl, rl)
    fsdp_send(late_mid, late_two, sl2, rl2)
    lax.fori_loop(0, parts, drain, 0)
    fsdp_sum(late_mid, late_out, late_two, sl2, rl2)
    for copy in sent:
        copy.wait_send()


def leave(grad, normed, w, kept, came, widths, early, x, gain, resid, number, parts=4):
    rows, width = grad.shape[0] // 4, w.shape[0]
    dma = pltpu.SemaphoreType.DMA
    hops = bits_of("fsdp")
    count = len(hops)
    shards = lax.axis_size("fsdp")
    shard = width // shards
    widths = [*widths, grad.shape[1]]
    split = (shards // 2, 2, shard)
    current = [pltpu.VMEM((*split, n), bf16) for n in widths]
    boxes = [pltpu.VMEM((shards >> (k + 1), shard, n), bf16) for n in widths for k in range(count)]
    keeps = [pltpu.VMEM((shards >> (k + 2), 2, shard, n), bf16) for n in widths for k in range(count - 1)]
    late = (4, width)
    return comm_call(
        functools.partial(leave_kernel, parts=parts, hops=hops),
        "leave",
        number,
        [jax.ShapeDtypeStruct((rows, width), bf16)]
        + [jax.ShapeDtypeStruct((shard, n), f32) for n in widths]
        + [jax.ShapeDtypeStruct(early.shape, f32), jax.ShapeDtypeStruct(late, f32)],
        [in_vmem(), anywhere()] + [in_vmem()] * 4 + [anywhere(), in_vmem(), anywhere()],
        [in_vmem()] * 7,
        [pltpu.VMEM((rows, width), f32)]
        + [pltpu.VMEM((rows, width), bf16)] * 6
        + [pltpu.VMEM((width, grad.shape[1]), f32), pltpu.VMEM((8, grad.shape[1]), f32)]
        + [pltpu.VMEM(late, f32), pltpu.VMEM(early.shape, f32), pltpu.VMEM(late, f32)]
        + [pltpu.VMEM((n, *shape), f32) for shape in (early.shape, late) for n in (4, shards)]
        + [pltpu.VMEM(v.shape, v.dtype) for v in (normed, x, resid)]
        + [dma((3,))]
        + [dma((parts,))] * 6
        + [dma((4, count))] * 2
        + [dma((3,)), dma((4,))] * 2
        + [dma((shards,))] * 4
        + current
        + boxes
        + keeps,
        60 << 20,
        grad,
        normed,
        w,
        kept.reshape(*split, kept.shape[1]),
        came.reshape(*split, came.shape[1]),
        early,
        x,
        gain,
        resid,
    )


def finish_kernel(
    rows_in, fc_in, proj_in, out_in, qkv_in, early_in, late_in,
    rows_ref, fc_ref, proj_ref, out_ref, qkv_ref, qv_ref, *vectors
):
    rows_ref[...] = rows_in[...]
    fc_ref[...] = fc_in[...]
    proj_ref[...] = proj_in[...]
    out_ref[...] = out_in[...]
    width = qkv_ref.shape[2]
    for n in range(3):
        qkv_ref[n] = qkv_in[:, n * width : (n + 1) * width]
    qv_ref[...] = late_in[2:4, :]
    lanes = early_in.shape[1]
    for n, ref in enumerate(vectors[0:2]):
        for row in range(ref.shape[0]):
            ref[row : row + 1, :] = late_in[n : n + 1, row * lanes : (row + 1) * lanes]
    at = 0
    for ref in vectors[2:]:
        ref[...] = early_in[at : at + ref.shape[0], :]
        at += ref.shape[0]


def finish(rows, fc, proj, out, qkv, early, late, sizes):
    lanes = early.shape[1]
    shapes = [rows, fc, proj, out]
    outs = [jax.ShapeDtypeStruct(v.shape, v.dtype) for v in shapes]
    outs.append(jax.ShapeDtypeStruct((3, qkv.shape[0], qkv.shape[1] // 3), f32))
    outs.append(jax.ShapeDtypeStruct((2, late.shape[1]), f32))
    outs += [jax.ShapeDtypeStruct((n // lanes, lanes), f32) for n in (late.shape[1], late.shape[1], *sizes)]
    rows, fc, proj, out, qkv, qv, *vectors = pl.pallas_call(
        finish_kernel,
        out_shape=outs,
        in_specs=[in_vmem()] * 7,
        out_specs=[in_vmem()] * len(outs),
        cost_estimate=pl.CostEstimate(flops=0, bytes_accessed=3 << 20, transcendentals=0),
        name="finish",
    )(rows, fc, proj, out, qkv, early, late)
    return rows, fc, proj.T, out.T, qkv.transpose(1, 0, 2), qv, [v.reshape(-1) for v in vectors]


def flip(axis, bit):
    me = lax.axis_index(axis)
    return me + bit - 2 * bit * lax.rem(me // bit, 2)


def bits_of(axis):
    size, bits, bit = lax.axis_size(axis), [], 1
    while bit < size:
        bits.append((axis, bit))
        bit *= 2
    return bits


def relative(value):
    me = lax.axis_index("tp")
    pairs = value.reshape(2, 2, *value.shape[1:])
    pairs = jnp.where(lax.rem(me, 2) == 1, pairs[:, ::-1], pairs)
    pairs = jnp.where(me // 2 == 1, pairs[::-1], pairs)
    return pairs.reshape(value.shape)


def across(value):
    return lax.ppermute(value, "tp", [(n, n ^ 2) for n in range(4)])


def local(
    inputs,
    segments,
    out_grad,
    first_gain,
    first_shift,
    qkv_weight,
    qv_bias,
    out_weight,
    out_bias,
    second_gain,
    second_shift,
    fc_weight,
    fc_bias,
    proj_weight,
    proj_bias,
):
    slices = lax.axis_size("tp")
    rows_here, model_width = inputs.shape
    shard_rows = qkv_weight.shape[0]
    head_cols = qkv_weight.shape[2]
    hidden_cols = fc_weight.shape[1]
    seq_normed, seg_parts, qa, ka, va, vt, kt, qkv_full, own = enter(
        inputs,
        first_gain[None],
        first_shift[None],
        qv_bias,
        segments,
        (qkv_weight.reshape(shard_rows, 3 * head_cols), fc_weight, proj_weight.T, out_weight.T),
        0,
    )
    qkv_full = qkv_full.reshape(model_width, 3 * head_cols)
    own = own.reshape(model_width, own.shape[2])
    over = across(own)
    widths = (hidden_cols, hidden_cols, head_cols)

    resid_in = inputs.astype(f32)
    seq_rows = seq_normed.shape[0]
    seg_all = seg_parts.reshape(seq_rows)
    size = min(BLOCK, rows_here)
    low = first_blocks(seg_all, size)
    attn_out, qb = attend(low, qa, ka, vt, seg_parts, size)
    attn_here, fc_full, proj_full, out_full = exchange_out(attn_out, own, over, widths, 1)

    hidden = (
        resid_in
        + jnp.einsum("prc,pdc->rd", attn_here, out_full, preferred_element_type=f32)
        + out_bias.astype(f32)
    )
    normed_two, hat_two, inv_two = layer_norm(
        hidden, second_gain.astype(f32), second_shift.astype(f32)
    )
    mlp_in = normed_two.astype(bf16)
    pre_act = jnp.einsum("sd,tdf->tsf", mlp_in, fc_full, preferred_element_type=f32) + relative(
        fc_bias.astype(f32).reshape(slices, 1, hidden_cols)
    )
    sigmoid_pre = jax.nn.sigmoid(gelu_slope * pre_act)
    act_low = (pre_act * sigmoid_pre).astype(bf16)
    layer_out = (
        hidden
        + jnp.einsum("tsf,tdf->sd", act_low, proj_full, preferred_element_type=f32)
        + proj_bias.astype(f32)
    ).astype(bf16)
    proj_grad = jnp.einsum("sd,tsf->tdf", out_grad, act_low, preferred_element_type=f32)
    grad_act = jnp.einsum("sd,tdf->tsf", out_grad, proj_full, preferred_element_type=f32)
    grad_pre = grad_act * (sigmoid_pre + gelu_slope * pre_act * sigmoid_pre * (1.0 - sigmoid_pre))
    grad_pre_low = grad_pre.astype(bf16)
    fc_grad = jnp.einsum("sd,tsf->tdf", mlp_in, grad_pre_low, preferred_element_type=f32)
    fc_bias_part = relative(jnp.sum(grad_pre_low.astype(f32), axis=1)).reshape(-1)
    grad_normed_two = jnp.einsum("tsf,tdf->sd", grad_pre_low, fc_full, preferred_element_type=f32)
    resid_grad = out_grad.astype(f32)
    grad_hidden_ln, second_gain_part, second_shift_part = norm_back(
        grad_normed_two, hat_two, inv_two, second_gain.astype(f32)
    )
    grad_hidden = resid_grad + grad_hidden_ln
    grad_hidden_low = grad_hidden.astype(bf16)
    out_bias_part = jnp.sum(grad_hidden_low.astype(f32), axis=0)
    proj_bias_part = jnp.sum(resid_grad, axis=0)
    out_grad_part = jnp.einsum(
        "sd,psc->pdc", grad_hidden_low, attn_here, preferred_element_type=f32
    )
    live_here = (segments[0] != 0).astype(bf16)
    grad_attn = jnp.einsum("sd,pdc->psc", grad_hidden_low, out_full, preferred_element_type=f32).astype(
        bf16
    ) * live_here[None, :, None]
    grad_attn_seq, kept, passed = exchange_grad(
        grad_attn, (fc_grad.astype(bf16), proj_grad.astype(bf16), out_grad_part.astype(bf16)), 2
    )
    came = across(passed)
    grad_qkv = attend_back(low, qb, ka, va, kt, grad_attn_seq, attn_out, seg_parts, size)
    early = [out_bias_part, second_gain_part, second_shift_part, fc_bias_part, proj_bias_part]
    input_grad, fc_w_grad, proj_w_grad, out_w_grad, qkv_grad, early_sums, late_sums = leave(
        grad_qkv,
        seq_normed,
        qkv_full,
        kept,
        came,
        widths,
        jnp.concatenate(early).reshape(-1, 128),
        inputs,
        first_gain[None],
        grad_hidden,
        3,
    )
    input_grad, fc_w_grad, proj_w_grad, out_w_grad, qkv_grad, qv_bias_grad, vectors = finish(
        input_grad,
        fc_w_grad,
        proj_w_grad,
        out_w_grad,
        qkv_grad,
        early_sums,
        late_sums,
        [vector.shape[0] for vector in early],
    )
    first_gain_grad, first_shift_grad, out_bias_grad, second_gain_grad, second_shift_grad = vectors[0:5]
    fc_bias_grad, proj_bias_grad = vectors[5:7]

    return (
        layer_out,
        input_grad,
        first_gain_grad,
        first_shift_grad,
        qkv_grad,
        qv_bias_grad,
        out_w_grad,
        out_bias_grad,
        second_gain_grad,
        second_shift_grad,
        fc_w_grad,
        fc_bias_grad,
        proj_w_grad,
        proj_bias_grad,
    )


def solution(mesh):
    return jax.shard_map(
        local,
        mesh=mesh,
        in_specs=(
            P(("fsdp", "tp"), None),
            P("fsdp", "tp"),
            P(("fsdp", "tp"), None),
            P(),
            P(),
            P("fsdp", None, "tp"),
            P(),
            P("tp", "fsdp"),
            P(),
            P(),
            P(),
            P("fsdp", "tp"),
            P(),
            P("tp", "fsdp"),
            P(),
        ),
        out_specs=(
            P(("fsdp", "tp"), None),
            P(("fsdp", "tp"), None),
            P(),
            P(),
            P("fsdp", None, "tp"),
            P(),
            P("tp", "fsdp"),
            P(),
            P(),
            P(),
            P("fsdp", "tp"),
            P(),
            P("tp", "fsdp"),
            P(),
        ),
        check_vma=False,
    )
```

```python
import functools

import jax
import jax.numpy as jnp
from jax import lax
from jax.experimental import pallas as pl
from jax.experimental.pallas import tpu as pltpu
from jax.sharding import PartitionSpec as P

HD = 64
VMEM_LIMIT = 60 << 20
epsilon = 1e-05
gelu_slope = 1.702


def layer_norm(values_in, gain_vec, shift_vec):
    mean_row = jnp.mean(values_in, axis=-1, keepdims=True)
    centred = values_in - mean_row
    inverse = lax.rsqrt(jnp.mean(centred * centred, axis=-1, keepdims=True) + epsilon)
    normed = centred * inverse
    return (normed * gain_vec + shift_vec, normed, inverse)


def norm_back(grad_out, normed, inverse, gain_vec):
    scaled = grad_out * gain_vec
    grad_in = inverse * (
        scaled
        - jnp.mean(scaled, axis=-1, keepdims=True)
        - normed * jnp.mean(scaled * normed, axis=-1, keepdims=True)
    )
    return (grad_in, jnp.sum(grad_out * normed, axis=0), jnp.sum(grad_out, axis=0))


f32 = jnp.float32
bf16 = jnp.bfloat16
LOG2E = 1.4426950408889634
BLOCK = 512
TRANSPOSED = (((1,), (1,)), ((), ()))


def dot_t(left, right):
    return lax.dot_general(left, right, TRANSPOSED, preferred_element_type=f32)


def dot_n(left, right):
    return jnp.dot(left, right, preferred_element_type=f32)


def three_parts(value):
    top = value.astype(bf16)
    rest = value - top.astype(f32)
    mid = rest.astype(bf16)
    return top, mid, (rest - mid.astype(f32)).astype(bf16)


def diagonal_mask(seg_ref, row_at, size):
    key_pos = lax.broadcasted_iota(jnp.int32, (size, 1), 0)
    query_pos = lax.broadcasted_iota(jnp.int32, (1, size), 1)
    here = seg_ref.shape[2]
    seg = seg_ref[row_at // here, 0:1, pl.ds(pl.multiple_of(lax.rem(row_at, here), size), size)]
    first = jnp.where(seg == 0, query_pos, 0)
    return (key_pos >= first) & (key_pos <= query_pos)


def attend_kernel(
    low_ref, qa_ref, ka_ref, vt_ref, start_ref, out_ref, qb_ref, s0, s1, a0, a1, *, size, blocks
):
    score_bufs, acc_bufs = (s0, s1), (a0, a1)
    heads = range(qa_ref.shape[0])
    lane = lax.broadcasted_iota(jnp.int32, (size, 128), 1)

    def query_block(i, carry):
        row_at = pl.multiple_of(i * size, size)

        def score(h, j, top, diag):
            keys = ka_ref[h, pl.ds(pl.multiple_of(j * size, size), size), :]
            s = dot_t(keys, qa_ref[h, pl.ds(row_at, size), :])
            if diag:
                s = jnp.where(diagonal_mask(start_ref, row_at, size), s, -3e38)
            score_bufs[h][...] = s
            col_max = jnp.max(s, axis=0, keepdims=True)
            return col_max if top is None else jnp.maximum(top, col_max)

        def gather_values(h, j, old, new, first):
            p = jnp.exp2(score_bufs[h][...] * LOG2E - new * LOG2E).astype(bf16)
            part = dot_n(vt_ref[h, :, pl.ds(pl.multiple_of(j * size, size), size)], p)
            if first:
                acc_bufs[h][...] = part
            else:
                acc_bufs[h][...] = acc_bufs[h][...] * jnp.exp2((old - new) * LOG2E) + part

        low = low_ref[i]
        m0 = score(0, i, None, True)
        m1 = score(1, i, None, True)
        gather_values(0, i, None, m0, True)
        m0n = score(0, jnp.minimum(low, i), m0, False)
        gather_values(1, i, None, m1, True)

        def body(j, c):
            m0, m0n, m1 = c
            m1n = score(1, j, m1, False)
            gather_values(0, j, m0, m0n, False)
            m0nn = score(0, jnp.minimum(j + 1, blocks - 1), m0n, False)
            gather_values(1, j, m1, m1n, False)
            return m0n, m0nn, m1n

        m0, _, m1 = lax.fori_loop(low, i, body, (m0, m0n, m1))
        for h, top in ((0, m0), (1, m1)):
            total = acc_bufs[h][64:65, :]
            out = acc_bufs[h][0:64, :] / total
            rows = qa_ref[h, pl.ds(row_at, size), :]
            live = jnp.where(rows[:, 64:65].astype(f32) != 0.0, 1.0, 0.0)
            out_ref[pl.ds(row_at, size), 64 * h : 64 * h + 64] = (out.T * live).astype(out_ref.dtype)
            norm = jnp.broadcast_to(-(top + jnp.log(total)), (8, size)).T[:, 0:1]
            n0, n1, n2 = three_parts(norm)
            rows = jnp.where(lane == 96, n0, jnp.where(lane == 97, n1, jnp.where(lane == 98, n2, rows)))
            qb_ref[h, pl.ds(row_at, size), :] = rows
        return carry

    lax.fori_loop(0, blocks, query_block, 0)


def attend(low, qa, ka, vt, start, size):
    heads, rows, _ = qa.shape
    vmem = pl.BlockSpec(memory_space=pltpu.VMEM)
    return pl.pallas_call(
        functools.partial(attend_kernel, size=size, blocks=rows // size),
        grid_spec=pltpu.PrefetchScalarGridSpec(
            num_scalar_prefetch=1,
            grid=(),
            in_specs=[vmem] * 4,
            out_specs=[vmem] * 2,
            scratch_shapes=[pltpu.VMEM((size, size), f32)] * heads
            + [pltpu.VMEM((vt.shape[1], size), f32)] * heads,
        ),
        out_shape=[
            jax.ShapeDtypeStruct((rows, HD * heads), bf16),
            jax.ShapeDtypeStruct(qa.shape, bf16),
        ],
        compiler_params=pltpu.CompilerParams(vmem_limit_bytes=VMEM_LIMIT),
        cost_estimate=pl.CostEstimate(
            flops=14 * rows * rows * HD * heads, bytes_accessed=8 << 20, transcendentals=rows * rows
        ),
        name="attend",
    )(low, qa, ka, vt, start)


def attend_back_kernel(
    low_ref, qb_ref, ka_ref, va_ref, kt_ref, g_ref, o_ref, start_ref, grad_ref,
    ga_ref, dk_ref, dv_ref, q0, q1, *, size, blocks
):
    query_accs = (q0, q1)
    lane = lax.broadcasted_iota(jnp.int32, (size, 64), 1)

    def query_block(i, carry):
        row_at = pl.multiple_of(i * size, size)
        g_rows = g_ref[pl.ds(row_at, size), :]
        product = g_rows.astype(f32) * o_ref[pl.ds(row_at, size), :].astype(f32)
        for h in range(2):
            cols = slice(64 * h, 64 * h + 64)
            n0, n1, n2 = three_parts(-jnp.sum(product[:, cols], axis=1, keepdims=True))
            zero = jnp.zeros((size, 64), bf16)
            extra = jnp.where(lane == 0, n0, jnp.where(lane == 1, n1, jnp.where(lane == 2, n2, zero)))
            ga_ref[h] = jnp.concatenate([g_rows[:, cols], extra], axis=1)

        def block(h, j, diag):
            key_at = pl.multiple_of(j * size, size)
            keys = ka_ref[h, pl.ds(key_at, size), :]
            q_rows = qb_ref[h, pl.ds(row_at, size), :]
            g_head = ga_ref[h]
            s = dot_t(keys, q_rows)
            if diag:
                s = jnp.where(diagonal_mask(start_ref, row_at, size), s, -3e38)
            p = jnp.exp2(s * LOG2E)
            dp = dot_t(va_ref[h, pl.ds(key_at, size), :], g_head)
            ds = (p * dp).astype(bf16)
            dv = dot_n(p.astype(bf16), g_head[:, 0:64])
            dk = dot_n(ds, q_rows[:, 0:64])
            dq = dot_n(kt_ref[h, :, pl.ds(key_at, size)], ds)
            if diag:
                dv_ref[h, pl.ds(key_at, size), :] = dv
                dk_ref[h, pl.ds(key_at, size), :] = dk
                query_accs[h][...] = dq
            else:
                dv_ref[h, pl.ds(key_at, size), :] += dv
                dk_ref[h, pl.ds(key_at, size), :] += dk
                query_accs[h][...] += dq

        block(0, i, True)
        block(1, i, True)

        def body(j, c):
            block(0, j, False)
            block(1, j, False)
            return c

        lax.fori_loop(low_ref[i], i, body, 0)
        both = jnp.concatenate([query_accs[0][...], query_accs[1][...]], axis=0) * HD ** (-0.5)
        grad_ref[pl.ds(row_at, size), 0:128] = both.T.astype(bf16)
        return carry

    lax.fori_loop(0, blocks, query_block, 0)

    def finish(i, carry):
        row_at = pl.multiple_of(i * size, size)
        for ref, at in ((dk_ref, 128), (dv_ref, 256)):
            both = jnp.concatenate([ref[0, pl.ds(row_at, size), :], ref[1, pl.ds(row_at, size), :]], axis=1)
            grad_ref[pl.ds(row_at, size), at : at + 128] = both.astype(bf16)
        return carry

    lax.fori_loop(0, blocks, finish, 0)


def attend_back(low, qb, ka, va, kt, g, o, start, size):
    heads, rows, _ = qb.shape
    vmem = pl.BlockSpec(memory_space=pltpu.VMEM)
    return pl.pallas_call(
        functools.partial(attend_back_kernel, size=size, blocks=rows // size),
        grid_spec=pltpu.PrefetchScalarGridSpec(
            num_scalar_prefetch=1,
            grid=(),
            in_specs=[vmem] * 7,
            out_specs=vmem,
            scratch_shapes=[
                pltpu.VMEM((heads, size, 128), bf16),
                pltpu.VMEM((heads, rows, HD), f32),
                pltpu.VMEM((heads, rows, HD), f32),
            ]
            + [pltpu.VMEM((HD, size), f32)] * heads,
        ),
        out_shape=jax.ShapeDtypeStruct((rows, 3 * HD * heads), bf16),
        compiler_params=pltpu.CompilerParams(vmem_limit_bytes=VMEM_LIMIT),
        cost_estimate=pl.CostEstimate(
            flops=24 * rows * rows * HD * heads, bytes_accessed=16 << 20, transcendentals=rows * rows
        ),
        name="attend_back",
    )(low, qb, ka, va, kt, g, o, start)


def first_blocks(seg_all, size):
    firsts = seg_all[::size]
    before = jnp.sum(((seg_all > 0) & (seg_all < firsts[:, None])).astype(jnp.int32), axis=1)
    own = jnp.arange(firsts.shape[0], dtype=jnp.int32)
    return jnp.where(firsts == 0, own, before // size)


MESH = pl.DeviceIdType.MESH


def greet(peers):
    barrier = pltpu.get_barrier_semaphore()
    for peer in peers:
        pl.semaphore_signal(barrier, inc=1, device_id=peer, device_id_type=MESH)
    pl.semaphore_wait(barrier, len(peers))


def push(source, target, send_sem, recv_sem, peer):
    copy = pltpu.make_async_remote_copy(
        src_ref=source,
        dst_ref=target,
        send_sem=send_sem,
        recv_sem=recv_sem,
        device_id=peer,
        device_id_type=MESH,
    )
    copy.start()
    return copy


def quad():
    me = lax.axis_index("tp")
    side = me + 1 - 2 * lax.rem(me, 2)
    across = lax.rem(me + 2, 4)
    far = lax.rem(side + 2, 4)
    return me, side, across, far


def comm_call(kernel, name, number, out_shape, in_specs, out_specs, scratch, moved, *operands):
    return pl.pallas_call(
        kernel,
        out_shape=out_shape,
        in_specs=in_specs,
        out_specs=out_specs,
        scratch_shapes=scratch,
        compiler_params=pltpu.CompilerParams(
            collective_id=number, has_side_effects=True, vmem_limit_bytes=VMEM_LIMIT
        ),
        cost_estimate=pl.CostEstimate(flops=0, bytes_accessed=moved, transcendentals=0),
        name=name,
    )(*operands)


def in_vmem():
    return pl.BlockSpec(memory_space=pltpu.VMEM)


def anywhere():
    return pl.BlockSpec(memory_space=pl.ANY)


def flipped(axis, mask):
    me, index, bit = lax.axis_index(axis), lax.axis_index(axis), 1
    while bit <= mask:
        if mask & bit:
            index = index + bit - 2 * bit * lax.rem(me // bit, 2)
        bit *= 2
    return index


def awaited(ref, send_sem, recv_sem, peer):
    return pltpu.make_async_remote_copy(ref, ref, send_sem, recv_sem, peer, MESH)


def hop_masks(size):
    hops, bit = [], size // 2
    while bit >= 1:
        hops.append((bit, [high + bit for high in range(0, size, 2 * bit)]))
        bit //= 2
    return hops


def enter_kernel(
    x_ref, gain_ref, shift_ref, bias_ref, seg_ref, w0, w1, w2, w3,
    normed_ref, segs_ref, qa_ref, ka_ref, va_ref, vt_ref, kt_ref, f0, f1,
    x_all, normed_s, qa_s, ka_s, va_s, vt_s, kt_s,
    sy, ry, ss, rs, sf, rf, sg, rg, sw, rw, own, own_w, outs, *, parts
):
    me, side, across, far = quad()
    rows = x_ref.shape[0]
    step = rows // parts
    shards = f0.shape[0]
    heads = qa_ref.shape[0]
    width = HD * heads
    shard = lax.axis_index("fsdp")
    hops = hop_masks(shards)
    greet(
        [{"tp": side}, {"tp": across}, {"tp": far}]
        + [{"fsdp": flipped("fsdp", bit)} for bit, _ in hops]
    )
    sent = []

    def rows_of(owner, part):
        return x_all.at[pl.ds(pl.multiple_of(owner * rows + part * step, step), step)]

    sources = (w0, w1, w2, w3)

    def block_of(g, index):
        if g == 0:
            return f0.at[index]
        at = sum(w.shape[1] for w in sources[1:g])
        return f1.at[index, :, pl.ds(at, sources[g].shape[1])]

    def send_hop(g, hop):
        bit, masks = hops[hop]
        peer = {"fsdp": flipped("fsdp", bit)}
        if hop > 0:
            before, arrived = hops[hop - 1]
            for mask in arrived:
                block = block_of(g, flipped("fsdp", mask))
                awaited(block, sw.at[g, mask], rw.at[g, mask], {"fsdp": flipped("fsdp", before)}).wait_recv()
        for mask in masks:
            target = block_of(g, flipped("fsdp", mask - bit))
            block = sources[g] if mask == bit else target
            sent.append(push(block, target, sw.at[g, mask], rw.at[g, mask], peer))

    def end_hops(g):
        bit, arrived = hops[-1]
        for mask in arrived:
            block = block_of(g, flipped("fsdp", mask))
            awaited(block, sw.at[g, mask], rw.at[g, mask], {"fsdp": flipped("fsdp", bit)}).wait_recv()

    for k, peer in enumerate((across, far, side)):
        sent.append(push(seg_ref, segs_ref.at[me], sg.at[k], rg.at[k], {"tp": peer}))
    send_hop(0, 0)
    for part in range(parts):
        mine = x_ref.at[pl.ds(part * step, step)]
        sent.append(push(mine, rows_of(me, part), sy.at[part], ry.at[part], {"tp": across}))
    send_hop(0, 1)
    for g in (1, 2, 3):
        send_hop(g, 0)
    for part in range(parts):
        mine = x_ref.at[pl.ds(part * step, step)]
        sent.append(push(mine, rows_of(me, part), ss.at[part], rs.at[part], {"tp": side}))
    kept = [
        pltpu.make_async_copy(x_ref, x_all.at[pl.ds(pl.multiple_of(me * rows, rows), rows)], own.at[0]),
        pltpu.make_async_copy(seg_ref, segs_ref.at[me], own.at[1]),
    ] + [pltpu.make_async_copy(source, block_of(g, shard), own_w.at[g]) for g, source in enumerate(sources)]
    for copy in kept:
        copy.start()
    waves = sorted(
        ((hop + g, g, hop) for hop in range(1, len(hops)) for g in range(4)), key=lambda w: (w[0], w[1])
    )
    for _, g, hop in waves[1:2]:
        send_hop(g, hop)
    for k, peer in enumerate((across, far, side)):
        awaited(segs_ref.at[peer], sg.at[k], rg.at[k], {"tp": peer}).wait_recv()
    for part in range(parts):
        awaited(rows_of(side, part), ss.at[part], rs.at[part], {"tp": side}).wait_recv()
    for copy in kept:
        copy.wait()
    gain, shift = gain_ref[...].astype(f32), shift_ref[...].astype(f32)

    def norm(owner, part):
        span = pl.ds(pl.multiple_of(owner * rows + part * step, step), step)
        x = x_all[span, :].astype(f32)
        centred = x - jnp.mean(x, axis=-1, keepdims=True)
        inverse = lax.rsqrt(jnp.mean(centred * centred, axis=-1, keepdims=True) + epsilon)
        normed_s[span, :] = (centred * inverse * gain + shift).astype(bf16)

    def norm_near(k, carry):
        norm(me + lax.rem(k, 2) * (side - me), k // 2)
        return carry

    lax.fori_loop(0, 2 * parts, norm_near, 0)
    for _, g, hop in waves[2:]:
        send_hop(g, hop)
    end_hops(0)
    bias_at = pl.ds(pl.multiple_of(me * width, width), width)
    query_bias = bias_ref[0:1, bias_at].astype(f32)
    value_bias = bias_ref[1:2, bias_at].astype(f32)
    number = lax.broadcasted_iota(jnp.int32, (step, 64), 1)
    number_f = number.astype(f32)
    key_ones = (number >= 32) & (number < 35)
    value_tail = jnp.where(number < 3, 1.0, 0.0).astype(bf16)
    ones_row = jnp.where(lax.broadcasted_iota(jnp.int32, (16, step), 0) == 0, 1.0, 0.0).astype(bf16)

    def copies_out(owner, part):
        row = pl.multiple_of(owner * rows + part * step, step)
        slot = owner * parts + part
        span = pl.ds(row, step)
        pairs = [(normed_s.at[span], normed_ref.at[span])]
        for a, b in ((qa_s, qa_ref), (ka_s, ka_ref), (va_s, va_ref)):
            pairs.append((a.at[:, span, :], b.at[:, span, :]))
        for a, b in ((vt_s, vt_ref), (kt_s, kt_ref)):
            pairs.append((a.at[:, :, span], b.at[:, :, span]))
        return [pltpu.make_async_copy(a, b, outs.at[n, slot]) for n, (a, b) in enumerate(pairs)]

    def compute(owner, part):
        row = pl.multiple_of(owner * rows + part * step, step)
        span = pl.ds(row, step)
        normed = normed_s[span, :]
        weights = f0[...].reshape(shards * f0.shape[1], 3 * width)
        projected = dot_n(normed, weights)
        queries = ((projected[:, 0:width] + query_bias).astype(bf16).astype(f32) * HD ** (-0.5)).astype(bf16)
        keys = projected[:, width : 2 * width].astype(bf16)
        values = (projected[:, 2 * width : 3 * width] + value_bias).astype(bf16)
        seg = segs_ref[owner, 0:1, pl.ds(pl.multiple_of(part * step, step), step)].astype(f32)
        seg = jnp.broadcast_to(seg, (8, step)).T[:, 0:1]
        same = (seg == number_f) & (number < 32)
        other = jnp.where(same | (number > 31), 0.0, -1e30).astype(bf16)
        key_tail = jnp.where(same | key_ones, 1.0, 0.0).astype(bf16)
        for h in range(heads):
            cols = slice(HD * h, HD * h + HD)
            qa_s[h, span, :] = jnp.concatenate([queries[:, cols], other], axis=1)
            ka_s[h, span, :] = jnp.concatenate([keys[:, cols], key_tail], axis=1)
            va_s[h, span, :] = jnp.concatenate([values[:, cols], value_tail], axis=1)
            turned = jnp.concatenate([values[:, cols], keys[:, cols]], axis=1).astype(f32).T.astype(bf16)
            vt_s[h, 0:64, span] = turned[0:64, :]
            vt_s[h, 64:80, span] = ones_row
            kt_s[h, :, span] = turned[64:128, :]
        for copy in copies_out(owner, part):
            copy.start()

    def work(k, carry):
        distant = k // (2 * parts)
        part = lax.rem(k // 2, parts)
        second = lax.rem(k, 2)

        @pl.when((distant == 0) & (second == 0))
        def _():
            here = rows_of(across, part)
            awaited(here, sy.at[part], ry.at[part], {"tp": across}).wait_recv()
            push(here, here, sf.at[part], rf.at[part], {"tp": side})

        @pl.when((distant == 1) & (second == 1))
        def _():
            awaited(rows_of(far, part), sf.at[part], rf.at[part], {"tp": side}).wait_recv()

        @pl.when(distant == 1)
        def _():
            norm(across + second * (far - across), part)

        first = me + distant * (across - me)
        compute(first + second * (side - me + distant * (far - across - side + me)), part)
        return carry

    lax.fori_loop(0, 4 * parts, work, 0)
    for g in (1, 2, 3):
        end_hops(g)

    def drain(k, carry):
        for copy in copies_out(k // parts, lax.rem(k, parts)):
            copy.wait()
        return carry

    lax.fori_loop(0, 4 * parts, drain, 0)
    for part in range(parts):
        awaited(rows_of(across, part), sf.at[part], rf.at[part], {"tp": side}).wait_send()
    for copy in sent:
        copy.wait_send()


def enter(x, gain, shift, bias, segments, weights, number, parts=4):
    rows, width = x.shape
    seq_rows = 4 * rows
    shards = lax.axis_size("fsdp")
    heads = weights[0].shape[1] // (3 * HD)
    dma = pltpu.SemaphoreType.DMA
    wide = (heads, seq_rows, 128)
    shard_rows = weights[0].shape[0]
    full = [(shards, *weights[0].shape), (shards, shard_rows, sum(w.shape[1] for w in weights[1:]))]
    shapes = [(seq_rows, width), wide, wide, wide, (heads, 80, seq_rows), (heads, 64, seq_rows)]
    made = [jax.ShapeDtypeStruct(s, bf16) for s in shapes]
    return comm_call(
        functools.partial(enter_kernel, parts=parts),
        "enter",
        number,
        [made[0], jax.ShapeDtypeStruct((4, *segments.shape), segments.dtype)]
        + made[1:]
        + [jax.ShapeDtypeStruct(s, bf16) for s in full],
        [in_vmem()] * 9,
        [anywhere(), in_vmem()] + [anywhere()] * 5 + [in_vmem(), anywhere()],
        [pltpu.VMEM((seq_rows, width), bf16)]
        + [pltpu.VMEM(s, bf16) for s in shapes]
        + [dma((parts,))] * 6
        + [dma((3,))] * 2
        + [dma((4, shards))] * 2
        + [dma((2,)), dma((4,)), dma((6, 4 * parts))],
        60 << 20,
        x,
        gain,
        shift,
        bias,
        segments,
        *weights,
    )


def exchange_out_kernel(x_ref, o_ref, c_ref, out_ref, g0, g1, g2, sems, rems, ws, wr, own):
    me, side, across, far = quad()
    rows = x_ref.shape[0] // 4
    greet([{"tp": side}, {"tp": across}, {"tp": far}])
    peers = {1: side, 2: across, 3: far}

    def mine(owner):
        return x_ref.at[pl.ds(pl.multiple_of(owner * rows, rows), rows)]

    weights, at = [], 0
    for full in (g0, g1, g2):
        cols = pl.ds(at, full.shape[2])
        weights.append((o_ref.at[:, cols], c_ref.at[:, cols], full))
        at += full.shape[2]
    sent = [push(mine(peers[k]), out_ref.at[k], sems.at[k], rems.at[k], {"tp": peers[k]}) for k in (3, 2, 1)]
    for n, (here, over, full) in enumerate(weights):
        sent.append(push(here, full.at[1], ws.at[0, n], wr.at[0, n], {"tp": side}))
        sent.append(push(over, full.at[3], ws.at[1, n], wr.at[1, n], {"tp": side}))
    kept = [pltpu.make_async_copy(mine(me), out_ref.at[0], own.at[0])]
    for n, (here, over, full) in enumerate(weights):
        kept.append(pltpu.make_async_copy(here, full.at[0], own.at[2 * n + 1]))
        kept.append(pltpu.make_async_copy(over, full.at[2], own.at[2 * n + 2]))
    for copy in kept:
        copy.start()
    for copy in kept:
        copy.wait()
    for copy in sent:
        copy.wait()


def exchange_out(x, own, over, widths, number):
    rows, width = x.shape
    dma = pltpu.SemaphoreType.DMA
    return comm_call(
        exchange_out_kernel,
        "exchange_out",
        number,
        [jax.ShapeDtypeStruct((4, rows // 4, width), x.dtype)]
        + [jax.ShapeDtypeStruct((4, own.shape[0], w), own.dtype) for w in widths],
        [in_vmem()] * 3,
        [in_vmem()] + [anywhere()] * 3,
        [dma((4,)), dma((4,)), dma((2, 3)), dma((2, 3)), dma((7,))],
        60 << 20,
        x,
        own,
        over,
    )


def middle_kernel(
    attn_ref, x_ref, g_ref, seg_ref, par_ref, fc_ref, pj_ref, ow_ref,
    layer_ref, resid_ref, seq_ref, kept_ref, over_ref, sums_ref,
    attn_cat, ow_cat, act_s, gp_s, in_s, in_t, g_t, low_t, ga_s, out_acc, gn_acc,
    fc_g, pj_g, ow_g, fc_box, pj_box, ow_box,
    sems, rems, ws, wr, *, parts
):
    me, side, across, far = quad()
    greet([{"tp": side}, {"tp": across}, {"tp": far}])
    peers = {1: side, 2: across, 3: far}
    rows = x_ref.shape[0]
    step = rows // parts
    lanes = ow_ref.shape[2]
    sums_ref[...] = jnp.zeros_like(sums_ref)
    for p in range(4):
        ow_cat[:, p * lanes : (p + 1) * lanes] = ow_ref[p]

    def owner(t):
        near = me + lax.rem(t, 2) * (1 - 2 * lax.rem(me, 2))
        return lax.rem(near + 2 * (t // 2), 4)

    def add_row(row, value):
        at = pl.ds(row, 1)
        sums_ref[at, :] = sums_ref[at, :] + jnp.sum(value, axis=0, keepdims=True)

    def landing(who, part):
        return seq_ref.at[pl.ds(pl.multiple_of(who * rows + part * step, step), step)]

    def row_block(part, carry):
        here = pl.ds(pl.multiple_of(part * step, step), step)
        attn = jnp.concatenate([attn_ref[p, here, :] for p in range(4)], axis=1)
        attn_cat[here, :] = attn
        hidden = x_ref[here, :].astype(f32) + dot_t(attn, ow_cat[...]) + par_ref[0:1, :]
        gain = par_ref[1:2, :]
        normed, hat, inverse = layer_norm(hidden, gain, par_ref[2:3, :])
        in_s[...] = normed.astype(bf16)
        in_t[:, here] = normed.T.astype(bf16)
        grad = g_ref[here, :]
        g_t[:, here] = grad.astype(f32).T.astype(bf16)
        out_acc[...] = hidden + par_ref[3:4, :]
        gn_acc[...] = jnp.zeros_like(gn_acc)

        def hidden_block(t, c):
            bias_at = 4 + owner(t)
            pre = dot_n(in_s[...], fc_ref[t]) + par_ref[pl.ds(bias_at, 1), :]
            gate = jax.nn.sigmoid(gelu_slope * pre)
            raised = pre * gate
            act = raised.astype(bf16)
            act_s[t, here, :] = act
            out_acc[...] += dot_t(act, pj_ref[t])
            grad_act = dot_n(g_ref[here, :], pj_ref[t])
            grad_pre = (grad_act * (gate + gelu_slope * raised * (1.0 - gate))).astype(bf16)
            gp_s[t, here, :] = grad_pre
            add_row(bias_at, grad_pre.astype(f32))
            gn_acc[...] += dot_t(grad_pre, fc_ref[t])
            return c

        lax.fori_loop(0, 4, hidden_block, 0)
        layer_ref[here, :] = out_acc[...].astype(bf16)
        grad_in, gain_part, shift_part = norm_back(gn_acc[...], hat, inverse, gain)
        grad_hidden = grad.astype(f32) + grad_in
        resid_ref[here, :] = grad_hidden
        low = grad_hidden.astype(bf16)
        low_t[:, here] = grad_hidden.T.astype(bf16)
        sums_ref[1:2, :] += gain_part[None]
        sums_ref[2:3, :] += shift_part[None]
        add_row(0, low.astype(f32))
        add_row(3, grad.astype(f32))
        seg = jnp.broadcast_to(seg_ref[0:1, here].astype(f32), (8, step)).T[:, 0:1]
        live = jnp.where(seg != 0.0, 1.0, 0.0)
        grad_attn = (dot_n(low, ow_cat[...]).astype(bf16).astype(f32) * live).astype(bf16)
        for k in (1, 2, 3):
            ga_s[k, here, :] = grad_attn[:, k * lanes : (k + 1) * lanes]
        seq_ref[pl.ds(pl.multiple_of(me * rows + part * step, step), step), :] = grad_attn[:, 0:lanes]
        for k in (3, 2, 1):
            push(ga_s.at[k, here], landing(me, part), sems.at[k, part], rems.at[k, part], {"tp": peers[k]})
        return carry

    lax.fori_loop(0, parts, row_block, 0)
    width = out_acc.shape[1]
    tall = 128

    def out_block(n, carry):
        at = pl.ds(pl.multiple_of(n * tall, tall), tall)
        grad = dot_n(low_t[at, :], attn_cat[...]).astype(bf16)
        for p in range(4):
            ow_g[p, at, :] = grad[:, p * lanes : (p + 1) * lanes]
        return carry

    lax.fori_loop(0, width // tall, out_block, 0)
    triples = ((fc_g, fc_box), (pj_g, pj_box), (ow_g, ow_box))

    def fold(n, b):
        grad, box = triples[n]
        return grad.at[2 * b + 1], box.at[b], ws.at[n, b], wr.at[n, b], {"tp": side}

    for b in (1, 0):
        push(*fold(2, b))

    def slice_block(u, carry):
        t = 3 - 2 * u + 3 * (u // 2)

        def fc_block(n, c):
            at = pl.ds(pl.multiple_of(n * tall, tall), tall)
            fc_g[t, at, :] = dot_n(in_t[at, :], gp_s[t]).astype(bf16)
            pj_g[t, at, :] = dot_n(g_t[at, :], act_s[t]).astype(bf16)
            return c

        lax.fori_loop(0, width // tall, fc_block, 0)
        for b in (1, 0):

            @pl.when(u == 1 - b)
            def _():
                push(*fold(0, b))
                push(*fold(1, b))

        return carry

    lax.fori_loop(0, 4, slice_block, 0)
    for b, target in ((1, over_ref), (0, kept_ref)):
        at = 0
        for n, (grad, box) in enumerate(triples):
            cols = slice(at, at + grad.shape[2])
            at += grad.shape[2]
            awaited(box.at[b], ws.at[n, b], wr.at[n, b], {"tp": side}).wait_recv()
            target[:, cols] = (grad[2 * b].astype(f32) + box[b].astype(f32)).astype(bf16)

    def drain(part, carry):
        here = pl.ds(pl.multiple_of(part * step, step), step)
        for k in (1, 2, 3):
            peer = {"tp": peers[k]}
            awaited(landing(peers[k], part), sems.at[k, part], rems.at[k, part], peer).wait_recv()
            awaited(ga_s.at[k, here], sems.at[k, part], rems.at[k, part], peer).wait_send()
        return carry

    lax.fori_loop(0, parts, drain, 0)
    for n, (grad, box) in enumerate(triples):
        for b in (1, 0):
            awaited(grad.at[2 * b + 1], ws.at[n, b], wr.at[n, b], {"tp": side}).wait_send()


def middle(attn, x, grad, segments, params, fc, pj, ow, number, parts=4):
    _, rows, lanes = attn.shape
    width, hidden = x.shape[1], fc.shape[2]
    step = rows // parts
    dma = pltpu.SemaphoreType.DMA
    total = 2 * hidden + lanes
    low, wide = bf16, f32
    scratch = [
        ((rows, width), low), ((width, 4 * lanes), low),
        ((4, rows, hidden), low), ((4, rows, hidden), low),
        ((step, width), low), ((width, rows), low), ((width, rows), low), ((width, rows), low),
        ((4, rows, lanes), low), ((step, width), wide), ((step, width), wide),
        (fc.shape, low), (pj.shape, low), (ow.shape, low),
        ((2, *fc.shape[1:]), low), ((2, *pj.shape[1:]), low), ((2, *ow.shape[1:]), low),
    ]
    outs = [
        ((rows, width), low), ((rows, width), wide), ((4 * rows, lanes), low),
        ((width, total), low), ((width, total), low), (params.shape, wide),
    ]
    return comm_call(
        functools.partial(middle_kernel, parts=parts),
        "middle",
        number,
        [jax.ShapeDtypeStruct(s, d) for s, d in outs],
        [in_vmem()] * 8,
        [in_vmem()] * 6,
        [pltpu.VMEM(s, d) for s, d in scratch]
        + [dma((4, parts)), dma((4, parts)), dma((3, 2)), dma((3, 2))],
        60 << 20,
        attn,
        x,
        grad,
        segments,
        params,
        fc,
        pj,
        ow,
    )


def leave_kernel(
    grad_ref, normed_in, w_ref, kept_ref, came_ref, early_ref, x_in, gain_ref, resid_in,
    input_ref, s0, s1, s2, s3, early_out, late_out,
    rows_ref, far_out, own_out, sum_buf, side_far, side_own, over, dw_acc, cols_ref,
    late_ref, early_mid, late_mid, early_one, early_two, late_one, late_two,
    normed_ref, x_ref, resid_ref, loads,
    sa, ra, sb, rb, sy, ry, sw, rw, se, re, sl, rl, se2, re2, sl2, rl2, *bufs, parts, hops
):
    me, side, across, far = quad()
    rows = rows_ref.shape[0]
    step = rows // parts
    shard, shards = lax.axis_index("fsdp"), early_two.shape[0]
    pairs = ((normed_in, normed_ref), (x_in, x_ref), (resid_in, resid_ref))
    loading = [pltpu.make_async_copy(a, b, loads.at[n]) for n, (a, b) in enumerate(pairs)]
    for copy in loading:
        copy.start()
    barrier = pltpu.get_barrier_semaphore()
    for peer in (side, across, far):
        pl.semaphore_signal(barrier, inc=1, device_id={"tp": peer}, device_id_type=MESH)

    def other(k):
        return {"fsdp": lax.rem(shard + k, shards)}

    def signal(k, carry):
        pl.semaphore_signal(barrier, inc=1, device_id=other(k), device_id_type=MESH)
        return carry

    lax.fori_loop(1, shards, signal, 0)
    pl.semaphore_wait(barrier, 3 + shards - 1)
    count = len(hops)
    outs = (s0, s1, s2, s3)
    current = bufs[0:4]
    boxes = [bufs[4 + g * count : 4 + (g + 1) * count] for g in range(4)]
    keeps = [bufs[4 + 4 * count + g * (count - 1) : 4 + 4 * count + (g + 1) * (count - 1)] for g in range(4)]
    sent = []

    def begin(g):
        at = sum(c.shape[3] for c in current[0:g])
        cols = slice(at, at + current[g].shape[3])
        total = kept_ref[:, :, :, cols].astype(f32) + came_ref[:, :, :, cols].astype(f32)
        current[g][...] = total.astype(bf16)

    def hop_parts(g, k):
        axis, bit = hops[k]
        source = current[g] if k == 0 else keeps[g][k - 1]
        half = lax.rem(lax.axis_index(axis) // bit, 2)
        return {axis: flip(axis, bit)}, source, half, boxes[g][k]

    def hop_send(g, k):
        peer, source, half, box = hop_parts(g, k)
        sent.append(push(source.at[:, 1 - half], box, sw.at[g, k], rw.at[g, k], peer))

    def hop_add(g, k):
        peer, source, half, box = hop_parts(g, k)
        awaited(box, sw.at[g, k], rw.at[g, k], peer).wait_recv()
        if k == count - 1:
            outs[g][...] = source[0, half].astype(f32) + box[0].astype(f32)
        else:
            target = keeps[g][k]
            for n in range(box.shape[0]):
                total = source[n, half].astype(f32) + box[n].astype(f32)
                target[n // 2, n % 2] = total.astype(bf16)
            hop_send(g, k + 1)

    def tp_send(value, box, send, recv):
        box[me] = value[...]
        for k, peer in enumerate((side, across, far)):
            sent.append(push(value, box.at[me], send.at[k], recv.at[me], {"tp": peer}))

    def tp_sum(value, box, send, recv):
        for k, peer in enumerate((side, across, far)):
            awaited(box.at[peer], send.at[k], recv.at[peer], {"tp": peer}).wait_recv()
        value[...] = box[0] + box[1] + box[2] + box[3]

    def fsdp_send(value, box, send, recv):
        box[shard] = value[...]

        def give(k, carry):
            push(value, box.at[shard], send.at[k], recv.at[shard], other(k))
            return carry

        lax.fori_loop(1, shards, give, 0)

    def fsdp_sum(value, target, box, send, recv):
        def take(k, carry):
            peer = lax.rem(shard + k, shards)
            copy = awaited(box.at[peer], send.at[k], recv.at[peer], other(k))
            copy.wait_recv()
            copy.wait_send()
            return carry

        lax.fori_loop(1, shards, take, 0)
        target[...] = lax.fori_loop(1, shards, lambda n, total: total + box[n], box[0])

    def span(owner, part):
        return pl.ds(pl.multiple_of(owner * rows + part * step, step), step)

    def piece(part):
        return pl.ds(pl.multiple_of(part * step, step), step)

    def partial(owner, part):
        return dot_t(grad_ref[span(owner, part), :], w_ref[...])

    def give_far(part, carry):
        here = piece(part)
        far_out[here, :] = partial(far, part).astype(bf16)
        push(far_out.at[here], side_far.at[here], sa.at[part], ra.at[part], {"tp": side})
        return carry

    def give_over(part, carry):
        here = piece(part)
        mine = partial(across, part)
        awaited(side_far.at[here], sa.at[part], ra.at[part], {"tp": side}).wait_recv()
        sum_buf[here, :] = (mine + side_far[here, :].astype(f32)).astype(bf16)
        push(sum_buf.at[here], over.at[here], sy.at[part], ry.at[part], {"tp": across})
        return carry

    def give_own(part, carry):
        here = piece(part)
        own_out[here, :] = partial(side, part).astype(bf16)
        push(own_out.at[here], side_own.at[here], sb.at[part], rb.at[part], {"tp": side})
        return carry

    def take_own(part, carry):
        here = piece(part)
        mine = partial(me, part)
        awaited(side_own.at[here], sb.at[part], rb.at[part], {"tp": side}).wait_recv()
        rows_ref[here, :] = mine + side_own[here, :].astype(f32)
        return carry

    gain = gain_ref[...].astype(f32)

    def take_over(part, carry):
        here = piece(part)
        x = x_ref[here, :].astype(f32)
        centred = x - jnp.mean(x, axis=-1, keepdims=True)
        inverse = lax.rsqrt(jnp.mean(centred * centred, axis=-1, keepdims=True) + epsilon)
        normed = centred * inverse
        awaited(over.at[here], sy.at[part], ry.at[part], {"tp": across}).wait_recv()
        grad = rows_ref[here, :] + over[here, :].astype(f32)
        grad_in, gain_part, shift_part = norm_back(grad, normed, inverse, gain)
        input_ref[here, :] = (resid_ref[here, :] + grad_in).astype(bf16)
        late_ref[0:1, :] += gain_part[None]
        late_ref[1:2, :] += shift_part[None]
        return carry

    def drain(part, carry):
        here = piece(part)
        awaited(far_out.at[here], sa.at[part], ra.at[part], {"tp": side}).wait_send()
        awaited(own_out.at[here], sb.at[part], rb.at[part], {"tp": side}).wait_send()
        awaited(sum_buf.at[here], sy.at[part], ry.at[part], {"tp": across}).wait_send()
        return carry

    chunk = 512
    steps = grad_ref.shape[0] // chunk
    dw_acc[...] = jnp.zeros_like(dw_acc)
    cols_ref[...] = jnp.zeros_like(cols_ref)
    ones = jnp.ones((8, chunk), bf16)

    def weight_grad(n, carry):
        at = pl.ds(pl.multiple_of(n * chunk, chunk), chunk)
        g = grad_ref[at, :]
        dw_acc[...] += lax.dot_general(
            normed_ref[at, :], g, (((0,), (0,)), ((), ())), preferred_element_type=f32
        )
        cols_ref[...] += dot_n(ones, g)
        return carry

    tp_send(early_ref, early_one, se, re)
    lax.fori_loop(0, parts, give_far, 0)
    for g in (0, 1):
        begin(g)
        hop_send(g, 0)
    lax.fori_loop(0, parts, give_over, 0)
    begin(2)
    hop_send(2, 0)
    for copy in loading:
        copy.wait()
    lax.fori_loop(0, steps // 2, weight_grad, 0)
    hop_add(0, 0)
    lax.fori_loop(steps // 2, steps, weight_grad, 0)
    current[3][...] = dw_acc[...].astype(bf16).reshape(current[3].shape)
    hop_send(3, 0)
    tp_sum(early_mid, early_one, se, re)
    fsdp_send(early_mid, early_two, se2, re2)
    hop_add(1, 0)
    late_ref[...] = jnp.zeros_like(late_ref)
    wide = cols_ref.shape[1] // 3
    qv_at = pl.ds(pl.multiple_of(me * wide, wide), wide)
    late_ref[2:3, qv_at] = cols_ref[0:1, 0:wide]
    late_ref[3:4, qv_at] = cols_ref[0:1, 2 * wide : 3 * wide]
    lax.fori_loop(0, parts, give_own, 0)
    order = sorted(((k + g, g, k) for g in range(4) for k in range(count)), key=lambda w: (w[0], w[1]))
    order = [(g, k) for _, g, k in order if (g, k) not in ((0, 0), (1, 0))]
    lax.fori_loop(0, parts, take_own, 0)
    taken = {len(order) * share // 10: span for share, span in ((6, (0, 2)), (7, (2, 3)), (9, (3, 4)))}
    for n, (g, k) in enumerate(order):
        if n in taken:
            first, last = taken[n]
            lax.fori_loop(first * parts // 4, last * parts // 4, take_over, 0)
        if n == len(order) - 1:
            tp_send(late_ref, late_one, sl, rl)
        hop_add(g, k)
    fsdp_sum(early_mid, early_out, early_two, se2, re2)
    tp_sum(late_mid, late_one, sl, rl)
    fsdp_send(late_mid, late_two, sl2, rl2)
    lax.fori_loop(0, parts, drain, 0)
    fsdp_sum(late_mid, late_out, late_two, sl2, rl2)
    for copy in sent:
        copy.wait_send()


def leave(grad, normed, w, kept, came, widths, early, x, gain, resid, number, parts=4):
    rows, width = grad.shape[0] // 4, w.shape[0]
    dma = pltpu.SemaphoreType.DMA
    hops = bits_of("fsdp")
    count = len(hops)
    shards = lax.axis_size("fsdp")
    shard = width // shards
    widths = [*widths, grad.shape[1]]
    split = (shards // 2, 2, shard)
    current = [pltpu.VMEM((*split, n), bf16) for n in widths]
    boxes = [pltpu.VMEM((shards >> (k + 1), shard, n), bf16) for n in widths for k in range(count)]
    keeps = [pltpu.VMEM((shards >> (k + 2), 2, shard, n), bf16) for n in widths for k in range(count - 1)]
    late = (4, width)
    return comm_call(
        functools.partial(leave_kernel, parts=parts, hops=hops),
        "leave",
        number,
        [jax.ShapeDtypeStruct((rows, width), bf16)]
        + [jax.ShapeDtypeStruct((shard, n), f32) for n in widths]
        + [jax.ShapeDtypeStruct(early.shape, f32), jax.ShapeDtypeStruct(late, f32)],
        [in_vmem(), anywhere()] + [in_vmem()] * 4 + [anywhere(), in_vmem(), anywhere()],
        [in_vmem()] * 7,
        [pltpu.VMEM((rows, width), f32)]
        + [pltpu.VMEM((rows, width), bf16)] * 6
        + [pltpu.VMEM((width, grad.shape[1]), f32), pltpu.VMEM((8, grad.shape[1]), f32)]
        + [pltpu.VMEM(late, f32), pltpu.VMEM(early.shape, f32), pltpu.VMEM(late, f32)]
        + [pltpu.VMEM((n, *shape), f32) for shape in (early.shape, late) for n in (4, shards)]
        + [pltpu.VMEM(v.shape, v.dtype) for v in (normed, x, resid)]
        + [dma((3,))]
        + [dma((parts,))] * 6
        + [dma((4, count))] * 2
        + [dma((3,)), dma((4,))] * 2
        + [dma((shards,))] * 4
        + current
        + boxes
        + keeps,
        60 << 20,
        grad,
        normed,
        w,
        kept.reshape(*split, kept.shape[1]),
        came.reshape(*split, came.shape[1]),
        early,
        x,
        gain,
        resid,
    )


def finish_kernel(
    rows_in, fc_in, proj_in, out_in, qkv_in, early_in, late_in,
    rows_ref, fc_ref, proj_ref, out_ref, qkv_ref, qv_ref, *vectors
):
    rows_ref[...] = rows_in[...]
    fc_ref[...] = fc_in[...]
    proj_ref[...] = proj_in[...]
    out_ref[...] = out_in[...]
    width = qkv_ref.shape[2]
    for n in range(3):
        qkv_ref[n] = qkv_in[:, n * width : (n + 1) * width]
    qv_ref[...] = late_in[2:4, :]
    first_gain, first_shift, out_bias, gain, shift, fc_bias, proj_bias = vectors
    lanes = first_gain.shape[1]
    count = first_gain.shape[0]
    singles = ((first_gain, late_in, 0), (first_shift, late_in, 1), (out_bias, early_in, 0))
    singles += ((gain, early_in, 1), (shift, early_in, 2), (proj_bias, early_in, 3))
    for ref, source, row in singles:
        for n in range(count):
            ref[n : n + 1, :] = source[row : row + 1, n * lanes : (n + 1) * lanes]
    for row in range(4):
        for n in range(count):
            at = row * count + n
            fc_bias[at : at + 1, :] = early_in[4 + row : 5 + row, n * lanes : (n + 1) * lanes]


def finish(rows, fc, proj, out, qkv, early, late):
    lanes = 128
    width = late.shape[1]
    shapes = [rows, fc, proj, out]
    outs = [jax.ShapeDtypeStruct(v.shape, v.dtype) for v in shapes]
    outs.append(jax.ShapeDtypeStruct((3, qkv.shape[0], qkv.shape[1] // 3), f32))
    outs.append(jax.ShapeDtypeStruct((2, width), f32))
    sizes = [width] * 5 + [4 * early.shape[1], width]
    outs += [jax.ShapeDtypeStruct((n // lanes, lanes), f32) for n in sizes]
    rows, fc, proj, out, qkv, qv, *vectors = pl.pallas_call(
        finish_kernel,
        out_shape=outs,
        in_specs=[in_vmem()] * 7,
        out_specs=[in_vmem()] * len(outs),
        cost_estimate=pl.CostEstimate(flops=0, bytes_accessed=3 << 20, transcendentals=0),
        name="finish",
    )(rows, fc, proj, out, qkv, early, late)
    return rows, fc, proj.T, out.T, qkv.transpose(1, 0, 2), qv, [v.reshape(-1) for v in vectors]


def flip(axis, bit):
    me = lax.axis_index(axis)
    return me + bit - 2 * bit * lax.rem(me // bit, 2)


def bits_of(axis):
    size, bits, bit = lax.axis_size(axis), [], 1
    while bit < size:
        bits.append((axis, bit))
        bit *= 2
    return bits


def across(value):
    return lax.ppermute(value, "tp", [(n, n ^ 2) for n in range(4)])


def local(
    inputs,
    segments,
    out_grad,
    first_gain,
    first_shift,
    qkv_weight,
    qv_bias,
    out_weight,
    out_bias,
    second_gain,
    second_shift,
    fc_weight,
    fc_bias,
    proj_weight,
    proj_bias,
):
    slices = lax.axis_size("tp")
    rows_here, model_width = inputs.shape
    shard_rows = qkv_weight.shape[0]
    head_cols = qkv_weight.shape[2]
    hidden_cols = fc_weight.shape[1]
    seq_normed, seg_parts, qa, ka, va, vt, kt, qkv_full, own = enter(
        inputs,
        first_gain[None],
        first_shift[None],
        qv_bias,
        segments,
        (qkv_weight.reshape(shard_rows, 3 * head_cols), fc_weight, proj_weight.T, out_weight.T),
        0,
    )
    qkv_full = qkv_full.reshape(model_width, 3 * head_cols)
    own = own.reshape(model_width, own.shape[2])
    over = across(own)
    widths = (hidden_cols, hidden_cols, head_cols)

    seq_rows = seq_normed.shape[0]
    seg_all = seg_parts.reshape(seq_rows)
    size = min(BLOCK, rows_here)
    low = first_blocks(seg_all, size)
    attn_out, qb = attend(low, qa, ka, vt, seg_parts, size)
    attn_here, fc_full, proj_full, out_full = exchange_out(attn_out, own, over, widths, 1)

    params = jnp.concatenate(
        [jnp.stack([out_bias, second_gain, second_shift, proj_bias]), fc_bias.reshape(slices, hidden_cols)]
    ).astype(f32)
    layer_out, grad_hidden, grad_attn_seq, kept, passed, early = middle(
        attn_here, inputs, out_grad, segments, params, fc_full, proj_full, out_full, 2
    )
    came = across(passed)
    grad_qkv = attend_back(low, qb, ka, va, kt, grad_attn_seq, attn_out, seg_parts, size)
    input_grad, fc_w_grad, proj_w_grad, out_w_grad, qkv_grad, early_sums, late_sums = leave(
        grad_qkv,
        seq_normed,
        qkv_full,
        kept,
        came,
        widths,
        early,
        inputs,
        first_gain[None],
        grad_hidden,
        3,
    )
    input_grad, fc_w_grad, proj_w_grad, out_w_grad, qkv_grad, qv_bias_grad, vectors = finish(
        input_grad,
        fc_w_grad,
        proj_w_grad,
        out_w_grad,
        qkv_grad,
        early_sums,
        late_sums,
    )
    first_gain_grad, first_shift_grad, out_bias_grad, second_gain_grad, second_shift_grad = vectors[0:5]
    fc_bias_grad, proj_bias_grad = vectors[5:7]

    return (
        layer_out,
        input_grad,
        first_gain_grad,
        first_shift_grad,
        qkv_grad,
        qv_bias_grad,
        out_w_grad,
        out_bias_grad,
        second_gain_grad,
        second_shift_grad,
        fc_w_grad,
        fc_bias_grad,
        proj_w_grad,
        proj_bias_grad,
    )


def solution(mesh):
    return jax.shard_map(
        local,
        mesh=mesh,
        in_specs=(
            P(("fsdp", "tp"), None),
            P("fsdp", "tp"),
            P(("fsdp", "tp"), None),
            P(),
            P(),
            P("fsdp", None, "tp"),
            P(),
            P("tp", "fsdp"),
            P(),
            P(),
            P(),
            P("fsdp", "tp"),
            P(),
            P("tp", "fsdp"),
            P(),
        ),
        out_specs=(
            P(("fsdp", "tp"), None),
            P(("fsdp", "tp"), None),
            P(),
            P(),
            P("fsdp", None, "tp"),
            P(),
            P("tp", "fsdp"),
            P(),
            P(),
            P(),
            P("fsdp", "tp"),
            P(),
            P("tp", "fsdp"),
            P(),
        ),
        check_vma=False,
    )
```

```python
import functools

import jax
import jax.numpy as jnp
from jax import lax
from jax.experimental import pallas as pl
from jax.experimental.pallas import tpu as pltpu
from jax.sharding import PartitionSpec as P

HD = 64
VMEM_LIMIT = 60 << 20
epsilon = 1e-05
gelu_slope = 1.702


def layer_norm(values_in, gain_vec, shift_vec):
    mean_row = jnp.mean(values_in, axis=-1, keepdims=True)
    centred = values_in - mean_row
    inverse = lax.rsqrt(jnp.mean(centred * centred, axis=-1, keepdims=True) + epsilon)
    normed = centred * inverse
    return (normed * gain_vec + shift_vec, normed, inverse)


def norm_back(grad_out, normed, inverse, gain_vec):
    scaled = grad_out * gain_vec
    grad_in = inverse * (
        scaled
        - jnp.mean(scaled, axis=-1, keepdims=True)
        - normed * jnp.mean(scaled * normed, axis=-1, keepdims=True)
    )
    return (grad_in, jnp.sum(grad_out * normed, axis=0), jnp.sum(grad_out, axis=0))


f32 = jnp.float32
bf16 = jnp.bfloat16
LOG2E = 1.4426950408889634
BLOCK = 512
TRANSPOSED = (((1,), (1,)), ((), ()))


def dot_t(left, right):
    return lax.dot_general(left, right, TRANSPOSED, preferred_element_type=f32)


def dot_n(left, right):
    return jnp.dot(left, right, preferred_element_type=f32)


def three_parts(value):
    top = value.astype(bf16)
    rest = value - top.astype(f32)
    mid = rest.astype(bf16)
    return top, mid, (rest - mid.astype(f32)).astype(bf16)


def diagonal_mask(seg_ref, row_at, size):
    key_pos = lax.broadcasted_iota(jnp.int32, (size, 1), 0)
    query_pos = lax.broadcasted_iota(jnp.int32, (1, size), 1)
    here = seg_ref.shape[2]
    seg = seg_ref[row_at // here, 0:1, pl.ds(pl.multiple_of(lax.rem(row_at, here), size), size)]
    first = jnp.where(seg == 0, query_pos, 0)
    return (key_pos >= first) & (key_pos <= query_pos)


def attend_kernel(
    low_ref, qa_ref, ka_ref, vt_ref, start_ref, out_ref, qb_ref, s0, s1, a0, a1, *, size, blocks
):
    score_bufs, acc_bufs = (s0, s1), (a0, a1)
    heads = range(qa_ref.shape[0])
    lane = lax.broadcasted_iota(jnp.int32, (size, 128), 1)

    def query_block(i, carry):
        row_at = pl.multiple_of(i * size, size)

        def score(h, j, top, diag):
            keys = ka_ref[h, pl.ds(pl.multiple_of(j * size, size), size), :]
            s = dot_t(keys, qa_ref[h, pl.ds(row_at, size), :])
            if diag:
                s = jnp.where(diagonal_mask(start_ref, row_at, size), s, -3e38)
            score_bufs[h][...] = s
            col_max = jnp.max(s, axis=0, keepdims=True)
            return col_max if top is None else jnp.maximum(top, col_max)

        def gather_values(h, j, old, new, first):
            p = jnp.exp2(score_bufs[h][...] * LOG2E - new * LOG2E).astype(bf16)
            part = dot_n(vt_ref[h, :, pl.ds(pl.multiple_of(j * size, size), size)], p)
            if first:
                acc_bufs[h][...] = part
            else:
                acc_bufs[h][...] = acc_bufs[h][...] * jnp.exp2((old - new) * LOG2E) + part

        low = low_ref[i, 0]
        m0 = score(0, i, None, True)
        m1 = score(1, i, None, True)
        gather_values(0, i, None, m0, True)
        m0n = score(0, jnp.minimum(low, i), m0, False)
        gather_values(1, i, None, m1, True)

        def body(j, c):
            m0, m0n, m1 = c
            m1n = score(1, j, m1, False)
            gather_values(0, j, m0, m0n, False)
            m0nn = score(0, jnp.minimum(j + 1, blocks - 1), m0n, False)
            gather_values(1, j, m1, m1n, False)
            return m0n, m0nn, m1n

        m0, _, m1 = lax.fori_loop(low, i, body, (m0, m0n, m1))
        for h, top in ((0, m0), (1, m1)):
            total = acc_bufs[h][64:65, :]
            out = acc_bufs[h][0:64, :] / total
            rows = qa_ref[h, pl.ds(row_at, size), :]
            live = jnp.where(rows[:, 64:65].astype(f32) != 0.0, 1.0, 0.0)
            out_ref[pl.ds(row_at, size), 64 * h : 64 * h + 64] = (out.T * live).astype(out_ref.dtype)
            norm = jnp.broadcast_to(-(top + jnp.log(total)), (8, size)).T[:, 0:1]
            n0, n1, n2 = three_parts(norm)
            rows = jnp.where(lane == 96, n0, jnp.where(lane == 97, n1, jnp.where(lane == 98, n2, rows)))
            qb_ref[h, pl.ds(row_at, size), :] = rows
        return carry

    lax.fori_loop(0, blocks, query_block, 0)


def attend(low, qa, ka, vt, start, size):
    heads, rows, _ = qa.shape
    vmem = pl.BlockSpec(memory_space=pltpu.VMEM)
    return pl.pallas_call(
        functools.partial(attend_kernel, size=size, blocks=rows // size),
        grid_spec=pltpu.PrefetchScalarGridSpec(
            num_scalar_prefetch=0,
            grid=(),
            in_specs=[pl.BlockSpec(memory_space=pltpu.SMEM)] + [vmem] * 4,
            out_specs=[vmem] * 2,
            scratch_shapes=[pltpu.VMEM((size, size), f32)] * heads
            + [pltpu.VMEM((vt.shape[1], size), f32)] * heads,
        ),
        out_shape=[
            jax.ShapeDtypeStruct((rows, HD * heads), bf16),
            jax.ShapeDtypeStruct(qa.shape, bf16),
        ],
        compiler_params=pltpu.CompilerParams(vmem_limit_bytes=VMEM_LIMIT),
        cost_estimate=pl.CostEstimate(
            flops=14 * rows * rows * HD * heads, bytes_accessed=8 << 20, transcendentals=rows * rows
        ),
        name="attend",
    )(low, qa, ka, vt, start)


def attend_back_kernel(
    low_ref, qb_ref, ka_ref, va_ref, kt_ref, g_ref, o_ref, start_ref, grad_ref,
    ga_ref, dk_ref, dv_ref, q0, q1, *, size, blocks
):
    query_accs = (q0, q1)
    lane = lax.broadcasted_iota(jnp.int32, (size, 64), 1)

    def query_block(i, carry):
        row_at = pl.multiple_of(i * size, size)
        g_rows = g_ref[pl.ds(row_at, size), :]
        product = g_rows.astype(f32) * o_ref[pl.ds(row_at, size), :].astype(f32)
        for h in range(2):
            cols = slice(64 * h, 64 * h + 64)
            n0, n1, n2 = three_parts(-jnp.sum(product[:, cols], axis=1, keepdims=True))
            zero = jnp.zeros((size, 64), bf16)
            extra = jnp.where(lane == 0, n0, jnp.where(lane == 1, n1, jnp.where(lane == 2, n2, zero)))
            ga_ref[h] = jnp.concatenate([g_rows[:, cols], extra], axis=1)

        def block(h, j, diag):
            key_at = pl.multiple_of(j * size, size)
            keys = ka_ref[h, pl.ds(key_at, size), :]
            q_rows = qb_ref[h, pl.ds(row_at, size), :]
            g_head = ga_ref[h]
            s = dot_t(keys, q_rows)
            if diag:
                s = jnp.where(diagonal_mask(start_ref, row_at, size), s, -3e38)
            p = jnp.exp2(s * LOG2E)
            dp = dot_t(va_ref[h, pl.ds(key_at, size), :], g_head)
            ds = (p * dp).astype(bf16)
            dv = dot_n(p.astype(bf16), g_head[:, 0:64])
            dk = dot_n(ds, q_rows[:, 0:64])
            dq = dot_n(kt_ref[h, :, pl.ds(key_at, size)], ds)
            if diag:
                dv_ref[h, pl.ds(key_at, size), :] = dv
                dk_ref[h, pl.ds(key_at, size), :] = dk
                query_accs[h][...] = dq
            else:
                dv_ref[h, pl.ds(key_at, size), :] += dv
                dk_ref[h, pl.ds(key_at, size), :] += dk
                query_accs[h][...] += dq

        block(0, i, True)
        block(1, i, True)

        def body(j, c):
            block(0, j, False)
            block(1, j, False)
            return c

        lax.fori_loop(low_ref[i, 0], i, body, 0)
        both = jnp.concatenate([query_accs[0][...], query_accs[1][...]], axis=0) * HD ** (-0.5)
        grad_ref[pl.ds(row_at, size), 0:128] = both.T.astype(bf16)
        return carry

    lax.fori_loop(0, blocks, query_block, 0)

    def finish(i, carry):
        row_at = pl.multiple_of(i * size, size)
        for ref, at in ((dk_ref, 128), (dv_ref, 256)):
            both = jnp.concatenate([ref[0, pl.ds(row_at, size), :], ref[1, pl.ds(row_at, size), :]], axis=1)
            grad_ref[pl.ds(row_at, size), at : at + 128] = both.astype(bf16)
        return carry

    lax.fori_loop(0, blocks, finish, 0)


def attend_back(low, qb, ka, va, kt, g, o, start, size):
    heads, rows, _ = qb.shape
    vmem = pl.BlockSpec(memory_space=pltpu.VMEM)
    return pl.pallas_call(
        functools.partial(attend_back_kernel, size=size, blocks=rows // size),
        grid_spec=pltpu.PrefetchScalarGridSpec(
            num_scalar_prefetch=0,
            grid=(),
            in_specs=[pl.BlockSpec(memory_space=pltpu.SMEM)] + [vmem] * 7,
            out_specs=vmem,
            scratch_shapes=[
                pltpu.VMEM((heads, size, 128), bf16),
                pltpu.VMEM((heads, rows, HD), f32),
                pltpu.VMEM((heads, rows, HD), f32),
            ]
            + [pltpu.VMEM((HD, size), f32)] * heads,
        ),
        out_shape=jax.ShapeDtypeStruct((rows, 3 * HD * heads), bf16),
        compiler_params=pltpu.CompilerParams(vmem_limit_bytes=VMEM_LIMIT),
        cost_estimate=pl.CostEstimate(
            flops=24 * rows * rows * HD * heads, bytes_accessed=16 << 20, transcendentals=rows * rows
        ),
        name="attend_back",
    )(low, qb, ka, va, kt, g, o, start)


MESH = pl.DeviceIdType.MESH


def greet(peers):
    barrier = pltpu.get_barrier_semaphore()
    for peer in peers:
        pl.semaphore_signal(barrier, inc=1, device_id=peer, device_id_type=MESH)
    pl.semaphore_wait(barrier, len(peers))


def push(source, target, send_sem, recv_sem, peer):
    copy = pltpu.make_async_remote_copy(
        src_ref=source,
        dst_ref=target,
        send_sem=send_sem,
        recv_sem=recv_sem,
        device_id=peer,
        device_id_type=MESH,
    )
    copy.start()
    return copy


def quad():
    me = lax.axis_index("tp")
    side = me + 1 - 2 * lax.rem(me, 2)
    across = lax.rem(me + 2, 4)
    far = lax.rem(side + 2, 4)
    return me, side, across, far


def comm_call(kernel, name, number, out_shape, in_specs, out_specs, scratch, moved, *operands):
    return pl.pallas_call(
        kernel,
        out_shape=out_shape,
        in_specs=in_specs,
        out_specs=out_specs,
        scratch_shapes=scratch,
        compiler_params=pltpu.CompilerParams(
            collective_id=number, has_side_effects=True, vmem_limit_bytes=VMEM_LIMIT
        ),
        cost_estimate=pl.CostEstimate(flops=0, bytes_accessed=moved, transcendentals=0),
        name=name,
    )(*operands)


def in_vmem():
    return pl.BlockSpec(memory_space=pltpu.VMEM)


def anywhere():
    return pl.BlockSpec(memory_space=pl.ANY)


def flipped(axis, mask):
    me, index, bit = lax.axis_index(axis), lax.axis_index(axis), 1
    while bit <= mask:
        if mask & bit:
            index = index + bit - 2 * bit * lax.rem(me // bit, 2)
        bit *= 2
    return index


def awaited(ref, send_sem, recv_sem, peer):
    return pltpu.make_async_remote_copy(ref, ref, send_sem, recv_sem, peer, MESH)


def hop_masks(size):
    hops, bit = [], size // 2
    while bit >= 1:
        hops.append((bit, [high + bit for high in range(0, size, 2 * bit)]))
        bit //= 2
    return hops


def enter_kernel(
    x_ref, par_ref, seg_ref, w0, w1, w2, w3,
    normed_ref, segs_ref, low_ref, qa_ref, ka_ref, va_ref, vt_ref, kt_ref, f0, f1,
    x_all, normed_s, qa_s, ka_s, va_s, vt_s, kt_s,
    sy, ry, ss, rs, sf, rf, sg, rg, sw, rw, own, own_w, outs, *, parts, size
):
    me, side, across, far = quad()
    rows = x_ref.shape[0]
    step = rows // parts
    shards = f0.shape[0]
    heads = qa_ref.shape[0]
    width = HD * heads
    shard = lax.axis_index("fsdp")
    hops = hop_masks(shards)
    greet(
        [{"tp": side}, {"tp": across}, {"tp": far}]
        + [{"fsdp": flipped("fsdp", bit)} for bit, _ in hops]
    )
    sent = []

    def rows_of(owner, part):
        return x_all.at[pl.ds(pl.multiple_of(owner * rows + part * step, step), step)]

    sources = (w0, w1, w2, w3)

    def block_of(g, index):
        if g == 0:
            return f0.at[index]
        at = sum(w.shape[1] for w in sources[1:g])
        return f1.at[index, :, pl.ds(at, sources[g].shape[1])]

    def send_hop(g, hop):
        bit, masks = hops[hop]
        peer = {"fsdp": flipped("fsdp", bit)}
        if hop > 0:
            before, arrived = hops[hop - 1]
            for mask in arrived:
                block = block_of(g, flipped("fsdp", mask))
                awaited(block, sw.at[g, mask], rw.at[g, mask], {"fsdp": flipped("fsdp", before)}).wait_recv()
        for mask in masks:
            target = block_of(g, flipped("fsdp", mask - bit))
            block = sources[g] if mask == bit else target
            sent.append(push(block, target, sw.at[g, mask], rw.at[g, mask], peer))

    def end_hops(g):
        bit, arrived = hops[-1]
        for mask in arrived:
            block = block_of(g, flipped("fsdp", mask))
            awaited(block, sw.at[g, mask], rw.at[g, mask], {"fsdp": flipped("fsdp", bit)}).wait_recv()

    for k, peer in enumerate((across, far, side)):
        sent.append(push(seg_ref, segs_ref.at[me], sg.at[k], rg.at[k], {"tp": peer}))
    send_hop(0, 0)
    for part in range(parts):
        mine = x_ref.at[pl.ds(part * step, step)]
        sent.append(push(mine, rows_of(me, part), sy.at[part], ry.at[part], {"tp": across}))
    send_hop(0, 1)
    for g in (1, 2, 3):
        send_hop(g, 0)
    for part in range(parts):
        mine = x_ref.at[pl.ds(part * step, step)]
        sent.append(push(mine, rows_of(me, part), ss.at[part], rs.at[part], {"tp": side}))
    kept = [
        pltpu.make_async_copy(x_ref, x_all.at[pl.ds(pl.multiple_of(me * rows, rows), rows)], own.at[0]),
        pltpu.make_async_copy(seg_ref, segs_ref.at[me], own.at[1]),
    ] + [pltpu.make_async_copy(source, block_of(g, shard), own_w.at[g]) for g, source in enumerate(sources)]
    for copy in kept:
        copy.start()
    waves = sorted(
        ((hop + g, g, hop) for hop in range(1, len(hops)) for g in range(4)), key=lambda w: (w[0], w[1])
    )
    for _, g, hop in waves[1:2]:
        send_hop(g, hop)
    for k, peer in enumerate((across, far, side)):
        awaited(segs_ref.at[peer], sg.at[k], rg.at[k], {"tp": peer}).wait_recv()
    for part in range(parts):
        awaited(rows_of(side, part), ss.at[part], rs.at[part], {"tp": side}).wait_recv()
    for copy in kept:
        copy.wait()
    gain, shift = par_ref[8:9, :], par_ref[9:10, :]

    def norm(owner, part):
        span = pl.ds(pl.multiple_of(owner * rows + part * step, step), step)
        x = x_all[span, :].astype(f32)
        centred = x - jnp.mean(x, axis=-1, keepdims=True)
        inverse = lax.rsqrt(jnp.mean(centred * centred, axis=-1, keepdims=True) + epsilon)
        normed_s[span, :] = (centred * inverse * gain + shift).astype(bf16)

    def norm_near(k, carry):
        norm(me + lax.rem(k, 2) * (side - me), k // 2)
        return carry

    lax.fori_loop(0, 2 * parts, norm_near, 0)
    whole = [segs_ref[n, 0:1, :] for n in range(4)]
    for n in range(4 * rows // size):
        at = n * size
        first = whole[at // rows][:, at % rows : at % rows + 1]
        before = sum(
            jnp.sum(jnp.where((seg > 0) & (seg < first), 1.0, 0.0), axis=1, keepdims=True) for seg in whole
        )
        block = jnp.where(first == 0, n * size, before.astype(jnp.int32)) // size
        low_ref[n : n + 1, :] = jnp.broadcast_to(block, (1, low_ref.shape[1]))
    for _, g, hop in waves[2:]:
        send_hop(g, hop)
    end_hops(0)
    bias_at = pl.ds(pl.multiple_of(me * width, width), width)
    query_bias = par_ref[10:11, bias_at]
    value_bias = par_ref[11:12, bias_at]
    number = lax.broadcasted_iota(jnp.int32, (step, 64), 1)
    number_f = number.astype(f32)
    key_ones = (number >= 32) & (number < 35)
    value_tail = jnp.where(number < 3, 1.0, 0.0).astype(bf16)
    ones_row = jnp.where(lax.broadcasted_iota(jnp.int32, (16, step), 0) == 0, 1.0, 0.0).astype(bf16)

    def copies_out(owner, part):
        row = pl.multiple_of(owner * rows + part * step, step)
        slot = owner * parts + part
        span = pl.ds(row, step)
        pairs = [(normed_s.at[span], normed_ref.at[span])]
        for a, b in ((qa_s, qa_ref), (ka_s, ka_ref), (va_s, va_ref)):
            pairs.append((a.at[:, span, :], b.at[:, span, :]))
        for a, b in ((vt_s, vt_ref), (kt_s, kt_ref)):
            pairs.append((a.at[:, :, span], b.at[:, :, span]))
        return [pltpu.make_async_copy(a, b, outs.at[n, slot]) for n, (a, b) in enumerate(pairs)]

    def compute(owner, part):
        row = pl.multiple_of(owner * rows + part * step, step)
        span = pl.ds(row, step)
        normed = normed_s[span, :]
        weights = f0[...].reshape(shards * f0.shape[1], 3 * width)
        projected = dot_n(normed, weights)
        queries = ((projected[:, 0:width] + query_bias).astype(bf16).astype(f32) * HD ** (-0.5)).astype(bf16)
        keys = projected[:, width : 2 * width].astype(bf16)
        values = (projected[:, 2 * width : 3 * width] + value_bias).astype(bf16)
        seg = segs_ref[owner, 0:1, pl.ds(pl.multiple_of(part * step, step), step)].astype(f32)
        seg = jnp.broadcast_to(seg, (8, step)).T[:, 0:1]
        same = (seg == number_f) & (number < 32)
        other = jnp.where(same | (number > 31), 0.0, -1e30).astype(bf16)
        key_tail = jnp.where(same | key_ones, 1.0, 0.0).astype(bf16)
        for h in range(heads):
            cols = slice(HD * h, HD * h + HD)
            qa_s[h, span, :] = jnp.concatenate([queries[:, cols], other], axis=1)
            ka_s[h, span, :] = jnp.concatenate([keys[:, cols], key_tail], axis=1)
            va_s[h, span, :] = jnp.concatenate([values[:, cols], value_tail], axis=1)
            turned = jnp.concatenate([values[:, cols], keys[:, cols]], axis=1).astype(f32).T.astype(bf16)
            vt_s[h, 0:64, span] = turned[0:64, :]
            vt_s[h, 64:80, span] = ones_row
            kt_s[h, :, span] = turned[64:128, :]
        for copy in copies_out(owner, part):
            copy.start()

    def work(k, carry):
        distant = k // (2 * parts)
        part = lax.rem(k // 2, parts)
        second = lax.rem(k, 2)

        @pl.when((distant == 0) & (second == 0))
        def _():
            here = rows_of(across, part)
            awaited(here, sy.at[part], ry.at[part], {"tp": across}).wait_recv()
            push(here, here, sf.at[part], rf.at[part], {"tp": side})

        @pl.when((distant == 1) & (second == 1))
        def _():
            awaited(rows_of(far, part), sf.at[part], rf.at[part], {"tp": side}).wait_recv()

        @pl.when(distant == 1)
        def _():
            norm(across + second * (far - across), part)

        first = me + distant * (across - me)
        compute(first + second * (side - me + distant * (far - across - side + me)), part)
        return carry

    lax.fori_loop(0, 4 * parts, work, 0)
    for g in (1, 2, 3):
        end_hops(g)

    def drain(k, carry):
        for copy in copies_out(k // parts, lax.rem(k, parts)):
            copy.wait()
        return carry

    lax.fori_loop(0, 4 * parts, drain, 0)
    for part in range(parts):
        awaited(rows_of(across, part), sf.at[part], rf.at[part], {"tp": side}).wait_send()
    for copy in sent:
        copy.wait_send()


def enter(x, params, segments, weights, size, number, parts=4):
    rows, width = x.shape
    seq_rows = 4 * rows
    shards = lax.axis_size("fsdp")
    heads = weights[0].shape[1] // (3 * HD)
    dma = pltpu.SemaphoreType.DMA
    wide = (heads, seq_rows, 128)
    shard_rows = weights[0].shape[0]
    full = [(shards, *weights[0].shape), (shards, shard_rows, sum(w.shape[1] for w in weights[1:]))]
    shapes = [(seq_rows, width), wide, wide, wide, (heads, 80, seq_rows), (heads, 64, seq_rows)]
    made = [jax.ShapeDtypeStruct(s, bf16) for s in shapes]
    return comm_call(
        functools.partial(enter_kernel, parts=parts, size=size),
        "enter",
        number,
        [made[0], jax.ShapeDtypeStruct((4, *segments.shape), segments.dtype)]
        + [jax.ShapeDtypeStruct((seq_rows // size, 128), jnp.int32)]
        + made[1:]
        + [jax.ShapeDtypeStruct(s, bf16) for s in full],
        [in_vmem()] * 7,
        [anywhere(), in_vmem(), in_vmem()] + [anywhere()] * 5 + [in_vmem(), anywhere()],
        [pltpu.VMEM((seq_rows, width), bf16)]
        + [pltpu.VMEM(s, bf16) for s in shapes]
        + [dma((parts,))] * 6
        + [dma((3,))] * 2
        + [dma((4, shards))] * 2
        + [dma((2,)), dma((4,)), dma((6, 4 * parts))],
        60 << 20,
        x,
        params,
        segments,
        *weights,
    )


def middle_kernel(
    seq_out, own_ref, passed_ref, x_ref, g_ref, seg_ref, par_ref,
    layer_ref, resid_ref, seq_ref, kept_ref, over_ref, sums_ref,
    attn_ref, fc_ref, pj_ref, ow_ref, attn_cat, ow_cat, act_s, gp_s, in_s, in_t, g_t, low_t, ga_s, out_acc, gn_acc,
    fc_g, pj_g, ow_g, fc_box, pj_box, ow_box,
    sems, rems, ws, wr, sa, ra, sv, rv, own_sem, *, parts
):
    me, side, across, far = quad()
    greet([{"tp": side}, {"tp": across}, {"tp": far}])
    peers = {1: side, 2: across, 3: far}
    rows = x_ref.shape[0]
    step = rows // parts
    lanes = ow_ref.shape[2]
    sums_ref[...] = jnp.zeros_like(sums_ref)

    def own_rows(who, part):
        return seq_out.at[pl.ds(pl.multiple_of(who * rows + part * step, step), step)]

    def send_rows(part, carry):
        here = pl.ds(pl.multiple_of(part * step, step), step)
        for k in (3, 2, 1):
            push(own_rows(peers[k], part), attn_ref.at[k, here], sa.at[k, part], ra.at[k, part], {"tp": peers[k]})
        return carry

    lax.fori_loop(0, parts, send_rows, 0)
    sent, kept, at = [], [], 0
    for n, full in enumerate((fc_ref, pj_ref, ow_ref)):
        cols = pl.ds(at, full.shape[2])
        at += full.shape[2]
        for k, source in ((0, own_ref), (2, passed_ref)):
            block = source.at[:, cols]
            sent.append(push(block, full.at[k + 1], sv.at[k // 2, n], rv.at[k // 2, n], {"tp": side}))
            kept.append(pltpu.make_async_copy(block, full.at[k], own_sem.at[2 * n + k // 2]))
    mine = seq_out.at[pl.ds(pl.multiple_of(me * rows, rows), rows)]
    kept.append(pltpu.make_async_copy(mine, attn_ref.at[0], own_sem.at[6]))
    for copy in kept:
        copy.start()
    for copy in kept:
        copy.wait()
    for copy in sent:
        copy.wait()
    for p in range(4):
        ow_cat[:, p * lanes : (p + 1) * lanes] = ow_ref[p]

    def owner(t):
        near = me + lax.rem(t, 2) * (1 - 2 * lax.rem(me, 2))
        return lax.rem(near + 2 * (t // 2), 4)

    def add_row(row, value):
        at = pl.ds(row, 1)
        sums_ref[at, :] = sums_ref[at, :] + jnp.sum(value, axis=0, keepdims=True)

    def landing(who, part):
        return seq_ref.at[pl.ds(pl.multiple_of(who * rows + part * step, step), step)]

    def row_block(part, carry):
        here = pl.ds(pl.multiple_of(part * step, step), step)
        for k in (1, 2, 3):
            awaited(attn_ref.at[k, here], sa.at[k, part], ra.at[k, part], {"tp": peers[k]}).wait_recv()
        attn = jnp.concatenate([attn_ref[p, here, :] for p in range(4)], axis=1)
        attn_cat[here, :] = attn
        hidden = x_ref[here, :].astype(f32) + dot_t(attn, ow_cat[...]) + par_ref[0:1, :]
        gain = par_ref[1:2, :]
        normed, hat, inverse = layer_norm(hidden, gain, par_ref[2:3, :])
        in_s[...] = normed.astype(bf16)
        in_t[:, here] = normed.T.astype(bf16)
        grad = g_ref[here, :]
        g_t[:, here] = grad.astype(f32).T.astype(bf16)
        out_acc[...] = hidden + par_ref[3:4, :]
        gn_acc[...] = jnp.zeros_like(gn_acc)

        def hidden_block(t, c):
            bias_at = 4 + owner(t)
            pre = dot_n(in_s[...], fc_ref[t]) + par_ref[pl.ds(bias_at, 1), :]
            gate = jax.nn.sigmoid(gelu_slope * pre)
            raised = pre * gate
            act = raised.astype(bf16)
            act_s[t, here, :] = act
            out_acc[...] += dot_t(act, pj_ref[t])
            grad_act = dot_n(g_ref[here, :], pj_ref[t])
            grad_pre = (grad_act * (gate + gelu_slope * raised * (1.0 - gate))).astype(bf16)
            gp_s[t, here, :] = grad_pre
            add_row(bias_at, grad_pre.astype(f32))
            gn_acc[...] += dot_t(grad_pre, fc_ref[t])
            return c

        lax.fori_loop(0, 4, hidden_block, 0)
        layer_ref[here, :] = out_acc[...].astype(bf16)
        grad_in, gain_part, shift_part = norm_back(gn_acc[...], hat, inverse, gain)
        grad_hidden = grad.astype(f32) + grad_in
        resid_ref[here, :] = grad_hidden
        low = grad_hidden.astype(bf16)
        low_t[:, here] = grad_hidden.T.astype(bf16)
        sums_ref[1:2, :] += gain_part[None]
        sums_ref[2:3, :] += shift_part[None]
        add_row(0, low.astype(f32))
        add_row(3, grad.astype(f32))
        seg = jnp.broadcast_to(seg_ref[0:1, here].astype(f32), (8, step)).T[:, 0:1]
        live = jnp.where(seg != 0.0, 1.0, 0.0)
        grad_attn = (dot_n(low, ow_cat[...]).astype(bf16).astype(f32) * live).astype(bf16)
        for k in (1, 2, 3):
            ga_s[k, here, :] = grad_attn[:, k * lanes : (k + 1) * lanes]
        seq_ref[pl.ds(pl.multiple_of(me * rows + part * step, step), step), :] = grad_attn[:, 0:lanes]
        for k in (3, 2, 1):
            push(ga_s.at[k, here], landing(me, part), sems.at[k, part], rems.at[k, part], {"tp": peers[k]})
        return carry

    lax.fori_loop(0, parts, row_block, 0)
    width = out_acc.shape[1]
    tall = 128

    def out_block(n, carry):
        at = pl.ds(pl.multiple_of(n * tall, tall), tall)
        grad = dot_n(low_t[at, :], attn_cat[...]).astype(bf16)
        for p in range(4):
            ow_g[p, at, :] = grad[:, p * lanes : (p + 1) * lanes]
        return carry

    lax.fori_loop(0, width // tall, out_block, 0)
    triples = ((fc_g, fc_box), (pj_g, pj_box), (ow_g, ow_box))

    def fold(n, b):
        grad, box = triples[n]
        return grad.at[2 * b + 1], box.at[b], ws.at[n, b], wr.at[n, b], {"tp": side}

    for b in (1, 0):
        push(*fold(2, b))

    def slice_block(u, carry):
        t = 3 - 2 * u + 3 * (u // 2)

        def fc_block(n, c):
            at = pl.ds(pl.multiple_of(n * tall, tall), tall)
            fc_g[t, at, :] = dot_n(in_t[at, :], gp_s[t]).astype(bf16)
            pj_g[t, at, :] = dot_n(g_t[at, :], act_s[t]).astype(bf16)
            return c

        lax.fori_loop(0, width // tall, fc_block, 0)
        for b in (1, 0):

            @pl.when(u == 1 - b)
            def _():
                push(*fold(0, b))
                push(*fold(1, b))

        return carry

    lax.fori_loop(0, 4, slice_block, 0)
    for b, target in ((1, over_ref), (0, kept_ref)):
        at = 0
        for n, (grad, box) in enumerate(triples):
            cols = slice(at, at + grad.shape[2])
            at += grad.shape[2]
            awaited(box.at[b], ws.at[n, b], wr.at[n, b], {"tp": side}).wait_recv()
            target[:, cols] = (grad[2 * b].astype(f32) + box[b].astype(f32)).astype(bf16)

    def drain(part, carry):
        here = pl.ds(pl.multiple_of(part * step, step), step)
        for k in (1, 2, 3):
            peer = {"tp": peers[k]}
            awaited(landing(peers[k], part), sems.at[k, part], rems.at[k, part], peer).wait_recv()
            awaited(ga_s.at[k, here], sems.at[k, part], rems.at[k, part], peer).wait_send()
            awaited(own_rows(peers[k], part), sa.at[k, part], ra.at[k, part], peer).wait_send()
        return carry

    lax.fori_loop(0, parts, drain, 0)
    for n, (grad, box) in enumerate(triples):
        for b in (1, 0):
            awaited(grad.at[2 * b + 1], ws.at[n, b], wr.at[n, b], {"tp": side}).wait_send()


def middle(attn, own, passed, x, grad, segments, params, hidden, number, parts=4):
    rows, lanes = x.shape[0], attn.shape[1]
    width = x.shape[1]
    fc = pj = (4, width, hidden)
    ow = (4, width, lanes)
    step = rows // parts
    dma = pltpu.SemaphoreType.DMA
    total = 2 * hidden + lanes
    low, wide = bf16, f32
    scratch = [
        ((4, rows, lanes), low), (fc, low), (pj, low), (ow, low),
        ((rows, width), low), ((width, 4 * lanes), low),
        ((4, rows, hidden), low), ((4, rows, hidden), low),
        ((step, width), low), ((width, rows), low), ((width, rows), low), ((width, rows), low),
        ((4, rows, lanes), low), ((step, width), wide), ((step, width), wide),
        (fc, low), (pj, low), (ow, low),
        ((2, *fc[1:]), low), ((2, *pj[1:]), low), ((2, *ow[1:]), low),
    ]
    outs = [
        ((rows, width), low), ((rows, width), wide), ((4 * rows, lanes), low),
        ((width, total), low), ((width, total), low), ((8, width), wide),
    ]
    return comm_call(
        functools.partial(middle_kernel, parts=parts),
        "middle",
        number,
        [jax.ShapeDtypeStruct(s, d) for s, d in outs],
        [in_vmem(), anywhere(), anywhere()] + [in_vmem()] * 4,
        [in_vmem()] * 6,
        [pltpu.VMEM(s, d) for s, d in scratch]
        + [dma((4, parts)), dma((4, parts)), dma((3, 2)), dma((3, 2))]
        + [dma((4, parts)), dma((4, parts)), dma((2, 3)), dma((2, 3)), dma((7,))],
        60 << 20,
        attn,
        own,
        passed,
        x,
        grad,
        segments,
        params,
    )


def leave_kernel(
    grad_ref, normed_in, w_ref, kept_ref, came_ref, early_ref, x_in, gain_ref, resid_in,
    input_ref, s0, s1, s2, s3, early_out, late_out,
    rows_ref, far_out, own_out, sum_buf, side_far, side_own, over, dw_acc, cols_ref,
    late_ref, early_mid, late_mid, early_one, early_two, late_one, late_two,
    normed_ref, x_ref, resid_ref, loads,
    sa, ra, sb, rb, sy, ry, sw, rw, se, re, sl, rl, se2, re2, sl2, rl2, *bufs, parts, hops
):
    me, side, across, far = quad()
    rows = rows_ref.shape[0]
    step = rows // parts
    shard, shards = lax.axis_index("fsdp"), early_two.shape[0]
    pairs = ((normed_in, normed_ref), (x_in, x_ref), (resid_in, resid_ref))
    loading = [pltpu.make_async_copy(a, b, loads.at[n]) for n, (a, b) in enumerate(pairs)]
    for copy in loading:
        copy.start()
    barrier = pltpu.get_barrier_semaphore()
    for peer in (side, across, far):
        pl.semaphore_signal(barrier, inc=1, device_id={"tp": peer}, device_id_type=MESH)

    def other(k):
        return {"fsdp": lax.rem(shard + k, shards)}

    def signal(k, carry):
        pl.semaphore_signal(barrier, inc=1, device_id=other(k), device_id_type=MESH)
        return carry

    lax.fori_loop(1, shards, signal, 0)
    pl.semaphore_wait(barrier, 3 + shards - 1)
    count = len(hops)
    outs = (s0, s1, s2, s3)
    current = bufs[0:4]
    boxes = [bufs[4 + g * count : 4 + (g + 1) * count] for g in range(4)]
    keeps = [bufs[4 + 4 * count + g * (count - 1) : 4 + 4 * count + (g + 1) * (count - 1)] for g in range(4)]
    sent = []

    def begin(g):
        at = sum(c.shape[3] for c in current[0:g])
        cols = slice(at, at + current[g].shape[3])
        total = kept_ref[:, :, :, cols].astype(f32) + came_ref[:, :, :, cols].astype(f32)
        current[g][...] = total.astype(bf16)

    def hop_parts(g, k):
        axis, bit = hops[k]
        source = current[g] if k == 0 else keeps[g][k - 1]
        half = lax.rem(lax.axis_index(axis) // bit, 2)
        return {axis: flip(axis, bit)}, source, half, boxes[g][k]

    def hop_send(g, k):
        peer, source, half, box = hop_parts(g, k)
        sent.append(push(source.at[:, 1 - half], box, sw.at[g, k], rw.at[g, k], peer))

    def hop_add(g, k):
        peer, source, half, box = hop_parts(g, k)
        awaited(box, sw.at[g, k], rw.at[g, k], peer).wait_recv()
        if k == count - 1:
            outs[g][...] = source[0, half].astype(f32) + box[0].astype(f32)
        else:
            target = keeps[g][k]
            for n in range(box.shape[0]):
                total = source[n, half].astype(f32) + box[n].astype(f32)
                target[n // 2, n % 2] = total.astype(bf16)
            hop_send(g, k + 1)

    def tp_send(value, box, send, recv):
        box[me] = value[...]
        for k, peer in enumerate((side, across, far)):
            sent.append(push(value, box.at[me], send.at[k], recv.at[me], {"tp": peer}))

    def tp_sum(value, box, send, recv):
        for k, peer in enumerate((side, across, far)):
            awaited(box.at[peer], send.at[k], recv.at[peer], {"tp": peer}).wait_recv()
        value[...] = box[0] + box[1] + box[2] + box[3]

    def fsdp_send(value, box, send, recv):
        box[shard] = value[...]

        def give(k, carry):
            push(value, box.at[shard], send.at[k], recv.at[shard], other(k))
            return carry

        lax.fori_loop(1, shards, give, 0)

    def fsdp_sum(value, target, box, send, recv):
        def take(k, carry):
            peer = lax.rem(shard + k, shards)
            copy = awaited(box.at[peer], send.at[k], recv.at[peer], other(k))
            copy.wait_recv()
            copy.wait_send()
            return carry

        lax.fori_loop(1, shards, take, 0)
        target[...] = lax.fori_loop(1, shards, lambda n, total: total + box[n], box[0])

    def span(owner, part):
        return pl.ds(pl.multiple_of(owner * rows + part * step, step), step)

    def piece(part):
        return pl.ds(pl.multiple_of(part * step, step), step)

    def partial(owner, part):
        return dot_t(grad_ref[span(owner, part), :], w_ref[...])

    def give_far(part, carry):
        here = piece(part)
        far_out[here, :] = partial(far, part).astype(bf16)
        push(far_out.at[here], side_far.at[here], sa.at[part], ra.at[part], {"tp": side})
        return carry

    def give_over(part, carry):
        here = piece(part)
        mine = partial(across, part)
        awaited(side_far.at[here], sa.at[part], ra.at[part], {"tp": side}).wait_recv()
        sum_buf[here, :] = (mine + side_far[here, :].astype(f32)).astype(bf16)
        push(sum_buf.at[here], over.at[here], sy.at[part], ry.at[part], {"tp": across})
        return carry

    def give_own(part, carry):
        here = piece(part)
        own_out[here, :] = partial(side, part).astype(bf16)
        push(own_out.at[here], side_own.at[here], sb.at[part], rb.at[part], {"tp": side})
        return carry

    def take_own(part, carry):
        here = piece(part)
        mine = partial(me, part)
        awaited(side_own.at[here], sb.at[part], rb.at[part], {"tp": side}).wait_recv()
        rows_ref[here, :] = mine + side_own[here, :].astype(f32)
        return carry

    gain = gain_ref[8:9, :]

    def take_over(part, carry):
        here = piece(part)
        x = x_ref[here, :].astype(f32)
        centred = x - jnp.mean(x, axis=-1, keepdims=True)
        inverse = lax.rsqrt(jnp.mean(centred * centred, axis=-1, keepdims=True) + epsilon)
        normed = centred * inverse
        awaited(over.at[here], sy.at[part], ry.at[part], {"tp": across}).wait_recv()
        grad = rows_ref[here, :] + over[here, :].astype(f32)
        grad_in, gain_part, shift_part = norm_back(grad, normed, inverse, gain)
        input_ref[here, :] = (resid_ref[here, :] + grad_in).astype(bf16)
        late_ref[0:1, :] += gain_part[None]
        late_ref[1:2, :] += shift_part[None]
        return carry

    def drain(part, carry):
        here = piece(part)
        awaited(far_out.at[here], sa.at[part], ra.at[part], {"tp": side}).wait_send()
        awaited(own_out.at[here], sb.at[part], rb.at[part], {"tp": side}).wait_send()
        awaited(sum_buf.at[here], sy.at[part], ry.at[part], {"tp": across}).wait_send()
        return carry

    chunk = 512
    steps = grad_ref.shape[0] // chunk
    dw_acc[...] = jnp.zeros_like(dw_acc)
    cols_ref[...] = jnp.zeros_like(cols_ref)
    ones = jnp.ones((8, chunk), bf16)

    def weight_grad(n, carry):
        at = pl.ds(pl.multiple_of(n * chunk, chunk), chunk)
        g = grad_ref[at, :]
        dw_acc[...] += lax.dot_general(
            normed_ref[at, :], g, (((0,), (0,)), ((), ())), preferred_element_type=f32
        )
        cols_ref[...] += dot_n(ones, g)
        return carry

    tp_send(early_ref, early_one, se, re)
    lax.fori_loop(0, parts, give_far, 0)
    for g in (0, 1):
        begin(g)
        hop_send(g, 0)
    lax.fori_loop(0, parts, give_over, 0)
    begin(2)
    for copy in loading:
        copy.wait()
    lax.fori_loop(0, steps // 2, weight_grad, 0)
    hop_add(0, 0)
    lax.fori_loop(steps // 2, steps, weight_grad, 0)
    current[3][...] = dw_acc[...].astype(bf16).reshape(current[3].shape)
    hop_send(3, 0)
    hop_send(2, 0)
    tp_sum(early_mid, early_one, se, re)
    fsdp_send(early_mid, early_two, se2, re2)
    hop_add(1, 0)
    late_ref[...] = jnp.zeros_like(late_ref)
    wide = cols_ref.shape[1] // 3
    qv_at = pl.ds(pl.multiple_of(me * wide, wide), wide)
    late_ref[2:3, qv_at] = cols_ref[0:1, 0:wide]
    late_ref[3:4, qv_at] = cols_ref[0:1, 2 * wide : 3 * wide]
    lax.fori_loop(0, parts, give_own, 0)
    turns = enumerate((0, 1, 3, 2))
    order = sorted((k + turn, turn, g, k) for turn, g in turns for k in range(count))
    order = [(g, k) for _, _, g, k in order if (g, k) not in ((0, 0), (1, 0))]
    lax.fori_loop(0, parts, take_own, 0)
    taken = {len(order) * share // 10: span for share, span in ((6, (0, 2)), (7, (2, 3)), (9, (3, 4)))}
    for n, (g, k) in enumerate(order):
        if n in taken:
            first, last = taken[n]
            lax.fori_loop(first * parts // 4, last * parts // 4, take_over, 0)
        if n == len(order) - 1:
            tp_send(late_ref, late_one, sl, rl)
        hop_add(g, k)
    fsdp_sum(early_mid, early_out, early_two, se2, re2)
    tp_sum(late_mid, late_one, sl, rl)
    fsdp_send(late_mid, late_two, sl2, rl2)
    lax.fori_loop(0, parts, drain, 0)
    fsdp_sum(late_mid, late_out, late_two, sl2, rl2)
    for copy in sent:
        copy.wait_send()


def leave(grad, normed, w, kept, came, widths, early, x, gain, resid, number, parts=4):
    rows, width = grad.shape[0] // 4, w.shape[0]
    dma = pltpu.SemaphoreType.DMA
    hops = bits_of("fsdp")
    count = len(hops)
    shards = lax.axis_size("fsdp")
    shard = width // shards
    widths = [*widths, grad.shape[1]]
    split = (shards // 2, 2, shard)
    current = [pltpu.VMEM((*split, n), bf16) for n in widths]
    boxes = [pltpu.VMEM((shards >> (k + 1), shard, n), bf16) for n in widths for k in range(count)]
    keeps = [pltpu.VMEM((shards >> (k + 2), 2, shard, n), bf16) for n in widths for k in range(count - 1)]
    late = (4, width)
    return comm_call(
        functools.partial(leave_kernel, parts=parts, hops=hops),
        "leave",
        number,
        [jax.ShapeDtypeStruct((rows, width), bf16)]
        + [jax.ShapeDtypeStruct((shard, n), f32) for n in widths]
        + [jax.ShapeDtypeStruct(early.shape, f32), jax.ShapeDtypeStruct(late, f32)],
        [in_vmem(), anywhere()] + [in_vmem()] * 4 + [anywhere(), in_vmem(), anywhere()],
        [in_vmem()] * 7,
        [pltpu.VMEM((rows, width), f32)]
        + [pltpu.VMEM((rows, width), bf16)] * 6
        + [pltpu.VMEM((width, grad.shape[1]), f32), pltpu.VMEM((8, grad.shape[1]), f32)]
        + [pltpu.VMEM(late, f32), pltpu.VMEM(early.shape, f32), pltpu.VMEM(late, f32)]
        + [pltpu.VMEM((n, *shape), f32) for shape in (early.shape, late) for n in (4, shards)]
        + [pltpu.VMEM(v.shape, v.dtype) for v in (normed, x, resid)]
        + [dma((3,))]
        + [dma((parts,))] * 6
        + [dma((4, count))] * 2
        + [dma((3,)), dma((4,))] * 2
        + [dma((shards,))] * 4
        + current
        + boxes
        + keeps,
        60 << 20,
        grad,
        normed,
        w,
        kept.reshape(*split, kept.shape[1]),
        came.reshape(*split, came.shape[1]),
        early,
        x,
        gain,
        resid,
    )


def finish_kernel(
    rows_in, fc_in, proj_in, out_in, qkv_in, early_in, late_in,
    rows_ref, fc_ref, proj_ref, out_ref, qkv_ref, qv_ref, *vectors
):
    rows_ref[...] = rows_in[...]
    fc_ref[...] = fc_in[...]
    proj_ref[...] = proj_in[...]
    out_ref[...] = out_in[...]
    width = qkv_ref.shape[2]
    for n in range(3):
        qkv_ref[n] = qkv_in[:, n * width : (n + 1) * width]
    qv_ref[...] = late_in[2:4, :]
    first_gain, first_shift, out_bias, gain, shift, fc_bias, proj_bias = vectors
    lanes = first_gain.shape[1]
    count = first_gain.shape[0]
    singles = ((first_gain, late_in, 0), (first_shift, late_in, 1), (out_bias, early_in, 0))
    singles += ((gain, early_in, 1), (shift, early_in, 2), (proj_bias, early_in, 3))
    for ref, source, row in singles:
        for n in range(count):
            ref[n : n + 1, :] = source[row : row + 1, n * lanes : (n + 1) * lanes]
    for row in range(4):
        for n in range(count):
            at = row * count + n
            fc_bias[at : at + 1, :] = early_in[4 + row : 5 + row, n * lanes : (n + 1) * lanes]


def finish(rows, fc, proj, out, qkv, early, late):
    lanes = 128
    width = late.shape[1]
    shapes = [rows, fc, proj, out]
    outs = [jax.ShapeDtypeStruct(v.shape, v.dtype) for v in shapes]
    outs.append(jax.ShapeDtypeStruct((3, qkv.shape[0], qkv.shape[1] // 3), f32))
    outs.append(jax.ShapeDtypeStruct((2, width), f32))
    sizes = [width] * 5 + [4 * early.shape[1], width]
    outs += [jax.ShapeDtypeStruct((n // lanes, lanes), f32) for n in sizes]
    rows, fc, proj, out, qkv, qv, *vectors = pl.pallas_call(
        finish_kernel,
        out_shape=outs,
        in_specs=[in_vmem()] * 7,
        out_specs=[in_vmem()] * len(outs),
        cost_estimate=pl.CostEstimate(flops=0, bytes_accessed=3 << 20, transcendentals=0),
        name="finish",
    )(rows, fc, proj, out, qkv, early, late)
    return rows, fc, proj.T, out.T, qkv.transpose(1, 0, 2), qv, [v.reshape(-1) for v in vectors]


def flip(axis, bit):
    me = lax.axis_index(axis)
    return me + bit - 2 * bit * lax.rem(me // bit, 2)


def bits_of(axis):
    size, bits, bit = lax.axis_size(axis), [], 1
    while bit < size:
        bits.append((axis, bit))
        bit *= 2
    return bits


def across(value):
    return lax.ppermute(value, "tp", [(n, n ^ 2) for n in range(4)])


def local(
    inputs,
    segments,
    out_grad,
    first_gain,
    first_shift,
    qkv_weight,
    qv_bias,
    out_weight,
    out_bias,
    second_gain,
    second_shift,
    fc_weight,
    fc_bias,
    proj_weight,
    proj_bias,
):
    slices = lax.axis_size("tp")
    rows_here, model_width = inputs.shape
    shard_rows = qkv_weight.shape[0]
    head_cols = qkv_weight.shape[2]
    hidden_cols = fc_weight.shape[1]
    params = jnp.concatenate(
        [
            jnp.stack([out_bias, second_gain, second_shift, proj_bias]),
            fc_bias.reshape(slices, hidden_cols),
            jnp.stack([first_gain, first_shift]),
            qv_bias,
            jnp.zeros((4, model_width), bf16),
        ]
    ).astype(f32)
    size = min(BLOCK, rows_here)
    seq_normed, seg_parts, low, qa, ka, va, vt, kt, qkv_full, own = enter(
        inputs,
        params,
        segments,
        (qkv_weight.reshape(shard_rows, 3 * head_cols), fc_weight, proj_weight.T, out_weight.T),
        size,
        0,
    )
    qkv_full = qkv_full.reshape(model_width, 3 * head_cols)
    own = own.reshape(model_width, own.shape[2])
    over = across(own)
    widths = (hidden_cols, hidden_cols, head_cols)

    attn_out, qb = attend(low, qa, ka, vt, seg_parts, size)

    layer_out, grad_hidden, grad_attn_seq, kept, passed, early = middle(
        attn_out, own, over, inputs, out_grad, segments, params, hidden_cols, 2
    )
    came = across(passed)
    grad_qkv = attend_back(low, qb, ka, va, kt, grad_attn_seq, attn_out, seg_parts, size)
    input_grad, fc_w_grad, proj_w_grad, out_w_grad, qkv_grad, early_sums, late_sums = leave(
        grad_qkv,
        seq_normed,
        qkv_full,
        kept,
        came,
        widths,
        early,
        inputs,
        params,
        grad_hidden,
        3,
    )
    input_grad, fc_w_grad, proj_w_grad, out_w_grad, qkv_grad, qv_bias_grad, vectors = finish(
        input_grad,
        fc_w_grad,
        proj_w_grad,
        out_w_grad,
        qkv_grad,
        early_sums,
        late_sums,
    )
    first_gain_grad, first_shift_grad, out_bias_grad, second_gain_grad, second_shift_grad = vectors[0:5]
    fc_bias_grad, proj_bias_grad = vectors[5:7]

    return (
        layer_out,
        input_grad,
        first_gain_grad,
        first_shift_grad,
        qkv_grad,
        qv_bias_grad,
        out_w_grad,
        out_bias_grad,
        second_gain_grad,
        second_shift_grad,
        fc_w_grad,
        fc_bias_grad,
        proj_w_grad,
        proj_bias_grad,
    )


def solution(mesh):
    return jax.shard_map(
        local,
        mesh=mesh,
        in_specs=(
            P(("fsdp", "tp"), None),
            P("fsdp", "tp"),
            P(("fsdp", "tp"), None),
            P(),
            P(),
            P("fsdp", None, "tp"),
            P(),
            P("tp", "fsdp"),
            P(),
            P(),
            P(),
            P("fsdp", "tp"),
            P(),
            P("tp", "fsdp"),
            P(),
        ),
        out_specs=(
            P(("fsdp", "tp"), None),
            P(("fsdp", "tp"), None),
            P(),
            P(),
            P("fsdp", None, "tp"),
            P(),
            P("tp", "fsdp"),
            P(),
            P(),
            P(),
            P("fsdp", "tp"),
            P(),
            P("tp", "fsdp"),
            P(),
        ),
        check_vma=False,
    )
```

```python
import functools

import jax
import jax.numpy as jnp
from jax import lax
from jax.experimental import pallas as pl
from jax.experimental.pallas import tpu as pltpu
from jax.sharding import PartitionSpec as P

HD = 64
VMEM_LIMIT = 60 << 20
epsilon = 1e-05
gelu_slope = 1.702


def layer_norm(values_in, gain_vec, shift_vec):
    mean_row = jnp.mean(values_in, axis=-1, keepdims=True)
    centred = values_in - mean_row
    inverse = lax.rsqrt(jnp.mean(centred * centred, axis=-1, keepdims=True) + epsilon)
    normed = centred * inverse
    return (normed * gain_vec + shift_vec, normed, inverse)


def norm_back(grad_out, normed, inverse, gain_vec):
    scaled = grad_out * gain_vec
    grad_in = inverse * (
        scaled
        - jnp.mean(scaled, axis=-1, keepdims=True)
        - normed * jnp.mean(scaled * normed, axis=-1, keepdims=True)
    )
    return (grad_in, jnp.sum(grad_out * normed, axis=0), jnp.sum(grad_out, axis=0))


f32 = jnp.float32
bf16 = jnp.bfloat16
LOG2E = 1.4426950408889634
BLOCK = 512
TRANSPOSED = (((1,), (1,)), ((), ()))


def dot_t(left, right):
    return lax.dot_general(left, right, TRANSPOSED, preferred_element_type=f32)


def dot_n(left, right):
    return jnp.dot(left, right, preferred_element_type=f32)


def three_parts(value):
    top = value.astype(bf16)
    rest = value - top.astype(f32)
    mid = rest.astype(bf16)
    return top, mid, (rest - mid.astype(f32)).astype(bf16)


def diagonal_mask(seg_ref, row_at, size):
    key_pos = lax.broadcasted_iota(jnp.int32, (size, 1), 0)
    query_pos = lax.broadcasted_iota(jnp.int32, (1, size), 1)
    here = seg_ref.shape[2]
    seg = seg_ref[row_at // here, 0:1, pl.ds(pl.multiple_of(lax.rem(row_at, here), size), size)]
    first = jnp.where(seg == 0, query_pos, 0)
    return (key_pos >= first) & (key_pos <= query_pos)


def attend_kernel(
    low_ref, qa_ref, ka_ref, vt_ref, start_ref, out_ref, qb_ref, s0, s1, a0, a1, *, size, blocks
):
    score_bufs, acc_bufs = (s0, s1), (a0, a1)
    heads = range(qa_ref.shape[0])
    lane = lax.broadcasted_iota(jnp.int32, (size, 128), 1)

    def query_block(i, carry):
        row_at = pl.multiple_of(i * size, size)

        def score(h, j, top, diag):
            keys = ka_ref[h, pl.ds(pl.multiple_of(j * size, size), size), :]
            s = dot_t(keys, qa_ref[h, pl.ds(row_at, size), :])
            if diag:
                s = jnp.where(diagonal_mask(start_ref, row_at, size), s, -3e38)
            score_bufs[h][...] = s
            col_max = jnp.max(s, axis=0, keepdims=True)
            return col_max if top is None else jnp.maximum(top, col_max)

        def gather_values(h, j, old, new, first):
            p = jnp.exp2(score_bufs[h][...] * LOG2E - new * LOG2E).astype(bf16)
            part = dot_n(vt_ref[h, :, pl.ds(pl.multiple_of(j * size, size), size)], p)
            if first:
                acc_bufs[h][...] = part
            else:
                acc_bufs[h][...] = acc_bufs[h][...] * jnp.exp2((old - new) * LOG2E) + part

        low = low_ref[i, 0]
        m0 = score(0, i, None, True)
        m1 = score(1, i, None, True)
        gather_values(0, i, None, m0, True)
        m0n = score(0, jnp.minimum(low, i), m0, False)
        gather_values(1, i, None, m1, True)

        def body(j, c):
            m0, m0n, m1 = c
            m1n = score(1, j, m1, False)
            gather_values(0, j, m0, m0n, False)
            m0nn = score(0, jnp.minimum(j + 1, blocks - 1), m0n, False)
            gather_values(1, j, m1, m1n, False)
            return m0n, m0nn, m1n

        m0, _, m1 = lax.fori_loop(low, i, body, (m0, m0n, m1))
        for h, top in ((0, m0), (1, m1)):
            total = acc_bufs[h][64:65, :]
            out = acc_bufs[h][0:64, :] / total
            rows = qa_ref[h, pl.ds(row_at, size), :]
            live = jnp.where(rows[:, 64:65].astype(f32) != 0.0, 1.0, 0.0)
            out_ref[pl.ds(row_at, size), 64 * h : 64 * h + 64] = (out.T * live).astype(out_ref.dtype)
            norm = jnp.broadcast_to(-(top + jnp.log(total)), (8, size)).T[:, 0:1]
            n0, n1, n2 = three_parts(norm)
            rows = jnp.where(lane == 96, n0, jnp.where(lane == 97, n1, jnp.where(lane == 98, n2, rows)))
            qb_ref[h, pl.ds(row_at, size), :] = rows
        return carry

    lax.fori_loop(0, blocks, query_block, 0)


def attend(low, qa, ka, vt, start, size):
    heads, rows, _ = qa.shape
    vmem = pl.BlockSpec(memory_space=pltpu.VMEM)
    return pl.pallas_call(
        functools.partial(attend_kernel, size=size, blocks=rows // size),
        grid_spec=pltpu.PrefetchScalarGridSpec(
            num_scalar_prefetch=0,
            grid=(),
            in_specs=[pl.BlockSpec(memory_space=pltpu.SMEM)] + [vmem] * 4,
            out_specs=[vmem] * 2,
            scratch_shapes=[pltpu.VMEM((size, size), f32)] * heads
            + [pltpu.VMEM((vt.shape[1], size), f32)] * heads,
        ),
        out_shape=[
            jax.ShapeDtypeStruct((rows, HD * heads), bf16),
            jax.ShapeDtypeStruct(qa.shape, bf16),
        ],
        compiler_params=pltpu.CompilerParams(vmem_limit_bytes=VMEM_LIMIT),
        cost_estimate=pl.CostEstimate(
            flops=14 * rows * rows * HD * heads, bytes_accessed=8 << 20, transcendentals=rows * rows
        ),
        name="attend",
    )(low, qa, ka, vt, start)


def attend_back_kernel(
    low_ref, qb_ref, ka_ref, va_ref, kt_ref, g_ref, o_ref, start_ref, grad_ref,
    ga_ref, dk_ref, dv_ref, q0, q1, *, size, blocks
):
    query_accs = (q0, q1)
    lane = lax.broadcasted_iota(jnp.int32, (size, 64), 1)

    def query_block(i, carry):
        row_at = pl.multiple_of(i * size, size)
        g_rows = g_ref[pl.ds(row_at, size), :]
        product = g_rows.astype(f32) * o_ref[pl.ds(row_at, size), :].astype(f32)
        for h in range(2):
            cols = slice(64 * h, 64 * h + 64)
            n0, n1, n2 = three_parts(-jnp.sum(product[:, cols], axis=1, keepdims=True))
            zero = jnp.zeros((size, 64), bf16)
            extra = jnp.where(lane == 0, n0, jnp.where(lane == 1, n1, jnp.where(lane == 2, n2, zero)))
            ga_ref[h] = jnp.concatenate([g_rows[:, cols], extra], axis=1)

        def block(h, j, diag):
            key_at = pl.multiple_of(j * size, size)
            keys = ka_ref[h, pl.ds(key_at, size), :]
            q_rows = qb_ref[h, pl.ds(row_at, size), :]
            g_head = ga_ref[h]
            s = dot_t(keys, q_rows)
            if diag:
                s = jnp.where(diagonal_mask(start_ref, row_at, size), s, -3e38)
            p = jnp.exp2(s * LOG2E)
            dp = dot_t(va_ref[h, pl.ds(key_at, size), :], g_head)
            ds = (p * dp).astype(bf16)
            dv = dot_n(p.astype(bf16), g_head[:, 0:64])
            dk = dot_n(ds, q_rows[:, 0:64])
            dq = dot_n(kt_ref[h, :, pl.ds(key_at, size)], ds)
            if diag:
                dv_ref[h, pl.ds(key_at, size), :] = dv
                dk_ref[h, pl.ds(key_at, size), :] = dk
                query_accs[h][...] = dq
            else:
                dv_ref[h, pl.ds(key_at, size), :] += dv
                dk_ref[h, pl.ds(key_at, size), :] += dk
                query_accs[h][...] += dq

        block(0, i, True)
        block(1, i, True)

        def body(j, c):
            block(0, j, False)
            block(1, j, False)
            return c

        lax.fori_loop(low_ref[i, 0], i, body, 0)
        both = jnp.concatenate([query_accs[0][...], query_accs[1][...]], axis=0) * HD ** (-0.5)
        grad_ref[pl.ds(row_at, size), 0:128] = both.T.astype(bf16)
        return carry

    lax.fori_loop(0, blocks, query_block, 0)

    def finish(i, carry):
        row_at = pl.multiple_of(i * size, size)
        for ref, at in ((dk_ref, 128), (dv_ref, 256)):
            both = jnp.concatenate([ref[0, pl.ds(row_at, size), :], ref[1, pl.ds(row_at, size), :]], axis=1)
            grad_ref[pl.ds(row_at, size), at : at + 128] = both.astype(bf16)
        return carry

    lax.fori_loop(0, blocks, finish, 0)


def attend_back(low, qb, ka, va, kt, g, o, start, size):
    heads, rows, _ = qb.shape
    vmem = pl.BlockSpec(memory_space=pltpu.VMEM)
    return pl.pallas_call(
        functools.partial(attend_back_kernel, size=size, blocks=rows // size),
        grid_spec=pltpu.PrefetchScalarGridSpec(
            num_scalar_prefetch=0,
            grid=(),
            in_specs=[pl.BlockSpec(memory_space=pltpu.SMEM)] + [vmem] * 7,
            out_specs=vmem,
            scratch_shapes=[
                pltpu.VMEM((heads, size, 128), bf16),
                pltpu.VMEM((heads, rows, HD), f32),
                pltpu.VMEM((heads, rows, HD), f32),
            ]
            + [pltpu.VMEM((HD, size), f32)] * heads,
        ),
        out_shape=jax.ShapeDtypeStruct((rows, 3 * HD * heads), bf16),
        compiler_params=pltpu.CompilerParams(vmem_limit_bytes=VMEM_LIMIT),
        cost_estimate=pl.CostEstimate(
            flops=24 * rows * rows * HD * heads, bytes_accessed=16 << 20, transcendentals=rows * rows
        ),
        name="attend_back",
    )(low, qb, ka, va, kt, g, o, start)


MESH = pl.DeviceIdType.MESH


def greet(peers):
    barrier = pltpu.get_barrier_semaphore()
    for peer in peers:
        pl.semaphore_signal(barrier, inc=1, device_id=peer, device_id_type=MESH)
    pl.semaphore_wait(barrier, len(peers))


def push(source, target, send_sem, recv_sem, peer):
    copy = pltpu.make_async_remote_copy(
        src_ref=source,
        dst_ref=target,
        send_sem=send_sem,
        recv_sem=recv_sem,
        device_id=peer,
        device_id_type=MESH,
    )
    copy.start()
    return copy


def quad():
    me = lax.axis_index("tp")
    side = me + 1 - 2 * lax.rem(me, 2)
    across = lax.rem(me + 2, 4)
    far = lax.rem(side + 2, 4)
    return me, side, across, far


def comm_call(kernel, name, number, out_shape, in_specs, out_specs, scratch, moved, *operands):
    return pl.pallas_call(
        kernel,
        out_shape=out_shape,
        in_specs=in_specs,
        out_specs=out_specs,
        scratch_shapes=scratch,
        compiler_params=pltpu.CompilerParams(
            collective_id=number, has_side_effects=True, vmem_limit_bytes=VMEM_LIMIT
        ),
        cost_estimate=pl.CostEstimate(flops=0, bytes_accessed=moved, transcendentals=0),
        name=name,
    )(*operands)


def in_vmem():
    return pl.BlockSpec(memory_space=pltpu.VMEM)


def anywhere():
    return pl.BlockSpec(memory_space=pl.ANY)


def flipped(axis, mask):
    me, index, bit = lax.axis_index(axis), lax.axis_index(axis), 1
    while bit <= mask:
        if mask & bit:
            index = index + bit - 2 * bit * lax.rem(me // bit, 2)
        bit *= 2
    return index


def awaited(ref, send_sem, recv_sem, peer):
    return pltpu.make_async_remote_copy(ref, ref, send_sem, recv_sem, peer, MESH)


def hop_masks(size):
    hops, bit = [], size // 2
    while bit >= 1:
        hops.append((bit, [high + bit for high in range(0, size, 2 * bit)]))
        bit //= 2
    return hops


def enter_kernel(
    x_ref, seg_ref, w0, w1, w2, w3, v0, v1, v2, v3, v4, v5, v6, v7,
    normed_ref, segs_ref, low_ref, par_ref, qa_ref, ka_ref, va_ref, vt_ref, kt_ref, f0, f1,
    x_all, normed_s, qa_s, ka_s, va_s, vt_s, kt_s,
    sy, ry, ss, rs, sf, rf, sg, rg, sw, rw, own, own_w, outs, *, parts, size
):
    me, side, across, far = quad()
    rows = x_ref.shape[0]
    step = rows // parts
    shards = f0.shape[0]
    heads = qa_ref.shape[0]
    width = HD * heads
    shard = lax.axis_index("fsdp")
    hops = hop_masks(shards)
    greet(
        [{"tp": side}, {"tp": across}, {"tp": far}]
        + [{"fsdp": flipped("fsdp", bit)} for bit, _ in hops]
    )
    sent = []

    def rows_of(owner, part):
        return x_all.at[pl.ds(pl.multiple_of(owner * rows + part * step, step), step)]

    sources = (w0, w1, w2, w3)

    def block_of(g, index):
        if g == 0:
            return f0.at[index]
        at = sum(w.shape[1] for w in sources[1:g])
        return f1.at[index, :, pl.ds(at, sources[g].shape[1])]

    def send_hop(g, hop):
        bit, masks = hops[hop]
        peer = {"fsdp": flipped("fsdp", bit)}
        if hop > 0:
            before, arrived = hops[hop - 1]
            for mask in arrived:
                block = block_of(g, flipped("fsdp", mask))
                awaited(block, sw.at[g, mask], rw.at[g, mask], {"fsdp": flipped("fsdp", before)}).wait_recv()
        for mask in masks:
            target = block_of(g, flipped("fsdp", mask - bit))
            block = sources[g] if mask == bit else target
            sent.append(push(block, target, sw.at[g, mask], rw.at[g, mask], peer))

    def end_hops(g):
        bit, arrived = hops[-1]
        for mask in arrived:
            block = block_of(g, flipped("fsdp", mask))
            awaited(block, sw.at[g, mask], rw.at[g, mask], {"fsdp": flipped("fsdp", bit)}).wait_recv()

    for k, peer in enumerate((across, far, side)):
        sent.append(push(seg_ref, segs_ref.at[me], sg.at[k], rg.at[k], {"tp": peer}))
    send_hop(0, 0)
    for part in range(parts):
        mine = x_ref.at[pl.ds(part * step, step)]
        sent.append(push(mine, rows_of(me, part), sy.at[part], ry.at[part], {"tp": across}))
    send_hop(0, 1)
    for g in (1, 2, 3):
        send_hop(g, 0)
    for part in range(parts):
        mine = x_ref.at[pl.ds(part * step, step)]
        sent.append(push(mine, rows_of(me, part), ss.at[part], rs.at[part], {"tp": side}))
    kept = [
        pltpu.make_async_copy(x_ref, x_all.at[pl.ds(pl.multiple_of(me * rows, rows), rows)], own.at[0]),
        pltpu.make_async_copy(seg_ref, segs_ref.at[me], own.at[1]),
    ] + [pltpu.make_async_copy(source, block_of(g, shard), own_w.at[g]) for g, source in enumerate(sources)]
    for copy in kept:
        copy.start()
    waves = sorted(
        ((hop + g, g, hop) for hop in range(1, len(hops)) for g in range(4)), key=lambda w: (w[0], w[1])
    )
    for _, g, hop in waves[1:2]:
        send_hop(g, hop)
    for k, peer in enumerate((across, far, side)):
        awaited(segs_ref.at[peer], sg.at[k], rg.at[k], {"tp": peer}).wait_recv()
    for part in range(parts):
        awaited(rows_of(side, part), ss.at[part], rs.at[part], {"tp": side}).wait_recv()
    for copy in kept:
        copy.wait()

    line, columns = 0, par_ref.shape[1]
    par_ref[...] = jnp.zeros_like(par_ref)
    for ref in (v0, v1, v2, v3, v4, v5, v6):
        value = ref[...].astype(f32).reshape(1, ref.shape[0])
        for n in range(ref.shape[0] // columns):
            par_ref[line : line + 1, :] = value[:, n * columns : (n + 1) * columns]
            line += 1
    par_ref[line : line + 2, :] = v7[...].astype(f32)
    gain, shift = par_ref[8:9, :], par_ref[9:10, :]

    def norm(owner, part):
        span = pl.ds(pl.multiple_of(owner * rows + part * step, step), step)
        x = x_all[span, :].astype(f32)
        centred = x - jnp.mean(x, axis=-1, keepdims=True)
        inverse = lax.rsqrt(jnp.mean(centred * centred, axis=-1, keepdims=True) + epsilon)
        normed_s[span, :] = (centred * inverse * gain + shift).astype(bf16)

    def norm_near(k, carry):
        norm(me + lax.rem(k, 2) * (side - me), k // 2)
        return carry

    lax.fori_loop(0, 2 * parts, norm_near, 0)
    whole = [segs_ref[n, 0:1, :] for n in range(4)]
    for n in range(4 * rows // size):
        at = n * size
        first = whole[at // rows][:, at % rows : at % rows + 1]
        before = sum(
            jnp.sum(jnp.where((seg > 0) & (seg < first), 1.0, 0.0), axis=1, keepdims=True) for seg in whole
        )
        block = jnp.where(first == 0, n * size, before.astype(jnp.int32)) // size
        low_ref[n : n + 1, :] = jnp.broadcast_to(block, (1, low_ref.shape[1]))
    for _, g, hop in waves[2:]:
        send_hop(g, hop)
    end_hops(0)
    bias_at = pl.ds(pl.multiple_of(me * width, width), width)
    query_bias = par_ref[10:11, bias_at]
    value_bias = par_ref[11:12, bias_at]
    number = lax.broadcasted_iota(jnp.int32, (step, 64), 1)
    number_f = number.astype(f32)
    key_ones = (number >= 32) & (number < 35)
    value_tail = jnp.where(number < 3, 1.0, 0.0).astype(bf16)
    ones_row = jnp.where(lax.broadcasted_iota(jnp.int32, (16, step), 0) == 0, 1.0, 0.0).astype(bf16)

    def copies_out(owner, part):
        row = pl.multiple_of(owner * rows + part * step, step)
        slot = owner * parts + part
        span = pl.ds(row, step)
        pairs = [(normed_s.at[span], normed_ref.at[span])]
        for a, b in ((qa_s, qa_ref), (ka_s, ka_ref), (va_s, va_ref)):
            pairs.append((a.at[:, span, :], b.at[:, span, :]))
        for a, b in ((vt_s, vt_ref), (kt_s, kt_ref)):
            pairs.append((a.at[:, :, span], b.at[:, :, span]))
        return [pltpu.make_async_copy(a, b, outs.at[n, slot]) for n, (a, b) in enumerate(pairs)]

    def compute(owner, part):
        row = pl.multiple_of(owner * rows + part * step, step)
        span = pl.ds(row, step)
        normed = normed_s[span, :]
        weights = f0[...].reshape(shards * f0.shape[1], 3 * width)
        projected = dot_n(normed, weights)
        queries = ((projected[:, 0:width] + query_bias).astype(bf16).astype(f32) * HD ** (-0.5)).astype(bf16)
        keys = projected[:, width : 2 * width].astype(bf16)
        values = (projected[:, 2 * width : 3 * width] + value_bias).astype(bf16)
        seg = segs_ref[owner, 0:1, pl.ds(pl.multiple_of(part * step, step), step)].astype(f32)
        seg = jnp.broadcast_to(seg, (8, step)).T[:, 0:1]
        same = (seg == number_f) & (number < 32)
        other = jnp.where(same | (number > 31), 0.0, -1e30).astype(bf16)
        key_tail = jnp.where(same | key_ones, 1.0, 0.0).astype(bf16)
        for h in range(heads):
            cols = slice(HD * h, HD * h + HD)
            qa_s[h, span, :] = jnp.concatenate([queries[:, cols], other], axis=1)
            ka_s[h, span, :] = jnp.concatenate([keys[:, cols], key_tail], axis=1)
            va_s[h, span, :] = jnp.concatenate([values[:, cols], value_tail], axis=1)
            turned = jnp.concatenate([values[:, cols], keys[:, cols]], axis=1).astype(f32).T.astype(bf16)
            vt_s[h, 0:64, span] = turned[0:64, :]
            vt_s[h, 64:80, span] = ones_row
            kt_s[h, :, span] = turned[64:128, :]
        for copy in copies_out(owner, part):
            copy.start()

    def work(k, carry):
        distant = k // (2 * parts)
        part = lax.rem(k // 2, parts)
        second = lax.rem(k, 2)

        @pl.when((distant == 0) & (second == 0))
        def _():
            here = rows_of(across, part)
            awaited(here, sy.at[part], ry.at[part], {"tp": across}).wait_recv()
            push(here, here, sf.at[part], rf.at[part], {"tp": side})

        @pl.when((distant == 1) & (second == 1))
        def _():
            awaited(rows_of(far, part), sf.at[part], rf.at[part], {"tp": side}).wait_recv()

        @pl.when(distant == 1)
        def _():
            norm(across + second * (far - across), part)

        first = me + distant * (across - me)
        compute(first + second * (side - me + distant * (far - across - side + me)), part)
        return carry

    lax.fori_loop(0, 4 * parts, work, 0)
    for g in (1, 2, 3):
        end_hops(g)

    def drain(k, carry):
        for copy in copies_out(k // parts, lax.rem(k, parts)):
            copy.wait()
        return carry

    lax.fori_loop(0, 4 * parts, drain, 0)
    for part in range(parts):
        awaited(rows_of(across, part), sf.at[part], rf.at[part], {"tp": side}).wait_send()
    for copy in sent:
        copy.wait_send()


def enter(x, vectors, segments, weights, size, number, parts=2):
    rows, width = x.shape
    seq_rows = 4 * rows
    shards = lax.axis_size("fsdp")
    heads = weights[0].shape[1] // (3 * HD)
    dma = pltpu.SemaphoreType.DMA
    wide = (heads, seq_rows, 128)
    shard_rows = weights[0].shape[0]
    full = [(shards, *weights[0].shape), (shards, shard_rows, sum(w.shape[1] for w in weights[1:]))]
    shapes = [(seq_rows, width), wide, wide, wide, (heads, 80, seq_rows), (heads, 64, seq_rows)]
    made = [jax.ShapeDtypeStruct(s, bf16) for s in shapes]
    return comm_call(
        functools.partial(enter_kernel, parts=parts, size=size),
        "enter",
        number,
        [made[0], jax.ShapeDtypeStruct((4, *segments.shape), segments.dtype)]
        + [jax.ShapeDtypeStruct((seq_rows // size, 128), jnp.int32), jax.ShapeDtypeStruct((16, width), f32)]
        + made[1:]
        + [jax.ShapeDtypeStruct(s, bf16) for s in full],
        [in_vmem()] * (6 + len(vectors)),
        [anywhere()] + [in_vmem()] * 3 + [anywhere()] * 5 + [in_vmem(), anywhere()],
        [pltpu.VMEM((seq_rows, width), bf16)]
        + [pltpu.VMEM(s, bf16) for s in shapes]
        + [dma((parts,))] * 6
        + [dma((3,))] * 2
        + [dma((4, shards))] * 2
        + [dma((2,)), dma((4,)), dma((6, 4 * parts))],
        60 << 20,
        x,
        segments,
        *weights,
        *vectors,
    )


def middle_kernel(
    seq_out, own_ref, passed_ref, x_ref, g_ref, seg_ref, par_ref,
    layer_ref, resid_ref, seq_ref, kept_ref, over_ref, sums_ref,
    attn_ref, fc_ref, pj_ref, ow_ref, attn_cat, ow_cat, act_s, gp_s, in_s, in_t, g_t, low_t, ga_s, out_acc, gn_acc,
    fc_g, pj_g, ow_g, fc_box, pj_box, ow_box,
    sems, rems, ws, wr, sa, ra, sv, rv, own_sem, *, parts
):
    me, side, across, far = quad()
    greet([{"tp": side}, {"tp": across}, {"tp": far}])
    peers = {1: side, 2: across, 3: far}
    rows = x_ref.shape[0]
    step = rows // parts
    lanes = ow_ref.shape[2]
    sums_ref[...] = jnp.zeros_like(sums_ref)

    def own_rows(who, part):
        return seq_out.at[pl.ds(pl.multiple_of(who * rows + part * step, step), step)]

    def send_rows(part, carry):
        here = pl.ds(pl.multiple_of(part * step, step), step)
        for k in (3, 2, 1):
            push(own_rows(peers[k], part), attn_ref.at[k, here], sa.at[k, part], ra.at[k, part], {"tp": peers[k]})
        return carry

    lax.fori_loop(0, parts, send_rows, 0)
    sent, kept, at = [], [], 0
    for n, full in enumerate((fc_ref, pj_ref, ow_ref)):
        cols = pl.ds(at, full.shape[2])
        at += full.shape[2]
        for k, source in ((0, own_ref), (2, passed_ref)):
            block = source.at[:, cols]
            sent.append(push(block, full.at[k + 1], sv.at[k // 2, n], rv.at[k // 2, n], {"tp": side}))
            kept.append(pltpu.make_async_copy(block, full.at[k], own_sem.at[2 * n + k // 2]))
    mine = seq_out.at[pl.ds(pl.multiple_of(me * rows, rows), rows)]
    kept.append(pltpu.make_async_copy(mine, attn_ref.at[0], own_sem.at[6]))
    for copy in kept:
        copy.start()
    for copy in kept:
        copy.wait()
    for copy in sent:
        copy.wait()
    for p in range(4):
        ow_cat[:, p * lanes : (p + 1) * lanes] = ow_ref[p]

    def owner(t):
        near = me + lax.rem(t, 2) * (1 - 2 * lax.rem(me, 2))
        return lax.rem(near + 2 * (t // 2), 4)

    def add_row(row, value):
        at = pl.ds(row, 1)
        sums_ref[at, :] = sums_ref[at, :] + jnp.sum(value, axis=0, keepdims=True)

    def landing(who, part):
        return seq_ref.at[pl.ds(pl.multiple_of(who * rows + part * step, step), step)]

    def row_block(part, carry):
        here = pl.ds(pl.multiple_of(part * step, step), step)
        for k in (1, 2, 3):
            awaited(attn_ref.at[k, here], sa.at[k, part], ra.at[k, part], {"tp": peers[k]}).wait_recv()
        attn = jnp.concatenate([attn_ref[p, here, :] for p in range(4)], axis=1)
        attn_cat[here, :] = attn
        hidden = x_ref[here, :].astype(f32) + dot_t(attn, ow_cat[...]) + par_ref[0:1, :]
        gain = par_ref[1:2, :]
        normed, hat, inverse = layer_norm(hidden, gain, par_ref[2:3, :])
        in_s[...] = normed.astype(bf16)
        in_t[:, here] = normed.T.astype(bf16)
        grad = g_ref[here, :]
        g_t[:, here] = grad.astype(f32).T.astype(bf16)
        out_acc[...] = hidden + par_ref[3:4, :]
        gn_acc[...] = jnp.zeros_like(gn_acc)

        def hidden_block(t, c):
            bias_at = 4 + owner(t)
            pre = dot_n(in_s[...], fc_ref[t]) + par_ref[pl.ds(bias_at, 1), :]
            gate = jax.nn.sigmoid(gelu_slope * pre)
            raised = pre * gate
            act = raised.astype(bf16)
            act_s[t, here, :] = act
            out_acc[...] += dot_t(act, pj_ref[t])
            grad_act = dot_n(g_ref[here, :], pj_ref[t])
            grad_pre = (grad_act * (gate + gelu_slope * raised * (1.0 - gate))).astype(bf16)
            gp_s[t, here, :] = grad_pre
            add_row(bias_at, grad_pre.astype(f32))
            gn_acc[...] += dot_t(grad_pre, fc_ref[t])
            return c

        lax.fori_loop(0, 4, hidden_block, 0)
        layer_ref[here, :] = out_acc[...].astype(bf16)
        grad_in, gain_part, shift_part = norm_back(gn_acc[...], hat, inverse, gain)
        grad_hidden = grad.astype(f32) + grad_in
        resid_ref[here, :] = grad_hidden
        low = grad_hidden.astype(bf16)
        low_t[:, here] = grad_hidden.T.astype(bf16)
        sums_ref[1:2, :] += gain_part[None]
        sums_ref[2:3, :] += shift_part[None]
        add_row(0, low.astype(f32))
        add_row(3, grad.astype(f32))
        seg = jnp.broadcast_to(seg_ref[0:1, here].astype(f32), (8, step)).T[:, 0:1]
        live = jnp.where(seg != 0.0, 1.0, 0.0)
        grad_attn = (dot_n(low, ow_cat[...]).astype(bf16).astype(f32) * live).astype(bf16)
        for k in (1, 2, 3):
            ga_s[k, here, :] = grad_attn[:, k * lanes : (k + 1) * lanes]
        seq_ref[pl.ds(pl.multiple_of(me * rows + part * step, step), step), :] = grad_attn[:, 0:lanes]
        for k in (3, 2, 1):
            push(ga_s.at[k, here], landing(me, part), sems.at[k, part], rems.at[k, part], {"tp": peers[k]})
        return carry

    lax.fori_loop(0, parts, row_block, 0)
    width = out_acc.shape[1]
    tall = 256

    def out_block(n, carry):
        at = pl.ds(pl.multiple_of(n * tall, tall), tall)
        grad = dot_n(low_t[at, :], attn_cat[...]).astype(bf16)
        for p in range(4):
            ow_g[p, at, :] = grad[:, p * lanes : (p + 1) * lanes]
        return carry

    lax.fori_loop(0, width // tall, out_block, 0)
    triples = ((fc_g, fc_box), (pj_g, pj_box), (ow_g, ow_box))

    def fold(n, b):
        grad, box = triples[n]
        return grad.at[2 * b + 1], box.at[b], ws.at[n, b], wr.at[n, b], {"tp": side}

    for b in (1, 0):
        push(*fold(2, b))

    def slice_block(u, carry):
        t = 3 - 2 * u + 3 * (u // 2)

        def fc_block(n, c):
            at = pl.ds(pl.multiple_of(n * tall, tall), tall)
            fc_g[t, at, :] = dot_n(in_t[at, :], gp_s[t]).astype(bf16)
            pj_g[t, at, :] = dot_n(g_t[at, :], act_s[t]).astype(bf16)
            return c

        lax.fori_loop(0, width // tall, fc_block, 0)
        for b in (1, 0):

            @pl.when(u == 1 - b)
            def _():
                push(*fold(0, b))
                push(*fold(1, b))

        return carry

    lax.fori_loop(0, 4, slice_block, 0)
    for b, target in ((1, over_ref), (0, kept_ref)):
        at = 0
        for n, (grad, box) in enumerate(triples):
            cols = slice(at, at + grad.shape[2])
            at += grad.shape[2]
            awaited(box.at[b], ws.at[n, b], wr.at[n, b], {"tp": side}).wait_recv()
            target[:, cols] = (grad[2 * b].astype(f32) + box[b].astype(f32)).astype(bf16)

    def drain(part, carry):
        here = pl.ds(pl.multiple_of(part * step, step), step)
        for k in (1, 2, 3):
            peer = {"tp": peers[k]}
            awaited(landing(peers[k], part), sems.at[k, part], rems.at[k, part], peer).wait_recv()
            awaited(ga_s.at[k, here], sems.at[k, part], rems.at[k, part], peer).wait_send()
            awaited(own_rows(peers[k], part), sa.at[k, part], ra.at[k, part], peer).wait_send()
        return carry

    lax.fori_loop(0, parts, drain, 0)
    for n, (grad, box) in enumerate(triples):
        for b in (1, 0):
            awaited(grad.at[2 * b + 1], ws.at[n, b], wr.at[n, b], {"tp": side}).wait_send()


def middle(attn, own, passed, x, grad, segments, params, hidden, number, parts=2):
    rows, lanes = x.shape[0], attn.shape[1]
    width = x.shape[1]
    fc = pj = (4, width, hidden)
    ow = (4, width, lanes)
    step = rows // parts
    dma = pltpu.SemaphoreType.DMA
    total = 2 * hidden + lanes
    low, wide = bf16, f32
    scratch = [
        ((4, rows, lanes), low), (fc, low), (pj, low), (ow, low),
        ((rows, width), low), ((width, 4 * lanes), low),
        ((4, rows, hidden), low), ((4, rows, hidden), low),
        ((step, width), low), ((width, rows), low), ((width, rows), low), ((width, rows), low),
        ((4, rows, lanes), low), ((step, width), wide), ((step, width), wide),
        (fc, low), (pj, low), (ow, low),
        ((2, *fc[1:]), low), ((2, *pj[1:]), low), ((2, *ow[1:]), low),
    ]
    outs = [
        ((rows, width), low), ((rows, width), wide), ((4 * rows, lanes), low),
        ((width, total), low), ((width, total), low), ((8, width), wide),
    ]
    return comm_call(
        functools.partial(middle_kernel, parts=parts),
        "middle",
        number,
        [jax.ShapeDtypeStruct(s, d) for s, d in outs],
        [in_vmem(), anywhere(), anywhere()] + [in_vmem()] * 4,
        [in_vmem()] * 6,
        [pltpu.VMEM(s, d) for s, d in scratch]
        + [dma((4, parts)), dma((4, parts)), dma((3, 2)), dma((3, 2))]
        + [dma((4, parts)), dma((4, parts)), dma((2, 3)), dma((2, 3)), dma((7,))],
        60 << 20,
        attn,
        own,
        passed,
        x,
        grad,
        segments,
        params,
    )


def leave_kernel(
    grad_ref, normed_in, w_ref, kept_ref, came_ref, early_ref, x_in, gain_ref, resid_in,
    input_ref, s0, s1, s2, s3, early_out, late_out,
    rows_ref, far_out, own_out, sum_buf, side_far, side_own, over, dw_acc, cols_ref,
    late_ref, early_mid, late_mid, early_one, early_two, late_one, late_two,
    normed_ref, x_ref, resid_ref, loads,
    sa, ra, sb, rb, sy, ry, sw, rw, se, re, sl, rl, se2, re2, sl2, rl2, *bufs, parts, hops
):
    me, side, across, far = quad()
    rows = rows_ref.shape[0]
    step = rows // parts
    shard, shards = lax.axis_index("fsdp"), early_two.shape[0]
    pairs = ((normed_in, normed_ref), (x_in, x_ref), (resid_in, resid_ref))
    loading = [pltpu.make_async_copy(a, b, loads.at[n]) for n, (a, b) in enumerate(pairs)]
    for copy in loading:
        copy.start()
    barrier = pltpu.get_barrier_semaphore()
    for peer in (side, across, far):
        pl.semaphore_signal(barrier, inc=1, device_id={"tp": peer}, device_id_type=MESH)

    def other(k):
        return {"fsdp": lax.rem(shard + k, shards)}

    def signal(k, carry):
        pl.semaphore_signal(barrier, inc=1, device_id=other(k), device_id_type=MESH)
        return carry

    lax.fori_loop(1, shards, signal, 0)
    pl.semaphore_wait(barrier, 3 + shards - 1)
    count = len(hops)
    outs = (s0, s1, s2, s3)
    current = bufs[0:4]
    boxes = [bufs[4 + g * count : 4 + (g + 1) * count] for g in range(4)]
    keeps = [bufs[4 + 4 * count + g * (count - 1) : 4 + 4 * count + (g + 1) * (count - 1)] for g in range(4)]
    sent = []

    def begin(g):
        at = sum(c.shape[3] for c in current[0:g])
        cols = slice(at, at + current[g].shape[3])
        total = kept_ref[:, :, :, cols].astype(f32) + came_ref[:, :, :, cols].astype(f32)
        current[g][...] = total.astype(bf16)

    def hop_parts(g, k):
        axis, bit = hops[k]
        source = current[g] if k == 0 else keeps[g][k - 1]
        half = lax.rem(lax.axis_index(axis) // bit, 2)
        return {axis: flip(axis, bit)}, source, half, boxes[g][k]

    def hop_send(g, k):
        peer, source, half, box = hop_parts(g, k)
        sent.append(push(source.at[:, 1 - half], box, sw.at[g, k], rw.at[g, k], peer))

    def hop_add(g, k):
        peer, source, half, box = hop_parts(g, k)
        awaited(box, sw.at[g, k], rw.at[g, k], peer).wait_recv()
        if k == count - 1:
            outs[g][...] = source[0, half].astype(f32) + box[0].astype(f32)
        else:
            target = keeps[g][k]
            for n in range(box.shape[0]):
                total = source[n, half].astype(f32) + box[n].astype(f32)
                target[n // 2, n % 2] = total.astype(bf16)
            hop_send(g, k + 1)

    def tp_send(value, box, send, recv):
        box[me] = value[...]
        for k, peer in enumerate((side, across, far)):
            sent.append(push(value, box.at[me], send.at[k], recv.at[me], {"tp": peer}))

    def tp_sum(value, box, send, recv):
        for k, peer in enumerate((side, across, far)):
            awaited(box.at[peer], send.at[k], recv.at[peer], {"tp": peer}).wait_recv()
        value[...] = box[0] + box[1] + box[2] + box[3]

    def fsdp_send(value, box, send, recv):
        box[shard] = value[...]

        def give(k, carry):
            push(value, box.at[shard], send.at[k], recv.at[shard], other(k))
            return carry

        lax.fori_loop(1, shards, give, 0)

    def fsdp_sum(value, target, box, send, recv):
        def take(k, carry):
            peer = lax.rem(shard + k, shards)
            copy = awaited(box.at[peer], send.at[k], recv.at[peer], other(k))
            copy.wait_recv()
            copy.wait_send()
            return carry

        lax.fori_loop(1, shards, take, 0)
        target[...] = lax.fori_loop(1, shards, lambda n, total: total + box[n], box[0])

    def span(owner, part):
        return pl.ds(pl.multiple_of(owner * rows + part * step, step), step)

    def piece(part):
        return pl.ds(pl.multiple_of(part * step, step), step)

    def partial(owner, part):
        return dot_t(grad_ref[span(owner, part), :], w_ref[...])

    def give_far(part, carry):
        here = piece(part)
        far_out[here, :] = partial(far, part).astype(bf16)
        push(far_out.at[here], side_far.at[here], sa.at[part], ra.at[part], {"tp": side})
        return carry

    def give_over(part, carry):
        here = piece(part)
        mine = partial(across, part)
        awaited(side_far.at[here], sa.at[part], ra.at[part], {"tp": side}).wait_recv()
        sum_buf[here, :] = (mine + side_far[here, :].astype(f32)).astype(bf16)
        push(sum_buf.at[here], over.at[here], sy.at[part], ry.at[part], {"tp": across})
        return carry

    def give_own(part, carry):
        here = piece(part)
        own_out[here, :] = partial(side, part).astype(bf16)
        push(own_out.at[here], side_own.at[here], sb.at[part], rb.at[part], {"tp": side})
        return carry

    def take_own(part, carry):
        here = piece(part)
        mine = partial(me, part)
        awaited(side_own.at[here], sb.at[part], rb.at[part], {"tp": side}).wait_recv()
        rows_ref[here, :] = mine + side_own[here, :].astype(f32)
        return carry

    gain = gain_ref[8:9, :]

    def take_over(part, carry):
        here = piece(part)
        x = x_ref[here, :].astype(f32)
        centred = x - jnp.mean(x, axis=-1, keepdims=True)
        inverse = lax.rsqrt(jnp.mean(centred * centred, axis=-1, keepdims=True) + epsilon)
        normed = centred * inverse
        awaited(over.at[here], sy.at[part], ry.at[part], {"tp": across}).wait_recv()
        grad = rows_ref[here, :] + over[here, :].astype(f32)
        grad_in, gain_part, shift_part = norm_back(grad, normed, inverse, gain)
        input_ref[here, :] = (resid_ref[here, :] + grad_in).astype(bf16)
        late_ref[0:1, :] += gain_part[None]
        late_ref[1:2, :] += shift_part[None]
        return carry

    def drain(part, carry):
        here = piece(part)
        awaited(far_out.at[here], sa.at[part], ra.at[part], {"tp": side}).wait_send()
        awaited(own_out.at[here], sb.at[part], rb.at[part], {"tp": side}).wait_send()
        awaited(sum_buf.at[here], sy.at[part], ry.at[part], {"tp": across}).wait_send()
        return carry

    chunk = 512
    steps = grad_ref.shape[0] // chunk
    dw_acc[...] = jnp.zeros_like(dw_acc)
    cols_ref[...] = jnp.zeros_like(cols_ref)
    ones = jnp.ones((8, chunk), bf16)

    def weight_grad(n, carry):
        at = pl.ds(pl.multiple_of(n * chunk, chunk), chunk)
        g = grad_ref[at, :]
        dw_acc[...] += lax.dot_general(
            normed_ref[at, :], g, (((0,), (0,)), ((), ())), preferred_element_type=f32
        )
        cols_ref[...] += dot_n(ones, g)
        return carry

    tp_send(early_ref, early_one, se, re)
    lax.fori_loop(0, parts, give_far, 0)
    for g in (0, 1):
        begin(g)
        hop_send(g, 0)
    lax.fori_loop(0, parts, give_over, 0)
    begin(2)
    for copy in loading:
        copy.wait()
    lax.fori_loop(0, steps // 2, weight_grad, 0)
    hop_add(0, 0)
    lax.fori_loop(steps // 2, steps, weight_grad, 0)
    current[3][...] = dw_acc[...].astype(bf16).reshape(current[3].shape)
    hop_send(3, 0)
    hop_send(2, 0)
    tp_sum(early_mid, early_one, se, re)
    fsdp_send(early_mid, early_two, se2, re2)
    hop_add(1, 0)
    late_ref[...] = jnp.zeros_like(late_ref)
    wide = cols_ref.shape[1] // 3
    qv_at = pl.ds(pl.multiple_of(me * wide, wide), wide)
    late_ref[2:3, qv_at] = cols_ref[0:1, 0:wide]
    late_ref[3:4, qv_at] = cols_ref[0:1, 2 * wide : 3 * wide]
    lax.fori_loop(0, parts, give_own, 0)
    turns = enumerate((0, 1, 3, 2))
    order = sorted((k + turn, turn, g, k) for turn, g in turns for k in range(count))
    order = [(g, k) for _, _, g, k in order if (g, k) not in ((0, 0), (1, 0))]
    lax.fori_loop(0, parts, take_own, 0)
    taken = {len(order) * share // 10: span for share, span in ((6, (0, 2)), (7, (2, 3)), (9, (3, 4)))}
    for n, (g, k) in enumerate(order):
        if n in taken:
            first, last = taken[n]
            lax.fori_loop(first * parts // 4, last * parts // 4, take_over, 0)
        if n == len(order) - 1:
            tp_send(late_ref, late_one, sl, rl)
        hop_add(g, k)
    fsdp_sum(early_mid, early_out, early_two, se2, re2)
    tp_sum(late_mid, late_one, sl, rl)
    fsdp_send(late_mid, late_two, sl2, rl2)
    lax.fori_loop(0, parts, drain, 0)
    fsdp_sum(late_mid, late_out, late_two, sl2, rl2)
    for copy in sent:
        copy.wait_send()


def leave(grad, normed, w, kept, came, widths, early, x, gain, resid, number, parts=2):
    rows, width = grad.shape[0] // 4, w.shape[0]
    dma = pltpu.SemaphoreType.DMA
    hops = bits_of("fsdp")
    count = len(hops)
    shards = lax.axis_size("fsdp")
    shard = width // shards
    widths = [*widths, grad.shape[1]]
    split = (shards // 2, 2, shard)
    current = [pltpu.VMEM((*split, n), bf16) for n in widths]
    boxes = [pltpu.VMEM((shards >> (k + 1), shard, n), bf16) for n in widths for k in range(count)]
    keeps = [pltpu.VMEM((shards >> (k + 2), 2, shard, n), bf16) for n in widths for k in range(count - 1)]
    late = (4, width)
    return comm_call(
        functools.partial(leave_kernel, parts=parts, hops=hops),
        "leave",
        number,
        [jax.ShapeDtypeStruct((rows, width), bf16)]
        + [jax.ShapeDtypeStruct((shard, n), f32) for n in widths]
        + [jax.ShapeDtypeStruct(early.shape, f32), jax.ShapeDtypeStruct(late, f32)],
        [in_vmem(), anywhere()] + [in_vmem()] * 4 + [anywhere(), in_vmem(), anywhere()],
        [in_vmem()] * 7,
        [pltpu.VMEM((rows, width), f32)]
        + [pltpu.VMEM((rows, width), bf16)] * 6
        + [pltpu.VMEM((width, grad.shape[1]), f32), pltpu.VMEM((8, grad.shape[1]), f32)]
        + [pltpu.VMEM(late, f32), pltpu.VMEM(early.shape, f32), pltpu.VMEM(late, f32)]
        + [pltpu.VMEM((n, *shape), f32) for shape in (early.shape, late) for n in (4, shards)]
        + [pltpu.VMEM(v.shape, v.dtype) for v in (normed, x, resid)]
        + [dma((3,))]
        + [dma((parts,))] * 6
        + [dma((4, count))] * 2
        + [dma((3,)), dma((4,))] * 2
        + [dma((shards,))] * 4
        + current
        + boxes
        + keeps,
        60 << 20,
        grad,
        normed,
        w,
        kept.reshape(*split, kept.shape[1]),
        came.reshape(*split, came.shape[1]),
        early,
        x,
        gain,
        resid,
    )


def finish_kernel(
    rows_in, fc_in, proj_in, out_in, qkv_in, early_in, late_in,
    rows_ref, fc_ref, proj_ref, out_ref, qkv_ref, qv_ref, *vectors
):
    rows_ref[...] = rows_in[...]
    fc_ref[...] = fc_in[...]
    proj_ref[...] = proj_in[...]
    out_ref[...] = out_in[...]
    width = qkv_ref.shape[2]
    for n in range(3):
        qkv_ref[n] = qkv_in[:, n * width : (n + 1) * width]
    qv_ref[...] = late_in[2:4, :]
    first_gain, first_shift, out_bias, gain, shift, fc_bias, proj_bias = vectors
    lanes = first_gain.shape[1]
    count = first_gain.shape[0]
    singles = ((first_gain, late_in, 0), (first_shift, late_in, 1), (out_bias, early_in, 0))
    singles += ((gain, early_in, 1), (shift, early_in, 2), (proj_bias, early_in, 3))
    for ref, source, row in singles:
        for n in range(count):
            ref[n : n + 1, :] = source[row : row + 1, n * lanes : (n + 1) * lanes]
    for row in range(4):
        for n in range(count):
            at = row * count + n
            fc_bias[at : at + 1, :] = early_in[4 + row : 5 + row, n * lanes : (n + 1) * lanes]


def finish(rows, fc, proj, out, qkv, early, late):
    lanes = 128
    width = late.shape[1]
    shapes = [rows, fc, proj, out]
    outs = [jax.ShapeDtypeStruct(v.shape, v.dtype) for v in shapes]
    outs.append(jax.ShapeDtypeStruct((3, qkv.shape[0], qkv.shape[1] // 3), f32))
    outs.append(jax.ShapeDtypeStruct((2, width), f32))
    sizes = [width] * 5 + [4 * early.shape[1], width]
    outs += [jax.ShapeDtypeStruct((n // lanes, lanes), f32) for n in sizes]
    rows, fc, proj, out, qkv, qv, *vectors = pl.pallas_call(
        finish_kernel,
        out_shape=outs,
        in_specs=[in_vmem()] * 7,
        out_specs=[in_vmem()] * len(outs),
        cost_estimate=pl.CostEstimate(flops=0, bytes_accessed=3 << 20, transcendentals=0),
        name="finish",
    )(rows, fc, proj, out, qkv, early, late)
    return rows, fc, proj.T, out.T, qkv.transpose(1, 0, 2), qv, [v.reshape(-1) for v in vectors]


def flip(axis, bit):
    me = lax.axis_index(axis)
    return me + bit - 2 * bit * lax.rem(me // bit, 2)


def bits_of(axis):
    size, bits, bit = lax.axis_size(axis), [], 1
    while bit < size:
        bits.append((axis, bit))
        bit *= 2
    return bits


def across(value):
    return lax.ppermute(value, "tp", [(n, n ^ 2) for n in range(4)])


def local(
    inputs,
    segments,
    out_grad,
    first_gain,
    first_shift,
    qkv_weight,
    qv_bias,
    out_weight,
    out_bias,
    second_gain,
    second_shift,
    fc_weight,
    fc_bias,
    proj_weight,
    proj_bias,
):
    slices = lax.axis_size("tp")
    rows_here, model_width = inputs.shape
    shard_rows = qkv_weight.shape[0]
    head_cols = qkv_weight.shape[2]
    hidden_cols = fc_weight.shape[1]
    vectors = (out_bias, second_gain, second_shift, proj_bias, fc_bias, first_gain, first_shift, qv_bias)
    size = min(BLOCK, rows_here)
    seq_normed, seg_parts, low, params, qa, ka, va, vt, kt, qkv_full, own = enter(
        inputs,
        vectors,
        segments,
        (qkv_weight.reshape(shard_rows, 3 * head_cols), fc_weight, proj_weight.T, out_weight.T),
        size,
        0,
    )
    qkv_full = qkv_full.reshape(model_width, 3 * head_cols)
    own = own.reshape(model_width, own.shape[2])
    over = across(own)
    widths = (hidden_cols, hidden_cols, head_cols)

    attn_out, qb = attend(low, qa, ka, vt, seg_parts, size)

    layer_out, grad_hidden, grad_attn_seq, kept, passed, early = middle(
        attn_out, own, over, inputs, out_grad, segments, params, hidden_cols, 2
    )
    came = across(passed)
    grad_qkv = attend_back(low, qb, ka, va, kt, grad_attn_seq, attn_out, seg_parts, size)
    input_grad, fc_w_grad, proj_w_grad, out_w_grad, qkv_grad, early_sums, late_sums = leave(
        grad_qkv,
        seq_normed,
        qkv_full,
        kept,
        came,
        widths,
        early,
        inputs,
        params,
        grad_hidden,
        3,
    )
    input_grad, fc_w_grad, proj_w_grad, out_w_grad, qkv_grad, qv_bias_grad, vectors = finish(
        input_grad,
        fc_w_grad,
        proj_w_grad,
        out_w_grad,
        qkv_grad,
        early_sums,
        late_sums,
    )
    first_gain_grad, first_shift_grad, out_bias_grad, second_gain_grad, second_shift_grad = vectors[0:5]
    fc_bias_grad, proj_bias_grad = vectors[5:7]

    return (
        layer_out,
        input_grad,
        first_gain_grad,
        first_shift_grad,
        qkv_grad,
        qv_bias_grad,
        out_w_grad,
        out_bias_grad,
        second_gain_grad,
        second_shift_grad,
        fc_w_grad,
        fc_bias_grad,
        proj_w_grad,
        proj_bias_grad,
    )


def solution(mesh):
    return jax.shard_map(
        local,
        mesh=mesh,
        in_specs=(
            P(("fsdp", "tp"), None),
            P("fsdp", "tp"),
            P(("fsdp", "tp"), None),
            P(),
            P(),
            P("fsdp", None, "tp"),
            P(),
            P("tp", "fsdp"),
            P(),
            P(),
            P(),
            P("fsdp", "tp"),
            P(),
            P("tp", "fsdp"),
            P(),
        ),
        out_specs=(
            P(("fsdp", "tp"), None),
            P(("fsdp", "tp"), None),
            P(),
            P(),
            P("fsdp", None, "tp"),
            P(),
            P("tp", "fsdp"),
            P(),
            P(),
            P(),
            P("fsdp", "tp"),
            P(),
            P("tp", "fsdp"),
            P(),
        ),
        check_vma=False,
    )
```

```python
import functools

import jax
import jax.numpy as jnp
from jax import lax
from jax.experimental import pallas as pl
from jax.experimental.pallas import tpu as pltpu
from jax.sharding import PartitionSpec as P

HD = 64
VMEM_LIMIT = 60 << 20
epsilon = 1e-05
gelu_slope = 1.702


def layer_norm(values_in, gain_vec, shift_vec):
    mean_row = jnp.mean(values_in, axis=-1, keepdims=True)
    centred = values_in - mean_row
    inverse = lax.rsqrt(jnp.mean(centred * centred, axis=-1, keepdims=True) + epsilon)
    normed = centred * inverse
    return (normed * gain_vec + shift_vec, normed, inverse)


def norm_back(grad_out, normed, inverse, gain_vec):
    scaled = grad_out * gain_vec
    grad_in = inverse * (
        scaled
        - jnp.mean(scaled, axis=-1, keepdims=True)
        - normed * jnp.mean(scaled * normed, axis=-1, keepdims=True)
    )
    return (grad_in, jnp.sum(grad_out * normed, axis=0), jnp.sum(grad_out, axis=0))


f32 = jnp.float32
bf16 = jnp.bfloat16
LOG2E = 1.4426950408889634
BLOCK = 512
TRANSPOSED = (((1,), (1,)), ((), ()))


def dot_t(left, right):
    return lax.dot_general(left, right, TRANSPOSED, preferred_element_type=f32)


def dot_n(left, right):
    return jnp.dot(left, right, preferred_element_type=f32)


def three_parts(value):
    top = value.astype(bf16)
    rest = value - top.astype(f32)
    mid = rest.astype(bf16)
    return top, mid, (rest - mid.astype(f32)).astype(bf16)


def diagonal_mask(seg_ref, row_at, size):
    key_pos = lax.broadcasted_iota(jnp.int32, (size, 1), 0)
    query_pos = lax.broadcasted_iota(jnp.int32, (1, size), 1)
    here = seg_ref.shape[2]
    seg = seg_ref[row_at // here, 0:1, pl.ds(pl.multiple_of(lax.rem(row_at, here), size), size)]
    first = jnp.where(seg == 0, query_pos, 0)
    return (key_pos >= first) & (key_pos <= query_pos)


def attend_kernel(
    low_ref, qa_ref, ka_ref, vt_ref, start_ref, out_ref, qb_ref, s0, s1, a0, a1, *, size, blocks
):
    score_bufs, acc_bufs = (s0, s1), (a0, a1)
    heads = range(qa_ref.shape[0])
    lane = lax.broadcasted_iota(jnp.int32, (size, 128), 1)

    def query_block(i, carry):
        row_at = pl.multiple_of(i * size, size)

        def score(h, j, top, diag):
            keys = ka_ref[h, pl.ds(pl.multiple_of(j * size, size), size), :]
            s = dot_t(keys, qa_ref[h, pl.ds(row_at, size), :])
            if diag:
                s = jnp.where(diagonal_mask(start_ref, row_at, size), s, -3e38)
            score_bufs[h][...] = s
            col_max = jnp.max(s, axis=0, keepdims=True)
            return col_max if top is None else jnp.maximum(top, col_max)

        def gather_values(h, j, old, new, first):
            p = jnp.exp2(score_bufs[h][...] * LOG2E - new * LOG2E).astype(bf16)
            part = dot_n(vt_ref[h, :, pl.ds(pl.multiple_of(j * size, size), size)], p)
            if first:
                acc_bufs[h][...] = part
            else:
                acc_bufs[h][...] = acc_bufs[h][...] * jnp.exp2((old - new) * LOG2E) + part

        low = low_ref[i, 0]
        m0 = score(0, i, None, True)
        m1 = score(1, i, None, True)
        gather_values(0, i, None, m0, True)
        m0n = score(0, jnp.minimum(low, i), m0, False)
        gather_values(1, i, None, m1, True)

        def body(j, c):
            m0, m0n, m1 = c
            m1n = score(1, j, m1, False)
            gather_values(0, j, m0, m0n, False)
            m0nn = score(0, jnp.minimum(j + 1, blocks - 1), m0n, False)
            gather_values(1, j, m1, m1n, False)
            return m0n, m0nn, m1n

        m0, _, m1 = lax.fori_loop(low, i, body, (m0, m0n, m1))
        for h, top in ((0, m0), (1, m1)):
            total = acc_bufs[h][64:65, :]
            out = acc_bufs[h][0:64, :] / total
            rows = qa_ref[h, pl.ds(row_at, size), :]
            live = jnp.where(rows[:, 64:65].astype(f32) != 0.0, 1.0, 0.0)
            out_ref[pl.ds(row_at, size), 64 * h : 64 * h + 64] = (out.T * live).astype(out_ref.dtype)
            norm = jnp.broadcast_to(-(top + jnp.log(total)), (8, size)).T[:, 0:1]
            n0, n1, n2 = three_parts(norm)
            rows = jnp.where(lane == 96, n0, jnp.where(lane == 97, n1, jnp.where(lane == 98, n2, rows)))
            qb_ref[h, pl.ds(row_at, size), :] = rows
        return carry

    lax.fori_loop(0, blocks, query_block, 0)


def attend(low, qa, ka, vt, start, size):
    heads, rows, _ = qa.shape
    vmem = pl.BlockSpec(memory_space=pltpu.VMEM)
    return pl.pallas_call(
        functools.partial(attend_kernel, size=size, blocks=rows // size),
        grid_spec=pltpu.PrefetchScalarGridSpec(
            num_scalar_prefetch=0,
            grid=(),
            in_specs=[pl.BlockSpec(memory_space=pltpu.SMEM)] + [vmem] * 4,
            out_specs=[vmem] * 2,
            scratch_shapes=[pltpu.VMEM((size, size), f32)] * heads
            + [pltpu.VMEM((vt.shape[1], size), f32)] * heads,
        ),
        out_shape=[
            jax.ShapeDtypeStruct((rows, HD * heads), bf16),
            jax.ShapeDtypeStruct(qa.shape, bf16),
        ],
        compiler_params=pltpu.CompilerParams(vmem_limit_bytes=VMEM_LIMIT),
        cost_estimate=pl.CostEstimate(
            flops=14 * rows * rows * HD * heads, bytes_accessed=8 << 20, transcendentals=rows * rows
        ),
        name="attend",
    )(low, qa, ka, vt, start)


def attend_back_kernel(
    low_ref, qb_ref, ka_ref, va_ref, kt_ref, g_ref, o_ref, start_ref, grad_ref,
    ga_ref, dk_ref, dv_ref, q0, q1, *, size, blocks
):
    query_accs = (q0, q1)
    lane = lax.broadcasted_iota(jnp.int32, (size, 64), 1)

    def query_block(i, carry):
        row_at = pl.multiple_of(i * size, size)
        g_rows = g_ref[pl.ds(row_at, size), :]
        product = g_rows.astype(f32) * o_ref[pl.ds(row_at, size), :].astype(f32)
        for h in range(2):
            cols = slice(64 * h, 64 * h + 64)
            n0, n1, n2 = three_parts(-jnp.sum(product[:, cols], axis=1, keepdims=True))
            zero = jnp.zeros((size, 64), bf16)
            extra = jnp.where(lane == 0, n0, jnp.where(lane == 1, n1, jnp.where(lane == 2, n2, zero)))
            ga_ref[h] = jnp.concatenate([g_rows[:, cols], extra], axis=1)

        def block(h, j, diag):
            key_at = pl.multiple_of(j * size, size)
            keys = ka_ref[h, pl.ds(key_at, size), :]
            q_rows = qb_ref[h, pl.ds(row_at, size), :]
            g_head = ga_ref[h]
            s = dot_t(keys, q_rows)
            if diag:
                s = jnp.where(diagonal_mask(start_ref, row_at, size), s, -3e38)
            p = jnp.exp2(s * LOG2E)
            dp = dot_t(va_ref[h, pl.ds(key_at, size), :], g_head)
            ds = (p * dp).astype(bf16)
            dv = dot_n(p.astype(bf16), g_head[:, 0:64])
            dk = dot_n(ds, q_rows[:, 0:64])
            dq = dot_n(kt_ref[h, :, pl.ds(key_at, size)], ds)
            if diag:
                dv_ref[h, pl.ds(key_at, size), :] = dv
                dk_ref[h, pl.ds(key_at, size), :] = dk
                query_accs[h][...] = dq
            else:
                dv_ref[h, pl.ds(key_at, size), :] += dv
                dk_ref[h, pl.ds(key_at, size), :] += dk
                query_accs[h][...] += dq

        block(0, i, True)
        block(1, i, True)

        def body(j, c):
            block(0, j, False)
            block(1, j, False)
            return c

        lax.fori_loop(low_ref[i, 0], i, body, 0)
        both = jnp.concatenate([query_accs[0][...], query_accs[1][...]], axis=0) * HD ** (-0.5)
        grad_ref[pl.ds(row_at, size), 0:128] = both.T.astype(bf16)
        return carry

    lax.fori_loop(0, blocks, query_block, 0)

    def finish(i, carry):
        row_at = pl.multiple_of(i * size, size)
        for ref, at in ((dk_ref, 128), (dv_ref, 256)):
            both = jnp.concatenate([ref[0, pl.ds(row_at, size), :], ref[1, pl.ds(row_at, size), :]], axis=1)
            grad_ref[pl.ds(row_at, size), at : at + 128] = both.astype(bf16)
        return carry

    lax.fori_loop(0, blocks, finish, 0)


def attend_back(low, qb, ka, va, kt, g, o, start, size):
    heads, rows, _ = qb.shape
    vmem = pl.BlockSpec(memory_space=pltpu.VMEM)
    return pl.pallas_call(
        functools.partial(attend_back_kernel, size=size, blocks=rows // size),
        grid_spec=pltpu.PrefetchScalarGridSpec(
            num_scalar_prefetch=0,
            grid=(),
            in_specs=[pl.BlockSpec(memory_space=pltpu.SMEM)] + [vmem] * 7,
            out_specs=vmem,
            scratch_shapes=[
                pltpu.VMEM((heads, size, 128), bf16),
                pltpu.VMEM((heads, rows, HD), f32),
                pltpu.VMEM((heads, rows, HD), f32),
            ]
            + [pltpu.VMEM((HD, size), f32)] * heads,
        ),
        out_shape=jax.ShapeDtypeStruct((rows, 3 * HD * heads), bf16),
        compiler_params=pltpu.CompilerParams(vmem_limit_bytes=VMEM_LIMIT),
        cost_estimate=pl.CostEstimate(
            flops=24 * rows * rows * HD * heads, bytes_accessed=16 << 20, transcendentals=rows * rows
        ),
        name="attend_back",
    )(low, qb, ka, va, kt, g, o, start)


MESH = pl.DeviceIdType.MESH


def greet(peers):
    barrier = pltpu.get_barrier_semaphore()
    for peer in peers:
        pl.semaphore_signal(barrier, inc=1, device_id=peer, device_id_type=MESH)
    pl.semaphore_wait(barrier, len(peers))


def push(source, target, send_sem, recv_sem, peer):
    copy = pltpu.make_async_remote_copy(
        src_ref=source,
        dst_ref=target,
        send_sem=send_sem,
        recv_sem=recv_sem,
        device_id=peer,
        device_id_type=MESH,
    )
    copy.start()
    return copy


def quad():
    me = lax.axis_index("tp")
    side = me + 1 - 2 * lax.rem(me, 2)
    across = lax.rem(me + 2, 4)
    far = lax.rem(side + 2, 4)
    return me, side, across, far


def comm_call(kernel, name, number, out_shape, in_specs, out_specs, scratch, moved, *operands):
    return pl.pallas_call(
        kernel,
        out_shape=out_shape,
        in_specs=in_specs,
        out_specs=out_specs,
        scratch_shapes=scratch,
        compiler_params=pltpu.CompilerParams(
            collective_id=number, has_side_effects=True, vmem_limit_bytes=VMEM_LIMIT
        ),
        cost_estimate=pl.CostEstimate(flops=0, bytes_accessed=moved, transcendentals=0),
        name=name,
    )(*operands)


def in_vmem():
    return pl.BlockSpec(memory_space=pltpu.VMEM)


def anywhere():
    return pl.BlockSpec(memory_space=pl.ANY)


def flipped(axis, mask):
    me, index, bit = lax.axis_index(axis), lax.axis_index(axis), 1
    while bit <= mask:
        if mask & bit:
            index = index + bit - 2 * bit * lax.rem(me // bit, 2)
        bit *= 2
    return index


def awaited(ref, send_sem, recv_sem, peer):
    return pltpu.make_async_remote_copy(ref, ref, send_sem, recv_sem, peer, MESH)


def hop_masks(size):
    hops, bit = [], size // 2
    while bit >= 1:
        hops.append((bit, [high + bit for high in range(0, size, 2 * bit)]))
        bit //= 2
    return hops


def enter_kernel(
    x_ref, seg_ref, w0, w1, w2, w3, v0, v1, v2, v3, v4, v5, v6, v7,
    normed_ref, segs_ref, low_ref, par_ref, qa_ref, ka_ref, va_ref, vt_ref, kt_ref, f0, f1,
    x_all, normed_s, qa_s, ka_s, va_s, vt_s, kt_s,
    sy, ry, ss, rs, sf, rf, sg, rg, sw, rw, own, own_w, outs, *, parts, size
):
    me, side, across, far = quad()
    rows = x_ref.shape[0]
    step = rows // parts
    shards = f0.shape[0]
    heads = qa_ref.shape[0]
    width = HD * heads
    shard = lax.axis_index("fsdp")
    hops = hop_masks(shards)
    greet(
        [{"tp": side}, {"tp": across}, {"tp": far}]
        + [{"fsdp": flipped("fsdp", bit)} for bit, _ in hops]
    )
    sent = []

    def rows_of(owner, part):
        return x_all.at[pl.ds(pl.multiple_of(owner * rows + part * step, step), step)]

    sources = (w0, w1, w2, w3)

    def block_of(g, index):
        if g == 0:
            return f0.at[index]
        at = sum(w.shape[1] for w in sources[1:g])
        return f1.at[index, :, pl.ds(at, sources[g].shape[1])]

    def send_hop(g, hop):
        bit, masks = hops[hop]
        peer = {"fsdp": flipped("fsdp", bit)}
        if hop > 0:
            before, arrived = hops[hop - 1]
            for mask in arrived:
                block = block_of(g, flipped("fsdp", mask))
                awaited(block, sw.at[g, mask], rw.at[g, mask], {"fsdp": flipped("fsdp", before)}).wait_recv()
        for mask in masks:
            target = block_of(g, flipped("fsdp", mask - bit))
            block = sources[g] if mask == bit else target
            sent.append(push(block, target, sw.at[g, mask], rw.at[g, mask], peer))

    def end_hops(g):
        bit, arrived = hops[-1]
        for mask in arrived:
            block = block_of(g, flipped("fsdp", mask))
            awaited(block, sw.at[g, mask], rw.at[g, mask], {"fsdp": flipped("fsdp", bit)}).wait_recv()

    for k, peer in enumerate((across, far, side)):
        sent.append(push(seg_ref, segs_ref.at[me], sg.at[k], rg.at[k], {"tp": peer}))
    send_hop(0, 0)
    for part in range(parts):
        mine = x_ref.at[pl.ds(part * step, step)]
        sent.append(push(mine, rows_of(me, part), sy.at[part], ry.at[part], {"tp": across}))
    send_hop(0, 1)
    for g in (1, 2, 3):
        send_hop(g, 0)
    for part in range(parts):
        mine = x_ref.at[pl.ds(part * step, step)]
        sent.append(push(mine, rows_of(me, part), ss.at[part], rs.at[part], {"tp": side}))
    kept = [
        pltpu.make_async_copy(x_ref, x_all.at[pl.ds(pl.multiple_of(me * rows, rows), rows)], own.at[0]),
        pltpu.make_async_copy(seg_ref, segs_ref.at[me], own.at[1]),
    ] + [pltpu.make_async_copy(source, block_of(g, shard), own_w.at[g]) for g, source in enumerate(sources)]
    for copy in kept:
        copy.start()
    waves = sorted(
        ((hop + g, g, hop) for hop in range(1, len(hops)) for g in range(4)), key=lambda w: (w[0], w[1])
    )
    for _, g, hop in waves[1:2]:
        send_hop(g, hop)
    for k, peer in enumerate((across, far, side)):
        awaited(segs_ref.at[peer], sg.at[k], rg.at[k], {"tp": peer}).wait_recv()
    for part in range(parts):
        awaited(rows_of(side, part), ss.at[part], rs.at[part], {"tp": side}).wait_recv()
    for copy in kept:
        copy.wait()

    line, columns = 0, par_ref.shape[1]
    par_ref[...] = jnp.zeros_like(par_ref)
    for ref in (v0, v1, v2, v3, v4, v5, v6):
        value = ref[...].astype(f32).reshape(1, ref.shape[0])
        for n in range(ref.shape[0] // columns):
            par_ref[line : line + 1, :] = value[:, n * columns : (n + 1) * columns]
            line += 1
    par_ref[line : line + 2, :] = v7[...].astype(f32)
    gain, shift = par_ref[8:9, :], par_ref[9:10, :]

    def norm(owner, part):
        span = pl.ds(pl.multiple_of(owner * rows + part * step, step), step)
        x = x_all[span, :].astype(f32)
        centred = x - jnp.mean(x, axis=-1, keepdims=True)
        inverse = lax.rsqrt(jnp.mean(centred * centred, axis=-1, keepdims=True) + epsilon)
        normed_s[span, :] = (centred * inverse * gain + shift).astype(bf16)

    def norm_near(k, carry):
        norm(me + lax.rem(k, 2) * (side - me), k // 2)
        return carry

    lax.fori_loop(0, 2 * parts, norm_near, 0)
    whole = [segs_ref[n, 0:1, :] for n in range(4)]
    for n in range(4 * rows // size):
        at = n * size
        first = whole[at // rows][:, at % rows : at % rows + 1]
        before = sum(
            jnp.sum(jnp.where((seg > 0) & (seg < first), 1.0, 0.0), axis=1, keepdims=True) for seg in whole
        )
        block = jnp.where(first == 0, n * size, before.astype(jnp.int32)) // size
        low_ref[n : n + 1, :] = jnp.broadcast_to(block, (1, low_ref.shape[1]))
    for _, g, hop in waves[2:]:
        send_hop(g, hop)
    end_hops(0)
    bias_at = pl.ds(pl.multiple_of(me * width, width), width)
    query_bias = par_ref[10:11, bias_at]
    value_bias = par_ref[11:12, bias_at]
    number = lax.broadcasted_iota(jnp.int32, (step, 64), 1)
    number_f = number.astype(f32)
    key_ones = (number >= 32) & (number < 35)
    value_tail = jnp.where(number < 3, 1.0, 0.0).astype(bf16)
    ones_row = jnp.where(lax.broadcasted_iota(jnp.int32, (16, step), 0) == 0, 1.0, 0.0).astype(bf16)

    def copies_out(owner, part):
        row = pl.multiple_of(owner * rows + part * step, step)
        slot = owner * parts + part
        span = pl.ds(row, step)
        pairs = [(normed_s.at[span], normed_ref.at[span])]
        for a, b in ((qa_s, qa_ref), (ka_s, ka_ref), (va_s, va_ref)):
            pairs.append((a.at[:, span, :], b.at[:, span, :]))
        for a, b in ((vt_s, vt_ref), (kt_s, kt_ref)):
            pairs.append((a.at[:, :, span], b.at[:, :, span]))
        return [pltpu.make_async_copy(a, b, outs.at[n, slot]) for n, (a, b) in enumerate(pairs)]

    def compute(owner, part):
        row = pl.multiple_of(owner * rows + part * step, step)
        span = pl.ds(row, step)
        normed = normed_s[span, :]
        weights = f0[...].reshape(shards * f0.shape[1], 3 * width)
        projected = dot_n(normed, weights)
        queries = ((projected[:, 0:width] + query_bias).astype(bf16).astype(f32) * HD ** (-0.5)).astype(bf16)
        keys = projected[:, width : 2 * width].astype(bf16)
        values = (projected[:, 2 * width : 3 * width] + value_bias).astype(bf16)
        seg = segs_ref[owner, 0:1, pl.ds(pl.multiple_of(part * step, step), step)].astype(f32)
        seg = jnp.broadcast_to(seg, (8, step)).T[:, 0:1]
        same = (seg == number_f) & (number < 32)
        other = jnp.where(same | (number > 31), 0.0, -1e30).astype(bf16)
        key_tail = jnp.where(same | key_ones, 1.0, 0.0).astype(bf16)
        for h in range(heads):
            cols = slice(HD * h, HD * h + HD)
            qa_s[h, span, :] = jnp.concatenate([queries[:, cols], other], axis=1)
            ka_s[h, span, :] = jnp.concatenate([keys[:, cols], key_tail], axis=1)
            va_s[h, span, :] = jnp.concatenate([values[:, cols], value_tail], axis=1)
            turned = jnp.concatenate([values[:, cols], keys[:, cols]], axis=1).astype(f32).T.astype(bf16)
            vt_s[h, 0:64, span] = turned[0:64, :]
            vt_s[h, 64:80, span] = ones_row
            kt_s[h, :, span] = turned[64:128, :]
        for copy in copies_out(owner, part):
            copy.start()

    def work(k, carry):
        distant = k // (2 * parts)
        part = lax.rem(k // 2, parts)
        second = lax.rem(k, 2)

        @pl.when((distant == 0) & (second == 0))
        def _():
            here = rows_of(across, part)
            awaited(here, sy.at[part], ry.at[part], {"tp": across}).wait_recv()
            push(here, here, sf.at[part], rf.at[part], {"tp": side})

        @pl.when((distant == 1) & (second == 1))
        def _():
            awaited(rows_of(far, part), sf.at[part], rf.at[part], {"tp": side}).wait_recv()

        @pl.when(distant == 1)
        def _():
            norm(across + second * (far - across), part)

        first = me + distant * (across - me)
        compute(first + second * (side - me + distant * (far - across - side + me)), part)
        return carry

    lax.fori_loop(0, 4 * parts, work, 0)
    for g in (1, 2, 3):
        end_hops(g)

    def drain(k, carry):
        for copy in copies_out(k // parts, lax.rem(k, parts)):
            copy.wait()
        return carry

    lax.fori_loop(0, 4 * parts, drain, 0)
    for part in range(parts):
        awaited(rows_of(across, part), sf.at[part], rf.at[part], {"tp": side}).wait_send()
    for copy in sent:
        copy.wait_send()


def enter(x, vectors, segments, weights, size, number, parts=2):
    rows, width = x.shape
    seq_rows = 4 * rows
    shards = lax.axis_size("fsdp")
    heads = weights[0].shape[1] // (3 * HD)
    dma = pltpu.SemaphoreType.DMA
    wide = (heads, seq_rows, 128)
    shard_rows = weights[0].shape[0]
    full = [(shards, *weights[0].shape), (shards, shard_rows, sum(w.shape[1] for w in weights[1:]))]
    shapes = [(seq_rows, width), wide, wide, wide, (heads, 80, seq_rows), (heads, 64, seq_rows)]
    made = [jax.ShapeDtypeStruct(s, bf16) for s in shapes]
    return comm_call(
        functools.partial(enter_kernel, parts=parts, size=size),
        "enter",
        number,
        [made[0], jax.ShapeDtypeStruct((4, *segments.shape), segments.dtype)]
        + [jax.ShapeDtypeStruct((seq_rows // size, 128), jnp.int32), jax.ShapeDtypeStruct((16, width), f32)]
        + made[1:]
        + [jax.ShapeDtypeStruct(s, bf16) for s in full],
        [in_vmem()] * (6 + len(vectors)),
        [anywhere()] + [in_vmem()] * 3 + [anywhere()] * 5 + [in_vmem(), anywhere()],
        [pltpu.VMEM((seq_rows, width), bf16)]
        + [pltpu.VMEM(s, bf16) for s in shapes]
        + [dma((parts,))] * 6
        + [dma((3,))] * 2
        + [dma((4, shards))] * 2
        + [dma((2,)), dma((4,)), dma((6, 4 * parts))],
        60 << 20,
        x,
        segments,
        *weights,
        *vectors,
    )


def middle_kernel(
    seq_out, own_ref, passed_ref, x_ref, g_ref, seg_ref, par_ref,
    layer_ref, resid_ref, seq_ref, kept_ref, over_ref, sums_ref,
    attn_ref, fc_ref, pj_ref, ow_ref, attn_cat, ow_cat, act_s, gp_s, in_s, in_t, g_t, low_t, ga_s, out_acc, gn_acc,
    fc_g, pj_g, ow_g, fc_box, pj_box, ow_box,
    sems, rems, ws, wr, sa, ra, sv, rv, own_sem, *, parts
):
    me, side, across, far = quad()
    greet([{"tp": side}, {"tp": across}, {"tp": far}])
    peers = {1: side, 2: across, 3: far}
    rows = x_ref.shape[0]
    step = rows // parts
    lanes = ow_ref.shape[2]
    sums_ref[...] = jnp.zeros_like(sums_ref)

    def own_rows(who, part):
        return seq_out.at[pl.ds(pl.multiple_of(who * rows + part * step, step), step)]

    def send_rows(part, carry):
        here = pl.ds(pl.multiple_of(part * step, step), step)
        for k in (3, 2, 1):
            push(own_rows(peers[k], part), attn_ref.at[k, here], sa.at[k, part], ra.at[k, part], {"tp": peers[k]})
        return carry

    lax.fori_loop(0, parts, send_rows, 0)
    sent, kept, at = [], [], 0
    for n, full in enumerate((fc_ref, pj_ref, ow_ref)):
        cols = pl.ds(at, full.shape[2])
        at += full.shape[2]
        for k, source in ((0, own_ref), (2, passed_ref)):
            block = source.at[:, cols]
            sent.append(push(block, full.at[k + 1], sv.at[k // 2, n], rv.at[k // 2, n], {"tp": side}))
            kept.append(pltpu.make_async_copy(block, full.at[k], own_sem.at[2 * n + k // 2]))
    mine = seq_out.at[pl.ds(pl.multiple_of(me * rows, rows), rows)]
    kept.append(pltpu.make_async_copy(mine, attn_ref.at[0], own_sem.at[6]))
    for copy in kept:
        copy.start()
    for copy in kept:
        copy.wait()
    for copy in sent:
        copy.wait()
    for p in range(4):
        ow_cat[:, p * lanes : (p + 1) * lanes] = ow_ref[p]

    def owner(t):
        near = me + lax.rem(t, 2) * (1 - 2 * lax.rem(me, 2))
        return lax.rem(near + 2 * (t // 2), 4)

    def add_row(row, value):
        at = pl.ds(row, 1)
        sums_ref[at, :] = sums_ref[at, :] + jnp.sum(value, axis=0, keepdims=True)

    def landing(who, part):
        return seq_ref.at[pl.ds(pl.multiple_of(who * rows + part * step, step), step)]

    def row_block(part, carry):
        here = pl.ds(pl.multiple_of(part * step, step), step)
        for k in (1, 2, 3):
            awaited(attn_ref.at[k, here], sa.at[k, part], ra.at[k, part], {"tp": peers[k]}).wait_recv()
        attn = jnp.concatenate([attn_ref[p, here, :] for p in range(4)], axis=1)
        attn_cat[here, :] = attn
        hidden = x_ref[here, :].astype(f32) + dot_t(attn, ow_cat[...]) + par_ref[0:1, :]
        gain = par_ref[1:2, :]
        normed, hat, inverse = layer_norm(hidden, gain, par_ref[2:3, :])
        in_s[...] = normed.astype(bf16)
        in_t[:, here] = normed.T.astype(bf16)
        grad = g_ref[here, :]
        g_t[:, here] = grad.astype(f32).T.astype(bf16)
        out_acc[...] = hidden + par_ref[3:4, :]
        gn_acc[...] = jnp.zeros_like(gn_acc)

        def hidden_block(t, c):
            bias_at = 4 + owner(t)
            pre = dot_n(in_s[...], fc_ref[t]) + par_ref[pl.ds(bias_at, 1), :]
            gate = jax.nn.sigmoid(gelu_slope * pre)
            raised = pre * gate
            act = raised.astype(bf16)
            act_s[t, here, :] = act
            out_acc[...] += dot_t(act, pj_ref[t])
            grad_act = dot_n(g_ref[here, :], pj_ref[t])
            grad_pre = (grad_act * (gate + gelu_slope * raised * (1.0 - gate))).astype(bf16)
            gp_s[t, here, :] = grad_pre
            add_row(bias_at, grad_pre.astype(f32))
            gn_acc[...] += dot_t(grad_pre, fc_ref[t])
            return c

        lax.fori_loop(0, 4, hidden_block, 0)
        layer_ref[here, :] = out_acc[...].astype(bf16)
        grad_in, gain_part, shift_part = norm_back(gn_acc[...], hat, inverse, gain)
        grad_hidden = grad.astype(f32) + grad_in
        resid_ref[here, :] = grad_hidden
        low = grad_hidden.astype(bf16)
        low_t[:, here] = grad_hidden.T.astype(bf16)
        sums_ref[1:2, :] += gain_part[None]
        sums_ref[2:3, :] += shift_part[None]
        add_row(0, low.astype(f32))
        add_row(3, grad.astype(f32))
        seg = jnp.broadcast_to(seg_ref[0:1, here].astype(f32), (8, step)).T[:, 0:1]
        live = jnp.where(seg != 0.0, 1.0, 0.0)
        grad_attn = (dot_n(low, ow_cat[...]).astype(bf16).astype(f32) * live).astype(bf16)
        for k in (1, 2, 3):
            ga_s[k, here, :] = grad_attn[:, k * lanes : (k + 1) * lanes]
        seq_ref[pl.ds(pl.multiple_of(me * rows + part * step, step), step), :] = grad_attn[:, 0:lanes]
        for k in (3, 2, 1):
            push(ga_s.at[k, here], landing(me, part), sems.at[k, part], rems.at[k, part], {"tp": peers[k]})
        return carry

    lax.fori_loop(0, parts, row_block, 0)
    width = out_acc.shape[1]
    tall = 512

    def out_block(n, carry):
        at = pl.ds(pl.multiple_of(n * tall, tall), tall)
        grad = dot_n(low_t[at, :], attn_cat[...]).astype(bf16)
        for p in range(4):
            ow_g[p, at, :] = grad[:, p * lanes : (p + 1) * lanes]
        return carry

    lax.fori_loop(0, width // tall, out_block, 0)
    triples = ((fc_g, fc_box), (pj_g, pj_box), (ow_g, ow_box))

    def fold(n, b):
        grad, box = triples[n]
        return grad.at[2 * b + 1], box.at[b], ws.at[n, b], wr.at[n, b], {"tp": side}

    for b in (1, 0):
        push(*fold(2, b))

    def slice_block(u, carry):
        t = 3 - 2 * u + 3 * (u // 2)

        def fc_block(n, c):
            at = pl.ds(pl.multiple_of(n * tall, tall), tall)
            fc_g[t, at, :] = dot_n(in_t[at, :], gp_s[t]).astype(bf16)
            pj_g[t, at, :] = dot_n(g_t[at, :], act_s[t]).astype(bf16)
            return c

        lax.fori_loop(0, width // tall, fc_block, 0)
        for b in (1, 0):

            @pl.when(u == 1 - b)
            def _():
                push(*fold(0, b))
                push(*fold(1, b))

        return carry

    lax.fori_loop(0, 4, slice_block, 0)
    for b, target in ((1, over_ref), (0, kept_ref)):
        at = 0
        for n, (grad, box) in enumerate(triples):
            cols = slice(at, at + grad.shape[2])
            at += grad.shape[2]
            awaited(box.at[b], ws.at[n, b], wr.at[n, b], {"tp": side}).wait_recv()
            target[:, cols] = (grad[2 * b].astype(f32) + box[b].astype(f32)).astype(bf16)

    def drain(part, carry):
        here = pl.ds(pl.multiple_of(part * step, step), step)
        for k in (1, 2, 3):
            peer = {"tp": peers[k]}
            awaited(landing(peers[k], part), sems.at[k, part], rems.at[k, part], peer).wait_recv()
            awaited(ga_s.at[k, here], sems.at[k, part], rems.at[k, part], peer).wait_send()
            awaited(own_rows(peers[k], part), sa.at[k, part], ra.at[k, part], peer).wait_send()
        return carry

    lax.fori_loop(0, parts, drain, 0)
    for n, (grad, box) in enumerate(triples):
        for b in (1, 0):
            awaited(grad.at[2 * b + 1], ws.at[n, b], wr.at[n, b], {"tp": side}).wait_send()


def middle(attn, own, passed, x, grad, segments, params, hidden, number, parts=2):
    rows, lanes = x.shape[0], attn.shape[1]
    width = x.shape[1]
    fc = pj = (4, width, hidden)
    ow = (4, width, lanes)
    step = rows // parts
    dma = pltpu.SemaphoreType.DMA
    total = 2 * hidden + lanes
    low, wide = bf16, f32
    scratch = [
        ((4, rows, lanes), low), (fc, low), (pj, low), (ow, low),
        ((rows, width), low), ((width, 4 * lanes), low),
        ((4, rows, hidden), low), ((4, rows, hidden), low),
        ((step, width), low), ((width, rows), low), ((width, rows), low), ((width, rows), low),
        ((4, rows, lanes), low), ((step, width), wide), ((step, width), wide),
        (fc, low), (pj, low), (ow, low),
        ((2, *fc[1:]), low), ((2, *pj[1:]), low), ((2, *ow[1:]), low),
    ]
    outs = [
        ((rows, width), low), ((rows, width), wide), ((4 * rows, lanes), low),
        ((width, total), low), ((width, total), low), ((8, width), wide),
    ]
    return comm_call(
        functools.partial(middle_kernel, parts=parts),
        "middle",
        number,
        [jax.ShapeDtypeStruct(s, d) for s, d in outs],
        [in_vmem(), anywhere(), anywhere()] + [in_vmem()] * 4,
        [in_vmem()] * 6,
        [pltpu.VMEM(s, d) for s, d in scratch]
        + [dma((4, parts)), dma((4, parts)), dma((3, 2)), dma((3, 2))]
        + [dma((4, parts)), dma((4, parts)), dma((2, 3)), dma((2, 3)), dma((7,))],
        60 << 20,
        attn,
        own,
        passed,
        x,
        grad,
        segments,
        params,
    )


def leave_kernel(
    grad_ref, normed_in, w_ref, kept_ref, came_ref, early_ref, x_in, gain_ref, resid_in,
    input_ref, s0, s1, s2, s3, early_out, late_out,
    rows_ref, far_out, own_out, sum_buf, side_far, side_own, over, dw_acc, cols_ref,
    late_ref, early_mid, late_mid, early_one, early_two, late_one, late_two,
    normed_ref, x_ref, resid_ref, loads,
    sa, ra, sb, rb, sy, ry, sw, rw, se, re, sl, rl, se2, re2, sl2, rl2, *bufs, parts, hops
):
    me, side, across, far = quad()
    rows = rows_ref.shape[0]
    step = rows // parts
    shard, shards = lax.axis_index("fsdp"), early_two.shape[0]
    pairs = ((normed_in, normed_ref), (x_in, x_ref), (resid_in, resid_ref))
    loading = [pltpu.make_async_copy(a, b, loads.at[n]) for n, (a, b) in enumerate(pairs)]
    for copy in loading:
        copy.start()
    barrier = pltpu.get_barrier_semaphore()
    for peer in (side, across, far):
        pl.semaphore_signal(barrier, inc=1, device_id={"tp": peer}, device_id_type=MESH)

    def other(k):
        return {"fsdp": lax.rem(shard + k, shards)}

    def signal(k, carry):
        pl.semaphore_signal(barrier, inc=1, device_id=other(k), device_id_type=MESH)
        return carry

    lax.fori_loop(1, shards, signal, 0)
    pl.semaphore_wait(barrier, 3 + shards - 1)
    count = len(hops)
    outs = (s0, s1, s2, s3)
    swapped = (0, 2) if count > 1 else ()
    current = bufs[0:4]
    boxes = [bufs[4 + g * count : 4 + (g + 1) * count] for g in range(4)]
    keeps = [bufs[4 + 4 * count + g * (count - 1) : 4 + 4 * count + (g + 1) * (count - 1)] for g in range(4)]
    sent = []

    def begin(g):
        at = sum(c.shape[3] for c in current[0:g])
        cols = slice(at, at + current[g].shape[3])
        if g not in swapped:
            total = kept_ref[:, :, :, cols].astype(f32) + came_ref[:, :, :, cols].astype(f32)
            current[g][...] = total.astype(bf16)
            return
        for p in range(current[g].shape[0]):
            for q in range(2):
                i, j = (p // 2) * 2 + q, p % 2
                total = kept_ref[i, j, :, cols].astype(f32) + came_ref[i, j, :, cols].astype(f32)
                current[g][p, q] = total.astype(bf16)

    def hop_parts(g, k):
        axis, bit = hops[(1, 0, *range(2, count))[k] if g in swapped else k]
        source = current[g] if k == 0 else keeps[g][k - 1]
        half = lax.rem(lax.axis_index(axis) // bit, 2)
        return {axis: flip(axis, bit)}, source, half, boxes[g][k]

    def hop_send(g, k):
        peer, source, half, box = hop_parts(g, k)
        sent.append(push(source.at[:, 1 - half], box, sw.at[g, k], rw.at[g, k], peer))

    def hop_add(g, k):
        peer, source, half, box = hop_parts(g, k)
        awaited(box, sw.at[g, k], rw.at[g, k], peer).wait_recv()
        if k == count - 1:
            outs[g][...] = source[0, half].astype(f32) + box[0].astype(f32)
        else:
            target = keeps[g][k]
            for n in range(box.shape[0]):
                total = source[n, half].astype(f32) + box[n].astype(f32)
                target[n // 2, n % 2] = total.astype(bf16)
            hop_send(g, k + 1)

    def tp_send(value, box, send, recv):
        box[me] = value[...]
        for k, peer in enumerate((side, across, far)):
            sent.append(push(value, box.at[me], send.at[k], recv.at[me], {"tp": peer}))

    def tp_sum(value, box, send, recv):
        for k, peer in enumerate((side, across, far)):
            awaited(box.at[peer], send.at[k], recv.at[peer], {"tp": peer}).wait_recv()
        value[...] = box[0] + box[1] + box[2] + box[3]

    def fsdp_send(value, box, send, recv):
        box[shard] = value[...]

        def give(k, carry):
            push(value, box.at[shard], send.at[k], recv.at[shard], other(k))
            return carry

        lax.fori_loop(1, shards, give, 0)

    def fsdp_sum(value, target, box, send, recv):
        def take(k, carry):
            peer = lax.rem(shard + k, shards)
            copy = awaited(box.at[peer], send.at[k], recv.at[peer], other(k))
            copy.wait_recv()
            copy.wait_send()
            return carry

        lax.fori_loop(1, shards, take, 0)
        target[...] = lax.fori_loop(1, shards, lambda n, total: total + box[n], box[0])

    def span(owner, part):
        return pl.ds(pl.multiple_of(owner * rows + part * step, step), step)

    def piece(part):
        return pl.ds(pl.multiple_of(part * step, step), step)

    def partial(owner, part):
        return dot_t(grad_ref[span(owner, part), :], w_ref[...])

    def give_far(part, carry):
        here = piece(part)
        far_out[here, :] = partial(far, part).astype(bf16)
        push(far_out.at[here], side_far.at[here], sa.at[part], ra.at[part], {"tp": side})
        return carry

    def give_over(part, carry):
        here = piece(part)
        mine = partial(across, part)
        awaited(side_far.at[here], sa.at[part], ra.at[part], {"tp": side}).wait_recv()
        sum_buf[here, :] = (mine + side_far[here, :].astype(f32)).astype(bf16)
        push(sum_buf.at[here], over.at[here], sy.at[part], ry.at[part], {"tp": across})
        return carry

    def give_own(part, carry):
        here = piece(part)
        own_out[here, :] = partial(side, part).astype(bf16)
        push(own_out.at[here], side_own.at[here], sb.at[part], rb.at[part], {"tp": side})
        return carry

    def take_own(part, carry):
        here = piece(part)
        mine = partial(me, part)
        awaited(side_own.at[here], sb.at[part], rb.at[part], {"tp": side}).wait_recv()
        rows_ref[here, :] = mine + side_own[here, :].astype(f32)
        return carry

    gain = gain_ref[8:9, :]

    def take_over(part, carry):
        here = piece(part)
        x = x_ref[here, :].astype(f32)
        centred = x - jnp.mean(x, axis=-1, keepdims=True)
        inverse = lax.rsqrt(jnp.mean(centred * centred, axis=-1, keepdims=True) + epsilon)
        normed = centred * inverse
        awaited(over.at[here], sy.at[part], ry.at[part], {"tp": across}).wait_recv()
        grad = rows_ref[here, :] + over[here, :].astype(f32)
        grad_in, gain_part, shift_part = norm_back(grad, normed, inverse, gain)
        input_ref[here, :] = (resid_ref[here, :] + grad_in).astype(bf16)
        late_ref[0:1, :] += gain_part[None]
        late_ref[1:2, :] += shift_part[None]
        return carry

    def drain(part, carry):
        here = piece(part)
        awaited(far_out.at[here], sa.at[part], ra.at[part], {"tp": side}).wait_send()
        awaited(own_out.at[here], sb.at[part], rb.at[part], {"tp": side}).wait_send()
        awaited(sum_buf.at[here], sy.at[part], ry.at[part], {"tp": across}).wait_send()
        return carry

    chunk = 512
    steps = grad_ref.shape[0] // chunk
    dw_acc[...] = jnp.zeros_like(dw_acc)
    cols_ref[...] = jnp.zeros_like(cols_ref)
    ones = jnp.ones((8, chunk), bf16)

    def weight_grad(n, carry):
        at = pl.ds(pl.multiple_of(n * chunk, chunk), chunk)
        g = grad_ref[at, :]
        dw_acc[...] += lax.dot_general(
            normed_ref[at, :], g, (((0,), (0,)), ((), ())), preferred_element_type=f32
        )
        cols_ref[...] += dot_n(ones, g)
        return carry

    tp_send(early_ref, early_one, se, re)
    begin(0)
    hop_send(0, 0)
    lax.fori_loop(0, parts, give_far, 0)
    begin(1)
    hop_send(1, 0)
    lax.fori_loop(0, parts, give_over, 0)
    begin(2)
    for copy in loading:
        copy.wait()
    lax.fori_loop(0, steps // 2, weight_grad, 0)
    hop_add(0, 0)
    lax.fori_loop(steps // 2, steps, weight_grad, 0)
    current[3][...] = dw_acc[...].astype(bf16).reshape(current[3].shape)
    hop_send(3, 0)
    hop_send(2, 0)
    tp_sum(early_mid, early_one, se, re)
    fsdp_send(early_mid, early_two, se2, re2)
    hop_add(1, 0)
    late_ref[...] = jnp.zeros_like(late_ref)
    wide = cols_ref.shape[1] // 3
    qv_at = pl.ds(pl.multiple_of(me * wide, wide), wide)
    late_ref[2:3, qv_at] = cols_ref[0:1, 0:wide]
    late_ref[3:4, qv_at] = cols_ref[0:1, 2 * wide : 3 * wide]
    lax.fori_loop(0, parts, give_own, 0)
    turns = enumerate((0, 1, 3, 2))
    order = sorted((k + turn, turn, g, k) for turn, g in turns for k in range(count))
    order = [(g, k) for _, _, g, k in order if (g, k) not in ((0, 0), (1, 0))]
    lax.fori_loop(0, parts, take_own, 0)
    taken = {len(order) * share // 10: span for share, span in ((6, (0, 2)), (7, (2, 3)), (9, (3, 4)))}
    for n, (g, k) in enumerate(order):
        if n in taken:
            first, last = taken[n]
            lax.fori_loop(first * parts // 4, last * parts // 4, take_over, 0)
        if n == len(order) - 1:
            tp_send(late_ref, late_one, sl, rl)
        hop_add(g, k)
    fsdp_sum(early_mid, early_out, early_two, se2, re2)
    tp_sum(late_mid, late_one, sl, rl)
    fsdp_send(late_mid, late_two, sl2, rl2)
    lax.fori_loop(0, parts, drain, 0)
    fsdp_sum(late_mid, late_out, late_two, sl2, rl2)
    for copy in sent:
        copy.wait_send()


def leave(grad, normed, w, kept, came, widths, early, x, gain, resid, number, parts=2):
    rows, width = grad.shape[0] // 4, w.shape[0]
    dma = pltpu.SemaphoreType.DMA
    hops = bits_of("fsdp")
    count = len(hops)
    shards = lax.axis_size("fsdp")
    shard = width // shards
    widths = [*widths, grad.shape[1]]
    split = (shards // 2, 2, shard)
    current = [pltpu.VMEM((*split, n), bf16) for n in widths]
    boxes = [pltpu.VMEM((shards >> (k + 1), shard, n), bf16) for n in widths for k in range(count)]
    keeps = [pltpu.VMEM((shards >> (k + 2), 2, shard, n), bf16) for n in widths for k in range(count - 1)]
    late = (4, width)
    return comm_call(
        functools.partial(leave_kernel, parts=parts, hops=hops),
        "leave",
        number,
        [jax.ShapeDtypeStruct((rows, width), bf16)]
        + [jax.ShapeDtypeStruct((shard, n), f32) for n in widths]
        + [jax.ShapeDtypeStruct(early.shape, f32), jax.ShapeDtypeStruct(late, f32)],
        [in_vmem(), anywhere()] + [in_vmem()] * 4 + [anywhere(), in_vmem(), anywhere()],
        [in_vmem()] * 7,
        [pltpu.VMEM((rows, width), f32)]
        + [pltpu.VMEM((rows, width), bf16)] * 6
        + [pltpu.VMEM((width, grad.shape[1]), f32), pltpu.VMEM((8, grad.shape[1]), f32)]
        + [pltpu.VMEM(late, f32), pltpu.VMEM(early.shape, f32), pltpu.VMEM(late, f32)]
        + [pltpu.VMEM((n, *shape), f32) for shape in (early.shape, late) for n in (4, shards)]
        + [pltpu.VMEM(v.shape, v.dtype) for v in (normed, x, resid)]
        + [dma((3,))]
        + [dma((parts,))] * 6
        + [dma((4, count))] * 2
        + [dma((3,)), dma((4,))] * 2
        + [dma((shards,))] * 4
        + current
        + boxes
        + keeps,
        60 << 20,
        grad,
        normed,
        w,
        kept.reshape(*split, kept.shape[1]),
        came.reshape(*split, came.shape[1]),
        early,
        x,
        gain,
        resid,
    )


def finish_kernel(
    rows_in, fc_in, proj_in, out_in, qkv_in, early_in, late_in,
    rows_ref, fc_ref, proj_ref, out_ref, qkv_ref, qv_ref, *vectors
):
    rows_ref[...] = rows_in[...]
    fc_ref[...] = fc_in[...]
    proj_ref[...] = proj_in[...]
    out_ref[...] = out_in[...]
    width = qkv_ref.shape[2]
    for n in range(3):
        qkv_ref[n] = qkv_in[:, n * width : (n + 1) * width]
    qv_ref[...] = late_in[2:4, :]
    first_gain, first_shift, out_bias, gain, shift, fc_bias, proj_bias = vectors
    lanes = first_gain.shape[1]
    count = first_gain.shape[0]
    singles = ((first_gain, late_in, 0), (first_shift, late_in, 1), (out_bias, early_in, 0))
    singles += ((gain, early_in, 1), (shift, early_in, 2), (proj_bias, early_in, 3))
    for ref, source, row in singles:
        for n in range(count):
            ref[n : n + 1, :] = source[row : row + 1, n * lanes : (n + 1) * lanes]
    for row in range(4):
        for n in range(count):
            at = row * count + n
            fc_bias[at : at + 1, :] = early_in[4 + row : 5 + row, n * lanes : (n + 1) * lanes]


def finish(rows, fc, proj, out, qkv, early, late):
    lanes = 128
    width = late.shape[1]
    shapes = [rows, fc, proj, out]
    outs = [jax.ShapeDtypeStruct(v.shape, v.dtype) for v in shapes]
    outs.append(jax.ShapeDtypeStruct((3, qkv.shape[0], qkv.shape[1] // 3), f32))
    outs.append(jax.ShapeDtypeStruct((2, width), f32))
    sizes = [width] * 5 + [4 * early.shape[1], width]
    outs += [jax.ShapeDtypeStruct((n // lanes, lanes), f32) for n in sizes]
    rows, fc, proj, out, qkv, qv, *vectors = pl.pallas_call(
        finish_kernel,
        out_shape=outs,
        in_specs=[in_vmem()] * 7,
        out_specs=[in_vmem()] * len(outs),
        cost_estimate=pl.CostEstimate(flops=0, bytes_accessed=3 << 20, transcendentals=0),
        name="finish",
    )(rows, fc, proj, out, qkv, early, late)
    return rows, fc, proj.T, out.T, qkv.transpose(1, 0, 2), qv, [v.reshape(-1) for v in vectors]


def flip(axis, bit):
    me = lax.axis_index(axis)
    return me + bit - 2 * bit * lax.rem(me // bit, 2)


def bits_of(axis):
    size, bits, bit = lax.axis_size(axis), [], 1
    while bit < size:
        bits.append((axis, bit))
        bit *= 2
    return bits


def across(value):
    return lax.ppermute(value, "tp", [(n, n ^ 2) for n in range(4)])


def local(
    inputs,
    segments,
    out_grad,
    first_gain,
    first_shift,
    qkv_weight,
    qv_bias,
    out_weight,
    out_bias,
    second_gain,
    second_shift,
    fc_weight,
    fc_bias,
    proj_weight,
    proj_bias,
):
    slices = lax.axis_size("tp")
    rows_here, model_width = inputs.shape
    shard_rows = qkv_weight.shape[0]
    head_cols = qkv_weight.shape[2]
    hidden_cols = fc_weight.shape[1]
    vectors = (out_bias, second_gain, second_shift, proj_bias, fc_bias, first_gain, first_shift, qv_bias)
    size = min(BLOCK, rows_here)
    seq_normed, seg_parts, low, params, qa, ka, va, vt, kt, qkv_full, own = enter(
        inputs,
        vectors,
        segments,
        (qkv_weight.reshape(shard_rows, 3 * head_cols), fc_weight, proj_weight.T, out_weight.T),
        size,
        0,
    )
    qkv_full = qkv_full.reshape(model_width, 3 * head_cols)
    own = own.reshape(model_width, own.shape[2])
    over = across(own)
    widths = (hidden_cols, hidden_cols, head_cols)

    attn_out, qb = attend(low, qa, ka, vt, seg_parts, size)

    layer_out, grad_hidden, grad_attn_seq, kept, passed, early = middle(
        attn_out, own, over, inputs, out_grad, segments, params, hidden_cols, 2
    )
    came = across(passed)
    grad_qkv = attend_back(low, qb, ka, va, kt, grad_attn_seq, attn_out, seg_parts, size)
    input_grad, fc_w_grad, proj_w_grad, out_w_grad, qkv_grad, early_sums, late_sums = leave(
        grad_qkv,
        seq_normed,
        qkv_full,
        kept,
        came,
        widths,
        early,
        inputs,
        params,
        grad_hidden,
        3,
    )
    input_grad, fc_w_grad, proj_w_grad, out_w_grad, qkv_grad, qv_bias_grad, vectors = finish(
        input_grad,
        fc_w_grad,
        proj_w_grad,
        out_w_grad,
        qkv_grad,
        early_sums,
        late_sums,
    )
    first_gain_grad, first_shift_grad, out_bias_grad, second_gain_grad, second_shift_grad = vectors[0:5]
    fc_bias_grad, proj_bias_grad = vectors[5:7]

    return (
        layer_out,
        input_grad,
        first_gain_grad,
        first_shift_grad,
        qkv_grad,
        qv_bias_grad,
        out_w_grad,
        out_bias_grad,
        second_gain_grad,
        second_shift_grad,
        fc_w_grad,
        fc_bias_grad,
        proj_w_grad,
        proj_bias_grad,
    )


def solution(mesh):
    return jax.shard_map(
        local,
        mesh=mesh,
        in_specs=(
            P(("fsdp", "tp"), None),
            P("fsdp", "tp"),
            P(("fsdp", "tp"), None),
            P(),
            P(),
            P("fsdp", None, "tp"),
            P(),
            P("tp", "fsdp"),
            P(),
            P(),
            P(),
            P("fsdp", "tp"),
            P(),
            P("tp", "fsdp"),
            P(),
        ),
        out_specs=(
            P(("fsdp", "tp"), None),
            P(("fsdp", "tp"), None),
            P(),
            P(),
            P("fsdp", None, "tp"),
            P(),
            P("tp", "fsdp"),
            P(),
            P(),
            P(),
            P("fsdp", "tp"),
            P(),
            P("tp", "fsdp"),
            P(),
        ),
        check_vma=False,
    )
```

```python
import functools

import jax
import jax.numpy as jnp
from jax import lax
from jax.experimental import pallas as pl
from jax.experimental.pallas import tpu as pltpu
from jax.sharding import PartitionSpec as P

HD = 64
VMEM_LIMIT = 60 << 20
epsilon = 1e-05
gelu_slope = 1.702


def layer_norm(values_in, gain_vec, shift_vec):
    mean_row = jnp.mean(values_in, axis=-1, keepdims=True)
    centred = values_in - mean_row
    inverse = lax.rsqrt(jnp.mean(centred * centred, axis=-1, keepdims=True) + epsilon)
    normed = centred * inverse
    return (normed * gain_vec + shift_vec, normed, inverse)


def norm_back(grad_out, normed, inverse, gain_vec):
    scaled = grad_out * gain_vec
    grad_in = inverse * (
        scaled
        - jnp.mean(scaled, axis=-1, keepdims=True)
        - normed * jnp.mean(scaled * normed, axis=-1, keepdims=True)
    )
    return (grad_in, jnp.sum(grad_out * normed, axis=0), jnp.sum(grad_out, axis=0))


f32 = jnp.float32
bf16 = jnp.bfloat16
LOG2E = 1.4426950408889634
BLOCK = 512
TRANSPOSED = (((1,), (1,)), ((), ()))


def dot_t(left, right):
    return lax.dot_general(left, right, TRANSPOSED, preferred_element_type=f32)


def dot_n(left, right):
    return jnp.dot(left, right, preferred_element_type=f32)


def three_parts(value):
    top = value.astype(bf16)
    rest = value - top.astype(f32)
    mid = rest.astype(bf16)
    return top, mid, (rest - mid.astype(f32)).astype(bf16)


def diagonal_mask(seg_ref, row_at, size):
    key_pos = lax.broadcasted_iota(jnp.int32, (size, 1), 0)
    query_pos = lax.broadcasted_iota(jnp.int32, (1, size), 1)
    here = seg_ref.shape[2]
    seg = seg_ref[row_at // here, 0:1, pl.ds(pl.multiple_of(lax.rem(row_at, here), size), size)]
    first = jnp.where(seg == 0, query_pos, 0)
    return (key_pos >= first) & (key_pos <= query_pos)


def attend_kernel(
    low_ref, qa_ref, ka_ref, vt_ref, start_ref, out_ref, qb_ref, s0, s1, a0, a1, *, size, blocks
):
    score_bufs, acc_bufs = (s0, s1), (a0, a1)
    heads = range(qa_ref.shape[0])
    lane = lax.broadcasted_iota(jnp.int32, (size, 128), 1)

    def query_block(i, carry):
        row_at = pl.multiple_of(i * size, size)

        def score(h, j, top, diag):
            keys = ka_ref[h, pl.ds(pl.multiple_of(j * size, size), size), :]
            s = dot_t(keys, qa_ref[h, pl.ds(row_at, size), :])
            if diag:
                s = jnp.where(diagonal_mask(start_ref, row_at, size), s, -3e38)
            score_bufs[h][...] = s
            col_max = jnp.max(s, axis=0, keepdims=True)
            return col_max if top is None else jnp.maximum(top, col_max)

        def gather_values(h, j, old, new, first):
            p = jnp.exp2(score_bufs[h][...] * LOG2E - new * LOG2E).astype(bf16)
            part = dot_n(vt_ref[h, :, pl.ds(pl.multiple_of(j * size, size), size)], p)
            if first:
                acc_bufs[h][...] = part
            else:
                acc_bufs[h][...] = acc_bufs[h][...] * jnp.exp2((old - new) * LOG2E) + part

        low = low_ref[i, 0]
        m0 = score(0, i, None, True)
        m1 = score(1, i, None, True)
        gather_values(0, i, None, m0, True)
        m0n = score(0, jnp.minimum(low, i), m0, False)
        gather_values(1, i, None, m1, True)

        def body(j, c):
            m0, m0n, m1 = c
            m1n = score(1, j, m1, False)
            gather_values(0, j, m0, m0n, False)
            m0nn = score(0, jnp.minimum(j + 1, blocks - 1), m0n, False)
            gather_values(1, j, m1, m1n, False)
            return m0n, m0nn, m1n

        m0, _, m1 = lax.fori_loop(low, i, body, (m0, m0n, m1))
        for h, top in ((0, m0), (1, m1)):
            total = acc_bufs[h][64:65, :]
            out = acc_bufs[h][0:64, :] / total
            rows = qa_ref[h, pl.ds(row_at, size), :]
            live = jnp.where(rows[:, 64:65].astype(f32) != 0.0, 1.0, 0.0)
            out_ref[pl.ds(row_at, size), 64 * h : 64 * h + 64] = (out.T * live).astype(out_ref.dtype)
            norm = jnp.broadcast_to(-(top + jnp.log(total)), (8, size)).T[:, 0:1]
            n0, n1, n2 = three_parts(norm)
            rows = jnp.where(lane == 96, n0, jnp.where(lane == 97, n1, jnp.where(lane == 98, n2, rows)))
            qb_ref[h, pl.ds(row_at, size), :] = rows
        return carry

    lax.fori_loop(0, blocks, query_block, 0)


def attend(low, qa, ka, vt, start, size):
    heads, rows, _ = qa.shape
    vmem = pl.BlockSpec(memory_space=pltpu.VMEM)
    return pl.pallas_call(
        functools.partial(attend_kernel, size=size, blocks=rows // size),
        grid_spec=pltpu.PrefetchScalarGridSpec(
            num_scalar_prefetch=0,
            grid=(),
            in_specs=[pl.BlockSpec(memory_space=pltpu.SMEM)] + [vmem] * 4,
            out_specs=[vmem] * 2,
            scratch_shapes=[pltpu.VMEM((size, size), f32)] * heads
            + [pltpu.VMEM((vt.shape[1], size), f32)] * heads,
        ),
        out_shape=[
            jax.ShapeDtypeStruct((rows, HD * heads), bf16),
            jax.ShapeDtypeStruct(qa.shape, bf16),
        ],
        compiler_params=pltpu.CompilerParams(vmem_limit_bytes=VMEM_LIMIT),
        cost_estimate=pl.CostEstimate(
            flops=14 * rows * rows * HD * heads, bytes_accessed=8 << 20, transcendentals=rows * rows
        ),
        name="attend",
    )(low, qa, ka, vt, start)


def attend_back_kernel(
    low_ref, qb_ref, ka_ref, va_ref, kt_ref, g_ref, o_ref, start_ref, grad_ref,
    ga_ref, dk_ref, dv_ref, q0, q1, *, size, blocks
):
    query_accs = (q0, q1)
    lane = lax.broadcasted_iota(jnp.int32, (size, 64), 1)

    def query_block(i, carry):
        row_at = pl.multiple_of(i * size, size)
        g_rows = g_ref[pl.ds(row_at, size), :]
        product = g_rows.astype(f32) * o_ref[pl.ds(row_at, size), :].astype(f32)
        for h in range(2):
            cols = slice(64 * h, 64 * h + 64)
            n0, n1, n2 = three_parts(-jnp.sum(product[:, cols], axis=1, keepdims=True))
            zero = jnp.zeros((size, 64), bf16)
            extra = jnp.where(lane == 0, n0, jnp.where(lane == 1, n1, jnp.where(lane == 2, n2, zero)))
            ga_ref[h] = jnp.concatenate([g_rows[:, cols], extra], axis=1)

        def block(h, j, diag):
            key_at = pl.multiple_of(j * size, size)
            keys = ka_ref[h, pl.ds(key_at, size), :]
            q_rows = qb_ref[h, pl.ds(row_at, size), :]
            g_head = ga_ref[h]
            s = dot_t(keys, q_rows)
            if diag:
                s = jnp.where(diagonal_mask(start_ref, row_at, size), s, -3e38)
            p = jnp.exp2(s * LOG2E)
            dp = dot_t(va_ref[h, pl.ds(key_at, size), :], g_head)
            ds = (p * dp).astype(bf16)
            dv = dot_n(p.astype(bf16), g_head[:, 0:64])
            dk = dot_n(ds, q_rows[:, 0:64])
            dq = dot_n(kt_ref[h, :, pl.ds(key_at, size)], ds)
            if diag:
                dv_ref[h, pl.ds(key_at, size), :] = dv
                dk_ref[h, pl.ds(key_at, size), :] = dk
                query_accs[h][...] = dq
            else:
                dv_ref[h, pl.ds(key_at, size), :] += dv
                dk_ref[h, pl.ds(key_at, size), :] += dk
                query_accs[h][...] += dq

        block(0, i, True)
        block(1, i, True)

        def body(j, c):
            block(0, j, False)
            block(1, j, False)
            return c

        lax.fori_loop(low_ref[i, 0], i, body, 0)
        both = jnp.concatenate([query_accs[0][...], query_accs[1][...]], axis=0) * HD ** (-0.5)
        grad_ref[pl.ds(row_at, size), 0:128] = both.T.astype(bf16)
        return carry

    lax.fori_loop(0, blocks, query_block, 0)

    def finish(i, carry):
        row_at = pl.multiple_of(i * size, size)
        for ref, at in ((dk_ref, 128), (dv_ref, 256)):
            both = jnp.concatenate([ref[0, pl.ds(row_at, size), :], ref[1, pl.ds(row_at, size), :]], axis=1)
            grad_ref[pl.ds(row_at, size), at : at + 128] = both.astype(bf16)
        return carry

    lax.fori_loop(0, blocks, finish, 0)


def attend_back(low, qb, ka, va, kt, g, o, start, size):
    heads, rows, _ = qb.shape
    vmem = pl.BlockSpec(memory_space=pltpu.VMEM)
    return pl.pallas_call(
        functools.partial(attend_back_kernel, size=size, blocks=rows // size),
        grid_spec=pltpu.PrefetchScalarGridSpec(
            num_scalar_prefetch=0,
            grid=(),
            in_specs=[pl.BlockSpec(memory_space=pltpu.SMEM)] + [vmem] * 7,
            out_specs=vmem,
            scratch_shapes=[
                pltpu.VMEM((heads, size, 128), bf16),
                pltpu.VMEM((heads, rows, HD), f32),
                pltpu.VMEM((heads, rows, HD), f32),
            ]
            + [pltpu.VMEM((HD, size), f32)] * heads,
        ),
        out_shape=jax.ShapeDtypeStruct((rows, 3 * HD * heads), bf16),
        compiler_params=pltpu.CompilerParams(vmem_limit_bytes=VMEM_LIMIT),
        cost_estimate=pl.CostEstimate(
            flops=24 * rows * rows * HD * heads, bytes_accessed=16 << 20, transcendentals=rows * rows
        ),
        name="attend_back",
    )(low, qb, ka, va, kt, g, o, start)


MESH = pl.DeviceIdType.MESH


def greet(peers):
    barrier = pltpu.get_barrier_semaphore()
    for peer in peers:
        pl.semaphore_signal(barrier, inc=1, device_id=peer, device_id_type=MESH)
    pl.semaphore_wait(barrier, len(peers))


def push(source, target, send_sem, recv_sem, peer):
    copy = pltpu.make_async_remote_copy(
        src_ref=source,
        dst_ref=target,
        send_sem=send_sem,
        recv_sem=recv_sem,
        device_id=peer,
        device_id_type=MESH,
    )
    copy.start()
    return copy


def quad():
    me = lax.axis_index("tp")
    side = me + 1 - 2 * lax.rem(me, 2)
    across = lax.rem(me + 2, 4)
    far = lax.rem(side + 2, 4)
    return me, side, across, far


def comm_call(kernel, name, number, out_shape, in_specs, out_specs, scratch, moved, *operands):
    return pl.pallas_call(
        kernel,
        out_shape=out_shape,
        in_specs=in_specs,
        out_specs=out_specs,
        scratch_shapes=scratch,
        compiler_params=pltpu.CompilerParams(
            collective_id=number, has_side_effects=True, vmem_limit_bytes=VMEM_LIMIT
        ),
        cost_estimate=pl.CostEstimate(flops=0, bytes_accessed=moved, transcendentals=0),
        name=name,
    )(*operands)


def in_vmem():
    return pl.BlockSpec(memory_space=pltpu.VMEM)


def anywhere():
    return pl.BlockSpec(memory_space=pl.ANY)


def flipped(axis, mask):
    me, index, bit = lax.axis_index(axis), lax.axis_index(axis), 1
    while bit <= mask:
        if mask & bit:
            index = index + bit - 2 * bit * lax.rem(me // bit, 2)
        bit *= 2
    return index


def awaited(ref, send_sem, recv_sem, peer):
    return pltpu.make_async_remote_copy(ref, ref, send_sem, recv_sem, peer, MESH)


def hop_masks(size):
    hops, bit = [], size // 2
    while bit >= 1:
        hops.append((bit, [high + bit for high in range(0, size, 2 * bit)]))
        bit //= 2
    return hops


def enter_kernel(
    x_ref, seg_ref, w0, w1, w2, w3, v0, v1, v2, v3, v4, v5, v6, v7,
    normed_ref, segs_ref, low_ref, par_ref, qa_ref, ka_ref, va_ref, vt_ref, kt_ref, f0, f1,
    x_all, normed_s, qa_s, ka_s, va_s, vt_s, kt_s,
    sy, ry, ss, rs, sf, rf, sg, rg, sw, rw, own, own_w, outs, *, parts, size
):
    me, side, across, far = quad()
    rows = x_ref.shape[0]
    step = rows // parts
    shards = f0.shape[0]
    heads = qa_ref.shape[0]
    width = HD * heads
    shard = lax.axis_index("fsdp")
    hops = hop_masks(shards)
    greet(
        [{"tp": side}, {"tp": across}, {"tp": far}]
        + [{"fsdp": flipped("fsdp", bit)} for bit, _ in hops]
    )
    sent = []

    def rows_of(owner, part):
        return x_all.at[pl.ds(pl.multiple_of(owner * rows + part * step, step), step)]

    sources = (w0, w1, w2, w3)

    def block_of(g, index):
        if g == 0:
            return f0.at[index]
        at = sum(w.shape[1] for w in sources[1:g])
        return f1.at[index, :, pl.ds(at, sources[g].shape[1])]

    def send_hop(g, hop):
        bit, masks = hops[hop]
        peer = {"fsdp": flipped("fsdp", bit)}
        if hop > 0:
            before, arrived = hops[hop - 1]
            for mask in arrived:
                block = block_of(g, flipped("fsdp", mask))
                awaited(block, sw.at[g, mask], rw.at[g, mask], {"fsdp": flipped("fsdp", before)}).wait_recv()
        for mask in masks:
            target = block_of(g, flipped("fsdp", mask - bit))
            block = sources[g] if mask == bit else target
            sent.append(push(block, target, sw.at[g, mask], rw.at[g, mask], peer))

    def end_hops(g):
        bit, arrived = hops[-1]
        for mask in arrived:
            block = block_of(g, flipped("fsdp", mask))
            awaited(block, sw.at[g, mask], rw.at[g, mask], {"fsdp": flipped("fsdp", bit)}).wait_recv()

    for k, peer in enumerate((across, far, side)):
        sent.append(push(seg_ref, segs_ref.at[me], sg.at[k], rg.at[k], {"tp": peer}))
    send_hop(0, 0)
    for part in range(parts):
        mine = x_ref.at[pl.ds(part * step, step)]
        sent.append(push(mine, rows_of(me, part), sy.at[part], ry.at[part], {"tp": across}))
    send_hop(0, 1)
    for g in (1, 2, 3):
        send_hop(g, 0)
    for part in range(parts):
        mine = x_ref.at[pl.ds(part * step, step)]
        sent.append(push(mine, rows_of(me, part), ss.at[part], rs.at[part], {"tp": side}))
    kept = [
        pltpu.make_async_copy(x_ref, x_all.at[pl.ds(pl.multiple_of(me * rows, rows), rows)], own.at[0]),
        pltpu.make_async_copy(seg_ref, segs_ref.at[me], own.at[1]),
    ] + [pltpu.make_async_copy(source, block_of(g, shard), own_w.at[g]) for g, source in enumerate(sources)]
    for copy in kept:
        copy.start()
    waves = sorted(
        ((hop + g, g, hop) for hop in range(1, len(hops)) for g in range(4)), key=lambda w: (w[0], w[1])
    )
    for _, g, hop in waves[1:2]:
        send_hop(g, hop)
    for k, peer in enumerate((across, far, side)):
        awaited(segs_ref.at[peer], sg.at[k], rg.at[k], {"tp": peer}).wait_recv()
    for part in range(parts):
        awaited(rows_of(side, part), ss.at[part], rs.at[part], {"tp": side}).wait_recv()
    for copy in kept:
        copy.wait()

    line, columns = 0, par_ref.shape[1]
    par_ref[...] = jnp.zeros_like(par_ref)
    for ref in (v0, v1, v2, v3, v4, v5, v6):
        value = ref[...].astype(f32).reshape(1, ref.shape[0])
        for n in range(ref.shape[0] // columns):
            par_ref[line : line + 1, :] = value[:, n * columns : (n + 1) * columns]
            line += 1
    par_ref[line : line + 2, :] = v7[...].astype(f32)
    gain, shift = par_ref[8:9, :], par_ref[9:10, :]

    def norm(owner, part):
        span = pl.ds(pl.multiple_of(owner * rows + part * step, step), step)
        x = x_all[span, :].astype(f32)
        centred = x - jnp.mean(x, axis=-1, keepdims=True)
        inverse = lax.rsqrt(jnp.mean(centred * centred, axis=-1, keepdims=True) + epsilon)
        normed_s[span, :] = (centred * inverse * gain + shift).astype(bf16)

    def norm_near(k, carry):
        norm(me + lax.rem(k, 2) * (side - me), k // 2)
        return carry

    lax.fori_loop(0, 2 * parts, norm_near, 0)
    whole = [segs_ref[n, 0:1, :] for n in range(4)]
    for n in range(4 * rows // size):
        at = n * size
        first = whole[at // rows][:, at % rows : at % rows + 1]
        before = sum(
            jnp.sum(jnp.where((seg > 0) & (seg < first), 1.0, 0.0), axis=1, keepdims=True) for seg in whole
        )
        block = jnp.where(first == 0, n * size, before.astype(jnp.int32)) // size
        low_ref[n : n + 1, :] = jnp.broadcast_to(block, (1, low_ref.shape[1]))
    for _, g, hop in waves[2:]:
        send_hop(g, hop)
    end_hops(0)
    bias_at = pl.ds(pl.multiple_of(me * width, width), width)
    query_bias = par_ref[10:11, bias_at]
    value_bias = par_ref[11:12, bias_at]
    number = lax.broadcasted_iota(jnp.int32, (step, 64), 1)
    number_f = number.astype(f32)
    key_ones = (number >= 32) & (number < 35)
    value_tail = jnp.where(number < 3, 1.0, 0.0).astype(bf16)
    ones_row = jnp.where(lax.broadcasted_iota(jnp.int32, (16, step), 0) == 0, 1.0, 0.0).astype(bf16)

    def copies_out(owner, part):
        row = pl.multiple_of(owner * rows + part * step, step)
        slot = owner * parts + part
        span = pl.ds(row, step)
        pairs = [(normed_s.at[span], normed_ref.at[span])]
        for a, b in ((qa_s, qa_ref), (ka_s, ka_ref), (va_s, va_ref)):
            pairs.append((a.at[:, span, :], b.at[:, span, :]))
        for a, b in ((vt_s, vt_ref), (kt_s, kt_ref)):
            pairs.append((a.at[:, :, span], b.at[:, :, span]))
        return [pltpu.make_async_copy(a, b, outs.at[n, slot]) for n, (a, b) in enumerate(pairs)]

    def compute(owner, part):
        row = pl.multiple_of(owner * rows + part * step, step)
        span = pl.ds(row, step)
        normed = normed_s[span, :]
        weights = f0[...].reshape(shards * f0.shape[1], 3 * width)
        projected = dot_n(normed, weights)
        queries = ((projected[:, 0:width] + query_bias).astype(bf16).astype(f32) * HD ** (-0.5)).astype(bf16)
        keys = projected[:, width : 2 * width].astype(bf16)
        values = (projected[:, 2 * width : 3 * width] + value_bias).astype(bf16)
        seg = segs_ref[owner, 0:1, pl.ds(pl.multiple_of(part * step, step), step)].astype(f32)
        seg = jnp.broadcast_to(seg, (8, step)).T[:, 0:1]
        same = (seg == number_f) & (number < 32)
        other = jnp.where(same | (number > 31), 0.0, -1e30).astype(bf16)
        key_tail = jnp.where(same | key_ones, 1.0, 0.0).astype(bf16)
        for h in range(heads):
            cols = slice(HD * h, HD * h + HD)
            qa_s[h, span, :] = jnp.concatenate([queries[:, cols], other], axis=1)
            ka_s[h, span, :] = jnp.concatenate([keys[:, cols], key_tail], axis=1)
            va_s[h, span, :] = jnp.concatenate([values[:, cols], value_tail], axis=1)
            turned = jnp.concatenate([values[:, cols], keys[:, cols]], axis=1).astype(f32).T.astype(bf16)
            vt_s[h, 0:64, span] = turned[0:64, :]
            vt_s[h, 64:80, span] = ones_row
            kt_s[h, :, span] = turned[64:128, :]
        for copy in copies_out(owner, part):
            copy.start()

    def work(k, carry):
        distant = k // (2 * parts)
        part = lax.rem(k // 2, parts)
        second = lax.rem(k, 2)

        @pl.when((distant == 0) & (second == 0))
        def _():
            here = rows_of(across, part)
            awaited(here, sy.at[part], ry.at[part], {"tp": across}).wait_recv()
            push(here, here, sf.at[part], rf.at[part], {"tp": side})

        @pl.when((distant == 1) & (second == 1))
        def _():
            awaited(rows_of(far, part), sf.at[part], rf.at[part], {"tp": side}).wait_recv()

        @pl.when(distant == 1)
        def _():
            norm(across + second * (far - across), part)

        first = me + distant * (across - me)
        compute(first + second * (side - me + distant * (far - across - side + me)), part)
        return carry

    lax.fori_loop(0, 4 * parts, work, 0)
    for g in (1, 2, 3):
        end_hops(g)

    def drain(k, carry):
        for copy in copies_out(k // parts, lax.rem(k, parts)):
            copy.wait()
        return carry

    lax.fori_loop(0, 4 * parts, drain, 0)
    for part in range(parts):
        awaited(rows_of(across, part), sf.at[part], rf.at[part], {"tp": side}).wait_send()
    for copy in sent:
        copy.wait_send()


def enter(x, vectors, segments, weights, size, number, parts=2):
    rows, width = x.shape
    seq_rows = 4 * rows
    shards = lax.axis_size("fsdp")
    heads = weights[0].shape[1] // (3 * HD)
    dma = pltpu.SemaphoreType.DMA
    wide = (heads, seq_rows, 128)
    shard_rows = weights[0].shape[0]
    full = [(shards, *weights[0].shape), (shards, shard_rows, sum(w.shape[1] for w in weights[1:]))]
    shapes = [(seq_rows, width), wide, wide, wide, (heads, 80, seq_rows), (heads, 64, seq_rows)]
    made = [jax.ShapeDtypeStruct(s, bf16) for s in shapes]
    return comm_call(
        functools.partial(enter_kernel, parts=parts, size=size),
        "enter",
        number,
        [made[0], jax.ShapeDtypeStruct((4, *segments.shape), segments.dtype)]
        + [jax.ShapeDtypeStruct((seq_rows // size, 128), jnp.int32), jax.ShapeDtypeStruct((16, width), f32)]
        + made[1:]
        + [jax.ShapeDtypeStruct(s, bf16) for s in full],
        [in_vmem()] * (6 + len(vectors)),
        [anywhere()] + [in_vmem()] * 3 + [anywhere()] * 5 + [in_vmem(), anywhere()],
        [pltpu.VMEM((seq_rows, width), bf16)]
        + [pltpu.VMEM(s, bf16) for s in shapes]
        + [dma((parts,))] * 6
        + [dma((3,))] * 2
        + [dma((4, shards))] * 2
        + [dma((2,)), dma((4,)), dma((6, 4 * parts))],
        60 << 20,
        x,
        segments,
        *weights,
        *vectors,
    )


def middle_kernel(
    seq_out, own_ref, passed_ref, x_ref, g_ref, seg_ref, par_ref,
    layer_ref, resid_ref, seq_ref, kept_ref, over_ref, sums_ref,
    attn_ref, fc_ref, pj_ref, ow_ref, attn_cat, ow_cat, act_s, gp_s, in_s, in_t, g_t, low_t, ga_s, out_acc, gn_acc,
    fc_g, pj_g, ow_g, fc_box, pj_box, ow_box,
    sems, rems, ws, wr, sa, ra, sv, rv, own_sem, *, parts
):
    me, side, across, far = quad()
    greet([{"tp": side}, {"tp": across}, {"tp": far}])
    peers = {1: side, 2: across, 3: far}
    rows = x_ref.shape[0]
    step = rows // parts
    lanes = ow_ref.shape[2]
    sums_ref[...] = jnp.zeros_like(sums_ref)

    def own_rows(who, part):
        return seq_out.at[pl.ds(pl.multiple_of(who * rows + part * step, step), step)]

    def send_rows(part, carry):
        here = pl.ds(pl.multiple_of(part * step, step), step)
        for k in (3, 2, 1):
            push(own_rows(peers[k], part), attn_ref.at[k, here], sa.at[k, part], ra.at[k, part], {"tp": peers[k]})
        return carry

    lax.fori_loop(0, parts, send_rows, 0)
    sent, kept, at = [], [], 0
    for n, full in enumerate((fc_ref, pj_ref, ow_ref)):
        cols = pl.ds(at, full.shape[2])
        at += full.shape[2]
        for k, source in ((0, own_ref), (2, passed_ref)):
            block = source.at[:, cols]
            sent.append(push(block, full.at[k + 1], sv.at[k // 2, n], rv.at[k // 2, n], {"tp": side}))
            kept.append(pltpu.make_async_copy(block, full.at[k], own_sem.at[2 * n + k // 2]))
    mine = seq_out.at[pl.ds(pl.multiple_of(me * rows, rows), rows)]
    kept.append(pltpu.make_async_copy(mine, attn_ref.at[0], own_sem.at[6]))
    for copy in kept:
        copy.start()
    for copy in kept:
        copy.wait()
    for copy in sent:
        copy.wait()
    for p in range(4):
        ow_cat[:, p * lanes : (p + 1) * lanes] = ow_ref[p]

    def owner(t):
        near = me + lax.rem(t, 2) * (1 - 2 * lax.rem(me, 2))
        return lax.rem(near + 2 * (t // 2), 4)

    def add_row(row, value):
        at = pl.ds(row, 1)
        sums_ref[at, :] = sums_ref[at, :] + jnp.sum(value, axis=0, keepdims=True)

    def landing(who, part):
        return seq_ref.at[pl.ds(pl.multiple_of(who * rows + part * step, step), step)]

    def row_block(part, carry):
        here = pl.ds(pl.multiple_of(part * step, step), step)
        for k in (1, 2, 3):
            awaited(attn_ref.at[k, here], sa.at[k, part], ra.at[k, part], {"tp": peers[k]}).wait_recv()
        attn = jnp.concatenate([attn_ref[p, here, :] for p in range(4)], axis=1)
        attn_cat[here, :] = attn
        hidden = x_ref[here, :].astype(f32) + dot_t(attn, ow_cat[...]) + par_ref[0:1, :]
        gain = par_ref[1:2, :]
        normed, hat, inverse = layer_norm(hidden, gain, par_ref[2:3, :])
        in_s[...] = normed.astype(bf16)
        in_t[:, here] = normed.T.astype(bf16)
        grad = g_ref[here, :]
        g_t[:, here] = grad.astype(f32).T.astype(bf16)
        out_acc[...] = hidden + par_ref[3:4, :]
        gn_acc[...] = jnp.zeros_like(gn_acc)

        def hidden_block(t, c):
            bias_at = 4 + owner(t)
            pre = dot_n(in_s[...], fc_ref[t]) + par_ref[pl.ds(bias_at, 1), :]
            gate = jax.nn.sigmoid(gelu_slope * pre)
            raised = pre * gate
            act = raised.astype(bf16)
            act_s[t, here, :] = act
            out_acc[...] += dot_t(act, pj_ref[t])
            grad_act = dot_n(g_ref[here, :], pj_ref[t])
            grad_pre = (grad_act * (gate + gelu_slope * raised * (1.0 - gate))).astype(bf16)
            gp_s[t, here, :] = grad_pre
            add_row(bias_at, grad_pre.astype(f32))
            gn_acc[...] += dot_t(grad_pre, fc_ref[t])
            return c

        lax.fori_loop(0, 4, hidden_block, 0)
        layer_ref[here, :] = out_acc[...].astype(bf16)
        grad_in, gain_part, shift_part = norm_back(gn_acc[...], hat, inverse, gain)
        grad_hidden = grad.astype(f32) + grad_in
        resid_ref[here, :] = grad_hidden
        low = grad_hidden.astype(bf16)
        low_t[:, here] = grad_hidden.T.astype(bf16)
        sums_ref[1:2, :] += gain_part[None]
        sums_ref[2:3, :] += shift_part[None]
        add_row(0, low.astype(f32))
        add_row(3, grad.astype(f32))
        seg = jnp.broadcast_to(seg_ref[0:1, here].astype(f32), (8, step)).T[:, 0:1]
        live = jnp.where(seg != 0.0, 1.0, 0.0)
        grad_attn = (dot_n(low, ow_cat[...]).astype(bf16).astype(f32) * live).astype(bf16)
        for k in (1, 2, 3):
            ga_s[k, here, :] = grad_attn[:, k * lanes : (k + 1) * lanes]
        seq_ref[pl.ds(pl.multiple_of(me * rows + part * step, step), step), :] = grad_attn[:, 0:lanes]
        for k in (3, 2, 1):
            push(ga_s.at[k, here], landing(me, part), sems.at[k, part], rems.at[k, part], {"tp": peers[k]})
        return carry

    lax.fori_loop(0, parts, row_block, 0)
    width = out_acc.shape[1]
    tall = 512

    def out_block(n, carry):
        at = pl.ds(pl.multiple_of(n * tall, tall), tall)
        grad = dot_n(low_t[at, :], attn_cat[...]).astype(bf16)
        for p in range(4):
            ow_g[p, at, :] = grad[:, p * lanes : (p + 1) * lanes]
        return carry

    lax.fori_loop(0, width // tall, out_block, 0)
    triples = ((fc_g, fc_box), (pj_g, pj_box), (ow_g, ow_box))

    def fold(n, b):
        grad, box = triples[n]
        return grad.at[2 * b + 1], box.at[b], ws.at[n, b], wr.at[n, b], {"tp": side}

    for b in (1, 0):
        push(*fold(2, b))

    def slice_block(u, carry):
        t = 3 - 2 * u + 3 * (u // 2)

        def fc_block(n, c):
            at = pl.ds(pl.multiple_of(n * tall, tall), tall)
            fc_g[t, at, :] = dot_n(in_t[at, :], gp_s[t]).astype(bf16)
            pj_g[t, at, :] = dot_n(g_t[at, :], act_s[t]).astype(bf16)
            return c

        lax.fori_loop(0, width // tall, fc_block, 0)
        for b in (1, 0):

            @pl.when(u == 1 - b)
            def _():
                push(*fold(0, b))
                push(*fold(1, b))

        return carry

    lax.fori_loop(0, 4, slice_block, 0)
    for b, target in ((1, over_ref), (0, kept_ref)):
        at = 0
        for n, (grad, box) in enumerate(triples):
            cols = slice(at, at + grad.shape[2])
            at += grad.shape[2]
            awaited(box.at[b], ws.at[n, b], wr.at[n, b], {"tp": side}).wait_recv()
            target[:, cols] = (grad[2 * b].astype(f32) + box[b].astype(f32)).astype(bf16)

    def drain(part, carry):
        here = pl.ds(pl.multiple_of(part * step, step), step)
        for k in (1, 2, 3):
            peer = {"tp": peers[k]}
            awaited(landing(peers[k], part), sems.at[k, part], rems.at[k, part], peer).wait_recv()
            awaited(ga_s.at[k, here], sems.at[k, part], rems.at[k, part], peer).wait_send()
            awaited(own_rows(peers[k], part), sa.at[k, part], ra.at[k, part], peer).wait_send()
        return carry

    lax.fori_loop(0, parts, drain, 0)
    for n, (grad, box) in enumerate(triples):
        for b in (1, 0):
            awaited(grad.at[2 * b + 1], ws.at[n, b], wr.at[n, b], {"tp": side}).wait_send()


def middle(attn, own, passed, x, grad, segments, params, hidden, number, parts=2):
    rows, lanes = x.shape[0], attn.shape[1]
    width = x.shape[1]
    fc = pj = (4, width, hidden)
    ow = (4, width, lanes)
    step = rows // parts
    dma = pltpu.SemaphoreType.DMA
    total = 2 * hidden + lanes
    low, wide = bf16, f32
    scratch = [
        ((4, rows, lanes), low), (fc, low), (pj, low), (ow, low),
        ((rows, width), low), ((width, 4 * lanes), low),
        ((4, rows, hidden), low), ((4, rows, hidden), low),
        ((step, width), low), ((width, rows), low), ((width, rows), low), ((width, rows), low),
        ((4, rows, lanes), low), ((step, width), wide), ((step, width), wide),
        (fc, low), (pj, low), (ow, low),
        ((2, *fc[1:]), low), ((2, *pj[1:]), low), ((2, *ow[1:]), low),
    ]
    outs = [
        ((rows, width), low), ((rows, width), wide), ((4 * rows, lanes), low),
        ((width, total), low), ((width, total), low), ((8, width), wide),
    ]
    return comm_call(
        functools.partial(middle_kernel, parts=parts),
        "middle",
        number,
        [jax.ShapeDtypeStruct(s, d) for s, d in outs],
        [in_vmem(), anywhere(), anywhere()] + [in_vmem()] * 4,
        [in_vmem()] * 6,
        [pltpu.VMEM(s, d) for s, d in scratch]
        + [dma((4, parts)), dma((4, parts)), dma((3, 2)), dma((3, 2))]
        + [dma((4, parts)), dma((4, parts)), dma((2, 3)), dma((2, 3)), dma((7,))],
        60 << 20,
        attn,
        own,
        passed,
        x,
        grad,
        segments,
        params,
    )


def leave_kernel(
    grad_ref, normed_in, w_ref, kept_ref, came_ref, early_ref, x_in, gain_ref, resid_in,
    input_ref, s0, s1, s2, s3, early_out, late_out,
    rows_ref, far_out, own_out, sum_buf, side_far, side_own, over, dw_acc, cols_ref,
    late_ref, early_mid, late_mid, early_one, early_two, late_one, late_two,
    normed_ref, x_ref, resid_ref, loads,
    sa, ra, sb, rb, sy, ry, sw, rw, se, re, sl, rl, se2, re2, sl2, rl2, *bufs, parts, hops
):
    me, side, across, far = quad()
    rows = rows_ref.shape[0]
    step = rows // parts
    shard, shards = lax.axis_index("fsdp"), early_two.shape[0]
    pairs = ((normed_in, normed_ref), (x_in, x_ref), (resid_in, resid_ref))
    loading = [pltpu.make_async_copy(a, b, loads.at[n]) for n, (a, b) in enumerate(pairs)]
    for copy in loading:
        copy.start()
    barrier = pltpu.get_barrier_semaphore()
    for peer in (side, across, far):
        pl.semaphore_signal(barrier, inc=1, device_id={"tp": peer}, device_id_type=MESH)

    def other(k):
        return {"fsdp": lax.rem(shard + k, shards)}

    def signal(k, carry):
        pl.semaphore_signal(barrier, inc=1, device_id=other(k), device_id_type=MESH)
        return carry

    lax.fori_loop(1, shards, signal, 0)
    pl.semaphore_wait(barrier, 3 + shards - 1)
    count = len(hops)
    outs = (s0, s1, s2, s3)
    swapped = (0, 2) if count > 1 else ()
    current = bufs[0:4]
    boxes = [bufs[4 + g * count : 4 + (g + 1) * count] for g in range(4)]
    keeps = [bufs[4 + 4 * count + g * (count - 1) : 4 + 4 * count + (g + 1) * (count - 1)] for g in range(4)]
    sent = []

    def begin(g):
        at = sum(c.shape[3] for c in current[0:g])
        cols = slice(at, at + current[g].shape[3])
        if g not in swapped:
            total = kept_ref[:, :, :, cols].astype(f32) + came_ref[:, :, :, cols].astype(f32)
            current[g][...] = total.astype(bf16)
            return
        for p in range(current[g].shape[0]):
            for q in range(2):
                i, j = (p // 2) * 2 + q, p % 2
                total = kept_ref[i, j, :, cols].astype(f32) + came_ref[i, j, :, cols].astype(f32)
                current[g][p, q] = total.astype(bf16)

    def hop_parts(g, k):
        axis, bit = hops[(1, 0, *range(2, count))[k] if g in swapped else k]
        source = current[g] if k == 0 else keeps[g][k - 1]
        half = lax.rem(lax.axis_index(axis) // bit, 2)
        return {axis: flip(axis, bit)}, source, half, boxes[g][k]

    def hop_send(g, k):
        peer, source, half, box = hop_parts(g, k)
        sent.append(push(source.at[:, 1 - half], box, sw.at[g, k], rw.at[g, k], peer))

    def hop_add(g, k):
        peer, source, half, box = hop_parts(g, k)
        awaited(box, sw.at[g, k], rw.at[g, k], peer).wait_recv()
        if k == count - 1:
            outs[g][...] = source[0, half].astype(f32) + box[0].astype(f32)
        else:
            target = keeps[g][k]
            for n in range(box.shape[0]):
                total = source[n, half].astype(f32) + box[n].astype(f32)
                target[n // 2, n % 2] = total.astype(bf16)
            hop_send(g, k + 1)

    def tp_send(value, box, send, recv):
        box[me] = value[...]
        for k, peer in enumerate((side, across, far)):
            sent.append(push(value, box.at[me], send.at[k], recv.at[me], {"tp": peer}))

    def tp_sum(value, box, send, recv):
        for k, peer in enumerate((side, across, far)):
            awaited(box.at[peer], send.at[k], recv.at[peer], {"tp": peer}).wait_recv()
        value[...] = box[0] + box[1] + box[2] + box[3]

    def fsdp_send(value, box, send, recv):
        box[shard] = value[...]

        def give(k, carry):
            push(value, box.at[shard], send.at[k], recv.at[shard], other(k))
            return carry

        lax.fori_loop(1, shards, give, 0)

    def fsdp_sum(value, target, box, send, recv):
        def take(k, carry):
            peer = lax.rem(shard + k, shards)
            copy = awaited(box.at[peer], send.at[k], recv.at[peer], other(k))
            copy.wait_recv()
            copy.wait_send()
            return carry

        lax.fori_loop(1, shards, take, 0)
        target[...] = lax.fori_loop(1, shards, lambda n, total: total + box[n], box[0])

    def span(owner, part):
        return pl.ds(pl.multiple_of(owner * rows + part * step, step), step)

    def piece(part):
        return pl.ds(pl.multiple_of(part * step, step), step)

    def partial(owner, part):
        return dot_t(grad_ref[span(owner, part), :], w_ref[...])

    def give_far(part, carry):
        here = piece(part)
        far_out[here, :] = partial(far, part).astype(bf16)
        push(far_out.at[here], side_far.at[here], sa.at[part], ra.at[part], {"tp": side})
        return carry

    def give_over(part, carry):
        here = piece(part)
        mine = partial(across, part)
        awaited(side_far.at[here], sa.at[part], ra.at[part], {"tp": side}).wait_recv()
        sum_buf[here, :] = (mine + side_far[here, :].astype(f32)).astype(bf16)
        push(sum_buf.at[here], over.at[here], sy.at[part], ry.at[part], {"tp": across})
        return carry

    def give_own(part, carry):
        here = piece(part)
        own_out[here, :] = partial(side, part).astype(bf16)
        push(own_out.at[here], side_own.at[here], sb.at[part], rb.at[part], {"tp": side})
        return carry

    def take_own(part, carry):
        here = piece(part)
        mine = partial(me, part)
        awaited(side_own.at[here], sb.at[part], rb.at[part], {"tp": side}).wait_recv()
        rows_ref[here, :] = mine + side_own[here, :].astype(f32)
        return carry

    gain = gain_ref[8:9, :]

    def take_over(part, carry):
        here = piece(part)
        x = x_ref[here, :].astype(f32)
        centred = x - jnp.mean(x, axis=-1, keepdims=True)
        inverse = lax.rsqrt(jnp.mean(centred * centred, axis=-1, keepdims=True) + epsilon)
        normed = centred * inverse
        awaited(over.at[here], sy.at[part], ry.at[part], {"tp": across}).wait_recv()
        grad = rows_ref[here, :] + over[here, :].astype(f32)
        grad_in, gain_part, shift_part = norm_back(grad, normed, inverse, gain)
        input_ref[here, :] = (resid_ref[here, :] + grad_in).astype(bf16)
        late_ref[0:1, :] += gain_part[None]
        late_ref[1:2, :] += shift_part[None]
        return carry

    def drain(part, carry):
        here = piece(part)
        awaited(far_out.at[here], sa.at[part], ra.at[part], {"tp": side}).wait_send()
        awaited(own_out.at[here], sb.at[part], rb.at[part], {"tp": side}).wait_send()
        awaited(sum_buf.at[here], sy.at[part], ry.at[part], {"tp": across}).wait_send()
        return carry

    chunk = 1024
    steps = grad_ref.shape[0] // chunk
    dw_acc[...] = jnp.zeros_like(dw_acc)
    cols_ref[...] = jnp.zeros_like(cols_ref)
    ones = jnp.ones((8, chunk), bf16)

    def weight_grad(n, carry):
        at = pl.ds(pl.multiple_of(n * chunk, chunk), chunk)
        g = grad_ref[at, :]
        dw_acc[...] += lax.dot_general(
            normed_ref[at, :], g, (((0,), (0,)), ((), ())), preferred_element_type=f32
        )
        cols_ref[...] += dot_n(ones, g)
        return carry

    tp_send(early_ref, early_one, se, re)
    begin(0)
    hop_send(0, 0)
    lax.fori_loop(0, parts, give_far, 0)
    begin(1)
    hop_send(1, 0)
    lax.fori_loop(0, parts, give_over, 0)
    begin(2)
    for copy in loading:
        copy.wait()
    lax.fori_loop(0, steps // 2, weight_grad, 0)
    hop_add(0, 0)
    lax.fori_loop(steps // 2, steps, weight_grad, 0)
    current[3][...] = dw_acc[...].astype(bf16).reshape(current[3].shape)
    hop_send(3, 0)
    hop_send(2, 0)
    tp_sum(early_mid, early_one, se, re)
    fsdp_send(early_mid, early_two, se2, re2)
    hop_add(1, 0)
    late_ref[...] = jnp.zeros_like(late_ref)
    wide = cols_ref.shape[1] // 3
    qv_at = pl.ds(pl.multiple_of(me * wide, wide), wide)
    late_ref[2:3, qv_at] = cols_ref[0:1, 0:wide]
    late_ref[3:4, qv_at] = cols_ref[0:1, 2 * wide : 3 * wide]
    lax.fori_loop(0, parts, give_own, 0)
    turns = enumerate((0, 1, 3, 2))
    order = sorted((k + turn, turn, g, k) for turn, g in turns for k in range(count))
    order = [(g, k) for _, _, g, k in order if (g, k) not in ((0, 0), (1, 0))]
    lax.fori_loop(0, parts, take_own, 0)
    taken = {len(order) * share // 10: span for share, span in ((6, (0, 2)), (7, (2, 3)), (9, (3, 4)))}
    for n, (g, k) in enumerate(order):
        if n in taken:
            first, last = taken[n]
            lax.fori_loop(first * parts // 4, last * parts // 4, take_over, 0)
        if n == len(order) - 1:
            tp_send(late_ref, late_one, sl, rl)
        hop_add(g, k)
    fsdp_sum(early_mid, early_out, early_two, se2, re2)
    tp_sum(late_mid, late_one, sl, rl)
    fsdp_send(late_mid, late_two, sl2, rl2)
    lax.fori_loop(0, parts, drain, 0)
    fsdp_sum(late_mid, late_out, late_two, sl2, rl2)
    for copy in sent:
        copy.wait_send()


def leave(grad, normed, w, kept, came, widths, early, x, gain, resid, number, parts=2):
    rows, width = grad.shape[0] // 4, w.shape[0]
    dma = pltpu.SemaphoreType.DMA
    hops = bits_of("fsdp")
    count = len(hops)
    shards = lax.axis_size("fsdp")
    shard = width // shards
    widths = [*widths, grad.shape[1]]
    split = (shards // 2, 2, shard)
    current = [pltpu.VMEM((*split, n), bf16) for n in widths]
    boxes = [pltpu.VMEM((shards >> (k + 1), shard, n), bf16) for n in widths for k in range(count)]
    keeps = [pltpu.VMEM((shards >> (k + 2), 2, shard, n), bf16) for n in widths for k in range(count - 1)]
    late = (4, width)
    return comm_call(
        functools.partial(leave_kernel, parts=parts, hops=hops),
        "leave",
        number,
        [jax.ShapeDtypeStruct((rows, width), bf16)]
        + [jax.ShapeDtypeStruct((shard, n), f32) for n in widths]
        + [jax.ShapeDtypeStruct(early.shape, f32), jax.ShapeDtypeStruct(late, f32)],
        [in_vmem(), anywhere()] + [in_vmem()] * 4 + [anywhere(), in_vmem(), anywhere()],
        [in_vmem()] * 7,
        [pltpu.VMEM((rows, width), f32)]
        + [pltpu.VMEM((rows, width), bf16)] * 6
        + [pltpu.VMEM((width, grad.shape[1]), f32), pltpu.VMEM((8, grad.shape[1]), f32)]
        + [pltpu.VMEM(late, f32), pltpu.VMEM(early.shape, f32), pltpu.VMEM(late, f32)]
        + [pltpu.VMEM((n, *shape), f32) for shape in (early.shape, late) for n in (4, shards)]
        + [pltpu.VMEM(v.shape, v.dtype) for v in (normed, x, resid)]
        + [dma((3,))]
        + [dma((parts,))] * 6
        + [dma((4, count))] * 2
        + [dma((3,)), dma((4,))] * 2
        + [dma((shards,))] * 4
        + current
        + boxes
        + keeps,
        60 << 20,
        grad,
        normed,
        w,
        kept.reshape(*split, kept.shape[1]),
        came.reshape(*split, came.shape[1]),
        early,
        x,
        gain,
        resid,
    )


def finish_kernel(
    rows_in, fc_in, proj_in, out_in, qkv_in, early_in, late_in,
    rows_ref, fc_ref, proj_ref, out_ref, qkv_ref, qv_ref, *vectors
):
    rows_ref[...] = rows_in[...]
    fc_ref[...] = fc_in[...]
    proj_ref[...] = proj_in[...]
    out_ref[...] = out_in[...]
    width = qkv_ref.shape[2]
    for n in range(3):
        qkv_ref[n] = qkv_in[:, n * width : (n + 1) * width]
    qv_ref[...] = late_in[2:4, :]
    first_gain, first_shift, out_bias, gain, shift, fc_bias, proj_bias = vectors
    lanes = first_gain.shape[1]
    count = first_gain.shape[0]
    singles = ((first_gain, late_in, 0), (first_shift, late_in, 1), (out_bias, early_in, 0))
    singles += ((gain, early_in, 1), (shift, early_in, 2), (proj_bias, early_in, 3))
    for ref, source, row in singles:
        for n in range(count):
            ref[n : n + 1, :] = source[row : row + 1, n * lanes : (n + 1) * lanes]
    for row in range(4):
        for n in range(count):
            at = row * count + n
            fc_bias[at : at + 1, :] = early_in[4 + row : 5 + row, n * lanes : (n + 1) * lanes]


def finish(rows, fc, proj, out, qkv, early, late):
    lanes = 128
    width = late.shape[1]
    shapes = [rows, fc, proj, out]
    outs = [jax.ShapeDtypeStruct(v.shape, v.dtype) for v in shapes]
    outs.append(jax.ShapeDtypeStruct((3, qkv.shape[0], qkv.shape[1] // 3), f32))
    outs.append(jax.ShapeDtypeStruct((2, width), f32))
    sizes = [width] * 5 + [4 * early.shape[1], width]
    outs += [jax.ShapeDtypeStruct((n // lanes, lanes), f32) for n in sizes]
    rows, fc, proj, out, qkv, qv, *vectors = pl.pallas_call(
        finish_kernel,
        out_shape=outs,
        in_specs=[in_vmem()] * 7,
        out_specs=[in_vmem()] * len(outs),
        cost_estimate=pl.CostEstimate(flops=0, bytes_accessed=3 << 20, transcendentals=0),
        name="finish",
    )(rows, fc, proj, out, qkv, early, late)
    return rows, fc, proj.T, out.T, qkv.transpose(1, 0, 2), qv, [v.reshape(-1) for v in vectors]


def flip(axis, bit):
    me = lax.axis_index(axis)
    return me + bit - 2 * bit * lax.rem(me // bit, 2)


def bits_of(axis):
    size, bits, bit = lax.axis_size(axis), [], 1
    while bit < size:
        bits.append((axis, bit))
        bit *= 2
    return bits


def across(value):
    return lax.ppermute(value, "tp", [(n, n ^ 2) for n in range(4)])


def local(
    inputs,
    segments,
    out_grad,
    first_gain,
    first_shift,
    qkv_weight,
    qv_bias,
    out_weight,
    out_bias,
    second_gain,
    second_shift,
    fc_weight,
    fc_bias,
    proj_weight,
    proj_bias,
):
    slices = lax.axis_size("tp")
    rows_here, model_width = inputs.shape
    shard_rows = qkv_weight.shape[0]
    head_cols = qkv_weight.shape[2]
    hidden_cols = fc_weight.shape[1]
    vectors = (out_bias, second_gain, second_shift, proj_bias, fc_bias, first_gain, first_shift, qv_bias)
    size = min(BLOCK, rows_here)
    seq_normed, seg_parts, low, params, qa, ka, va, vt, kt, qkv_full, own = enter(
        inputs,
        vectors,
        segments,
        (qkv_weight.reshape(shard_rows, 3 * head_cols), fc_weight, proj_weight.T, out_weight.T),
        size,
        0,
    )
    qkv_full = qkv_full.reshape(model_width, 3 * head_cols)
    own = own.reshape(model_width, own.shape[2])
    over = across(own)
    widths = (hidden_cols, hidden_cols, head_cols)

    attn_out, qb = attend(low, qa, ka, vt, seg_parts, size)

    layer_out, grad_hidden, grad_attn_seq, kept, passed, early = middle(
        attn_out, own, over, inputs, out_grad, segments, params, hidden_cols, 2
    )
    came = across(passed)
    grad_qkv = attend_back(low, qb, ka, va, kt, grad_attn_seq, attn_out, seg_parts, size)
    input_grad, fc_w_grad, proj_w_grad, out_w_grad, qkv_grad, early_sums, late_sums = leave(
        grad_qkv,
        seq_normed,
        qkv_full,
        kept,
        came,
        widths,
        early,
        inputs,
        params,
        grad_hidden,
        3,
    )
    input_grad, fc_w_grad, proj_w_grad, out_w_grad, qkv_grad, qv_bias_grad, vectors = finish(
        input_grad,
        fc_w_grad,
        proj_w_grad,
        out_w_grad,
        qkv_grad,
        early_sums,
        late_sums,
    )
    first_gain_grad, first_shift_grad, out_bias_grad, second_gain_grad, second_shift_grad = vectors[0:5]
    fc_bias_grad, proj_bias_grad = vectors[5:7]

    return (
        layer_out,
        input_grad,
        first_gain_grad,
        first_shift_grad,
        qkv_grad,
        qv_bias_grad,
        out_w_grad,
        out_bias_grad,
        second_gain_grad,
        second_shift_grad,
        fc_w_grad,
        fc_bias_grad,
        proj_w_grad,
        proj_bias_grad,
    )


def solution(mesh):
    return jax.shard_map(
        local,
        mesh=mesh,
        in_specs=(
            P(("fsdp", "tp"), None),
            P("fsdp", "tp"),
            P(("fsdp", "tp"), None),
            P(),
            P(),
            P("fsdp", None, "tp"),
            P(),
            P("tp", "fsdp"),
            P(),
            P(),
            P(),
            P("fsdp", "tp"),
            P(),
            P("tp", "fsdp"),
            P(),
        ),
        out_specs=(
            P(("fsdp", "tp"), None),
            P(("fsdp", "tp"), None),
            P(),
            P(),
            P("fsdp", None, "tp"),
            P(),
            P("tp", "fsdp"),
            P(),
            P(),
            P(),
            P("fsdp", "tp"),
            P(),
            P("tp", "fsdp"),
            P(),
        ),
        check_vma=False,
    )
```
